32 devices in a mesh: expert: 8 (over z, y), shard: 4 (over x, core).
Axes of the slice: x: 2, y: 2, z: 4, core: 2. Of those that a mesh axis runs over, the one named last changes fastest.
Arguments:
- inputs: bfloat16 [2048, 4, 1024], P('expert', 'shard'), may hold values from -6 to 6
- grad_out: bfloat16 [2048, 4, 1024], P('expert', 'shard'), may hold values from -6 to 6
- prefix: int32 [4], P('shard'), may hold values from 204 to 1024
- routes: int32 [2048, 4, 2], P('expert', 'shard'), may hold values from 0 to 31, all different within a row
- priority: int32 [8, 4, 256], P('expert', 'shard'), may hold values from 0 to 255, each once within a row
- loss_weights: float32 [2], replicated, may hold values from 4 to 32
- norm_attn: bfloat16 [1024], P('shard'), may hold values from 0.5 to 1.5
- norm_moe: bfloat16 [1024], P('shard'), may hold values from 0.5 to 1.5
- qkv_weight: bfloat16 [1024, 3072], P('shard'), may hold values from -0.1875 to 0.1875
- out_weight: bfloat16 [1024, 1024], P('shard'), may hold values from -3 to 3
- bias_table: bfloat16 [32, 16], P('shard'), may hold values from -5 to 5
- router_weight: bfloat16 [1024, 32], P('shard'), may hold values from -0.09375 to 0.09375
- gate_weight: bfloat16 [32, 1024, 2816], P('expert', None, 'shard'), may hold values from -0.1875 to 0.1875
- up_weight: bfloat16 [32, 1024, 2816], P('expert', None, 'shard'), may hold values from -0.1875 to 0.1875
- down_weight: bfloat16 [32, 1024, 2816], P('expert', None, 'shard'), may hold values from -0.109375 to 0.109375
Outputs:
- output: bfloat16 [2048, 4, 1024], P('expert', 'shard')
- input_grad: float32 [2048, 4, 1024], P('expert', 'shard')
- norm_attn_grad: float32 [1024], P('shard')
- norm_moe_grad: float32 [1024], P('shard')
- qkv_grad: float32 [1024, 3072], P('shard')
- out_grad: float32 [1024, 1024], P('shard')
- table_grad: float32 [32, 16], P('shard')
- router_grad: float32 [1024, 32], P('shard')
- gate_grad: float32 [32, 1024, 2816], P('expert', None, 'shard')
- up_grad: float32 [32, 1024, 2816], P('expert', None, 'shard')
- down_grad: float32 [32, 1024, 2816], P('expert', None, 'shard')
The draws below stay inside these ranges and needn't reach their ends.
Inputs may be any that keep to these rules, and one draw needn't show every extreme that they name: `routes`: the 2 experts of a token differ. Each row priority[g, s] is a permutation of 0 to 255.
All inputs are finite; a program needn't handle non-finite values.
Results may differ from the reference program's by a relative error of at most 0.04.
Values may be sent and summed in bfloat16 or wider, within the bound.
A program may use at most 448 MiB of HBM per device.

```python
import math
import jax
import jax.numpy as jnp
from jax import lax

D = 1024
HEADS = 16
HEAD = 64
FF = 2816
EXPERTS = 32
TOP = 2
BUCKETS = 32
TOK_DEV = 256
LENGTH = 2048
SEQS = 4
GROUPS = 32
CAP = 18
N_EXPERT = 8


def place_ends(values, stream_key, least, largest):
    place = [jax.random.randint(jax.random.fold_in(stream_key, axis), (), 0, length) for axis, length in enumerate(values.shape)]
    main_axis = values.shape.index(max(values.shape))
    neighbour = place[:main_axis] + [(place[main_axis] + 1) % values.shape[main_axis]] + place[main_axis + 1:]
    return values.at[tuple(place)].set(least).at[tuple(neighbour)].set(largest)


def levels(stream_key, shape, cuts, smallest, largest):
    level = 1.0
    for axis_at, shards_of in cuts:
        draws = jax.random.uniform(jax.random.fold_in(jax.random.fold_in(stream_key, 6), axis_at), (shards_of,), jnp.float32, smallest / len(cuts), largest / len(cuts))
        level = level * jnp.repeat(jnp.exp(draws), shape[axis_at] // shards_of).reshape((-1,) + (1,) * (len(shape) - 1 - axis_at))
    return level


def picks_of(rng, rows, amount, top, lift):
    sequence = jax.random.permutation(jax.random.fold_in(rng, 1), amount)
    pull = sequence
    for power in range(3):
        pull = pull * pull // amount
    pull = pull * lift // amount
    chance = jax.random.randint(jax.random.fold_in(rng, 2), (rows, amount), 0, 4096) + pull
    fixed_rows = jax.random.permutation(jax.random.fold_in(rng, 3), rows)[jnp.arange(amount) % rows]
    chance = jnp.where(jnp.arange(rows)[:, None] == fixed_rows[None, :], 1 << 14, chance)
    score = chance * amount + jnp.arange(amount)
    return lax.top_k(score.astype(jnp.int32), top)[1].astype(jnp.int32)


def noise(stream_key, extent, spread, limit, split=(), kind=jnp.bfloat16):
    values = spread * jax.random.normal(stream_key, extent, jnp.float32)
    if split:
        values = values * levels(stream_key, extent, split, -0.22, 0.18)
    return jnp.clip(values, -limit, limit).astype(kind)


def setup_inputs(seed: int = 0) -> dict:
    splits = jax.random.split(jax.random.key(seed), 16)
    return {
        "inputs": noise(splits[0], (LENGTH, SEQS, D), 1.0, 6.0, ((0, 8), (1, 4))),
        "grad_out": noise(splits[1], (LENGTH, SEQS, D), 1.0, 6.0, ((0, 8), (1, 4))),
        "prefix": place_ends(jax.random.randint(splits[2], (SEQS,), LENGTH // 10, LENGTH // 2 + 1), jax.random.fold_in(splits[2], 1), LENGTH // 10, (LENGTH // 2 + 1) - 1).astype(jnp.int32),
        "routes": picks_of(splits[3], LENGTH * SEQS, EXPERTS, TOP, 512).reshape((LENGTH, SEQS, TOP)),
        "priority": jax.vmap(lambda own: jax.random.permutation(own, TOK_DEV))(jax.random.split(splits[4], N_EXPERT * SEQS)).reshape((N_EXPERT, SEQS, TOK_DEV)).astype(jnp.int32),
        "loss_weights": jnp.clip(jnp.exp(jax.random.uniform(splits[5], (2,), jnp.float32, math.log(4.0), math.log(32.0))), 4.0, 32.0),
        "norm_attn": jnp.clip(1.0 + 0.1 * jax.random.normal(splits[6], (D,), jnp.float32), 0.5, 1.5).astype(jnp.bfloat16),
        "norm_moe": jnp.clip(1.0 + 0.1 * jax.random.normal(splits[7], (D,), jnp.float32), 0.5, 1.5).astype(jnp.bfloat16),
        "qkv_weight": noise(splits[8], (D, 3 * D), D ** -0.5, 0.1875, ((0, 4),)),
        "out_weight": noise(splits[9], (D, D), (max(D // 256, 1)) ** -0.5, 3.0, ((0, 4),)),
        "bias_table": noise(splits[10], (BUCKETS, HEADS), 1.0, 5.0, ((0, 4),)),
        "router_weight": noise(splits[11], (D, EXPERTS), (4 * D) ** -0.5, 0.09375, ((0, 4),)),
        "gate_weight": noise(splits[12], (EXPERTS, D, FF), D ** -0.5, 0.1875, ((0, 8), (2, 4))),
        "up_weight": noise(splits[13], (EXPERTS, D, FF), D ** -0.5, 0.1875, ((0, 8), (2, 4))),
        "down_weight": noise(splits[14], (EXPERTS, D, FF), FF ** -0.5, 0.109375, ((0, 8), (2, 4))),
    }


epsilon = 1e-06
masked_score = -1e+30
far_bounds = (12, 16, 23, 32, 46, 64, 91)

@jax.custom_vjp
def low(v):
    return lax.optimization_barrier(v.astype(jnp.bfloat16)).astype(jnp.float32)

@jax.custom_vjp
def low_back(v):
    return v

def low_keep(v):
    return (low(v), None)

def low_pass(kept, grad):
    return (grad,)

def back_keep(v):
    return (v, None)

def back_low(kept, grad):
    return (low(grad),)
low.defvjp(low_keep, low_pass)
low_back.defvjp(back_keep, back_low)

def widen(array_in):
    return array_in.astype(jnp.float32)

def rms_norm(features, scales):
    factor = lax.rsqrt(lax.optimization_barrier(jnp.mean(features * features, axis=-1, keepdims=True)) + epsilon)
    return features * factor * scales

def geglu(gate_act, up_act):
    return jax.nn.gelu(gate_act, approximate=True) * up_act

def bucket_of(offsets):
    distance = jnp.abs(offsets)
    thresholds = jnp.array(far_bounds, dtype=jnp.int32)
    beyond = 8 + lax.optimization_barrier(jnp.sum((distance[..., None] >= thresholds).astype(jnp.int32), axis=-1))
    nearby = jnp.where(distance < 8, distance, beyond)
    return (nearby + 16 * (offsets > 0).astype(jnp.int32)).astype(jnp.int32)

def pair_dest(token_routes, ranks):
    row_count = token_routes.shape[0]
    expert_pair = jnp.concatenate([token_routes[:, 0], token_routes[:, 1]])
    rank_pair = jnp.concatenate([ranks, ranks + row_count])
    earlier = (expert_pair[None, :] == expert_pair[:, None]) & (rank_pair[None, :] < rank_pair[:, None])
    slot_index = lax.optimization_barrier(jnp.sum(earlier.astype(jnp.int32), axis=1)).astype(jnp.int32)
    return jnp.where(slot_index < CAP, expert_pair * CAP + slot_index, EXPERTS * CAP).astype(jnp.int32)

def router_head(logits, token_routes, weights):
    token_count = logits.shape[0]
    probabilities = jax.nn.softmax(logits, axis=-1)
    log_totals = jax.nn.logsumexp(logits, axis=-1)
    picked = (token_routes[:, :, None] == jnp.arange(EXPERTS, dtype=jnp.int32)).astype(jnp.float32)
    chosen = lax.optimization_barrier(jnp.sum(picked * probabilities[:, None, :], axis=-1))
    gate_values = chosen / lax.optimization_barrier(jnp.sum(chosen, axis=1, keepdims=True))
    shares = lax.optimization_barrier(jnp.sum(picked, axis=(0, 1))) / (token_count * TOP)
    balance = EXPERTS * jnp.sum(shares * lax.optimization_barrier(jnp.sum(probabilities, axis=0)))
    return (gate_values, weights[0] * jnp.sum(log_totals * log_totals) + weights[1] * balance)

def by_group(array_in):
    width_last = array_in.shape[-1]
    grouped = jnp.transpose(array_in.reshape(N_EXPERT, TOK_DEV, SEQS, width_last), (0, 2, 1, 3))
    return grouped.reshape(GROUPS, TOK_DEV, width_last)

def by_sequence(array_in):
    return jnp.transpose(array_in, (1, 0, 2)).reshape(SEQS, LENGTH, HEADS, HEAD)

def attend_block(query_block, keys_seq, values_seq, block_start, prefix_len, table):
    block_rows = query_block.shape[0]
    row_pos = block_start + jnp.arange(block_rows, dtype=jnp.int32)
    key_pos = jnp.arange(LENGTH, dtype=jnp.int32)
    visible = (key_pos[None, :] <= row_pos[:, None]) | (key_pos[None, :] < prefix_len)
    bias_block = jnp.transpose(table[bucket_of(key_pos[None, :] - row_pos[:, None])], (2, 0, 1))
    raw_scores = low_back(jnp.einsum('qhc,khc->hqk', query_block, keys_seq, precision=lax.Precision.HIGHEST))
    scores = jnp.where(visible[None], raw_scores * HEAD ** (-0.5) + bias_block, masked_score)
    weights_low = low(jax.nn.softmax(scores, axis=-1))
    mixed = jnp.einsum('hqk,khc->qhc', weights_low, values_seq, precision=lax.Precision.HIGHEST)
    return low_back(low(mixed))

def attend_sequence(queries_seq, keys_seq, values_seq, prefix_len, table):
    block_rows = math.gcd(LENGTH, 512)
    blocks = LENGTH // block_rows
    starts = jnp.arange(blocks, dtype=jnp.int32) * block_rows
    step_block = jax.checkpoint(lambda packed: attend_block(packed[0], keys_seq, values_seq, packed[1], prefix_len, table))
    mixed = lax.map(step_block, (queries_seq.reshape(blocks, block_rows, HEADS, HEAD), starts))
    return mixed.reshape(LENGTH, HEADS * HEAD)

def expert_rows(slot_rows, gate_full, up_full, down_full):
    gate_act = low_back(jnp.dot(slot_rows, gate_full, precision=lax.Precision.HIGHEST))
    up_act = low_back(jnp.dot(slot_rows, up_full, precision=lax.Precision.HIGHEST))
    hidden = low(geglu(gate_act, up_act))
    result = jnp.dot(hidden, down_full.T, precision=lax.Precision.HIGHEST)
    return low_back(low(result))

def forward(tokens, gain_attn, gain_moe, qkv_full, out_full, table, router_full, gate_full, up_full, down_full, prefix, token_routes, destination, loss_weights):
    normed_one = low(rms_norm(tokens, gain_attn))
    projected = jnp.dot(normed_one, qkv_full, precision=lax.Precision.HIGHEST)
    queries = low_back(low(projected[..., :D]))
    keys_all = low_back(low(projected[..., D:2 * D]))
    values_all = low_back(low(projected[..., 2 * D:]))
    attended = lax.map(lambda packed: attend_sequence(packed[0], packed[1], packed[2], packed[3], table), (by_sequence(queries), by_sequence(keys_all), by_sequence(values_all), prefix))
    attended = jnp.transpose(attended, (1, 0, 2))
    middle = tokens + low_back(jnp.dot(attended, out_full, precision=lax.Precision.HIGHEST))
    normed_two = low(rms_norm(middle, gain_moe))
    logits = low_back(jnp.dot(normed_two, router_full, precision=lax.Precision.HIGHEST))
    gate_values, aux_terms = jax.vmap(router_head, in_axes=(0, 0, None))(by_group(logits), token_routes, loss_weights)
    grouped = by_group(normed_two)
    paired = jnp.concatenate([grouped, grouped], axis=1)
    buffers = jax.vmap(lambda rows_in, where_to: jnp.zeros((EXPERTS * CAP + 1, D), jnp.float32).at[where_to].add(rows_in))(paired, destination)
    slots_in = low_back(buffers[:, :EXPERTS * CAP].reshape(GROUPS, EXPERTS, CAP, D))
    by_expert = jnp.transpose(slots_in, (1, 0, 2, 3)).reshape(EXPERTS, GROUPS * CAP, D)
    results = lax.map(jax.checkpoint(lambda packed: expert_rows(packed[0], packed[1], packed[2], packed[3])), (by_expert, gate_full, up_full, down_full))
    results = jnp.transpose(results.reshape(EXPERTS, GROUPS, CAP, D), (1, 0, 2, 3)).reshape(GROUPS, EXPERTS * CAP, D)
    padded = jnp.concatenate([results, jnp.zeros((GROUPS, 1, D), jnp.float32)], axis=1)
    pair_out = jax.vmap(lambda result_rows, where_to: result_rows[where_to])(padded, destination)
    mixture = gate_values[:, :, 0:1] * pair_out[:, :TOK_DEV] + gate_values[:, :, 1:2] * pair_out[:, TOK_DEV:]
    mixture = jnp.transpose(mixture.reshape(N_EXPERT, SEQS, TOK_DEV, D), (0, 2, 1, 3)).reshape(LENGTH, SEQS, D)
    return (middle + mixture, jnp.sum(aux_terms))

def reference(inputs, grad_out, prefix, routes, priority, loss_weights, norm_attn, norm_moe, qkv_weight, out_weight, bias_table, router_weight, gate_weight, up_weight, down_weight):
    token_routes = by_group(routes)
    destination = jax.vmap(pair_dest)(token_routes, priority.reshape(GROUPS, TOK_DEV))

    def objective(tokens, gain_attn, gain_moe, qkv_full, out_full, table, router_full, gate_full, up_full, down_full):
        return forward(tokens, gain_attn, gain_moe, qkv_full, out_full, table, router_full, gate_full, up_full, down_full, prefix, token_routes, destination, loss_weights)
    primal, pullback = jax.vjp(objective, widen(inputs), widen(norm_attn), widen(norm_moe), widen(qkv_weight), widen(out_weight), widen(bias_table), widen(router_weight), widen(gate_weight), widen(up_weight), widen(down_weight))
    grads = pullback((widen(grad_out), jnp.ones((), jnp.float32)))
    return (primal[0].astype(jnp.bfloat16), grads[0], grads[1], grads[2], grads[3], grads[4], grads[5], grads[6], grads[7], grads[8], grads[9])
```

```python
import functools
import math

import jax
import jax.numpy as jnp
import numpy as np
from jax import lax
from jax.experimental import pallas as pl
from jax.experimental.pallas import tpu as pltpu
from jax.sharding import PartitionSpec as P

D = 1024
HEADS = 16
HEAD = 64
FF = 2816
EXPERTS = 32
TOP = 2
BUCKETS = 32
CAP = 18

epsilon = 1e-06
masked_score = -1e30
far_bounds = (12, 16, 23, 32, 46, 64, 91)
tile = 256
main_slots = 16
tail_slots = CAP - main_slots
log2e = math.log2(math.e)
score_scale = HEAD ** (-0.5)
mega = 1024 * 1024
part_sources = 32
spare = 128


MESH = pl.DeviceIdType.MESH


def flip(index, key):
    out, bit = index, 1
    while bit <= key:
        if key & bit:
            out = out + bit * (1 - 2 * ((index // bit) % 2))
        bit *= 2
    return out


class Spot:
    def __init__(self, groups, columns):
        self.groups, self.columns = groups, columns
        self.place = lax.axis_index("expert")
        self.lane = lax.axis_index("shard")
        self.half = columns // 2
        self.chip = self.lane // 2
        self.core = self.lane % 2
        self.partner = self.chip * 2 + 1 - self.core

    def across(self, step):
        return ((self.chip + step) % self.half) * 2 + self.core

    def behind(self, step):
        return ((self.chip + self.half - step) % self.half) * 2 + self.core

    def lane_at(self, step, other):
        chip = (self.chip + step) % self.half
        return chip * 2 + ((1 - self.core) if other else self.core)

    def meet(self):
        barrier = pltpu.get_barrier_semaphore()
        for key in range(1, self.groups):
            peer = (flip(self.place, key), self.lane)
            pl.semaphore_signal(barrier, inc=1, device_id=peer, device_id_type=MESH)
        for step in range(1, self.columns):
            peer = (self.place, (self.lane + step) % self.columns)
            pl.semaphore_signal(barrier, inc=1, device_id=peer, device_id_type=MESH)
        pl.semaphore_wait(barrier, self.groups + self.columns - 2)


def remote(source, target, send_sem, recv_sem, peer):
    return pltpu.make_async_remote_copy(
        src_ref=source,
        dst_ref=target,
        send_sem=send_sem,
        recv_sem=recv_sem,
        device_id=peer,
        device_id_type=MESH,
    )


def line_shape(groups):
    across = groups // 4
    return 4, across


class LineGather:
    def __init__(self, spot, own, full, local_sem, send_sems, recv_sems):
        self.spot, self.own, self.full = spot, own, full
        self.local_sem, self.send_sems, self.recv_sems = local_sem, send_sems, recv_sems
        self.long, self.wide = line_shape(spot.groups)
        self.z = spot.place // self.wide
        self.y = spot.place % self.wide

    @staticmethod
    def sems(groups):
        long, wide = line_shape(groups)
        return [
            pltpu.SemaphoreType.DMA(()),
            pltpu.SemaphoreType.DMA((2 * long - 1, wide + 1)),
            pltpu.SemaphoreType.DMA((groups,)),
        ]

    def copy(self, job, way, origin, source, target):
        return remote(
            source,
            self.full.at[origin],
            self.send_sems.at[job, way],
            self.recv_sems.at[origin],
            (target, self.spot.lane),
        )

    def each(self, job, origin, source, up, down, act):
        place, wide = self.spot.place, self.wide
        if up:

            @pl.when(self.z + 1 < self.long)
            def _():
                act(self.copy(job, 0, origin, source, place + wide))

        if down:

            @pl.when(self.z >= 1)
            def _():
                act(self.copy(job, 1, origin, source, place - wide))

        for step in range(1, wide):
            target = self.z * wide + (self.y + step) % wide
            act(self.copy(job, 1 + step, origin, source, target))

    def begin(self):
        place = self.spot.place
        self.each(0, place, self.own, True, True, lambda copy: copy.start())
        pltpu.make_async_copy(self.own, self.full.at[place], self.local_sem).start()

    def arrive(self, origin):
        self.copy(0, 0, origin, self.own, self.spot.place).wait_recv()

    def hop(self, k):
        place, wide = self.spot.place, self.wide

        @pl.when(self.z >= k)
        def _():
            origin = place - k * wide
            self.arrive(origin)
            self.each(k, origin, self.full.at[origin], True, False, lambda copy: copy.start())

        @pl.when(self.z + k < self.long)
        def _():
            origin = place + k * wide
            self.arrive(origin)
            job = self.long - 1 + k
            self.each(job, origin, self.full.at[origin], False, True, lambda copy: copy.start())

    def finish(self):
        place, wide = self.spot.place, self.wide
        for row in range(self.long):
            for step in range(1, wide):
                self.arrive(row * wide + (self.y + step) % wide)
        stop = lambda copy: copy.wait_send()
        self.each(0, place, self.own, True, True, stop)
        for k in range(1, self.long):

            @pl.when(self.z >= k)
            def _():
                origin = place - k * wide
                self.each(k, origin, self.full.at[origin], True, False, stop)

            @pl.when(self.z + k < self.long)
            def _():
                origin = place + k * wide
                job = self.long - 1 + k
                self.each(job, origin, self.full.at[origin], False, True, stop)

        pltpu.make_async_copy(self.own, self.full.at[place], self.local_sem).wait()


class ColumnGather:
    def __init__(self, spot, own, full, local_sem, across_send, across_recv, core_send, core_recv):
        self.spot, self.own, self.full = spot, own, full
        self.local_sem = local_sem
        self.across_send, self.across_recv = across_send, across_recv
        self.core_send, self.core_recv = core_send, core_recv

    @staticmethod
    def sems(columns):
        return [pltpu.SemaphoreType.DMA(())] + [pltpu.SemaphoreType.DMA((columns // 2,))] * 4

    def across_copy(self, step):
        spot = self.spot
        return remote(
            self.own,
            self.full.at[spot.lane],
            self.across_send.at[step],
            self.across_recv.at[step],
            (spot.place, spot.across(step)),
        )

    def core_copy(self, step):
        spot = self.spot
        source = self.own if step == 0 else self.full.at[spot.behind(step)]
        target = spot.lane if step == 0 else spot.behind(step)
        return remote(
            source,
            self.full.at[target],
            self.core_send.at[step],
            self.core_recv.at[step],
            (spot.place, spot.partner),
        )

    def begin(self):
        for step in range(1, self.spot.half):
            self.across_copy(step).start()
        self.core_copy(0).start()
        pltpu.make_async_copy(self.own, self.full.at[self.spot.lane], self.local_sem).start()

    def forward(self):
        for step in range(1, self.spot.half):
            self.across_copy(step).wait_recv()
            self.core_copy(step).start()

    def finish(self):
        for step in range(self.spot.half):
            self.core_copy(step).wait_recv()
        for step in range(self.spot.half):
            self.core_copy(step).wait_send()
        for step in range(1, self.spot.half):
            self.across_copy(step).wait_send()
        pltpu.make_async_copy(self.own, self.full.at[self.spot.lane], self.local_sem).wait()


def comm_params(which, limit=16):
    return pltpu.CompilerParams(
        collective_id=which, has_side_effects=True, vmem_limit_bytes=limit * mega
    )


anywhere = pl.BlockSpec(memory_space=pl.ANY)


def entry_kernel(groups, columns, count, *refs):
    tokens, refs = refs[0], refs[1:]
    owns, refs = refs[:count], refs[count:]
    tokens_all, refs = refs[0], refs[1:]
    fulls, sems = refs[:count], refs[count:]
    spot = Spot(groups, columns)
    line = LineGather(spot, tokens, tokens_all, *sems[:3])
    across = [
        ColumnGather(spot, owns[i], fulls[i], *sems[3 + 5 * i : 8 + 5 * i]) for i in range(count)
    ]
    spot.meet()
    line.begin()
    for gather in across:
        gather.begin()
    for k in range(1, 4):
        line.hop(k)
        if k <= count:
            across[k - 1].forward()
    for gather in across[3:]:
        gather.forward()
    for gather in across:
        gather.finish()
    line.finish()


def entry_gather(tokens, owns, groups, columns):
    count = len(owns)
    sems = LineGather.sems(groups) + ColumnGather.sems(columns) * count
    shapes = [jax.ShapeDtypeStruct((groups,) + tokens.shape, tokens.dtype)] + [
        jax.ShapeDtypeStruct((columns,) + own.shape, own.dtype) for own in owns
    ]
    return pl.pallas_call(
        functools.partial(entry_kernel, groups, columns, count),
        out_shape=shapes,
        in_specs=[anywhere] * (1 + count),
        out_specs=[anywhere] * (1 + count),
        scratch_shapes=sems,
        compiler_params=comm_params(1),
        name="entry_gather",
    )(tokens, *owns)


class Dispatch:
    def __init__(self, spot, rows, full, sems):
        self.spot, self.rows, self.full = spot, rows, full
        self.local, self.send, self.recv = sems[:3]
        self.across_send, self.across_recv, self.core_send, self.core_recv = sems[3:]

    @staticmethod
    def sems(groups, columns):
        return (
            [pltpu.SemaphoreType.DMA(())]
            + [pltpu.SemaphoreType.DMA((groups,))] * 2
            + [pltpu.SemaphoreType.DMA((groups, columns // 2))] * 4
        )

    def own(self):
        spot = self.spot
        return pltpu.make_async_copy(
            self.rows.at[spot.place], self.full.at[spot.lane, spot.place], self.local
        )

    def swap(self, key):
        spot = self.spot
        peer = flip(spot.place, key)
        return remote(
            self.rows.at[peer],
            self.full.at[spot.lane, spot.place],
            self.send.at[key],
            self.recv.at[key],
            (peer, spot.lane),
        )

    def across(self, key, step):
        spot = self.spot
        block = self.full.at[spot.lane, flip(spot.place, key)]
        return remote(
            block,
            block,
            self.across_send.at[key, step],
            self.across_recv.at[key, step],
            (spot.place, spot.across(step)),
        )

    def core(self, key, step):
        spot = self.spot
        block = self.full.at[spot.behind(step), flip(spot.place, key)]
        return remote(
            block,
            block,
            self.core_send.at[key, step],
            self.core_recv.at[key, step],
            (spot.place, spot.partner),
        )

    def begin(self):
        self.own().start()
        for key in range(1, self.spot.groups):
            self.swap(key).start()

    def pass_on(self, key):
        for step in range(1, self.spot.half):
            self.across(key, step).wait_recv()
            self.core(key, step).start()

    def advance(self, key):
        if key == 0:
            self.own().wait()
        else:
            self.swap(key).wait_recv()
        for step in range(1, self.spot.half):
            self.across(key, step).start()
        self.core(key, 0).start()
        if key > 0:
            self.pass_on(key - 1)

    def finish(self):
        groups, half = self.spot.groups, self.spot.half
        self.pass_on(groups - 1)
        for key in range(groups):
            for step in range(half):
                self.core(key, step).wait_recv()
        for key in range(groups):
            if key > 0:
                self.swap(key).wait_send()
            for step in range(1, half):
                self.across(key, step).wait_send()
            for step in range(half):
                self.core(key, step).wait_send()


def dispatch_kernel(groups, columns, rows, full, *sems):
    spot = Spot(groups, columns)
    job = Dispatch(spot, rows, full, sems)
    spot.meet()
    job.begin()
    for key in range(groups):
        job.advance(key)
    job.finish()


def dispatch(rows, columns, which):
    groups = rows.shape[0]
    return pl.pallas_call(
        functools.partial(dispatch_kernel, groups, columns),
        out_shape=jax.ShapeDtypeStruct((columns,) + rows.shape, rows.dtype),
        in_specs=[anywhere],
        out_specs=anywhere,
        scratch_shapes=Dispatch.sems(groups, columns),
        compiler_params=comm_params(which),
        name="dispatch_rows",
    )(rows)


class Exchange:
    def __init__(self, spot, blocks, thirds, local, send, recv):
        self.spot, self.blocks, self.thirds = spot, blocks, range(thirds)
        self.local, self.send, self.recv = local, send, recv

    @staticmethod
    def sems(groups, thirds):
        return [pltpu.SemaphoreType.DMA((thirds,))] + [
            pltpu.SemaphoreType.DMA((groups, thirds))
        ] * 2

    def copy(self, key, third):
        spot = self.spot
        peer = flip(spot.place, key)
        source, target = self.blocks(peer, third)
        if key == 0:
            return pltpu.make_async_copy(source, target, self.local.at[third])
        return remote(
            source,
            target,
            self.send.at[key, third],
            self.recv.at[key, third],
            (peer, spot.lane),
        )

    def start(self, key):
        for third in self.thirds:
            self.copy(key, third).start()

    def begin(self):
        for key in range(self.spot.groups):
            self.start(key)

    def arrive(self):
        for key in range(self.spot.groups):
            for third in self.thirds:
                copy = self.copy(key, third)
                copy.wait() if key == 0 else copy.wait_recv()

    def finish(self):
        for key in range(1, self.spot.groups):
            for third in self.thirds:
                self.copy(key, third).wait_send()


class ColumnSum:
    def __init__(self, spot, chunks, order, part, bufs, sems):
        self.spot, self.chunks, self.order, self.part = spot, chunks, order, part
        self.pair_in, self.mine, self.across_out, self.across_in = bufs
        self.local, self.pair_send, self.pair_recv, self.across_send, self.across_recv = sems

    @staticmethod
    def scratch(columns, chunks, block):
        half = columns // 2
        return [pltpu.VMEM((half, chunks) + block, jnp.bfloat16)] * 4 + [
            pltpu.SemaphoreType.DMA((half, chunks))
        ] * 5

    def pair_copy(self, step, k):
        spot = self.spot
        return remote(
            self.part.at[spot.lane_at(step, True), self.order(k)],
            self.pair_in.at[step, k],
            self.pair_send.at[step, k],
            self.pair_recv.at[step, k],
            (spot.place, spot.partner),
        )

    def mine_copy(self, step, k):
        return pltpu.make_async_copy(
            self.part.at[self.spot.lane_at(step, False), self.order(k)],
            self.mine.at[step, k],
            self.local.at[step, k],
        )

    def across_copy(self, step, k):
        spot = self.spot
        return remote(
            self.across_out.at[step, k],
            self.across_in.at[step, k],
            self.across_send.at[step, k],
            self.across_recv.at[step, k],
            (spot.place, spot.across(step)),
        )

    def begin(self):
        half = self.spot.half
        for k in range(self.chunks):
            for step in list(range(1, half)) + [0]:
                self.pair_copy(step, k).start()
                self.mine_copy(step, k).start()

    def pair_sum(self, step, k):
        self.pair_copy(step, k).wait_recv()
        self.mine_copy(step, k).wait()
        return self.mine[step, k].astype(jnp.float32) + self.pair_in[step, k].astype(jnp.float32)

    def middle(self, k):
        for step in range(1, self.spot.half):
            self.across_out[step, k] = self.pair_sum(step, k).astype(jnp.bfloat16)
            self.across_copy(step, k).start()

    def last(self, k):
        total = self.pair_sum(0, k)
        for step in range(1, self.spot.half):
            self.across_copy(step, k).wait_recv()
            total = total + self.across_in[step, k].astype(jnp.float32)
        return total.astype(jnp.bfloat16)

    def finish(self):
        for k in range(self.chunks):
            for step in range(self.spot.half):
                self.pair_copy(step, k).wait_send()
                if step:
                    self.across_copy(step, k).wait_send()


class Collect:
    def __init__(self, spot, part, out, scratch):
        self.spot, self.total = spot, scratch[9]
        self.sums = ColumnSum(
            spot, spot.groups, lambda k: flip(spot.place, k), part, scratch[:4], scratch[4:9]
        )
        self.out = out
        self.local, self.send, self.recv = scratch[10:]

    @staticmethod
    def scratch(columns, groups, block):
        return (
            ColumnSum.scratch(columns, groups, block)
            + [pltpu.VMEM((groups,) + block, jnp.bfloat16)]
            + [pltpu.SemaphoreType.DMA(())]
            + [pltpu.SemaphoreType.DMA((groups,))] * 2
        )

    def copy(self, key):
        spot = self.spot
        target = self.out.at[spot.place]
        if key == 0:
            return pltpu.make_async_copy(self.total.at[0], target, self.local)
        peer = flip(spot.place, key)
        return remote(
            self.total.at[key], target, self.send.at[key], self.recv.at[key], (peer, spot.lane)
        )

    def begin(self):
        self.sums.begin()

    def middle(self, key):
        self.sums.middle(key)

    def last(self, key):
        self.total[key] = self.sums.last(key)
        self.copy(key).start()

    def finish(self):
        for key in range(1, self.spot.groups):
            self.copy(key).wait_recv()
        for key in range(1, self.spot.groups):
            self.copy(key).wait_send()
        self.copy(0).wait()
        self.sums.finish()


def collect_kernel(groups, columns, part, out, *scratch):
    spot = Spot(groups, columns)
    job = Collect(spot, part, out, scratch)
    spot.meet()
    job.begin()
    ahead = 2
    for key in range(ahead):
        job.middle(key)
    for key in range(groups):
        if key + ahead < groups:
            job.middle(key + ahead)
        job.last(key)
    job.finish()


def collect(part, which):
    columns, groups = part.shape[:2]
    block = part.shape[2:]
    return pl.pallas_call(
        functools.partial(collect_kernel, groups, columns),
        out_shape=jax.ShapeDtypeStruct((groups,) + block, part.dtype),
        in_specs=[anywhere],
        out_specs=anywhere,
        scratch_shapes=Collect.scratch(columns, groups, block),
        compiler_params=comm_params(which, 56),
        name="collect_rows",
    )(part)


def lanes_at(place, width):
    return pl.ds(pl.multiple_of(place * width, 128), width)


def mixed_kernel(groups, columns, mixed, attended, *sems):
    spot = Spot(groups, columns)
    width = mixed.shape[2]

    def blocks(at, third):
        if width % 128:
            return mixed.at[at], attended.at[spot.place]
        return mixed.at[at], attended.at[:, lanes_at(spot.place, width)]

    job = Exchange(spot, blocks, 1, *sems)
    spot.meet()
    job.begin()
    job.arrive()
    job.finish()


def exchange_mixed(mixed, columns, which):
    groups, rows, width = mixed.shape
    shape = mixed.shape if width % 128 else (rows, groups * width)
    out = pl.pallas_call(
        functools.partial(mixed_kernel, groups, columns),
        out_shape=jax.ShapeDtypeStruct(shape, mixed.dtype),
        in_specs=[anywhere],
        out_specs=anywhere,
        scratch_shapes=Exchange.sems(groups, 1),
        compiler_params=comm_params(which),
        name="exchange_mixed",
    )(mixed)
    if width % 128:
        out = jnp.transpose(out, (1, 0, 2)).reshape(rows, groups * width)
    return out


def grad_mixed_kernel(groups, columns, chunks, grads, part, out, part_out, *scratch):
    spot = Spot(groups, columns)
    width = out.shape[2]

    def blocks(at, third):
        if width % 128:
            return grads.at[at], out.at[spot.place]
        return grads.at[:, lanes_at(at, width)], out.at[spot.place]

    sums = ColumnSum(spot, chunks, lambda k: k, part, scratch[:4], scratch[4:9])
    total, total_sem = scratch[9:11]
    job = Exchange(spot, blocks, 1, *scratch[11:])
    spot.meet()
    job.begin()
    sums.begin()
    for k in range(chunks):
        sums.middle(k)
    stores = [pltpu.make_async_copy(total.at[k], part_out.at[k], total_sem.at[k]) for k in range(chunks)]
    for k in range(chunks):
        total[k] = sums.last(k)
        stores[k].start()
    job.arrive()
    job.finish()
    sums.finish()
    for store in stores:
        store.wait()


def exchange_grad_mixed(grads, part, groups, which):
    rows = grads.shape[0]
    width = grads.shape[1] // groups
    if width % 128:
        grads = jnp.transpose(grads.reshape(rows, groups, width), (1, 0, 2))
    columns, chunks = part.shape[:2]
    block = part.shape[2:]
    return pl.pallas_call(
        functools.partial(grad_mixed_kernel, groups, columns, chunks),
        out_shape=(
            jax.ShapeDtypeStruct((groups, rows, width), grads.dtype),
            jax.ShapeDtypeStruct((chunks,) + block, part.dtype),
        ),
        in_specs=[anywhere, anywhere],
        out_specs=(anywhere, anywhere),
        scratch_shapes=ColumnSum.scratch(columns, chunks, block)
        + [pltpu.VMEM((chunks,) + block, part.dtype), pltpu.SemaphoreType.DMA((chunks,))]
        + Exchange.sems(groups, 1),
        compiler_params=comm_params(which, 32),
        name="exchange_grad_mixed",
    )(grads, part)


class Tail:
    def __init__(self, spot, chunks, refs, scratch):
        grads, part, piece, weight, grads_out, sum_all, piece_all, weight_all = refs
        groups = spot.groups
        width = grads.shape[2] // 3
        thirds = 3 if width % 128 == 0 else 1

        def blocks(at, third):
            if thirds == 1:
                return grads.at[at], grads_out.at[spot.place]
            columns_to = pl.ds(pl.multiple_of(third * D + spot.place * width, 128), width)
            return grads.at[at, :, pl.ds(third * width, width)], grads_out.at[:, columns_to]

        self.chunks = chunks
        self.sums = ColumnSum(spot, chunks, lambda k: k, part, scratch[:4], scratch[4:9])
        self.own_sum = scratch[9]
        self.swap = Exchange(spot, blocks, thirds, *scratch[10:13])
        self.line = LineGather(spot, self.own_sum, sum_all, *scratch[13:16])
        self.side = LineGather(spot, piece, piece_all, *scratch[16:19])
        self.column = ColumnGather(spot, weight, weight_all, *scratch[19:24])

    @staticmethod
    def scratch(columns, groups, chunks, block, thirds):
        return (
            ColumnSum.scratch(columns, chunks, block)
            + [pltpu.VMEM((chunks,) + block, jnp.bfloat16)]
            + Exchange.sems(groups, thirds)
            + LineGather.sems(groups) * 2
            + ColumnGather.sems(columns)
        )

    def begin(self):
        self.sums.begin()
        self.side.begin()
        self.swap.begin()
        for k in range(self.chunks):
            self.sums.middle(k)
        self.column.begin()

    def gather(self):
        for k in range(self.chunks):
            self.own_sum[k] = self.sums.last(k)
        self.line.begin()
        self.side.hop(1)

    def hop(self, k):
        self.line.hop(k)
        if k + 1 < 4:
            self.side.hop(k + 1)

    def finish(self):
        self.column.forward()
        self.swap.arrive()
        self.side.finish()
        self.line.finish()
        self.column.finish()
        self.swap.finish()
        self.sums.finish()


def unpack_kernel(width, packed, out):
    for group in range(packed.shape[0]):
        out[:, group * width : (group + 1) * width] = packed[group].astype(jnp.float32)


def unpack_columns(packed, width):
    groups, rows = packed.shape[:2]
    if width % 128:
        blocks = packed[:, :, : 3 * width].reshape(groups, rows, 3, width).astype(jnp.float32)
        return jnp.transpose(blocks, (1, 2, 0, 3)).reshape(rows, 3 * groups * width)
    return pl.pallas_call(
        functools.partial(unpack_kernel, width),
        grid=(3,),
        out_shape=jax.ShapeDtypeStruct((rows, 3 * groups * width), jnp.float32),
        in_specs=[pl.BlockSpec((groups, rows, width), lambda t: (0, 0, t))],
        out_specs=pl.BlockSpec((rows, groups * width), lambda t: (0, t)),
        name="unpack_columns",
    )(packed)


def rms_norm(features, scales):
    factor = lax.rsqrt(jnp.mean(features * features, axis=-1, keepdims=True) + epsilon)
    return features * factor * scales


def buckets_of(offsets):
    distance = np.abs(offsets)
    beyond = 8 + np.sum(distance[..., None] >= np.array(far_bounds), axis=-1)
    return np.where(distance < 8, distance, beyond) + 16 * (offsets > 0)


def skew_buckets():
    lanes = np.arange(2 * tile)
    from_query = np.where(lanes < tile, -lanes, 2 * tile - lanes)
    return np.concatenate([buckets_of(near * tile + from_query) for near in (-1, 0, 1)])


def lane_row_mask(head, width, rows):
    lanes = lax.broadcasted_iota(jnp.int32, (rows, width), 1)
    return (lanes >= head * HEAD) & (lanes < (head + 1) * HEAD)


def fold_rows(block, op):
    return op(block.reshape(block.shape[0] // 8, 8, block.shape[1]), axis=0)


def nt_dot(left, right):
    return lax.dot_general(left, right, (((1,), (1,)), ((), ())), preferred_element_type=jnp.float32)


def tn_dot(left, right):
    return lax.dot_general(left, right, (((0,), (0,)), ((), ())), preferred_element_type=jnp.float32)


def nn_dot(left, right):
    return jnp.dot(left, right, preferred_element_type=jnp.float32)


def build_bias(base_ref, far_ref, bias_sc, heads_here):
    for head in range(heads_here):
        for near in range(3):
            row = base_ref[pl.ds(head * 3 + near, 1), :]
            wide = jnp.broadcast_to(row, (tile, 2 * tile))
            skewed = pltpu.roll(wide, 0, 1, stride=1, stride_axis=0)
            bias_sc[head, near] = skewed[:, :tile]
        bias_sc[head, 3] = jnp.full((tile, tile), far_ref[head, 1], jnp.float32)


def unskew_sum(wide):
    lanes = wide.shape[1]
    half = wide.shape[0] // 2
    while half >= 8:
        wide = wide[:half] + pltpu.roll(wide[half:], lanes - half, 1)
        half //= 2
    total = wide[0:1]
    for row in range(1, 8):
        total = total + pltpu.roll(wide[row : row + 1], lanes - row, 1)
    return total


def rows_at(index):
    return pl.ds(pl.multiple_of(index * tile, tile), tile)


def visible_tile(key_tile, query_tile, prefix_length):
    key_pos = key_tile * tile + lax.broadcasted_iota(jnp.int32, (tile, tile), 0)
    query_pos = query_tile * tile + lax.broadcasted_iota(jnp.int32, (tile, tile), 1)
    return (key_pos <= query_pos) | (key_pos < prefix_length)


def attend_forward_kernel(
    heads_here,
    groups,
    columns,
    prefix_ref,
    far_ref,
    base_ref,
    qkv_ref,
    rows_ref,
    mixed_ref,
    totals_ref,
    full_ref,
    bias_sc,
    score_sc,
    value_sc,
    *sems,
):
    width = heads_here * HEAD
    query_tile = pl.program_id(0)
    tiles = qkv_ref.shape[0] // tile
    spot = Spot(groups, columns)
    job = Dispatch(spot, rows_ref, full_ref, sems)

    @pl.when(query_tile == 0)
    def _():
        spot.meet()
        job.begin()

    prefix_length = prefix_ref[0]
    heads = range(heads_here)

    @pl.when(query_tile == 0)
    def _():
        build_bias(base_ref, far_ref, bias_sc, heads_here)
        for key_tile in range(value_sc.shape[1] // tile):
            rows = pl.ds(key_tile * tile, tile)
            values = qkv_ref[rows, 2 * width : 3 * width].astype(jnp.float32)
            value_sc[:, rows] = jnp.transpose(values).astype(jnp.bfloat16)

    queries = qkv_ref[rows_at(query_tile), :width]
    head_queries = [
        jnp.where(lane_row_mask(head, width, tile), queries, jnp.zeros_like(queries)) for head in heads
    ]

    def score_tiles(key_tile, tops, finish):
        keys = qkv_ref[rows_at(key_tile), width : 2 * width]
        out = []
        for head in heads:
            scores = finish(head, nt_dot(keys, head_queries[head]) * (score_scale * log2e))
            score_sc[head, rows_at(key_tile), :] = scores
            out.append(jnp.maximum(tops[head], fold_rows(scores, jnp.max)))
        return tuple(out)

    def far_body(key_tile, tops):
        return score_tiles(key_tile, tops, lambda head, raw: raw + far_ref[head, 0])

    def near_body(key_tile, tops):
        return score_tiles(key_tile, tops, lambda head, raw: raw + bias_sc[head, 0])

    def tail_body(key_tile, tops):
        shown = visible_tile(key_tile, query_tile, prefix_length)
        which = 1 + jnp.minimum(key_tile - query_tile, 2)
        return score_tiles(
            key_tile, tops, lambda head, raw: jnp.where(shown, raw + bias_sc[head, which], masked_score)
        )

    tile_count = jnp.maximum(query_tile + 1, tiles // 2)
    near_start = jnp.maximum(query_tile - 1, 0)
    tops = tuple(jnp.full((8, tile), masked_score, jnp.float32) for _ in heads)
    tops = lax.fori_loop(0, near_start, far_body, tops)
    tops = lax.fori_loop(near_start, query_tile, near_body, tops)
    tops = lax.fori_loop(query_tile, tile_count, tail_body, tops)
    tops = [jnp.max(top, axis=0, keepdims=True) for top in tops]

    def mix_body(key_tile, carry):
        sums, mixes = carry
        new_sums, new_mixes = [], []
        for head in heads:
            expos = jnp.exp2(score_sc[head, rows_at(key_tile), :] - tops[head])
            new_sums.append(sums[head] + fold_rows(expos, jnp.sum))
            values = value_sc[head * HEAD : (head + 1) * HEAD, rows_at(key_tile)]
            new_mixes.append(mixes[head] + nn_dot(values, expos.astype(jnp.bfloat16)))
        return (tuple(new_sums), tuple(new_mixes))

    sums, mixes = lax.fori_loop(
        0,
        tile_count,
        mix_body,
        (
            tuple(jnp.zeros((8, tile), jnp.float32) for _ in heads),
            tuple(jnp.zeros((HEAD, tile), jnp.float32) for _ in heads),
        ),
    )
    parts = []
    for head in heads:
        total = jnp.sum(sums[head], axis=0, keepdims=True)
        parts.append(mixes[head] / total)
        totals_ref[0, pl.ds(head, 1), :] = tops[head] + jnp.log2(total)
    mixed_ref[...] = jnp.transpose(jnp.concatenate(parts, axis=0)).astype(jnp.bfloat16)

    for key in range(groups):

        @pl.when(query_tile == key * tiles // groups)
        def _():
            job.advance(key)

    @pl.when(query_tile == tiles - 1)
    def _():
        job.finish()


def attend_forward(prefix, far_bias, base_bias, qkv, rows, columns):
    length = qkv.shape[0]
    groups = rows.shape[0]
    width = qkv.shape[1] // 3
    heads_here = width // HEAD
    tiles = length // tile
    return pl.pallas_call(
        functools.partial(attend_forward_kernel, heads_here, groups, columns),
        grid=(tiles,),
        out_shape=(
            jax.ShapeDtypeStruct((length, width), jnp.bfloat16),
            jax.ShapeDtypeStruct((tiles, heads_here, tile), jnp.float32),
            jax.ShapeDtypeStruct((columns,) + rows.shape, rows.dtype),
        ),
        in_specs=[
            pl.BlockSpec(memory_space=pltpu.SMEM),
            pl.BlockSpec(memory_space=pltpu.SMEM),
            pl.BlockSpec(base_bias.shape, lambda i: (0, 0)),
            pl.BlockSpec(qkv.shape, lambda i: (0, 0)),
            anywhere,
        ],
        out_specs=(
            pl.BlockSpec((tile, width), lambda i: (i, 0)),
            pl.BlockSpec((1, heads_here, tile), lambda i: (i, 0, 0)),
            anywhere,
        ),
        scratch_shapes=[
            pltpu.VMEM((heads_here, 4, tile, tile), jnp.float32),
            pltpu.VMEM((heads_here, length, tile), jnp.float32),
            pltpu.VMEM((width, length), jnp.bfloat16),
        ]
        + Dispatch.sems(groups, columns),
        compiler_params=comm_params(5, 40),
        cost_estimate=pl.CostEstimate(
            flops=40 * length * length * width, transcendentals=length * length * heads_here,
            bytes_accessed=8 * length * width,
        ),
        name="attend_forward",
    )(prefix, far_bias, base_bias, qkv, rows)


def attend_backward_kernel(
    heads_here,
    groups,
    columns,
    prefix_ref,
    far_ref,
    base_ref,
    qkv_ref,
    mixed_ref,
    grad_ref,
    totals_ref,
    part_ref,
    sums_ref,
    out_ref,
    near_ref,
    side_ref,
    result_ref,
    piece_ref,
    bias_sc,
    key_sc,
    grad_key_sc,
    grad_value_sc,
    near_sc,
    *scratch,
):
    width = heads_here * HEAD
    query_tile = pl.program_id(0)
    tiles = qkv_ref.shape[0] // tile
    spot = Spot(groups, columns)
    pieces = scratch[0]
    swap = Exchange(
        spot, lambda at, third: (sums_ref.at[at], pieces.at[spot.place]), 1, *scratch[1:4]
    )
    job = Collect(spot, part_ref, result_ref, scratch[4:])

    @pl.when(query_tile == 0)
    def _():
        spot.meet()
        job.begin()
        swap.begin()

    prefix_length = prefix_ref[0]
    heads = range(heads_here)

    @pl.when(query_tile == 0)
    def _():
        build_bias(base_ref, far_ref, bias_sc, heads_here)
        for key_tile in range(key_sc.shape[1] // tile):
            rows = pl.ds(key_tile * tile, tile)
            keys = qkv_ref[rows, width : 2 * width].astype(jnp.float32)
            key_sc[:, rows] = jnp.transpose(keys).astype(jnp.bfloat16)
        grad_key_sc[...] = jnp.zeros_like(grad_key_sc)
        grad_value_sc[...] = jnp.zeros_like(grad_value_sc)
        near_sc[...] = jnp.zeros_like(near_sc)
        side_ref[...] = jnp.zeros_like(side_ref)

    queries = qkv_ref[rows_at(query_tile), :width]
    grads = grad_ref[rows_at(query_tile), :]
    products = grads.astype(jnp.float32) * mixed_ref[rows_at(query_tile), :].astype(jnp.float32)
    head_queries, head_grads, inners, totals = [], [], [], []
    for head in heads:
        mask = lane_row_mask(head, width, tile)
        head_queries.append(jnp.where(mask, queries, jnp.zeros_like(queries)))
        head_grads.append(jnp.where(mask, grads, jnp.zeros_like(grads)))
        ones = jnp.where(lane_row_mask(head, width, 8), 1.0, 0.0)
        inner = lax.dot_general(
            ones,
            products,
            (((1,), (1,)), ((), ())),
            precision=lax.Precision.HIGHEST,
            preferred_element_type=jnp.float32,
        )
        inners.append(inner[0:1, :])
        totals.append(totals_ref[0, pl.ds(head, 1), :])

    def step(key_tile, carry, finish, keep):
        sides, grad_queries = carry
        keys = qkv_ref[rows_at(key_tile), width : 2 * width]
        values = qkv_ref[rows_at(key_tile), 2 * width : 3 * width]
        new_sides, new_queries = [], []
        key_part, value_part = None, None
        for head in heads:
            raw = nt_dot(keys, head_queries[head]) * (score_scale * log2e)
            attention = jnp.exp2(finish(head, raw))
            grad_weights = nt_dot(values, head_grads[head])
            grad_scores = attention * (grad_weights - inners[head])
            new_sides.append(keep(head, grad_scores, sides[head]))
            low_scores = grad_scores.astype(jnp.bfloat16)
            keys_across = key_sc[head * HEAD : (head + 1) * HEAD, rows_at(key_tile)]
            new_queries.append(grad_queries[head] + nn_dot(keys_across, low_scores))
            value_one = nn_dot(attention.astype(jnp.bfloat16), head_grads[head])
            key_one = nn_dot(low_scores, head_queries[head])
            value_part = value_one if value_part is None else value_part + value_one
            key_part = key_one if key_part is None else key_part + key_one
        grad_key_sc[rows_at(key_tile), :] += key_part
        grad_value_sc[rows_at(key_tile), :] += value_part
        return (tuple(new_sides), tuple(new_queries))

    def add_side(head, grad_scores, side):
        return side + fold_rows(grad_scores, jnp.sum)

    def far_body(key_tile, carry):
        return step(
            key_tile, carry, lambda head, raw: raw + (far_ref[head, 0] - totals[head]), add_side
        )

    def near_body(key_tile, carry):
        def keep(head, grad_scores, side):
            near_sc[head, 0] += grad_scores
            return side

        return step(
            key_tile, carry, lambda head, raw: raw + bias_sc[head, 0] - totals[head], keep
        )

    def tail_body(key_tile, carry):
        shown = visible_tile(key_tile, query_tile, prefix_length)
        which = 1 + jnp.minimum(key_tile - query_tile, 2)

        def keep(head, grad_scores, side):
            near_sc[head, which] += grad_scores
            return side

        return step(
            key_tile,
            carry,
            lambda head, raw: jnp.where(
                shown, raw + bias_sc[head, which] - totals[head], masked_score
            ),
            keep,
        )

    tile_count = jnp.maximum(query_tile + 1, tiles // 2)
    near_start = jnp.maximum(query_tile - 1, 0)
    carry = (
        tuple(jnp.zeros((8, tile), jnp.float32) for _ in heads),
        tuple(jnp.zeros((HEAD, tile), jnp.float32) for _ in heads),
    )
    carry = lax.fori_loop(0, near_start, far_body, carry)
    carry = lax.fori_loop(near_start, query_tile, near_body, carry)
    carry = lax.fori_loop(query_tile, tile_count, tail_body, carry)
    sides, grad_queries = carry
    for head in heads:
        side_ref[head, 0] += sides[head]
    across = jnp.concatenate(grad_queries, axis=0) * score_scale
    out_ref[rows_at(query_tile), :width] = jnp.transpose(across).astype(jnp.bfloat16)

    @pl.when(query_tile == tiles - 1)
    def _():
        out_ref[:, width : 2 * width] = (grad_key_sc[...] * score_scale).astype(jnp.bfloat16)
        out_ref[:, 2 * width : 3 * width] = grad_value_sc[...].astype(jnp.bfloat16)
        for head in heads:
            side_ref[head, 1] = fold_rows(near_sc[head, 3], jnp.sum)
            for near in range(3):
                wide = jnp.concatenate(
                    [near_sc[head, near], jnp.zeros((tile, tile), jnp.float32)], axis=1
                )
                near_ref[pl.ds(head * 3 + near, 1), :] = unskew_sum(wide)

    for step in range(tiles):
        middles = [key for key in range(groups) if key * 2 // groups == step]
        lasts = [key for key in range(groups) if min(tiles - 1, 2 + key * 3 // 4) == step]

        @pl.when(query_tile == step)
        def _():
            for key in middles:
                job.middle(key)
            for key in lasts:
                job.last(key)

    @pl.when(query_tile == tiles - 1)
    def _():
        swap.arrive()
        piece_ref[...] = jnp.sum(pieces[...].astype(jnp.float32), axis=0).astype(jnp.bfloat16)
        job.finish()
        swap.finish()


def attend_backward(
    prefix, far_bias, base_bias, qkv, mixed, grad_mixed, totals, part, sums, columns
):
    length = qkv.shape[0]
    groups, piece_rows, piece_width = sums.shape
    block = part.shape[2:]
    width = qkv.shape[1] // 3
    heads_here = width // HEAD
    tiles = length // tile
    whole = lambda i: (0, 0)
    return pl.pallas_call(
        functools.partial(attend_backward_kernel, heads_here, groups, columns),
        grid=(tiles,),
        out_shape=(
            jax.ShapeDtypeStruct((length, 3 * width), jnp.bfloat16),
            jax.ShapeDtypeStruct((heads_here * 3, 2 * tile), jnp.float32),
            jax.ShapeDtypeStruct((heads_here, 2, 8, tile), jnp.float32),
            jax.ShapeDtypeStruct((groups,) + block, jnp.bfloat16),
            jax.ShapeDtypeStruct((piece_rows, piece_width), jnp.bfloat16),
        ),
        in_specs=[
            pl.BlockSpec(memory_space=pltpu.SMEM),
            pl.BlockSpec(memory_space=pltpu.SMEM),
            pl.BlockSpec(base_bias.shape, whole),
            pl.BlockSpec(qkv.shape, whole),
            pl.BlockSpec(mixed.shape, whole),
            pl.BlockSpec(mixed.shape, whole),
            pl.BlockSpec((1, heads_here, tile), lambda i: (i, 0, 0)),
            anywhere,
            anywhere,
        ],
        out_specs=(
            pl.BlockSpec((length, 3 * width), whole),
            pl.BlockSpec((heads_here * 3, 2 * tile), whole),
            pl.BlockSpec((heads_here, 2, 8, tile), lambda i: (0, 0, 0, 0)),
            anywhere,
            pl.BlockSpec((piece_rows, piece_width), whole),
        ),
        scratch_shapes=[
            pltpu.VMEM((heads_here, 4, tile, tile), jnp.float32),
            pltpu.VMEM((width, length), jnp.bfloat16),
            pltpu.VMEM((length, width), jnp.float32),
            pltpu.VMEM((length, width), jnp.float32),
            pltpu.VMEM((heads_here, 4, tile, tile), jnp.float32),
            pltpu.VMEM(sums.shape, jnp.bfloat16),
        ]
        + Exchange.sems(groups, 1)
        + Collect.scratch(columns, groups, block),
        compiler_params=comm_params(6, 60),
        cost_estimate=pl.CostEstimate(
            flops=70 * length * length * width, transcendentals=length * length * heads_here,
            bytes_accessed=16 * length * width,
        ),
        name="attend_backward",
    )(prefix, far_bias, base_bias, qkv, mixed, grad_mixed, totals, part, sums)


def gelu_parts(act):
    inner = math.sqrt(2.0 / math.pi) * (act + 0.044715 * act * act * act)
    tanh = jnp.tanh(inner)
    half = 0.5 * (1.0 + tanh)
    slope = math.sqrt(2.0 / math.pi) * (1.0 + 3.0 * 0.044715 * act * act)
    return act * half, half + 0.5 * act * (1.0 - tanh * tanh) * slope


def slot_rows(experts_here):
    return experts_here * main_slots + -(-experts_here * tail_slots // 8) * 8


def tail_select(expert, sources, tail_height):
    rows = lax.broadcasted_iota(jnp.int32, (sources * tail_slots, sources * tail_height), 0)
    columns = lax.broadcasted_iota(jnp.int32, (sources * tail_slots, sources * tail_height), 1)
    wanted = (rows // tail_slots) * tail_height + expert * tail_slots + rows % tail_slots
    return jnp.where(columns == wanted, 1.0, 0.0).astype(jnp.bfloat16)


def expert_input(main_ref, tail_ref, select):
    width = main_ref.shape[-1]
    main = main_ref[...].reshape(-1, width)
    tail = nn_dot(select, tail_ref[...].reshape(-1, width)).astype(jnp.bfloat16)
    return jnp.concatenate([main, tail], axis=0)


def gates_of(wide_rows):
    return wide_rows[:, D : D + 1].astype(jnp.float32) + wide_rows[:, D + 1 : D + 2].astype(
        jnp.float32
    )


def expert_output(value, select, expert, main_sc, tail_sc):
    low = value.astype(jnp.bfloat16)
    main_count = main_sc.shape[0] * main_sc.shape[1] * main_slots
    main_sc[...] = low[:main_count].reshape(main_sc.shape)
    spread = tn_dot(select, low[main_count:]).astype(jnp.bfloat16).reshape(tail_sc.shape)

    @pl.when(expert == 0)
    def _():
        tail_sc[...] = spread

    @pl.when(expert > 0)
    def _():
        tail_sc[...] += spread


def expert_act_kernel(
    experts_here,
    row_main,
    row_tail,
    grad_main,
    grad_tail,
    gate_weight,
    up_weight,
    down_weight,
    hidden_ref,
    grad_gate_ref,
    grad_up_ref,
    result_ref,
    back_ref,
    result_main,
    result_tail,
    back_main,
    back_tail,
    sems,
):
    part, expert = pl.program_id(0), pl.program_id(1)
    shards_part = row_main.shape[0]
    sources = shards_part * row_main.shape[1]
    tail_height = row_tail.shape[2]
    sources_at = pl.ds(part * shards_part, shards_part)
    select = tail_select(expert, sources, tail_height)
    wide_rows = expert_input(row_main, row_tail, select)
    rows, gates = wide_rows[:, :D], gates_of(wide_rows)
    grads = expert_input(grad_main, grad_tail, select)
    gate_act = nt_dot(rows, gate_weight[0])
    up_act = nt_dot(rows, up_weight[0])
    gelu, slope = gelu_parts(gate_act)
    hidden = (gelu * up_act).astype(jnp.bfloat16)
    hidden_ref[0] = hidden
    raw_hidden = nt_dot(grads, down_weight[0])
    grad_gates = jnp.sum(raw_hidden * hidden.astype(jnp.float32), axis=1, keepdims=True)
    grad_hidden = raw_hidden * gates
    grad_gate = (grad_hidden * up_act * slope).astype(jnp.bfloat16)
    grad_up = (grad_hidden * gelu).astype(jnp.bfloat16)
    grad_gate_ref[0] = grad_gate
    grad_up_ref[0] = grad_up
    back = nn_dot(grad_gate, gate_weight[0]) + nn_dot(grad_up, up_weight[0])
    lanes = lax.broadcasted_iota(jnp.int32, (back.shape[0], spare), 1)
    back = jnp.concatenate([back, jnp.where(lanes == 0, grad_gates, 0.0)], axis=1)
    result = nn_dot(hidden, down_weight[0])

    def main_copies(at):
        place = pl.ds(pl.multiple_of(at * main_slots, main_slots), main_slots)
        return (
            pltpu.make_async_copy(result_main, result_ref.at[sources_at, :, place, :], sems.at[0]),
            pltpu.make_async_copy(back_main, back_ref.at[sources_at, :, place, :], sems.at[1]),
        )

    @pl.when(expert > 0)
    def _():
        for copy in main_copies(expert - 1):
            copy.wait()

    expert_output(result, select, expert, result_main, result_tail)
    expert_output(back, select, expert, back_main, back_tail)
    for copy in main_copies(expert):
        copy.start()

    @pl.when(expert == experts_here - 1)
    def _():
        place = pl.ds(experts_here * main_slots, tail_height)
        tails = (
            pltpu.make_async_copy(result_tail, result_ref.at[sources_at, :, place, :], sems.at[2]),
            pltpu.make_async_copy(back_tail, back_ref.at[sources_at, :, place, :], sems.at[3]),
        )
        for copy in tails:
            copy.start()
        for copy in main_copies(expert):
            copy.wait()
        for copy in tails:
            copy.wait()


def parts_of(rows):
    shards, groups = rows.shape[:2]
    return max(1, shards * groups // part_sources)


def row_specs(rows, experts_here, order):
    shards, groups, height, width = rows.shape
    shards_part = shards // parts_of(rows)
    tail_height = slot_rows(experts_here) - experts_here * main_slots
    tail_at = experts_here * main_slots // tail_height
    main_at = lambda e, c: (c, 0, e, 0)
    side_at = lambda e, c: (c, 0, tail_at, 0)
    return [
        pl.BlockSpec((shards_part, groups, main_slots, width), order(main_at)),
        pl.BlockSpec((shards_part, groups, tail_height, width), order(side_at)),
    ]


def expert_act(rows, grads, gate_weight, up_weight, down_weight):
    experts_here, units, width = gate_weight.shape
    shards, groups = rows.shape[:2]
    count = shards * groups * CAP
    parts = parts_of(rows)
    height = slot_rows(experts_here)
    tail_height = height - experts_here * main_slots
    order = lambda index: lambda c, e: index(e, c)
    weight_spec = pl.BlockSpec((1, units, width), lambda c, e: (e, 0, 0))
    act_spec = pl.BlockSpec((1, count // parts, units), lambda c, e: (e, c, 0))
    act_shape = jax.ShapeDtypeStruct((experts_here, count, units), jnp.bfloat16)
    slot_shape = lambda lanes: jax.ShapeDtypeStruct(
        (shards, groups, height, lanes), jnp.bfloat16
    )
    scratch = [
        pltpu.VMEM((shards // parts, groups, rows_of, lanes), jnp.bfloat16)
        for lanes in (width, width + spare)
        for rows_of in (main_slots, tail_height)
    ]
    return pl.pallas_call(
        functools.partial(expert_act_kernel, experts_here),
        grid=(parts, experts_here),
        out_shape=(act_shape, act_shape, act_shape, slot_shape(width), slot_shape(width + spare)),
        in_specs=row_specs(rows, experts_here, order)
        + row_specs(grads, experts_here, order)
        + [weight_spec] * 3,
        out_specs=(
            act_spec,
            act_spec,
            act_spec,
            pl.BlockSpec(memory_space=pl.ANY),
            pl.BlockSpec(memory_space=pl.ANY),
        ),
        scratch_shapes=scratch + [pltpu.SemaphoreType.DMA((4,))],
        compiler_params=pltpu.CompilerParams(vmem_limit_bytes=60 * mega),
        cost_estimate=pl.CostEstimate(
            flops=12 * experts_here * count * width * units,
            transcendentals=experts_here * count * units,
            bytes_accessed=6 * experts_here * width * units + 8 * experts_here * count * width,
        ),
        name="expert_act",
    )(rows, rows, grads, grads, gate_weight, up_weight, down_weight)


def expert_weight_kernel(
    parts,
    groups,
    columns,
    chunks,
    row_main,
    row_tail,
    grad_main,
    grad_tail,
    hidden_ref,
    grad_gate_ref,
    grad_up_ref,
    grads_qkv,
    grads_own,
    piece,
    qkv_rows,
    gate_out,
    up_out,
    down_out,
    grads_out,
    sum_all,
    piece_all,
    qkv_all,
    *scratch,
):
    expert, part = pl.program_id(0), pl.program_id(1)
    steps = EXPERTS // groups * parts
    now = expert * parts + part
    spot = Spot(groups, columns)
    tail = Tail(
        spot,
        chunks,
        (grads_qkv, grads_own, piece, qkv_rows, grads_out, sum_all, piece_all, qkv_all),
        scratch,
    )

    @pl.when(now == 0)
    def _():
        spot.meet()
        tail.begin()

    sources = row_main.shape[0] * row_main.shape[1]
    select = tail_select(expert, sources, row_tail.shape[2])
    wide_rows = expert_input(row_main, row_tail, select)
    rows = wide_rows[:, :D]
    grads = expert_input(grad_main, grad_tail, select)
    grad_low = (grads.astype(jnp.float32) * gates_of(wide_rows)).astype(jnp.bfloat16)

    @pl.when(part == 0)
    def _():
        gate_out[0] = tn_dot(grad_gate_ref[0], rows)
        up_out[0] = tn_dot(grad_up_ref[0], rows)
        down_out[0] = tn_dot(hidden_ref[0], grad_low)

    if parts > 1:

        @pl.when(part > 0)
        def _():
            gate_out[0] += tn_dot(grad_gate_ref[0], rows)
            up_out[0] += tn_dot(grad_up_ref[0], rows)
            down_out[0] += tn_dot(hidden_ref[0], grad_low)

    @pl.when(now == 0)
    def _():
        tail.gather()

    @pl.when(now == steps // 2)
    def _():
        tail.hop(1)

    @pl.when(now == steps - 1)
    def _():
        tail.hop(2)
        tail.hop(3)
        tail.finish()


def expert_weight_grads(
    rows, grads, hidden, grad_gate, grad_up, grads_qkv, grads_own, piece, qkv_rows
):
    groups, row_count, thirds = grads_qkv.shape
    apart = thirds // 3 % 128 != 0
    grads_shape = grads_qkv.shape if apart else (row_count, thirds * groups)
    columns, chunks = grads_own.shape[:2]
    block = grads_own.shape[2:]
    shape_of = lambda shape: jax.ShapeDtypeStruct(shape, jnp.bfloat16)
    experts_here, count, units = hidden.shape
    width = grads.shape[-1]
    parts = parts_of(rows)
    order = lambda index: index
    act_spec = pl.BlockSpec((1, count // parts, units), lambda e, c: (e, c, 0))
    out_spec = pl.BlockSpec((1, units, width), lambda e, c: (e, 0, 0))
    out_shape = jax.ShapeDtypeStruct((experts_here, units, width), jnp.float32)
    return pl.pallas_call(
        functools.partial(expert_weight_kernel, parts, groups, columns, chunks),
        grid=(experts_here, parts),
        out_shape=(
            out_shape,
            out_shape,
            out_shape,
            shape_of(grads_shape),
            shape_of((groups, chunks) + block),
            shape_of((groups,) + piece.shape),
            shape_of((columns,) + qkv_rows.shape),
        ),
        in_specs=row_specs(rows, experts_here, order)
        + row_specs(grads, experts_here, order)
        + [act_spec] * 3
        + [anywhere] * 4,
        out_specs=(out_spec, out_spec, out_spec) + (anywhere,) * 4,
        scratch_shapes=Tail.scratch(columns, groups, chunks, block, 1 if apart else 3),
        compiler_params=comm_params(7, 60),
        cost_estimate=pl.CostEstimate(
            flops=6 * experts_here * count * width * units,
            transcendentals=0,
            bytes_accessed=12 * experts_here * width * units + 10 * experts_here * count * width,
        ),
        name="expert_weight_grads",
    )(
        rows,
        rows,
        grads,
        grads,
        hidden,
        grad_gate,
        grad_up,
        grads_qkv,
        grads_own,
        piece,
        qkv_rows,
    )


def pair_slots(token_routes, ranks, experts_here):
    row_count = token_routes.shape[0]
    expert_pair = jnp.concatenate([token_routes[:, 0], token_routes[:, 1]])
    rank_pair = jnp.concatenate([ranks, ranks + row_count])
    earlier = (expert_pair[None, :] == expert_pair[:, None]) & (
        rank_pair[None, :] < rank_pair[:, None]
    )
    slot_index = jnp.sum(earlier.astype(jnp.int32), axis=1)
    height = slot_rows(experts_here)
    local = expert_pair % experts_here
    main_at = local * main_slots + slot_index
    tail_at = experts_here * main_slots + local * tail_slots + slot_index - main_slots
    row = jnp.where(slot_index < main_slots, main_at, tail_at)
    slots = (expert_pair // experts_here) * height + row
    return jnp.where(slot_index < CAP, slots, -1)


def router_head(logits, token_routes, weights):
    token_count = logits.shape[0]
    probabilities = jax.nn.softmax(logits, axis=-1)
    log_totals = jax.nn.logsumexp(logits, axis=-1)
    picked = (token_routes[:, :, None] == jnp.arange(EXPERTS, dtype=jnp.int32)).astype(jnp.float32)
    chosen = jnp.sum(picked * probabilities[:, None, :], axis=-1)
    gate_values = chosen / jnp.sum(chosen, axis=1, keepdims=True)
    shares = jnp.sum(picked, axis=(0, 1)) / (token_count * TOP)
    balance = EXPERTS * jnp.sum(shares * jnp.sum(probabilities, axis=0))
    return (gate_values, weights[0] * jnp.sum(log_totals * log_totals) + weights[1] * balance)


def column(values, rows):
    return jnp.pad(values, (0, rows - values.shape[0]))[:, None]


def shards(
    inputs,
    grad_out,
    prefix,
    routes,
    priority,
    loss_weights,
    norm_attn,
    norm_moe,
    qkv_weight,
    out_weight,
    bias_table,
    router_weight,
    gate_weight,
    up_weight,
    down_weight,
):
    row_count = inputs.shape[0]
    groups = lax.axis_size("expert")
    columns_of = lax.axis_size("shard")
    place = lax.axis_index("expert")
    length = row_count * groups
    heads_here = HEADS // groups
    width = heads_here * HEAD
    experts_here = EXPERTS // groups
    shard_rows = D // columns_of
    height = slot_rows(experts_here)

    own_columns = lax.dynamic_slice_in_dim(
        qkv_weight.reshape(shard_rows, 3, groups, width), place, 1, 2
    ).reshape(shard_rows, 3 * width)
    packed_small = jnp.concatenate(
        [
            own_columns,
            router_weight,
            norm_attn[:, None],
            norm_moe[:, None],
            column(bias_table.reshape(-1), shard_rows),
            jnp.zeros((shard_rows, spare - EXPERTS - 3), jnp.bfloat16),
        ],
        axis=1,
    )
    tokens_all, small_full, out_full = entry_gather(
        inputs.reshape(row_count, D), [packed_small, out_weight], groups, columns_of
    )
    tokens_all = tokens_all.reshape(length, D)
    small_full = small_full.reshape(D, 3 * width + spare)
    out_full = out_full.reshape(D, D)
    own_weight = small_full[:, : 3 * width]
    extra = small_full[:, 3 * width :]
    router_full = extra[:, :EXPERTS]
    gain_attn = extra[:, EXPERTS].astype(jnp.float32)
    gain_moe = extra[:, EXPERTS + 1].astype(jnp.float32)
    table_rows = BUCKETS // columns_of
    table_full = (
        extra[:, EXPERTS + 2].reshape(columns_of, shard_rows)[:, : table_rows * HEADS]
    ).reshape(BUCKETS, HEADS)
    table_own = lax.dynamic_slice_in_dim(
        table_full.astype(jnp.float32), place * heads_here, heads_here, 1
    )
    near_ids = jnp.asarray(skew_buckets(), jnp.int32)
    near_hot = (near_ids[:, None] == jnp.arange(BUCKETS, dtype=jnp.int32)).astype(jnp.float32)
    base_bias = (
        jnp.dot(near_hot, table_own, precision=lax.Precision.HIGHEST).reshape(3, 2 * tile, heads_here)
        * log2e
    )
    base_bias = jnp.transpose(base_bias, (2, 0, 1)).reshape(heads_here * 3, 2 * tile)
    far_bias = jnp.stack([table_own[15], table_own[31]], axis=1) * log2e

    token_routes = routes.reshape(row_count, TOP)
    slots = pair_slots(token_routes, priority.reshape(row_count), experts_here)
    slot_map = (
        jnp.arange(groups * height, dtype=jnp.int32)[:, None] == slots[None, :]
    ).reshape(groups * height, TOP, row_count)
    slot_any = jnp.any(slot_map, axis=1).astype(jnp.bfloat16)
    slot_pairs = slot_map.astype(jnp.bfloat16).reshape(groups * height, TOP * row_count)

    grad_low = grad_out.reshape(row_count, D)
    grad_slots = nn_dot(slot_any, grad_low).astype(jnp.bfloat16).reshape(groups, height, D)
    normed_all = rms_norm(tokens_all.astype(jnp.float32), gain_attn).astype(jnp.bfloat16)
    qkv_own = nn_dot(normed_all, own_weight).astype(jnp.bfloat16)
    mixed_own, totals, grads_received = attend_forward(
        prefix, far_bias, base_bias, qkv_own, grad_slots, columns_of
    )
    attended = exchange_mixed(mixed_own.reshape(groups, row_count, width), columns_of, 8)

    tokens_in = inputs.reshape(row_count, D).astype(jnp.float32)
    middle = tokens_in + nn_dot(attended, out_full)
    normed_two, norm_two_back = jax.vjp(rms_norm, middle, gain_moe)
    low_two = normed_two.astype(jnp.bfloat16)
    logits = nn_dot(low_two, router_full)
    router_out, router_back = jax.vjp(
        lambda logit_in: router_head(logit_in, token_routes, loss_weights), logits
    )
    gate_values = router_out[0]
    gate_high = lax.reduce_precision(gate_values, 8, 7)
    gate_parts = jnp.stack([gate_high, gate_values - gate_high], axis=-1).astype(jnp.bfloat16)
    wide_rows = jnp.concatenate(
        [
            jnp.broadcast_to(low_two[None], (TOP, row_count, D)),
            jnp.pad(jnp.transpose(gate_parts, (1, 0, 2)), ((0, 0), (0, 0), (0, spare - 2))),
        ],
        axis=2,
    ).reshape(TOP * row_count, D + spare)
    outgoing = nn_dot(slot_pairs, wide_rows).astype(jnp.bfloat16)
    rows_received = dispatch(outgoing.reshape(groups, height, D + spare), columns_of, 2)
    gate_across, up_across, down_across = (
        jnp.transpose(weight, (0, 2, 1)) for weight in (gate_weight, up_weight, down_weight)
    )
    hidden, grad_gate, grad_up, result_part, back_part = expert_act(
        rows_received, grads_received, gate_across, up_across, down_across
    )
    grad_returned = collect(back_part, 3).reshape(groups * height, D + spare)
    grad_low_two = tn_dot(slot_any, grad_returned[:, :D])
    grad_gates = jnp.transpose(
        tn_dot(slot_pairs, grad_returned[:, D:])[:, 0].reshape(TOP, row_count)
    )
    grad_top = grad_low.astype(jnp.float32)
    grad_logits = router_back((grad_gates, jnp.ones((), jnp.float32)))[0]
    low_logits = grad_logits.astype(jnp.bfloat16)
    router_grad = tn_dot(low_two, low_logits)
    grad_low_two = grad_low_two + nt_dot(low_logits, router_full)
    grad_middle_norm, gain_moe_grad = norm_two_back(grad_low_two)
    grad_middle = grad_top + grad_middle_norm
    low_middle = grad_middle.astype(jnp.bfloat16)
    out_grad = tn_dot(attended, low_middle)
    grad_attended = nt_dot(low_middle, out_full).astype(jnp.bfloat16)
    grad_mixed, out_sums = exchange_grad_mixed(
        grad_attended,
        out_grad.astype(jnp.bfloat16).reshape(columns_of, groups, shard_rows // groups, D),
        groups,
        9,
    )
    grad_qkv, near_sums, side_sums, returned, out_piece = attend_backward(
        prefix,
        far_bias,
        base_bias,
        qkv_own,
        mixed_own,
        grad_mixed.reshape(length, width),
        totals,
        result_part,
        out_sums,
        columns_of,
    )
    pair_out = tn_dot(slot_pairs, returned.reshape(groups * height, D)).reshape(
        TOP, row_count, D
    )
    mixture = gate_values[:, 0:1] * pair_out[0] + gate_values[:, 1:2] * pair_out[1]
    output = (middle + mixture).astype(jnp.bfloat16)

    table_grad = jnp.einsum(
        "hil,ilb->bh",
        near_sums.reshape(heads_here, 3, 2 * tile),
        near_hot.reshape(3, 2 * tile, BUCKETS),
        precision=lax.Precision.HIGHEST,
    )
    far_sums = jnp.sum(side_sums, axis=(2, 3))
    bucket_ids = jnp.arange(BUCKETS, dtype=jnp.int32)[:, None]
    table_grad = table_grad + jnp.where(bucket_ids == 15, far_sums[:, 0][None], 0.0)
    table_grad = table_grad + jnp.where(bucket_ids == 31, far_sums[:, 1][None], 0.0)
    table_column = jnp.pad(
        table_grad.reshape(columns_of, table_rows * heads_here),
        ((0, 0), (0, shard_rows - table_rows * heads_here)),
    ).reshape(D, 1)

    own_grad = tn_dot(normed_all, grad_qkv)
    gain_part = jnp.sum(own_grad * own_weight.astype(jnp.float32), axis=1) / gain_attn
    last_pack = jnp.concatenate(
        [
            own_grad,
            gain_part[:, None],
            table_column,
            gain_moe_grad[:, None],
            router_grad,
            jnp.zeros((D, spare - 3 - EXPERTS), jnp.float32),
        ],
        axis=1,
    ).astype(jnp.bfloat16)
    chunks = 2
    gate_grad, up_grad, down_grad, grad_projected, last_all, out_all, qkv_full = (
        expert_weight_grads(
            rows_received,
            grads_received,
            hidden,
            grad_gate,
            grad_up,
            grad_qkv.reshape(groups, row_count, 3 * width),
            last_pack.reshape(columns_of, chunks, shard_rows // chunks, 3 * width + spare),
            out_piece,
            qkv_weight,
        )
    )
    qkv_full = qkv_full.reshape(D, 3 * D)
    out_total = out_all.reshape(shard_rows, D).astype(jnp.float32)
    last_all = last_all.reshape(groups, shard_rows, 3 * width + spare)
    qkv_total = unpack_columns(last_all, width)
    last_extra = last_all[:, :, 3 * width :].astype(jnp.float32)
    extra_total = jnp.sum(last_extra, axis=0)
    table_total = jnp.transpose(
        last_extra[:, : table_rows * heads_here, 1].reshape(groups, table_rows, heads_here),
        (1, 0, 2),
    ).reshape(table_rows, HEADS)

    if width % 128:
        grad_projected = jnp.transpose(
            grad_projected.reshape(groups, row_count, 3, width), (1, 2, 0, 3)
        ).reshape(row_count, 3 * D)
    grad_low_one = nt_dot(grad_projected, qkv_full)
    _, norm_one_back = jax.vjp(lambda features: rms_norm(features, gain_attn), tokens_in)
    input_grad = grad_middle + norm_one_back(grad_low_one)[0]
    return (
        output.reshape(row_count, 1, D),
        input_grad.reshape(row_count, 1, D),
        extra_total[:, 0],
        extra_total[:, 2],
        qkv_total,
        out_total,
        table_total,
        extra_total[:, 3 : 3 + EXPERTS],
        jnp.transpose(gate_grad, (0, 2, 1)),
        jnp.transpose(up_grad, (0, 2, 1)),
        jnp.transpose(down_grad, (0, 2, 1)),
    )


def solution(mesh):
    placed = (
        P("expert", "shard", None),
        P("expert", "shard", None),
        P("shard"),
        P("expert", "shard", None),
        P("expert", "shard", None),
        P(),
        P("shard"),
        P("shard"),
        P("shard", None),
        P("shard", None),
        P("shard", None),
        P("shard", None),
        P("expert", None, "shard"),
        P("expert", None, "shard"),
        P("expert", None, "shard"),
    )
    return jax.shard_map(
        shards,
        mesh=mesh,
        in_specs=placed,
        out_specs=(
            P("expert", "shard", None),
            P("expert", "shard", None),
            P("shard"),
            P("shard"),
            P("shard", None),
            P("shard", None),
            P("shard", None),
            P("shard", None),
            P("expert", None, "shard"),
            P("expert", None, "shard"),
            P("expert", None, "shard"),
        ),
        check_vma=False,
    )
```

```python
import functools
import math

import jax
import jax.numpy as jnp
import numpy as np
from jax import lax
from jax.experimental import pallas as pl
from jax.experimental.pallas import tpu as pltpu
from jax.sharding import PartitionSpec as P

D = 1024
HEADS = 16
HEAD = 64
FF = 2816
EXPERTS = 32
TOP = 2
BUCKETS = 32
CAP = 18

epsilon = 1e-06
masked_score = -1e30
far_bounds = (12, 16, 23, 32, 46, 64, 91)
tile = 256
main_slots = 16
tail_slots = CAP - main_slots
log2e = math.log2(math.e)
score_scale = HEAD ** (-0.5)
mega = 1024 * 1024
part_sources = 32
spare = 128


MESH = pl.DeviceIdType.MESH


def flip(index, key):
    out, bit = index, 1
    while bit <= key:
        if key & bit:
            out = out + bit * (1 - 2 * ((index // bit) % 2))
        bit *= 2
    return out


class Spot:
    def __init__(self, groups, columns):
        self.groups, self.columns = groups, columns
        self.place = lax.axis_index("expert")
        self.lane = lax.axis_index("shard")
        self.half = columns // 2
        self.chip = self.lane // 2
        self.core = self.lane % 2
        self.partner = self.chip * 2 + 1 - self.core

    def across(self, step):
        return ((self.chip + step) % self.half) * 2 + self.core

    def behind(self, step):
        return ((self.chip + self.half - step) % self.half) * 2 + self.core

    def lane_at(self, step, other):
        chip = (self.chip + step) % self.half
        return chip * 2 + ((1 - self.core) if other else self.core)

    def meet(self):
        barrier = pltpu.get_barrier_semaphore()
        for key in range(1, self.groups):
            peer = (flip(self.place, key), self.lane)
            pl.semaphore_signal(barrier, inc=1, device_id=peer, device_id_type=MESH)
        for step in range(1, self.columns):
            peer = (self.place, (self.lane + step) % self.columns)
            pl.semaphore_signal(barrier, inc=1, device_id=peer, device_id_type=MESH)
        pl.semaphore_wait(barrier, self.groups + self.columns - 2)


def remote(source, target, send_sem, recv_sem, peer):
    return pltpu.make_async_remote_copy(
        src_ref=source,
        dst_ref=target,
        send_sem=send_sem,
        recv_sem=recv_sem,
        device_id=peer,
        device_id_type=MESH,
    )


def line_shape(groups):
    across = groups // 4
    return 4, across


class LineGather:
    def __init__(self, spot, own, full, local_sem, send_sems, recv_sems):
        self.spot, self.own, self.full = spot, own, full
        self.local_sem, self.send_sems, self.recv_sems = local_sem, send_sems, recv_sems
        self.long, self.wide = line_shape(spot.groups)
        self.z = spot.place // self.wide
        self.y = spot.place % self.wide

    @staticmethod
    def sems(groups):
        long, wide = line_shape(groups)
        return [
            pltpu.SemaphoreType.DMA(()),
            pltpu.SemaphoreType.DMA((2 * long - 1, wide + 1)),
            pltpu.SemaphoreType.DMA((groups,)),
        ]

    def copy(self, job, way, origin, source, target):
        return remote(
            source,
            self.full.at[origin],
            self.send_sems.at[job, way],
            self.recv_sems.at[origin],
            (target, self.spot.lane),
        )

    def each(self, job, origin, source, up, down, act):
        place, wide = self.spot.place, self.wide
        if up:

            @pl.when(self.z + 1 < self.long)
            def _():
                act(self.copy(job, 0, origin, source, place + wide))

        if down:

            @pl.when(self.z >= 1)
            def _():
                act(self.copy(job, 1, origin, source, place - wide))

        for step in range(1, wide):
            target = self.z * wide + (self.y + step) % wide
            act(self.copy(job, 1 + step, origin, source, target))

    def begin(self):
        place = self.spot.place
        self.each(0, place, self.own, True, True, lambda copy: copy.start())
        pltpu.make_async_copy(self.own, self.full.at[place], self.local_sem).start()

    def arrive(self, origin):
        self.copy(0, 0, origin, self.own, self.spot.place).wait_recv()

    def hop(self, k):
        place, wide = self.spot.place, self.wide

        @pl.when(self.z >= k)
        def _():
            origin = place - k * wide
            self.arrive(origin)
            self.each(k, origin, self.full.at[origin], True, False, lambda copy: copy.start())

        @pl.when(self.z + k < self.long)
        def _():
            origin = place + k * wide
            self.arrive(origin)
            job = self.long - 1 + k
            self.each(job, origin, self.full.at[origin], False, True, lambda copy: copy.start())

    def finish(self):
        place, wide = self.spot.place, self.wide
        for row in range(self.long):
            for step in range(1, wide):
                self.arrive(row * wide + (self.y + step) % wide)
        stop = lambda copy: copy.wait_send()
        self.each(0, place, self.own, True, True, stop)
        for k in range(1, self.long):

            @pl.when(self.z >= k)
            def _():
                origin = place - k * wide
                self.each(k, origin, self.full.at[origin], True, False, stop)

            @pl.when(self.z + k < self.long)
            def _():
                origin = place + k * wide
                job = self.long - 1 + k
                self.each(job, origin, self.full.at[origin], False, True, stop)

        pltpu.make_async_copy(self.own, self.full.at[place], self.local_sem).wait()


class ColumnGather:
    def __init__(self, spot, own, full, local_sem, across_send, across_recv, core_send, core_recv):
        self.spot, self.own, self.full = spot, own, full
        self.local_sem = local_sem
        self.across_send, self.across_recv = across_send, across_recv
        self.core_send, self.core_recv = core_send, core_recv

    @staticmethod
    def sems(columns):
        return [pltpu.SemaphoreType.DMA(())] + [pltpu.SemaphoreType.DMA((columns // 2,))] * 4

    def across_copy(self, step):
        spot = self.spot
        return remote(
            self.own,
            self.full.at[spot.lane],
            self.across_send.at[step],
            self.across_recv.at[step],
            (spot.place, spot.across(step)),
        )

    def core_copy(self, step):
        spot = self.spot
        source = self.own if step == 0 else self.full.at[spot.behind(step)]
        target = spot.lane if step == 0 else spot.behind(step)
        return remote(
            source,
            self.full.at[target],
            self.core_send.at[step],
            self.core_recv.at[step],
            (spot.place, spot.partner),
        )

    def begin(self):
        for step in range(1, self.spot.half):
            self.across_copy(step).start()
        self.core_copy(0).start()
        pltpu.make_async_copy(self.own, self.full.at[self.spot.lane], self.local_sem).start()

    def forward(self):
        for step in range(1, self.spot.half):
            self.across_copy(step).wait_recv()
            self.core_copy(step).start()

    def finish(self):
        for step in range(self.spot.half):
            self.core_copy(step).wait_recv()
        for step in range(self.spot.half):
            self.core_copy(step).wait_send()
        for step in range(1, self.spot.half):
            self.across_copy(step).wait_send()
        pltpu.make_async_copy(self.own, self.full.at[self.spot.lane], self.local_sem).wait()


def comm_params(which, limit=16):
    return pltpu.CompilerParams(
        collective_id=which, has_side_effects=True, vmem_limit_bytes=limit * mega
    )


anywhere = pl.BlockSpec(memory_space=pl.ANY)


def entry_kernel(groups, columns, count, *refs):
    tokens, refs = refs[0], refs[1:]
    owns, refs = refs[:count], refs[count:]
    tokens_all, refs = refs[0], refs[1:]
    fulls, sems = refs[:count], refs[count:]
    spot = Spot(groups, columns)
    line = LineGather(spot, tokens, tokens_all, *sems[:3])
    across = [
        ColumnGather(spot, owns[i], fulls[i], *sems[3 + 5 * i : 8 + 5 * i]) for i in range(count)
    ]
    spot.meet()
    line.begin()
    for gather in across:
        gather.begin()
    for k in range(1, 4):
        line.hop(k)
        if k <= count:
            across[k - 1].forward()
    for gather in across[3:]:
        gather.forward()
    for gather in across:
        gather.finish()
    line.finish()


def entry_gather(tokens, owns, groups, columns):
    count = len(owns)
    sems = LineGather.sems(groups) + ColumnGather.sems(columns) * count
    shapes = [jax.ShapeDtypeStruct((groups,) + tokens.shape, tokens.dtype)] + [
        jax.ShapeDtypeStruct((columns,) + own.shape, own.dtype) for own in owns
    ]
    return pl.pallas_call(
        functools.partial(entry_kernel, groups, columns, count),
        out_shape=shapes,
        in_specs=[anywhere] * (1 + count),
        out_specs=[anywhere] * (1 + count),
        scratch_shapes=sems,
        compiler_params=comm_params(1),
        name="entry_gather",
    )(tokens, *owns)


class Dispatch:
    def __init__(self, spot, rows, full, sems):
        self.spot, self.rows, self.full = spot, rows, full
        self.local, self.send, self.recv = sems[:3]
        self.across_send, self.across_recv, self.core_send, self.core_recv = sems[3:]

    @staticmethod
    def sems(groups, columns):
        return (
            [pltpu.SemaphoreType.DMA(())]
            + [pltpu.SemaphoreType.DMA((groups,))] * 2
            + [pltpu.SemaphoreType.DMA((groups, columns // 2))] * 4
        )

    def own(self):
        spot = self.spot
        return pltpu.make_async_copy(
            self.rows.at[spot.place], self.full.at[spot.lane, spot.place], self.local
        )

    def swap(self, key):
        spot = self.spot
        peer = flip(spot.place, key)
        return remote(
            self.rows.at[peer],
            self.full.at[spot.lane, spot.place],
            self.send.at[key],
            self.recv.at[key],
            (peer, spot.lane),
        )

    def across(self, key, step):
        spot = self.spot
        block = self.full.at[spot.lane, flip(spot.place, key)]
        return remote(
            block,
            block,
            self.across_send.at[key, step],
            self.across_recv.at[key, step],
            (spot.place, spot.across(step)),
        )

    def core(self, key, step):
        spot = self.spot
        block = self.full.at[spot.behind(step), flip(spot.place, key)]
        return remote(
            block,
            block,
            self.core_send.at[key, step],
            self.core_recv.at[key, step],
            (spot.place, spot.partner),
        )

    def begin(self):
        self.own().start()
        for key in range(1, self.spot.groups):
            self.swap(key).start()

    def pass_on(self, key):
        for step in range(1, self.spot.half):
            self.across(key, step).wait_recv()
            self.core(key, step).start()

    def advance(self, key):
        if key == 0:
            self.own().wait()
        else:
            self.swap(key).wait_recv()
        for step in range(1, self.spot.half):
            self.across(key, step).start()
        self.core(key, 0).start()
        if key > 0:
            self.pass_on(key - 1)

    def finish(self):
        groups, half = self.spot.groups, self.spot.half
        self.pass_on(groups - 1)
        for key in range(groups):
            for step in range(half):
                self.core(key, step).wait_recv()
        for key in range(groups):
            if key > 0:
                self.swap(key).wait_send()
            for step in range(1, half):
                self.across(key, step).wait_send()
            for step in range(half):
                self.core(key, step).wait_send()


def dispatch_kernel(groups, columns, rows, full, *sems):
    spot = Spot(groups, columns)
    job = Dispatch(spot, rows, full, sems)
    spot.meet()
    job.begin()
    for key in range(groups):
        job.advance(key)
    job.finish()


def dispatch(rows, columns, which):
    groups = rows.shape[0]
    return pl.pallas_call(
        functools.partial(dispatch_kernel, groups, columns),
        out_shape=jax.ShapeDtypeStruct((columns,) + rows.shape, rows.dtype),
        in_specs=[anywhere],
        out_specs=anywhere,
        scratch_shapes=Dispatch.sems(groups, columns),
        compiler_params=comm_params(which),
        name="dispatch_rows",
    )(rows)


class Exchange:
    def __init__(self, spot, blocks, thirds, local, send, recv):
        self.spot, self.blocks, self.thirds = spot, blocks, range(thirds)
        self.local, self.send, self.recv = local, send, recv

    @staticmethod
    def sems(groups, thirds):
        return [pltpu.SemaphoreType.DMA((thirds,))] + [
            pltpu.SemaphoreType.DMA((groups, thirds))
        ] * 2

    def copy(self, key, third):
        spot = self.spot
        peer = flip(spot.place, key)
        source, target = self.blocks(peer, third)
        if key == 0:
            return pltpu.make_async_copy(source, target, self.local.at[third])
        return remote(
            source,
            target,
            self.send.at[key, third],
            self.recv.at[key, third],
            (peer, spot.lane),
        )

    def start(self, key):
        for third in self.thirds:
            self.copy(key, third).start()

    def begin(self):
        for key in range(self.spot.groups):
            self.start(key)

    def arrive(self):
        for key in range(self.spot.groups):
            for third in self.thirds:
                copy = self.copy(key, third)
                copy.wait() if key == 0 else copy.wait_recv()

    def finish(self):
        for key in range(1, self.spot.groups):
            for third in self.thirds:
                self.copy(key, third).wait_send()


class ColumnSum:
    def __init__(self, spot, chunks, order, part, bufs, sems):
        self.spot, self.chunks, self.order, self.part = spot, chunks, order, part
        self.pair_in, self.mine, self.across_out, self.across_in = bufs
        self.local, self.pair_send, self.pair_recv, self.across_send, self.across_recv = sems

    @staticmethod
    def scratch(columns, chunks, block):
        half = columns // 2
        return [pltpu.VMEM((half, chunks) + block, jnp.bfloat16)] * 4 + [
            pltpu.SemaphoreType.DMA((half, chunks))
        ] * 5

    def pair_copy(self, step, k):
        spot = self.spot
        return remote(
            self.part.at[spot.lane_at(step, True), self.order(k)],
            self.pair_in.at[step, k],
            self.pair_send.at[step, k],
            self.pair_recv.at[step, k],
            (spot.place, spot.partner),
        )

    def mine_copy(self, step, k):
        return pltpu.make_async_copy(
            self.part.at[self.spot.lane_at(step, False), self.order(k)],
            self.mine.at[step, k],
            self.local.at[step, k],
        )

    def across_copy(self, step, k):
        spot = self.spot
        return remote(
            self.across_out.at[step, k],
            self.across_in.at[step, k],
            self.across_send.at[step, k],
            self.across_recv.at[step, k],
            (spot.place, spot.across(step)),
        )

    def begin(self):
        half = self.spot.half
        for k in range(self.chunks):
            for step in list(range(1, half)) + [0]:
                self.pair_copy(step, k).start()
                self.mine_copy(step, k).start()

    def pair_sum(self, step, k):
        self.pair_copy(step, k).wait_recv()
        self.mine_copy(step, k).wait()
        return self.mine[step, k].astype(jnp.float32) + self.pair_in[step, k].astype(jnp.float32)

    def middle(self, k):
        for step in range(1, self.spot.half):
            self.across_out[step, k] = self.pair_sum(step, k).astype(jnp.bfloat16)
            self.across_copy(step, k).start()

    def last(self, k):
        total = self.pair_sum(0, k)
        for step in range(1, self.spot.half):
            self.across_copy(step, k).wait_recv()
            total = total + self.across_in[step, k].astype(jnp.float32)
        return total.astype(jnp.bfloat16)

    def finish(self):
        for k in range(self.chunks):
            for step in range(self.spot.half):
                self.pair_copy(step, k).wait_send()
                if step:
                    self.across_copy(step, k).wait_send()


class Collect:
    def __init__(self, spot, part, out, scratch):
        self.spot, self.total = spot, scratch[9]
        self.sums = ColumnSum(
            spot, spot.groups, lambda k: flip(spot.place, k), part, scratch[:4], scratch[4:9]
        )
        self.out = out
        self.local, self.send, self.recv = scratch[10:]

    @staticmethod
    def scratch(columns, groups, block):
        return (
            ColumnSum.scratch(columns, groups, block)
            + [pltpu.VMEM((groups,) + block, jnp.bfloat16)]
            + [pltpu.SemaphoreType.DMA(())]
            + [pltpu.SemaphoreType.DMA((groups,))] * 2
        )

    def copy(self, key):
        spot = self.spot
        target = self.out.at[spot.place]
        if key == 0:
            return pltpu.make_async_copy(self.total.at[0], target, self.local)
        peer = flip(spot.place, key)
        return remote(
            self.total.at[key], target, self.send.at[key], self.recv.at[key], (peer, spot.lane)
        )

    def begin(self):
        self.sums.begin()

    def middle(self, key):
        self.sums.middle(key)

    def last(self, key):
        self.total[key] = self.sums.last(key)
        self.copy(key).start()

    def finish(self):
        for key in range(1, self.spot.groups):
            self.copy(key).wait_recv()
        for key in range(1, self.spot.groups):
            self.copy(key).wait_send()
        self.copy(0).wait()
        self.sums.finish()


def collect_kernel(groups, columns, part, out, *scratch):
    spot = Spot(groups, columns)
    job = Collect(spot, part, out, scratch)
    spot.meet()
    job.begin()
    ahead = 2
    for key in range(ahead):
        job.middle(key)
    for key in range(groups):
        if key + ahead < groups:
            job.middle(key + ahead)
        job.last(key)
    job.finish()


def collect(part, which):
    columns, groups = part.shape[:2]
    block = part.shape[2:]
    return pl.pallas_call(
        functools.partial(collect_kernel, groups, columns),
        out_shape=jax.ShapeDtypeStruct((groups,) + block, part.dtype),
        in_specs=[anywhere],
        out_specs=anywhere,
        scratch_shapes=Collect.scratch(columns, groups, block),
        compiler_params=comm_params(which, 56),
        name="collect_rows",
    )(part)


def lanes_at(place, width):
    return pl.ds(pl.multiple_of(place * width, 128), width)


def mixed_kernel(groups, columns, mixed, attended, *sems):
    spot = Spot(groups, columns)
    width = mixed.shape[2]

    def blocks(at, third):
        if width % 128:
            return mixed.at[at], attended.at[spot.place]
        return mixed.at[at], attended.at[:, lanes_at(spot.place, width)]

    job = Exchange(spot, blocks, 1, *sems)
    spot.meet()
    job.begin()
    job.arrive()
    job.finish()


def exchange_mixed(mixed, columns, which):
    groups, rows, width = mixed.shape
    shape = mixed.shape if width % 128 else (rows, groups * width)
    out = pl.pallas_call(
        functools.partial(mixed_kernel, groups, columns),
        out_shape=jax.ShapeDtypeStruct(shape, mixed.dtype),
        in_specs=[anywhere],
        out_specs=anywhere,
        scratch_shapes=Exchange.sems(groups, 1),
        compiler_params=comm_params(which),
        name="exchange_mixed",
    )(mixed)
    if width % 128:
        out = jnp.transpose(out, (1, 0, 2)).reshape(rows, groups * width)
    return out


class Tail:
    def __init__(self, spot, chunks, refs, scratch):
        grads, part, piece, weight, grads_out, sum_all, piece_all, weight_all = refs
        groups = spot.groups
        width = grads.shape[2] // 3
        thirds = 3 if width % 128 == 0 else 1

        def blocks(at, third):
            if thirds == 1:
                return grads.at[at], grads_out.at[spot.place]
            columns_to = pl.ds(pl.multiple_of(third * D + spot.place * width, 128), width)
            return grads.at[at, :, pl.ds(third * width, width)], grads_out.at[:, columns_to]

        self.chunks = chunks
        self.sums = ColumnSum(spot, chunks, lambda k: k, part, scratch[:4], scratch[4:9])
        self.own_sum = scratch[9]
        self.swap = Exchange(spot, blocks, thirds, *scratch[10:13])
        self.line = LineGather(spot, self.own_sum, sum_all, *scratch[13:16])
        self.side = LineGather(spot, piece, piece_all, *scratch[16:19])
        self.column = ColumnGather(spot, weight, weight_all, *scratch[19:24])

    @staticmethod
    def scratch(columns, groups, chunks, block, thirds):
        return (
            ColumnSum.scratch(columns, chunks, block)
            + [pltpu.VMEM((chunks,) + block, jnp.bfloat16)]
            + Exchange.sems(groups, thirds)
            + LineGather.sems(groups) * 2
            + ColumnGather.sems(columns)
        )


def tail_kernel(
    groups,
    columns,
    chunks,
    grads,
    normed,
    own_weight,
    gains,
    extra,
    piece,
    weight,
    grads_out,
    sum_all,
    piece_all,
    weight_all,
    grads_sc,
    normed_sc,
    load_sems,
    part,
    *scratch,
):
    spot = Spot(groups, columns)
    refs = (grads, part, piece, weight, grads_out, sum_all, piece_all, weight_all)
    tail = Tail(spot, chunks, refs, scratch)
    wide = grads.shape[2]
    block_rows = D // (columns * chunks)
    loads = [
        pltpu.make_async_copy(grads, grads_sc, load_sems.at[0]),
        pltpu.make_async_copy(normed, normed_sc, load_sems.at[1]),
    ]
    for load in loads:
        load.start()
    spot.meet()
    tail.side.begin()
    tail.swap.begin()
    for load in loads:
        load.wait()
    all_grads = grads_sc[...].reshape(-1, wide)

    for at in range(columns * chunks):
        rows = pl.ds(at * block_rows, block_rows)
        grad = tn_dot(normed_sc[:, rows], all_grads)
        gain = jnp.sum(grad * own_weight[rows, :].astype(jnp.float32), axis=1, keepdims=True)
        gain = gain / gains[rows, :]
        lanes = lax.broadcasted_iota(jnp.int32, (block_rows, spare), 1)
        side = jnp.where(lanes == 0, gain, extra[rows, :].astype(jnp.float32))
        part[at // chunks, at % chunks] = jnp.concatenate([grad, side], axis=1).astype(jnp.bfloat16)
    tail.sums.begin()
    for k in range(chunks):
        tail.sums.middle(k)
    tail.column.begin()
    tail.side.hop(1)
    for k in range(chunks):
        tail.own_sum[k] = tail.sums.last(k)
    tail.line.begin()
    tail.side.hop(2)
    tail.line.hop(1)
    tail.side.hop(3)
    tail.line.hop(2)
    tail.column.forward()
    tail.line.hop(3)
    tail.side.finish()
    tail.swap.arrive()
    tail.line.finish()
    tail.column.finish()
    tail.swap.finish()
    tail.sums.finish()


def tail_exchange(grads, normed, own_weight, gains, extra, piece, weight, columns, which):
    groups, row_count, wide = grads.shape
    apart = wide // 3 % 128 != 0
    grads_shape = grads.shape if apart else (row_count, wide * groups)
    chunks = 2
    block = (D // columns // chunks, wide + spare)
    shape_of = lambda shape: jax.ShapeDtypeStruct(shape, jnp.bfloat16)
    inside = pl.BlockSpec(memory_space=pltpu.VMEM)
    return pl.pallas_call(
        functools.partial(tail_kernel, groups, columns, chunks),
        out_shape=(
            shape_of(grads_shape),
            shape_of((groups, chunks) + block),
            shape_of((groups,) + piece.shape),
            shape_of((columns,) + weight.shape),
        ),
        in_specs=[anywhere, anywhere, inside, inside, inside, anywhere, anywhere],
        out_specs=(anywhere,) * 4,
        scratch_shapes=[
            pltpu.VMEM(grads.shape, jnp.bfloat16),
            pltpu.VMEM(normed.shape, jnp.bfloat16),
            pltpu.SemaphoreType.DMA((2,)),
            pltpu.VMEM((columns, chunks) + block, jnp.bfloat16),
        ]
        + Tail.scratch(columns, groups, chunks, block, 1 if apart else 3),
        compiler_params=comm_params(which, 56),
        name="tail_exchange",
    )(grads, normed, own_weight, gains, extra, piece, weight)


def unpack_kernel(width, packed, out):
    for group in range(packed.shape[0]):
        out[:, group * width : (group + 1) * width] = packed[group].astype(jnp.float32)


def unpack_columns(packed, width):
    groups, rows = packed.shape[:2]
    if width % 128:
        blocks = packed[:, :, : 3 * width].reshape(groups, rows, 3, width).astype(jnp.float32)
        return jnp.transpose(blocks, (1, 2, 0, 3)).reshape(rows, 3 * groups * width)
    return pl.pallas_call(
        functools.partial(unpack_kernel, width),
        grid=(3,),
        out_shape=jax.ShapeDtypeStruct((rows, 3 * groups * width), jnp.float32),
        in_specs=[pl.BlockSpec((groups, rows, width), lambda t: (0, 0, t))],
        out_specs=pl.BlockSpec((rows, groups * width), lambda t: (0, t)),
        name="unpack_columns",
    )(packed)


def rms_norm(features, scales):
    factor = lax.rsqrt(jnp.mean(features * features, axis=-1, keepdims=True) + epsilon)
    return features * factor * scales


def buckets_of(offsets):
    distance = np.abs(offsets)
    beyond = 8 + np.sum(distance[..., None] >= np.array(far_bounds), axis=-1)
    return np.where(distance < 8, distance, beyond) + 16 * (offsets > 0)


def skew_buckets():
    lanes = np.arange(2 * tile)
    from_query = np.where(lanes < tile, -lanes, 2 * tile - lanes)
    return np.concatenate([buckets_of(near * tile + from_query) for near in (-1, 0, 1)])


def lane_row_mask(head, width, rows):
    lanes = lax.broadcasted_iota(jnp.int32, (rows, width), 1)
    return (lanes >= head * HEAD) & (lanes < (head + 1) * HEAD)


def fold_rows(block, op):
    return op(block.reshape(block.shape[0] // 8, 8, block.shape[1]), axis=0)


def nt_dot(left, right):
    return lax.dot_general(left, right, (((1,), (1,)), ((), ())), preferred_element_type=jnp.float32)


def tn_dot(left, right):
    return lax.dot_general(left, right, (((0,), (0,)), ((), ())), preferred_element_type=jnp.float32)


def nn_dot(left, right):
    return jnp.dot(left, right, preferred_element_type=jnp.float32)


def build_bias(base_ref, far_ref, bias_sc, heads_here):
    for head in range(heads_here):
        for near in range(3):
            row = base_ref[pl.ds(head * 3 + near, 1), :]
            wide = jnp.broadcast_to(row, (tile, 2 * tile))
            skewed = pltpu.roll(wide, 0, 1, stride=1, stride_axis=0)
            bias_sc[head, near] = skewed[:, :tile]
        bias_sc[head, 3] = jnp.full((tile, tile), far_ref[head, 1], jnp.float32)


def unskew_sum(wide):
    lanes = wide.shape[1]
    half = wide.shape[0] // 2
    while half >= 8:
        wide = wide[:half] + pltpu.roll(wide[half:], lanes - half, 1)
        half //= 2
    total = wide[0:1]
    for row in range(1, 8):
        total = total + pltpu.roll(wide[row : row + 1], lanes - row, 1)
    return total


def rows_at(index):
    return pl.ds(pl.multiple_of(index * tile, tile), tile)


def visible_tile(key_tile, query_tile, prefix_length):
    key_pos = key_tile * tile + lax.broadcasted_iota(jnp.int32, (tile, tile), 0)
    query_pos = query_tile * tile + lax.broadcasted_iota(jnp.int32, (tile, tile), 1)
    return (key_pos <= query_pos) | (key_pos < prefix_length)


def attend_forward_kernel(
    heads_here,
    groups,
    columns,
    prefix_ref,
    far_ref,
    base_ref,
    qkv_ref,
    rows_ref,
    mixed_ref,
    totals_ref,
    full_ref,
    bias_sc,
    score_sc,
    value_sc,
    *sems,
):
    width = heads_here * HEAD
    query_tile = pl.program_id(0)
    tiles = qkv_ref.shape[0] // tile
    spot = Spot(groups, columns)
    job = Dispatch(spot, rows_ref, full_ref, sems)

    @pl.when(query_tile == 0)
    def _():
        spot.meet()
        job.begin()

    prefix_length = prefix_ref[0]
    heads = range(heads_here)

    @pl.when(query_tile == 0)
    def _():
        build_bias(base_ref, far_ref, bias_sc, heads_here)
        for key_tile in range(value_sc.shape[1] // tile):
            rows = pl.ds(key_tile * tile, tile)
            values = qkv_ref[rows, 2 * width : 3 * width].astype(jnp.float32)
            value_sc[:, rows] = jnp.transpose(values).astype(jnp.bfloat16)

    queries = qkv_ref[rows_at(query_tile), :width]
    head_queries = [
        jnp.where(lane_row_mask(head, width, tile), queries, jnp.zeros_like(queries)) for head in heads
    ]

    def score_tiles(key_tile, tops, finish):
        keys = qkv_ref[rows_at(key_tile), width : 2 * width]
        out = []
        for head in heads:
            scores = finish(head, nt_dot(keys, head_queries[head]) * (score_scale * log2e))
            score_sc[head, rows_at(key_tile), :] = scores
            out.append(jnp.maximum(tops[head], fold_rows(scores, jnp.max)))
        return tuple(out)

    def far_body(key_tile, tops):
        return score_tiles(key_tile, tops, lambda head, raw: raw + far_ref[head, 0])

    def near_body(key_tile, tops):
        return score_tiles(key_tile, tops, lambda head, raw: raw + bias_sc[head, 0])

    def tail_body(key_tile, tops):
        shown = visible_tile(key_tile, query_tile, prefix_length)
        which = 1 + jnp.minimum(key_tile - query_tile, 2)
        return score_tiles(
            key_tile, tops, lambda head, raw: jnp.where(shown, raw + bias_sc[head, which], masked_score)
        )

    tile_count = jnp.maximum(query_tile + 1, tiles // 2)
    near_start = jnp.maximum(query_tile - 1, 0)
    tops = tuple(jnp.full((8, tile), masked_score, jnp.float32) for _ in heads)
    tops = lax.fori_loop(0, near_start, far_body, tops)
    tops = lax.fori_loop(near_start, query_tile, near_body, tops)
    tops = lax.fori_loop(query_tile, tile_count, tail_body, tops)
    tops = [jnp.max(top, axis=0, keepdims=True) for top in tops]

    def mix_body(key_tile, carry):
        sums, mixes = carry
        new_sums, new_mixes = [], []
        for head in heads:
            expos = jnp.exp2(score_sc[head, rows_at(key_tile), :] - tops[head])
            new_sums.append(sums[head] + fold_rows(expos, jnp.sum))
            values = value_sc[head * HEAD : (head + 1) * HEAD, rows_at(key_tile)]
            new_mixes.append(mixes[head] + nn_dot(values, expos.astype(jnp.bfloat16)))
        return (tuple(new_sums), tuple(new_mixes))

    sums, mixes = lax.fori_loop(
        0,
        tile_count,
        mix_body,
        (
            tuple(jnp.zeros((8, tile), jnp.float32) for _ in heads),
            tuple(jnp.zeros((HEAD, tile), jnp.float32) for _ in heads),
        ),
    )
    parts = []
    for head in heads:
        total = jnp.sum(sums[head], axis=0, keepdims=True)
        parts.append(mixes[head] / total)
        totals_ref[0, pl.ds(head, 1), :] = tops[head] + jnp.log2(total)
    mixed_ref[...] = jnp.transpose(jnp.concatenate(parts, axis=0)).astype(jnp.bfloat16)

    for key in range(groups):

        @pl.when(query_tile == key * tiles // groups)
        def _():
            job.advance(key)

    @pl.when(query_tile == tiles - 1)
    def _():
        job.finish()


def attend_forward(prefix, far_bias, base_bias, qkv, rows, columns):
    length = qkv.shape[0]
    groups = rows.shape[0]
    width = qkv.shape[1] // 3
    heads_here = width // HEAD
    tiles = length // tile
    return pl.pallas_call(
        functools.partial(attend_forward_kernel, heads_here, groups, columns),
        grid=(tiles,),
        out_shape=(
            jax.ShapeDtypeStruct((length, width), jnp.bfloat16),
            jax.ShapeDtypeStruct((tiles, heads_here, tile), jnp.float32),
            jax.ShapeDtypeStruct((columns,) + rows.shape, rows.dtype),
        ),
        in_specs=[
            pl.BlockSpec(memory_space=pltpu.SMEM),
            pl.BlockSpec(memory_space=pltpu.SMEM),
            pl.BlockSpec(base_bias.shape, lambda i: (0, 0)),
            pl.BlockSpec(qkv.shape, lambda i: (0, 0)),
            anywhere,
        ],
        out_specs=(
            pl.BlockSpec((tile, width), lambda i: (i, 0)),
            pl.BlockSpec((1, heads_here, tile), lambda i: (i, 0, 0)),
            anywhere,
        ),
        scratch_shapes=[
            pltpu.VMEM((heads_here, 4, tile, tile), jnp.float32),
            pltpu.VMEM((heads_here, length, tile), jnp.float32),
            pltpu.VMEM((width, length), jnp.bfloat16),
        ]
        + Dispatch.sems(groups, columns),
        compiler_params=comm_params(5, 40),
        cost_estimate=pl.CostEstimate(
            flops=40 * length * length * width, transcendentals=length * length * heads_here,
            bytes_accessed=8 * length * width,
        ),
        name="attend_forward",
    )(prefix, far_bias, base_bias, qkv, rows)


def attend_backward_kernel(
    heads_here,
    groups,
    columns,
    prefix_ref,
    far_ref,
    base_ref,
    qkv_ref,
    mixed_ref,
    grad_ref,
    totals_ref,
    part_ref,
    sums_ref,
    out_ref,
    near_ref,
    side_ref,
    result_ref,
    piece_ref,
    bias_sc,
    key_sc,
    grad_key_sc,
    grad_value_sc,
    near_sc,
    *scratch,
):
    width = heads_here * HEAD
    query_tile = pl.program_id(0)
    tiles = qkv_ref.shape[0] // tile
    spot = Spot(groups, columns)
    pieces = scratch[0]
    swap = Exchange(
        spot, lambda at, third: (sums_ref.at[at], pieces.at[spot.place]), 1, *scratch[1:4]
    )
    job = Collect(spot, part_ref, result_ref, scratch[4:])

    @pl.when(query_tile == 0)
    def _():
        spot.meet()
        job.begin()
        swap.begin()

    prefix_length = prefix_ref[0]
    heads = range(heads_here)

    @pl.when(query_tile == 0)
    def _():
        build_bias(base_ref, far_ref, bias_sc, heads_here)
        for key_tile in range(key_sc.shape[1] // tile):
            rows = pl.ds(key_tile * tile, tile)
            keys = qkv_ref[rows, width : 2 * width].astype(jnp.float32)
            key_sc[:, rows] = jnp.transpose(keys).astype(jnp.bfloat16)
        grad_key_sc[...] = jnp.zeros_like(grad_key_sc)
        grad_value_sc[...] = jnp.zeros_like(grad_value_sc)
        near_sc[...] = jnp.zeros_like(near_sc)
        side_ref[...] = jnp.zeros_like(side_ref)

    queries = qkv_ref[rows_at(query_tile), :width]
    grads = grad_ref[rows_at(query_tile), :]
    products = grads.astype(jnp.float32) * mixed_ref[rows_at(query_tile), :].astype(jnp.float32)
    head_queries, head_grads, inners, totals = [], [], [], []
    for head in heads:
        mask = lane_row_mask(head, width, tile)
        head_queries.append(jnp.where(mask, queries, jnp.zeros_like(queries)))
        head_grads.append(jnp.where(mask, grads, jnp.zeros_like(grads)))
        ones = jnp.where(lane_row_mask(head, width, 8), 1.0, 0.0)
        inner = lax.dot_general(
            ones,
            products,
            (((1,), (1,)), ((), ())),
            precision=lax.Precision.HIGHEST,
            preferred_element_type=jnp.float32,
        )
        inners.append(inner[0:1, :])
        totals.append(totals_ref[0, pl.ds(head, 1), :])

    def step(key_tile, carry, finish, keep):
        sides, grad_queries = carry
        keys = qkv_ref[rows_at(key_tile), width : 2 * width]
        values = qkv_ref[rows_at(key_tile), 2 * width : 3 * width]
        new_sides, new_queries = [], []
        key_part, value_part = None, None
        for head in heads:
            raw = nt_dot(keys, head_queries[head]) * (score_scale * log2e)
            attention = jnp.exp2(finish(head, raw))
            grad_weights = nt_dot(values, head_grads[head])
            grad_scores = attention * (grad_weights - inners[head])
            new_sides.append(keep(head, grad_scores, sides[head]))
            low_scores = grad_scores.astype(jnp.bfloat16)
            keys_across = key_sc[head * HEAD : (head + 1) * HEAD, rows_at(key_tile)]
            new_queries.append(grad_queries[head] + nn_dot(keys_across, low_scores))
            value_one = nn_dot(attention.astype(jnp.bfloat16), head_grads[head])
            key_one = nn_dot(low_scores, head_queries[head])
            value_part = value_one if value_part is None else value_part + value_one
            key_part = key_one if key_part is None else key_part + key_one
        grad_key_sc[rows_at(key_tile), :] += key_part
        grad_value_sc[rows_at(key_tile), :] += value_part
        return (tuple(new_sides), tuple(new_queries))

    def add_side(head, grad_scores, side):
        return side + fold_rows(grad_scores, jnp.sum)

    def far_body(key_tile, carry):
        return step(
            key_tile, carry, lambda head, raw: raw + (far_ref[head, 0] - totals[head]), add_side
        )

    def near_body(key_tile, carry):
        def keep(head, grad_scores, side):
            near_sc[head, 0] += grad_scores
            return side

        return step(
            key_tile, carry, lambda head, raw: raw + bias_sc[head, 0] - totals[head], keep
        )

    def tail_body(key_tile, carry):
        shown = visible_tile(key_tile, query_tile, prefix_length)
        which = 1 + jnp.minimum(key_tile - query_tile, 2)

        def keep(head, grad_scores, side):
            near_sc[head, which] += grad_scores
            return side

        return step(
            key_tile,
            carry,
            lambda head, raw: jnp.where(
                shown, raw + bias_sc[head, which] - totals[head], masked_score
            ),
            keep,
        )

    tile_count = jnp.maximum(query_tile + 1, tiles // 2)
    near_start = jnp.maximum(query_tile - 1, 0)
    carry = (
        tuple(jnp.zeros((8, tile), jnp.float32) for _ in heads),
        tuple(jnp.zeros((HEAD, tile), jnp.float32) for _ in heads),
    )
    carry = lax.fori_loop(0, near_start, far_body, carry)
    carry = lax.fori_loop(near_start, query_tile, near_body, carry)
    carry = lax.fori_loop(query_tile, tile_count, tail_body, carry)
    sides, grad_queries = carry
    for head in heads:
        side_ref[head, 0] += sides[head]
    across = jnp.concatenate(grad_queries, axis=0) * score_scale
    out_ref[rows_at(query_tile), :width] = jnp.transpose(across).astype(jnp.bfloat16)

    @pl.when(query_tile == tiles - 1)
    def _():
        out_ref[:, width : 2 * width] = (grad_key_sc[...] * score_scale).astype(jnp.bfloat16)
        out_ref[:, 2 * width : 3 * width] = grad_value_sc[...].astype(jnp.bfloat16)
        for head in heads:
            side_ref[head, 1] = fold_rows(near_sc[head, 3], jnp.sum)
            for near in range(3):
                wide = jnp.concatenate(
                    [near_sc[head, near], jnp.zeros((tile, tile), jnp.float32)], axis=1
                )
                near_ref[pl.ds(head * 3 + near, 1), :] = unskew_sum(wide)

    for step in range(tiles):
        middles = [key for key in range(groups) if key * 2 // groups == step]
        lasts = [key for key in range(groups) if min(tiles - 1, 2 + key * 3 // 4) == step]

        @pl.when(query_tile == step)
        def _():
            for key in middles:
                job.middle(key)
            for key in lasts:
                job.last(key)

    @pl.when(query_tile == tiles - 1)
    def _():
        swap.arrive()
        piece_ref[...] = jnp.sum(pieces[...].astype(jnp.float32), axis=0).astype(jnp.bfloat16)
        job.finish()
        swap.finish()


def attend_backward(
    prefix, far_bias, base_bias, qkv, mixed, grad_mixed, totals, part, sums, columns
):
    length = qkv.shape[0]
    groups, piece_rows, piece_width = sums.shape
    block = part.shape[2:]
    width = qkv.shape[1] // 3
    heads_here = width // HEAD
    tiles = length // tile
    whole = lambda i: (0, 0)
    return pl.pallas_call(
        functools.partial(attend_backward_kernel, heads_here, groups, columns),
        grid=(tiles,),
        out_shape=(
            jax.ShapeDtypeStruct((length, 3 * width), jnp.bfloat16),
            jax.ShapeDtypeStruct((heads_here * 3, 2 * tile), jnp.float32),
            jax.ShapeDtypeStruct((heads_here, 2, 8, tile), jnp.float32),
            jax.ShapeDtypeStruct((groups,) + block, jnp.bfloat16),
            jax.ShapeDtypeStruct((piece_rows, piece_width), jnp.bfloat16),
        ),
        in_specs=[
            pl.BlockSpec(memory_space=pltpu.SMEM),
            pl.BlockSpec(memory_space=pltpu.SMEM),
            pl.BlockSpec(base_bias.shape, whole),
            pl.BlockSpec(qkv.shape, whole),
            pl.BlockSpec(mixed.shape, whole),
            pl.BlockSpec(mixed.shape, whole),
            pl.BlockSpec((1, heads_here, tile), lambda i: (i, 0, 0)),
            anywhere,
            anywhere,
        ],
        out_specs=(
            pl.BlockSpec((length, 3 * width), whole),
            pl.BlockSpec((heads_here * 3, 2 * tile), whole),
            pl.BlockSpec((heads_here, 2, 8, tile), lambda i: (0, 0, 0, 0)),
            anywhere,
            pl.BlockSpec((piece_rows, piece_width), whole),
        ),
        scratch_shapes=[
            pltpu.VMEM((heads_here, 4, tile, tile), jnp.float32),
            pltpu.VMEM((width, length), jnp.bfloat16),
            pltpu.VMEM((length, width), jnp.float32),
            pltpu.VMEM((length, width), jnp.float32),
            pltpu.VMEM((heads_here, 4, tile, tile), jnp.float32),
            pltpu.VMEM(sums.shape, jnp.bfloat16),
        ]
        + Exchange.sems(groups, 1)
        + Collect.scratch(columns, groups, block),
        compiler_params=comm_params(6, 60),
        cost_estimate=pl.CostEstimate(
            flops=70 * length * length * width, transcendentals=length * length * heads_here,
            bytes_accessed=16 * length * width,
        ),
        name="attend_backward",
    )(prefix, far_bias, base_bias, qkv, mixed, grad_mixed, totals, part, sums)


def gelu_parts(act):
    inner = math.sqrt(2.0 / math.pi) * (act + 0.044715 * act * act * act)
    tanh = jnp.tanh(inner)
    half = 0.5 * (1.0 + tanh)
    slope = math.sqrt(2.0 / math.pi) * (1.0 + 3.0 * 0.044715 * act * act)
    return act * half, half + 0.5 * act * (1.0 - tanh * tanh) * slope


def slot_rows(experts_here):
    return experts_here * main_slots + -(-experts_here * tail_slots // 8) * 8


def tail_select(expert, sources, tail_height):
    rows = lax.broadcasted_iota(jnp.int32, (sources * tail_slots, sources * tail_height), 0)
    columns = lax.broadcasted_iota(jnp.int32, (sources * tail_slots, sources * tail_height), 1)
    wanted = (rows // tail_slots) * tail_height + expert * tail_slots + rows % tail_slots
    return jnp.where(columns == wanted, 1.0, 0.0).astype(jnp.bfloat16)


def expert_input(main_ref, tail_ref, select):
    width = main_ref.shape[-1]
    main = main_ref[...].reshape(-1, width)
    tail = nn_dot(select, tail_ref[...].reshape(-1, width)).astype(jnp.bfloat16)
    return jnp.concatenate([main, tail], axis=0)


def gates_of(wide_rows):
    return wide_rows[:, D : D + 1].astype(jnp.float32) + wide_rows[:, D + 1 : D + 2].astype(
        jnp.float32
    )


def expert_output(value, select, expert, main_sc, tail_sc):
    low = value.astype(jnp.bfloat16)
    main_count = main_sc.shape[0] * main_sc.shape[1] * main_slots
    main_sc[...] = low[:main_count].reshape(main_sc.shape)
    spread = tn_dot(select, low[main_count:]).astype(jnp.bfloat16).reshape(tail_sc.shape)

    @pl.when(expert == 0)
    def _():
        tail_sc[...] = spread

    @pl.when(expert > 0)
    def _():
        tail_sc[...] += spread


def expert_math(wide_rows, grads, gate_weight, up_weight, down_weight):
    rows, gates = wide_rows[:, :D], gates_of(wide_rows)
    gate_act = nt_dot(rows, gate_weight)
    up_act = nt_dot(rows, up_weight)
    gelu, slope = gelu_parts(gate_act)
    hidden = (gelu * up_act).astype(jnp.bfloat16)
    raw_hidden = nt_dot(grads, down_weight)
    grad_gates = jnp.sum(raw_hidden * hidden.astype(jnp.float32), axis=1, keepdims=True)
    grad_hidden = raw_hidden * gates
    grad_gate = (grad_hidden * up_act * slope).astype(jnp.bfloat16)
    grad_up = (grad_hidden * gelu).astype(jnp.bfloat16)
    back = nn_dot(grad_gate, gate_weight) + nn_dot(grad_up, up_weight)
    lanes = lax.broadcasted_iota(jnp.int32, (back.shape[0], spare), 1)
    back = jnp.concatenate([back, jnp.where(lanes == 0, grad_gates, 0.0)], axis=1)
    return hidden, grad_gate, grad_up, back, nn_dot(hidden, down_weight)


def expert_act_kernel(
    experts_here,
    row_main,
    row_tail,
    grad_main,
    grad_tail,
    gate_weight,
    up_weight,
    down_weight,
    hidden_ref,
    grad_gate_ref,
    grad_up_ref,
    result_ref,
    back_ref,
    result_main,
    result_tail,
    back_main,
    back_tail,
    sems,
):
    part, expert = pl.program_id(0), pl.program_id(1)
    shards_part = row_main.shape[0]
    sources = shards_part * row_main.shape[1]
    tail_height = row_tail.shape[2]
    sources_at = pl.ds(part * shards_part, shards_part)
    select = tail_select(expert, sources, tail_height)
    wide_rows = expert_input(row_main, row_tail, select)
    grads = expert_input(grad_main, grad_tail, select)
    hidden, grad_gate, grad_up, back, result = expert_math(
        wide_rows, grads, gate_weight[0], up_weight[0], down_weight[0]
    )
    hidden_ref[0] = hidden
    grad_gate_ref[0] = grad_gate
    grad_up_ref[0] = grad_up

    def main_copies(at):
        place = pl.ds(pl.multiple_of(at * main_slots, main_slots), main_slots)
        return (
            pltpu.make_async_copy(result_main, result_ref.at[sources_at, :, place, :], sems.at[0]),
            pltpu.make_async_copy(back_main, back_ref.at[sources_at, :, place, :], sems.at[1]),
        )

    @pl.when(expert > 0)
    def _():
        for copy in main_copies(expert - 1):
            copy.wait()

    expert_output(result, select, expert, result_main, result_tail)
    expert_output(back, select, expert, back_main, back_tail)
    for copy in main_copies(expert):
        copy.start()

    @pl.when(expert == experts_here - 1)
    def _():
        place = pl.ds(experts_here * main_slots, tail_height)
        tails = (
            pltpu.make_async_copy(result_tail, result_ref.at[sources_at, :, place, :], sems.at[2]),
            pltpu.make_async_copy(back_tail, back_ref.at[sources_at, :, place, :], sems.at[3]),
        )
        for copy in tails:
            copy.start()
        for copy in main_copies(expert):
            copy.wait()
        for copy in tails:
            copy.wait()


def parts_of(rows):
    shards, groups = rows.shape[:2]
    return max(1, shards * groups // part_sources)


def row_specs(rows, experts_here, order):
    shards, groups, height, width = rows.shape
    shards_part = shards // parts_of(rows)
    tail_height = slot_rows(experts_here) - experts_here * main_slots
    tail_at = experts_here * main_slots // tail_height
    main_at = lambda e, c: (c, 0, e, 0)
    side_at = lambda e, c: (c, 0, tail_at, 0)
    return [
        pl.BlockSpec((shards_part, groups, main_slots, width), order(main_at)),
        pl.BlockSpec((shards_part, groups, tail_height, width), order(side_at)),
    ]


def expert_act(rows, grads, gate_weight, up_weight, down_weight):
    experts_here, units, width = gate_weight.shape
    shards, groups = rows.shape[:2]
    count = shards * groups * CAP
    parts = parts_of(rows)
    height = slot_rows(experts_here)
    tail_height = height - experts_here * main_slots
    order = lambda index: lambda c, e: index(e, c)
    weight_spec = pl.BlockSpec((1, units, width), lambda c, e: (e, 0, 0))
    act_spec = pl.BlockSpec((1, count // parts, units), lambda c, e: (e, c, 0))
    act_shape = jax.ShapeDtypeStruct((experts_here, count, units), jnp.bfloat16)
    slot_shape = lambda lanes: jax.ShapeDtypeStruct(
        (shards, groups, height, lanes), jnp.bfloat16
    )
    scratch = [
        pltpu.VMEM((shards // parts, groups, rows_of, lanes), jnp.bfloat16)
        for lanes in (width, width + spare)
        for rows_of in (main_slots, tail_height)
    ]
    return pl.pallas_call(
        functools.partial(expert_act_kernel, experts_here),
        grid=(parts, experts_here),
        out_shape=(act_shape, act_shape, act_shape, slot_shape(width), slot_shape(width + spare)),
        in_specs=row_specs(rows, experts_here, order)
        + row_specs(grads, experts_here, order)
        + [weight_spec] * 3,
        out_specs=(
            act_spec,
            act_spec,
            act_spec,
            pl.BlockSpec(memory_space=pl.ANY),
            pl.BlockSpec(memory_space=pl.ANY),
        ),
        scratch_shapes=scratch + [pltpu.SemaphoreType.DMA((4,))],
        compiler_params=pltpu.CompilerParams(vmem_limit_bytes=60 * mega),
        cost_estimate=pl.CostEstimate(
            flops=12 * experts_here * count * width * units,
            transcendentals=experts_here * count * units,
            bytes_accessed=6 * experts_here * width * units + 8 * experts_here * count * width,
        ),
        name="expert_act",
    )(rows, rows, grads, grads, gate_weight, up_weight, down_weight)


class RowChunk:
    def __init__(self, spot, number, place_rows, rows_in, rows_all, back_out, bufs, sems):
        self.spot, self.number, self.place_rows = spot, number, place_rows
        self.rows_in, self.rows_all, self.back_out = rows_in, rows_all, back_out
        self.rows, self.back, self.pair_in, self.across_out, self.across_in, self.total = bufs
        (
            self.local,
            self.send,
            self.recv,
            self.across_send,
            self.across_recv,
            self.core_send,
            self.core_recv,
            self.pair_send,
            self.pair_recv,
            self.sum_send,
            self.sum_recv,
            self.back_send,
            self.back_recv,
        ) = sems

    @staticmethod
    def sems(groups, columns, chunks):
        half = columns // 2
        dma = pltpu.SemaphoreType.DMA
        return (
            [dma((chunks, 3))]
            + [dma((chunks, groups))] * 2
            + [dma((chunks, groups, half))] * 4
            + [dma((chunks, half))] * 4
            + [dma((chunks, groups))] * 2
        )

    def own(self):
        spot = self.spot
        return pltpu.make_async_copy(
            self.rows_in.at[spot.place, self.place_rows],
            self.rows.at[spot.lane, spot.place],
            self.local.at[self.number, 0],
        )

    def keep(self):
        return pltpu.make_async_copy(
            self.rows, self.rows_all.at[:, :, self.place_rows], self.local.at[self.number, 1]
        )

    def swap(self, key):
        spot, at = self.spot, self.number
        peer = flip(spot.place, key)
        return remote(
            self.rows_in.at[peer, self.place_rows],
            self.rows.at[spot.lane, spot.place],
            self.send.at[at, key],
            self.recv.at[at, key],
            (peer, spot.lane),
        )

    def across(self, key, step):
        spot, at = self.spot, self.number
        block = self.rows.at[spot.lane, flip(spot.place, key)]
        return remote(
            block,
            block,
            self.across_send.at[at, key, step],
            self.across_recv.at[at, key, step],
            (spot.place, spot.across(step)),
        )

    def core(self, key, step):
        spot, at = self.spot, self.number
        block = self.rows.at[spot.behind(step), flip(spot.place, key)]
        return remote(
            block,
            block,
            self.core_send.at[at, key, step],
            self.core_recv.at[at, key, step],
            (spot.place, spot.partner),
        )

    def begin(self):
        self.own().start()
        for key in range(1, self.spot.groups):
            self.swap(key).start()

    def advance(self):
        for key in range(self.spot.groups):
            if key == 0:
                self.own().wait()
            else:
                self.swap(key).wait_recv()
            for step in range(1, self.spot.half):
                self.across(key, step).start()
            self.core(key, 0).start()

    def complete(self):
        groups, half = self.spot.groups, self.spot.half
        for key in range(groups):
            for step in range(1, half):
                self.across(key, step).wait_recv()
                self.core(key, step).start()
        for key in range(groups):
            for step in range(half):
                self.core(key, step).wait_recv()
        self.keep().start()

    def pair_copy(self, step):
        spot, at = self.spot, self.number
        return remote(
            self.back.at[spot.lane_at(step, True)],
            self.pair_in.at[step],
            self.pair_send.at[at, step],
            self.pair_recv.at[at, step],
            (spot.place, spot.partner),
        )

    def sum_copy(self, step):
        spot, at = self.spot, self.number
        return remote(
            self.across_out.at[step],
            self.across_in.at[step],
            self.sum_send.at[at, step],
            self.sum_recv.at[at, step],
            (spot.place, spot.across(step)),
        )

    def back_copy(self, key):
        spot, at = self.spot, self.number
        peer = flip(spot.place, key)
        target = self.back_out.at[spot.place, self.place_rows]
        if key == 0:
            return pltpu.make_async_copy(self.total.at[peer], target, self.local.at[at, 2])
        return remote(
            self.total.at[peer],
            target,
            self.back_send.at[at, key],
            self.back_recv.at[at, key],
            (peer, spot.lane),
        )

    def pair(self):
        for step in list(range(1, self.spot.half)) + [0]:
            self.pair_copy(step).start()

    def pair_sum(self, step):
        self.pair_copy(step).wait_recv()
        mine = self.back[self.spot.lane_at(step, False)].astype(jnp.float32)
        return mine + self.pair_in[step].astype(jnp.float32)

    def middle(self):
        for step in range(1, self.spot.half):
            self.across_out[step] = self.pair_sum(step).astype(jnp.bfloat16)
            self.sum_copy(step).start()

    def last(self):
        total = self.pair_sum(0)
        for step in range(1, self.spot.half):
            self.sum_copy(step).wait_recv()
            total = total + self.across_in[step].astype(jnp.float32)
        self.total[...] = total.astype(jnp.bfloat16)
        for key in range(self.spot.groups):
            self.back_copy(key).start()

    def finish(self):
        groups, half = self.spot.groups, self.spot.half
        for key in range(1, groups):
            self.back_copy(key).wait_recv()
        self.back_copy(0).wait()
        self.keep().wait()
        for key in range(groups):
            if key:
                self.swap(key).wait_send()
                self.back_copy(key).wait_send()
            for step in range(half):
                self.core(key, step).wait_send()
                if step:
                    self.across(key, step).wait_send()
        for step in range(half):
            self.pair_copy(step).wait_send()
            if step:
                self.sum_copy(step).wait_send()


def experts_kernel(
    experts_here,
    groups,
    columns,
    rows_in,
    grad_main,
    grad_tail,
    gate_weight,
    up_weight,
    down_weight,
    hidden_ref,
    grad_gate_ref,
    grad_up_ref,
    result_ref,
    rows_all,
    back_out,
    result_main,
    result_tail,
    result_sems,
    *scratch,
):
    expert = pl.program_id(0)
    tail_height = result_tail.shape[2]
    spot = Spot(groups, columns)
    mains, tails, sems = scratch[:6], scratch[6:12], scratch[12:]
    chunks = [
        RowChunk(
            spot,
            at,
            pl.ds(at * main_slots, main_slots),
            rows_in,
            rows_all,
            back_out,
            [buf.at[at] for buf in mains],
            sems,
        )
        for at in range(experts_here)
    ]
    tail = RowChunk(
        spot,
        experts_here,
        pl.ds(experts_here * main_slots, tail_height),
        rows_in,
        rows_all,
        back_out,
        tails,
        sems,
    )

    @pl.when(expert == 0)
    def _():
        spot.meet()
        for chunk in [tail] + chunks:
            chunk.begin()
        tail.advance()
        chunks[0].advance()

    for at in range(experts_here):

        @pl.when(expert == at)
        def _():
            if at + 1 < experts_here:
                chunks[at + 1].advance()
            if at == 0:
                tail.complete()
            chunks[at].complete()
            if at:
                chunks[at - 1].middle()

    select = tail_select(expert, groups * columns, tail_height)
    main_rows, tail_rows, main_back, tail_back = mains[0], tails[0], mains[1], tails[1]
    wide_rows = expert_input(main_rows.at[expert], tail_rows, select)
    grads = expert_input(grad_main, grad_tail, select)
    hidden, grad_gate, grad_up, back, result = expert_math(
        wide_rows, grads, gate_weight[0], up_weight[0], down_weight[0]
    )
    hidden_ref[0] = hidden
    grad_gate_ref[0] = grad_gate
    grad_up_ref[0] = grad_up
    expert_output(back, select, expert, main_back.at[expert], tail_back)

    for at in range(experts_here):

        @pl.when(expert == at)
        def _():
            chunks[at].pair()
            if at == experts_here - 1:
                tail.pair()
                chunks[at].middle()
                tail.middle()
            if at:
                chunks[at - 1].last()

    def result_copy(at):
        place = pl.ds(pl.multiple_of(at * main_slots, main_slots), main_slots)
        return pltpu.make_async_copy(result_main, result_ref.at[:, :, place], result_sems.at[0])

    @pl.when(expert > 0)
    def _():
        result_copy(expert - 1).wait()

    expert_output(result, select, expert, result_main, result_tail)
    result_copy(expert).start()

    @pl.when(expert == experts_here - 1)
    def _():
        place = pl.ds(experts_here * main_slots, tail_height)
        side = pltpu.make_async_copy(result_tail, result_ref.at[:, :, place], result_sems.at[1])
        side.start()
        chunks[-1].last()
        tail.last()
        for chunk in chunks + [tail]:
            chunk.finish()
        result_copy(expert).wait()
        side.wait()


def experts(rows, grads, gate_weight, up_weight, down_weight, columns):
    experts_here, units, width = gate_weight.shape
    groups, height, wide = rows.shape
    half = columns // 2
    count = columns * groups * CAP
    tail_height = height - experts_here * main_slots
    weight_spec = pl.BlockSpec((1, units, width), lambda e: (e, 0, 0))
    act_spec = pl.BlockSpec((1, count, units), lambda e: (e, 0, 0))
    act_shape = jax.ShapeDtypeStruct((experts_here, count, units), jnp.bfloat16)
    low = lambda *shape: pltpu.VMEM(shape, jnp.bfloat16)
    bufs = lambda lead, rows_of: [
        low(*lead, columns, groups, rows_of, wide),
        low(*lead, columns, groups, rows_of, wide),
        low(*lead, half, groups, rows_of, wide),
        low(*lead, half, groups, rows_of, wide),
        low(*lead, half, groups, rows_of, wide),
        low(*lead, groups, rows_of, wide),
    ]
    return pl.pallas_call(
        functools.partial(experts_kernel, experts_here, groups, columns),
        grid=(experts_here,),
        out_shape=(
            act_shape,
            act_shape,
            act_shape,
            jax.ShapeDtypeStruct((columns, groups, height, width), jnp.bfloat16),
            jax.ShapeDtypeStruct((columns,) + rows.shape, jnp.bfloat16),
            jax.ShapeDtypeStruct(rows.shape, jnp.bfloat16),
        ),
        in_specs=[anywhere]
        + row_specs(grads, experts_here, lambda index: lambda e: index(e, 0))
        + [weight_spec] * 3,
        out_specs=(act_spec, act_spec, act_spec, anywhere, anywhere, anywhere),
        scratch_shapes=[
            low(columns, groups, main_slots, width),
            low(columns, groups, tail_height, width),
            pltpu.SemaphoreType.DMA((2,)),
        ]
        + bufs((experts_here,), main_slots)
        + bufs((), tail_height)
        + RowChunk.sems(groups, columns, experts_here + 1),
        compiler_params=comm_params(10, 60),
        cost_estimate=pl.CostEstimate(
            flops=12 * experts_here * count * width * units,
            transcendentals=experts_here * count * units,
            bytes_accessed=6 * experts_here * width * units + 8 * experts_here * count * width,
        ),
        name="experts",
    )(rows, grads, grads, gate_weight, up_weight, down_weight)


def expert_weight_kernel(
    parts,
    row_main,
    row_tail,
    grad_main,
    grad_tail,
    hidden_ref,
    grad_gate_ref,
    grad_up_ref,
    gate_out,
    up_out,
    down_out,
):
    expert, part = pl.program_id(0), pl.program_id(1)
    sources = row_main.shape[0] * row_main.shape[1]
    select = tail_select(expert, sources, row_tail.shape[2])
    wide_rows = expert_input(row_main, row_tail, select)
    rows = wide_rows[:, :D]
    grads = expert_input(grad_main, grad_tail, select)
    grad_low = (grads.astype(jnp.float32) * gates_of(wide_rows)).astype(jnp.bfloat16)

    @pl.when(part == 0)
    def _():
        gate_out[0] = tn_dot(grad_gate_ref[0], rows)
        up_out[0] = tn_dot(grad_up_ref[0], rows)
        down_out[0] = tn_dot(hidden_ref[0], grad_low)

    if parts > 1:

        @pl.when(part > 0)
        def _():
            gate_out[0] += tn_dot(grad_gate_ref[0], rows)
            up_out[0] += tn_dot(grad_up_ref[0], rows)
            down_out[0] += tn_dot(hidden_ref[0], grad_low)


def expert_weight_grads(rows, grads, hidden, grad_gate, grad_up):
    experts_here, count, units = hidden.shape
    width = grads.shape[-1]
    parts = parts_of(rows)
    order = lambda index: index
    act_spec = pl.BlockSpec((1, count // parts, units), lambda e, c: (e, c, 0))
    out_spec = pl.BlockSpec((1, units, width), lambda e, c: (e, 0, 0))
    out_shape = jax.ShapeDtypeStruct((experts_here, units, width), jnp.float32)
    return pl.pallas_call(
        functools.partial(expert_weight_kernel, parts),
        grid=(experts_here, parts),
        out_shape=(out_shape, out_shape, out_shape),
        in_specs=row_specs(rows, experts_here, order)
        + row_specs(grads, experts_here, order)
        + [act_spec] * 3,
        out_specs=(out_spec, out_spec, out_spec),
        compiler_params=pltpu.CompilerParams(vmem_limit_bytes=60 * mega),
        cost_estimate=pl.CostEstimate(
            flops=6 * experts_here * count * width * units,
            transcendentals=0,
            bytes_accessed=12 * experts_here * width * units + 10 * experts_here * count * width,
        ),
        name="expert_weight_grads",
    )(rows, rows, grads, grads, hidden, grad_gate, grad_up)


def pair_slots(token_routes, ranks, experts_here):
    row_count = token_routes.shape[0]
    expert_pair = jnp.concatenate([token_routes[:, 0], token_routes[:, 1]])
    rank_pair = jnp.concatenate([ranks, ranks + row_count])
    earlier = (expert_pair[None, :] == expert_pair[:, None]) & (
        rank_pair[None, :] < rank_pair[:, None]
    )
    slot_index = jnp.sum(earlier.astype(jnp.int32), axis=1)
    height = slot_rows(experts_here)
    local = expert_pair % experts_here
    main_at = local * main_slots + slot_index
    tail_at = experts_here * main_slots + local * tail_slots + slot_index - main_slots
    row = jnp.where(slot_index < main_slots, main_at, tail_at)
    slots = (expert_pair // experts_here) * height + row
    return jnp.where(slot_index < CAP, slots, -1)


def router_head(logits, token_routes, weights):
    token_count = logits.shape[0]
    probabilities = jax.nn.softmax(logits, axis=-1)
    log_totals = jax.nn.logsumexp(logits, axis=-1)
    picked = (token_routes[:, :, None] == jnp.arange(EXPERTS, dtype=jnp.int32)).astype(jnp.float32)
    chosen = jnp.sum(picked * probabilities[:, None, :], axis=-1)
    gate_values = chosen / jnp.sum(chosen, axis=1, keepdims=True)
    shares = jnp.sum(picked, axis=(0, 1)) / (token_count * TOP)
    balance = EXPERTS * jnp.sum(shares * jnp.sum(probabilities, axis=0))
    return (gate_values, weights[0] * jnp.sum(log_totals * log_totals) + weights[1] * balance)


def column(values, rows):
    return jnp.pad(values, (0, rows - values.shape[0]))[:, None]


def shards(
    inputs,
    grad_out,
    prefix,
    routes,
    priority,
    loss_weights,
    norm_attn,
    norm_moe,
    qkv_weight,
    out_weight,
    bias_table,
    router_weight,
    gate_weight,
    up_weight,
    down_weight,
):
    row_count = inputs.shape[0]
    groups = lax.axis_size("expert")
    columns_of = lax.axis_size("shard")
    place = lax.axis_index("expert")
    length = row_count * groups
    heads_here = HEADS // groups
    width = heads_here * HEAD
    experts_here = EXPERTS // groups
    shard_rows = D // columns_of
    height = slot_rows(experts_here)

    own_columns = lax.dynamic_slice_in_dim(
        qkv_weight.reshape(shard_rows, 3, groups, width), place, 1, 2
    ).reshape(shard_rows, 3 * width)
    packed_small = jnp.concatenate(
        [
            own_columns,
            router_weight,
            norm_attn[:, None],
            norm_moe[:, None],
            column(bias_table.reshape(-1), shard_rows),
            jnp.zeros((shard_rows, spare - EXPERTS - 3), jnp.bfloat16),
        ],
        axis=1,
    )
    tokens_all, small_full, out_full = entry_gather(
        inputs.reshape(row_count, D), [packed_small, out_weight], groups, columns_of
    )
    tokens_all = tokens_all.reshape(length, D)
    small_full = small_full.reshape(D, 3 * width + spare)
    out_full = out_full.reshape(D, D)
    own_weight = small_full[:, : 3 * width]
    extra = small_full[:, 3 * width :]
    router_full = extra[:, :EXPERTS]
    gain_attn = extra[:, EXPERTS].astype(jnp.float32)
    gain_moe = extra[:, EXPERTS + 1].astype(jnp.float32)
    table_rows = BUCKETS // columns_of
    table_full = (
        extra[:, EXPERTS + 2].reshape(columns_of, shard_rows)[:, : table_rows * HEADS]
    ).reshape(BUCKETS, HEADS)
    table_own = lax.dynamic_slice_in_dim(
        table_full.astype(jnp.float32), place * heads_here, heads_here, 1
    )
    near_ids = jnp.asarray(skew_buckets(), jnp.int32)
    near_hot = (near_ids[:, None] == jnp.arange(BUCKETS, dtype=jnp.int32)).astype(jnp.float32)
    base_bias = (
        jnp.dot(near_hot, table_own, precision=lax.Precision.HIGHEST).reshape(3, 2 * tile, heads_here)
        * log2e
    )
    base_bias = jnp.transpose(base_bias, (2, 0, 1)).reshape(heads_here * 3, 2 * tile)
    far_bias = jnp.stack([table_own[15], table_own[31]], axis=1) * log2e

    token_routes = routes.reshape(row_count, TOP)
    slots = pair_slots(token_routes, priority.reshape(row_count), experts_here)
    slot_map = (
        jnp.arange(groups * height, dtype=jnp.int32)[:, None] == slots[None, :]
    ).reshape(groups * height, TOP, row_count)
    slot_any = jnp.any(slot_map, axis=1).astype(jnp.bfloat16)
    slot_pairs = slot_map.astype(jnp.bfloat16).reshape(groups * height, TOP * row_count)

    grad_low = grad_out.reshape(row_count, D)
    grad_slots = nn_dot(slot_any, grad_low).astype(jnp.bfloat16).reshape(groups, height, D)
    normed_all = rms_norm(tokens_all.astype(jnp.float32), gain_attn).astype(jnp.bfloat16)
    qkv_own = nn_dot(normed_all, own_weight).astype(jnp.bfloat16)
    mixed_own, totals, grads_received = attend_forward(
        prefix, far_bias, base_bias, qkv_own, grad_slots, columns_of
    )
    attended = exchange_mixed(mixed_own.reshape(groups, row_count, width), columns_of, 8)

    tokens_in = inputs.reshape(row_count, D).astype(jnp.float32)
    middle = tokens_in + nn_dot(attended, out_full)
    normed_two, norm_two_back = jax.vjp(rms_norm, middle, gain_moe)
    low_two = normed_two.astype(jnp.bfloat16)
    logits = nn_dot(low_two, router_full)
    router_out, router_back = jax.vjp(
        lambda logit_in: router_head(logit_in, token_routes, loss_weights), logits
    )
    gate_values = router_out[0]
    gate_high = lax.reduce_precision(gate_values, 8, 7)
    gate_parts = jnp.stack([gate_high, gate_values - gate_high], axis=-1).astype(jnp.bfloat16)
    wide_rows = jnp.concatenate(
        [
            jnp.broadcast_to(low_two[None], (TOP, row_count, D)),
            jnp.pad(jnp.transpose(gate_parts, (1, 0, 2)), ((0, 0), (0, 0), (0, spare - 2))),
        ],
        axis=2,
    ).reshape(TOP * row_count, D + spare)
    outgoing = nn_dot(slot_pairs, wide_rows).astype(jnp.bfloat16)
    outgoing = outgoing.reshape(groups, height, D + spare)
    gate_across, up_across, down_across = (
        jnp.transpose(weight, (0, 2, 1)) for weight in (gate_weight, up_weight, down_weight)
    )
    if columns_of * groups <= part_sources:
        hidden, grad_gate, grad_up, result_part, rows_received, grad_returned = experts(
            outgoing, grads_received, gate_across, up_across, down_across, columns_of
        )
    else:
        rows_received = dispatch(outgoing, columns_of, 2)
        hidden, grad_gate, grad_up, result_part, back_part = expert_act(
            rows_received, grads_received, gate_across, up_across, down_across
        )
        grad_returned = collect(back_part, 3)
    grad_returned = grad_returned.reshape(groups * height, D + spare)
    grad_low_two = tn_dot(slot_any, grad_returned[:, :D])
    grad_gates = jnp.transpose(
        tn_dot(slot_pairs, grad_returned[:, D:])[:, 0].reshape(TOP, row_count)
    )
    grad_top = grad_low.astype(jnp.float32)
    grad_logits = router_back((grad_gates, jnp.ones((), jnp.float32)))[0]
    low_logits = grad_logits.astype(jnp.bfloat16)
    router_grad = tn_dot(low_two, low_logits)
    grad_low_two = grad_low_two + nt_dot(low_logits, router_full)
    grad_middle_norm, gain_moe_grad = norm_two_back(grad_low_two)
    grad_middle = grad_top + grad_middle_norm
    low_middle = grad_middle.astype(jnp.bfloat16)
    out_grad = tn_dot(attended, low_middle)
    grad_attended = nt_dot(low_middle, out_full).astype(jnp.bfloat16)
    grad_attended = jnp.transpose(grad_attended.reshape(row_count, groups, width), (1, 0, 2))
    grad_mixed = lax.all_to_all(
        grad_attended, "expert", split_axis=0, concat_axis=0, tiled=True
    )
    gate_grad, up_grad, down_grad = expert_weight_grads(
        rows_received, grads_received, hidden, grad_gate, grad_up
    )
    out_sums = lax.psum_scatter(
        out_grad.astype(jnp.bfloat16), "shard", scatter_dimension=0, tiled=True
    ).reshape(groups, shard_rows // groups, D)
    grad_qkv, near_sums, side_sums, returned, out_piece = attend_backward(
        prefix,
        far_bias,
        base_bias,
        qkv_own,
        mixed_own,
        grad_mixed.reshape(length, width),
        totals,
        result_part,
        out_sums,
        columns_of,
    )
    pair_out = tn_dot(slot_pairs, returned.reshape(groups * height, D)).reshape(
        TOP, row_count, D
    )
    mixture = gate_values[:, 0:1] * pair_out[0] + gate_values[:, 1:2] * pair_out[1]
    output = (middle + mixture).astype(jnp.bfloat16)

    table_grad = jnp.einsum(
        "hil,ilb->bh",
        near_sums.reshape(heads_here, 3, 2 * tile),
        near_hot.reshape(3, 2 * tile, BUCKETS),
        precision=lax.Precision.HIGHEST,
    )
    far_sums = jnp.sum(side_sums, axis=(2, 3))
    bucket_ids = jnp.arange(BUCKETS, dtype=jnp.int32)[:, None]
    table_grad = table_grad + jnp.where(bucket_ids == 15, far_sums[:, 0][None], 0.0)
    table_grad = table_grad + jnp.where(bucket_ids == 31, far_sums[:, 1][None], 0.0)
    table_column = jnp.pad(
        table_grad.reshape(columns_of, table_rows * heads_here),
        ((0, 0), (0, shard_rows - table_rows * heads_here)),
    ).reshape(D, 1)

    extra = jnp.concatenate(
        [
            jnp.zeros((D, 1), jnp.float32),
            table_column,
            gain_moe_grad[:, None],
            router_grad,
            jnp.zeros((D, spare - 3 - EXPERTS), jnp.float32),
        ],
        axis=1,
    ).astype(jnp.bfloat16)
    grad_projected, last_all, out_all, qkv_full = tail_exchange(
        grad_qkv.reshape(groups, row_count, 3 * width),
        normed_all,
        own_weight,
        gain_attn[:, None],
        extra,
        out_piece,
        qkv_weight,
        columns_of,
        7,
    )
    qkv_full = qkv_full.reshape(D, 3 * D)
    out_total = out_all.reshape(shard_rows, D).astype(jnp.float32)
    last_all = last_all.reshape(groups, shard_rows, 3 * width + spare)
    qkv_total = unpack_columns(last_all, width)
    last_extra = last_all[:, :, 3 * width :].astype(jnp.float32)
    extra_total = jnp.sum(last_extra, axis=0)
    table_total = jnp.transpose(
        last_extra[:, : table_rows * heads_here, 1].reshape(groups, table_rows, heads_here),
        (1, 0, 2),
    ).reshape(table_rows, HEADS)

    if width % 128:
        grad_projected = jnp.transpose(
            grad_projected.reshape(groups, row_count, 3, width), (1, 2, 0, 3)
        ).reshape(row_count, 3 * D)
    grad_low_one = nt_dot(grad_projected, qkv_full)
    _, norm_one_back = jax.vjp(lambda features: rms_norm(features, gain_attn), tokens_in)
    input_grad = grad_middle + norm_one_back(grad_low_one)[0]
    return (
        output.reshape(row_count, 1, D),
        input_grad.reshape(row_count, 1, D),
        extra_total[:, 0],
        extra_total[:, 2],
        qkv_total,
        out_total,
        table_total,
        extra_total[:, 3 : 3 + EXPERTS],
        jnp.transpose(gate_grad, (0, 2, 1)),
        jnp.transpose(up_grad, (0, 2, 1)),
        jnp.transpose(down_grad, (0, 2, 1)),
    )


def solution(mesh):
    placed = (
        P("expert", "shard", None),
        P("expert", "shard", None),
        P("shard"),
        P("expert", "shard", None),
        P("expert", "shard", None),
        P(),
        P("shard"),
        P("shard"),
        P("shard", None),
        P("shard", None),
        P("shard", None),
        P("shard", None),
        P("expert", None, "shard"),
        P("expert", None, "shard"),
        P("expert", None, "shard"),
    )
    return jax.shard_map(
        shards,
        mesh=mesh,
        in_specs=placed,
        out_specs=(
            P("expert", "shard", None),
            P("expert", "shard", None),
            P("shard"),
            P("shard"),
            P("shard", None),
            P("shard", None),
            P("shard", None),
            P("shard", None),
            P("expert", None, "shard"),
            P("expert", None, "shard"),
            P("expert", None, "shard"),
        ),
        check_vma=False,
    )
```

```python
import functools
import math

import jax
import jax.numpy as jnp
import numpy as np
from jax import lax
from jax.experimental import pallas as pl
from jax.experimental.pallas import tpu as pltpu
from jax.sharding import PartitionSpec as P

D = 1024
HEADS = 16
HEAD = 64
FF = 2816
EXPERTS = 32
TOP = 2
BUCKETS = 32
CAP = 18

epsilon = 1e-06
masked_score = -1e30
far_bounds = (12, 16, 23, 32, 46, 64, 91)
tile = 256
main_slots = 16
tail_slots = CAP - main_slots
log2e = math.log2(math.e)
score_scale = HEAD ** (-0.5)
mega = 1024 * 1024
part_sources = 32
spare = 128


MESH = pl.DeviceIdType.MESH


def flip(index, key):
    out, bit = index, 1
    while bit <= key:
        if key & bit:
            out = out + bit * (1 - 2 * ((index // bit) % 2))
        bit *= 2
    return out


def near_keys(groups):
    return list(range(1, groups // 2))


def far_keys(groups):
    return list(range(groups // 2, groups))


def early_keys(groups):
    return [key for key in far_keys(groups) if key % line_shape(groups)[1] == 0]


class Spot:
    def __init__(self, groups, columns):
        self.groups, self.columns = groups, columns
        self.place = lax.axis_index("expert")
        self.lane = lax.axis_index("shard")
        self.half = columns // 2
        self.chip = self.lane // 2
        self.core = self.lane % 2
        self.partner = self.chip * 2 + 1 - self.core

    def across(self, step):
        return ((self.chip + step) % self.half) * 2 + self.core

    def behind(self, step):
        return ((self.chip + self.half - step) % self.half) * 2 + self.core

    def lane_at(self, step, other):
        chip = (self.chip + step) % self.half
        return chip * 2 + ((1 - self.core) if other else self.core)

    def meet(self):
        barrier = pltpu.get_barrier_semaphore()
        for key in range(1, self.groups):
            peer = (flip(self.place, key), self.lane)
            pl.semaphore_signal(barrier, inc=1, device_id=peer, device_id_type=MESH)
        for step in range(1, self.columns):
            peer = (self.place, (self.lane + step) % self.columns)
            pl.semaphore_signal(barrier, inc=1, device_id=peer, device_id_type=MESH)
        pl.semaphore_wait(barrier, self.groups + self.columns - 2)


def remote(source, target, send_sem, recv_sem, peer):
    return pltpu.make_async_remote_copy(
        src_ref=source,
        dst_ref=target,
        send_sem=send_sem,
        recv_sem=recv_sem,
        device_id=peer,
        device_id_type=MESH,
    )


def line_shape(groups):
    across = groups // 4
    return 4, across


class LineGather:
    def __init__(self, spot, own, full, local_sem, send_sems, recv_sems):
        self.spot, self.own, self.full = spot, own, full
        self.local_sem, self.send_sems, self.recv_sems = local_sem, send_sems, recv_sems
        self.long, self.wide = line_shape(spot.groups)
        self.z = spot.place // self.wide
        self.y = spot.place % self.wide

    @staticmethod
    def sems(groups):
        long, wide = line_shape(groups)
        return [
            pltpu.SemaphoreType.DMA(()),
            pltpu.SemaphoreType.DMA((2 * long - 1, wide + 1)),
            pltpu.SemaphoreType.DMA((groups,)),
        ]

    def copy(self, job, way, origin, source, target):
        return remote(
            source,
            self.full.at[origin],
            self.send_sems.at[job, way],
            self.recv_sems.at[origin],
            (target, self.spot.lane),
        )

    def each(self, job, origin, source, up, down, act):
        place, wide = self.spot.place, self.wide
        if up:

            @pl.when(self.z + 1 < self.long)
            def _():
                act(self.copy(job, 0, origin, source, place + wide))

        if down:

            @pl.when(self.z >= 1)
            def _():
                act(self.copy(job, 1, origin, source, place - wide))

        for step in range(1, wide):
            target = self.z * wide + (self.y + step) % wide
            act(self.copy(job, 1 + step, origin, source, target))

    def begin(self):
        place = self.spot.place
        self.each(0, place, self.own, True, True, lambda copy: copy.start())
        pltpu.make_async_copy(self.own, self.full.at[place], self.local_sem).start()

    def arrive(self, origin):
        self.copy(0, 0, origin, self.own, self.spot.place).wait_recv()

    def hop(self, k):
        place, wide = self.spot.place, self.wide

        @pl.when(self.z >= k)
        def _():
            origin = place - k * wide
            self.arrive(origin)
            self.each(k, origin, self.full.at[origin], True, False, lambda copy: copy.start())

        @pl.when(self.z + k < self.long)
        def _():
            origin = place + k * wide
            self.arrive(origin)
            job = self.long - 1 + k
            self.each(job, origin, self.full.at[origin], False, True, lambda copy: copy.start())

    def finish(self):
        for row in range(self.long):
            for step in range(1, self.wide):
                self.arrive(row * self.wide + (self.y + step) % self.wide)
        self.settle()

    def settle(self):
        place, wide = self.spot.place, self.wide
        stop = lambda copy: copy.wait_send()
        self.each(0, place, self.own, True, True, stop)
        for k in range(1, self.long):

            @pl.when(self.z >= k)
            def _():
                origin = place - k * wide
                self.each(k, origin, self.full.at[origin], True, False, stop)

            @pl.when(self.z + k < self.long)
            def _():
                origin = place + k * wide
                job = self.long - 1 + k
                self.each(job, origin, self.full.at[origin], False, True, stop)

        pltpu.make_async_copy(self.own, self.full.at[place], self.local_sem).wait()


class ColumnGather:
    def __init__(self, spot, own, full, local_sem, across_send, across_recv, core_send, core_recv):
        self.spot, self.own, self.full = spot, own, full
        self.local_sem = local_sem
        self.across_send, self.across_recv = across_send, across_recv
        self.core_send, self.core_recv = core_send, core_recv

    @staticmethod
    def sems(columns):
        return [pltpu.SemaphoreType.DMA(())] + [pltpu.SemaphoreType.DMA((columns // 2,))] * 4

    def across_copy(self, step):
        spot = self.spot
        return remote(
            self.own,
            self.full.at[spot.lane],
            self.across_send.at[step],
            self.across_recv.at[step],
            (spot.place, spot.across(step)),
        )

    def core_copy(self, step):
        spot = self.spot
        source = self.own if step == 0 else self.full.at[spot.behind(step)]
        target = spot.lane if step == 0 else spot.behind(step)
        return remote(
            source,
            self.full.at[target],
            self.core_send.at[step],
            self.core_recv.at[step],
            (spot.place, spot.partner),
        )

    def begin(self):
        for step in range(1, self.spot.half):
            self.across_copy(step).start()
        self.core_copy(0).start()
        pltpu.make_async_copy(self.own, self.full.at[self.spot.lane], self.local_sem).start()

    def forward(self):
        for step in range(1, self.spot.half):
            self.across_copy(step).wait_recv()
            self.core_copy(step).start()

    def finish(self):
        for step in range(self.spot.half):
            self.core_copy(step).wait_recv()
        for step in range(self.spot.half):
            self.core_copy(step).wait_send()
        for step in range(1, self.spot.half):
            self.across_copy(step).wait_send()
        pltpu.make_async_copy(self.own, self.full.at[self.spot.lane], self.local_sem).wait()


def comm_params(which, limit=60):
    return pltpu.CompilerParams(
        collective_id=which, has_side_effects=True, vmem_limit_bytes=limit * mega
    )


anywhere = pl.BlockSpec(memory_space=pl.ANY)


def entry_kernel(
    groups,
    columns,
    tokens,
    gain,
    pack,
    out_weight,
    rows,
    tokens_all,
    normed_all,
    qkv_all,
    pack_all,
    out_all,
    far_rows,
    token_sc,
    normed_sc,
    qkv_sc,
    gain_sc,
    pack_sc,
    token_sem,
    normed_sems,
    qkv_sems,
    pack_sem,
    *sems,
):
    spot = Spot(groups, columns)
    line = LineGather(spot, tokens, tokens_all, *sems[:3])
    gains = ColumnGather(spot, gain, gain_sc, *sems[3:8])
    packs = ColumnGather(spot, pack, pack_sc, *sems[8:13])
    outs = ColumnGather(spot, out_weight, out_all, *sems[13:18])
    far_send, far_recv = sems[18:]
    wide = qkv_sc.shape[2]

    def far_copy(key):
        peer = flip(spot.place, key)
        return remote(
            rows.at[peer],
            far_rows.at[spot.place],
            far_send.at[key],
            far_recv.at[key],
            (peer, spot.lane),
        )

    def stores(origin):
        return (
            pltpu.make_async_copy(
                normed_sc.at[origin], normed_all.at[origin], normed_sems.at[origin]
            ),
            pltpu.make_async_copy(qkv_sc.at[origin], qkv_all.at[origin], qkv_sems.at[origin]),
        )

    def project(origin, source):
        load = pltpu.make_async_copy(source, token_sc, token_sem)
        load.start()
        load.wait()
        features = token_sc[...].astype(jnp.float32)
        factor = lax.rsqrt(jnp.mean(features * features, axis=-1, keepdims=True) + epsilon)
        gain_row = jnp.concatenate([gain_sc[at, 0:1, :] for at in range(columns)], axis=1)
        normed = (features * factor * gain_row).astype(jnp.bfloat16)
        normed_sc[origin] = normed
        weight = pack_sc[...].reshape(D, -1)[:, :wide]
        qkv_sc[origin] = nn_dot(normed, weight).astype(jnp.bfloat16)
        for store in stores(origin):
            store.start()

    spot.meet()
    line.begin()
    gains.begin()
    packs.begin()
    outs.begin()
    gains.forward()
    packs.forward()
    gains.finish()
    packs.finish()
    keep = pltpu.make_async_copy(pack_sc, pack_all, pack_sem)
    keep.start()
    project(spot.place, tokens)
    line.hop(1)
    outs.forward()
    line.hop(2)
    for key in early_keys(groups):
        far_copy(key).start()
    line.hop(3)

    def own_column(row, carry):
        @pl.when(row != line.z)
        def _():
            origin = row * line.wide + line.y
            project(origin, tokens_all.at[origin])

        return carry

    lax.fori_loop(0, line.long, own_column, 0)

    def other_column(at, carry):
        row = line.z + ((at + 1) // 2) * (1 - 2 * (at % 2))

        @pl.when((row >= 0) & (row < line.long))
        def _():
            for step in range(1, line.wide):
                origin = row * line.wide + (line.y + step) % line.wide
                line.arrive(origin)
                project(origin, tokens_all.at[origin])

        return carry

    lax.fori_loop(0, 2 * line.long - 1, other_column, 0)
    for key in early_keys(groups):
        far_copy(key).wait_recv()
    for key in early_keys(groups):
        far_copy(key).wait_send()
    line.settle()
    outs.finish()
    keep.wait()
    for origin in range(groups):
        for store in stores(origin):
            store.wait()


def entry_gather(tokens, gain, pack, out_weight, rows, wide, which):
    groups = rows.shape[0]
    columns = D // out_weight.shape[0]
    count = tokens.shape[0]
    low = lambda *shape: jax.ShapeDtypeStruct(shape, jnp.bfloat16)
    dma = pltpu.SemaphoreType.DMA
    return pl.pallas_call(
        functools.partial(entry_kernel, groups, columns),
        out_shape=(
            low(groups, *tokens.shape),
            low(groups, *tokens.shape),
            low(groups, count, wide),
            low(columns, *pack.shape),
            low(columns, *out_weight.shape),
            low(*rows.shape),
        ),
        in_specs=[anywhere] * 5,
        out_specs=(anywhere,) * 6,
        scratch_shapes=[
            pltpu.VMEM(tokens.shape, jnp.bfloat16),
            pltpu.VMEM((groups,) + tokens.shape, jnp.bfloat16),
            pltpu.VMEM((groups, count, wide), jnp.bfloat16),
            pltpu.VMEM((columns,) + gain.shape, jnp.float32),
            pltpu.VMEM((columns,) + pack.shape, jnp.bfloat16),
            dma(()),
            dma((groups,)),
            dma((groups,)),
            dma(()),
        ]
        + LineGather.sems(groups)
        + ColumnGather.sems(columns) * 3
        + [dma((groups,))] * 2,
        compiler_params=comm_params(which),
        name="entry_gather",
    )(tokens, gain, pack, out_weight, rows)


class Dispatch:
    def __init__(self, spot, rows, full, sems):
        self.spot, self.rows, self.full = spot, rows, full
        self.local, self.send, self.recv = sems[:3]
        self.across_send, self.across_recv, self.core_send, self.core_recv = sems[3:]

    @staticmethod
    def sems(groups, columns):
        return (
            [pltpu.SemaphoreType.DMA(())]
            + [pltpu.SemaphoreType.DMA((groups,))] * 2
            + [pltpu.SemaphoreType.DMA((groups, columns // 2))] * 4
        )

    def own(self):
        spot = self.spot
        return pltpu.make_async_copy(
            self.rows.at[spot.place], self.full.at[spot.lane, spot.place], self.local
        )

    def swap(self, key):
        spot = self.spot
        peer = flip(spot.place, key)
        return remote(
            self.rows.at[peer],
            self.full.at[spot.lane, spot.place],
            self.send.at[key],
            self.recv.at[key],
            (peer, spot.lane),
        )

    def across(self, key, step):
        spot = self.spot
        block = self.full.at[spot.lane, flip(spot.place, key)]
        return remote(
            block,
            block,
            self.across_send.at[key, step],
            self.across_recv.at[key, step],
            (spot.place, spot.across(step)),
        )

    def core(self, key, step):
        spot = self.spot
        block = self.full.at[spot.behind(step), flip(spot.place, key)]
        return remote(
            block,
            block,
            self.core_send.at[key, step],
            self.core_recv.at[key, step],
            (spot.place, spot.partner),
        )

    def begin(self):
        groups = self.spot.groups
        self.own().start()
        for key in far_keys(groups) + near_keys(groups):
            self.swap(key).start()

    def advance(self, key):
        if key == 0:
            self.own().wait()
        else:
            self.swap(key).wait_recv()
        for step in range(1, self.spot.half):
            self.across(key, step).start()
        self.core(key, 0).start()

    def pass_on(self, key):
        for step in range(1, self.spot.half):
            self.across(key, step).wait_recv()
            self.core(key, step).start()

    def finish(self):
        groups, half = self.spot.groups, self.spot.half
        for key in range(groups):
            for step in range(half):
                self.core(key, step).wait_recv()
        for key in range(groups):
            if key > 0:
                self.swap(key).wait_send()
            for step in range(1, half):
                self.across(key, step).wait_send()
            for step in range(half):
                self.core(key, step).wait_send()


def dispatch_kernel(groups, columns, rows, full, *sems):
    spot = Spot(groups, columns)
    job = Dispatch(spot, rows, full, sems)
    spot.meet()
    job.begin()
    for key in range(groups):
        job.advance(key)
        if key:
            job.pass_on(key - 1)
    job.pass_on(groups - 1)
    job.finish()


def dispatch(rows, columns, which):
    groups = rows.shape[0]
    return pl.pallas_call(
        functools.partial(dispatch_kernel, groups, columns),
        out_shape=jax.ShapeDtypeStruct((columns,) + rows.shape, rows.dtype),
        in_specs=[anywhere],
        out_specs=anywhere,
        scratch_shapes=Dispatch.sems(groups, columns),
        compiler_params=comm_params(which),
        name="dispatch_rows",
    )(rows)


class Exchange:
    def __init__(self, spot, blocks, thirds, local, send, recv):
        self.spot, self.blocks, self.thirds = spot, blocks, range(thirds)
        self.local, self.send, self.recv = local, send, recv

    @staticmethod
    def sems(groups, thirds):
        return [pltpu.SemaphoreType.DMA((thirds,))] + [
            pltpu.SemaphoreType.DMA((groups, thirds))
        ] * 2

    def copy(self, key, third):
        spot = self.spot
        peer = flip(spot.place, key)
        source, target = self.blocks(peer, third)
        if key == 0:
            return pltpu.make_async_copy(source, target, self.local.at[third])
        return remote(
            source,
            target,
            self.send.at[key, third],
            self.recv.at[key, third],
            (peer, spot.lane),
        )

    def start(self, key):
        for third in self.thirds:
            self.copy(key, third).start()

    def begin(self):
        groups = self.spot.groups
        for key in far_keys(groups) + near_keys(groups) + [0]:
            self.start(key)

    def arrive(self):
        for key in range(self.spot.groups):
            for third in self.thirds:
                copy = self.copy(key, third)
                copy.wait() if key == 0 else copy.wait_recv()

    def finish(self):
        for key in range(1, self.spot.groups):
            for third in self.thirds:
                self.copy(key, third).wait_send()


class ColumnSum:
    def __init__(self, spot, chunks, order, part, bufs, sems):
        self.spot, self.chunks, self.order, self.part = spot, chunks, order, part
        self.pair_in, self.mine, self.across_out, self.across_in = bufs
        self.local, self.pair_send, self.pair_recv, self.across_send, self.across_recv = sems

    @staticmethod
    def scratch(columns, chunks, block):
        half = columns // 2
        return [pltpu.VMEM((half, chunks) + block, jnp.bfloat16)] * 4 + [
            pltpu.SemaphoreType.DMA((half, chunks))
        ] * 5

    def pair_copy(self, step, k):
        spot = self.spot
        return remote(
            self.part.at[spot.lane_at(step, True), self.order(k)],
            self.pair_in.at[step, k],
            self.pair_send.at[step, k],
            self.pair_recv.at[step, k],
            (spot.place, spot.partner),
        )

    def mine_copy(self, step, k):
        return pltpu.make_async_copy(
            self.part.at[self.spot.lane_at(step, False), self.order(k)],
            self.mine.at[step, k],
            self.local.at[step, k],
        )

    def across_copy(self, step, k):
        spot = self.spot
        return remote(
            self.across_out.at[step, k],
            self.across_in.at[step, k],
            self.across_send.at[step, k],
            self.across_recv.at[step, k],
            (spot.place, spot.across(step)),
        )

    def begin(self):
        half = self.spot.half
        for k in range(self.chunks):
            for step in list(range(1, half)) + [0]:
                self.pair_copy(step, k).start()
                self.mine_copy(step, k).start()

    def pair_sum(self, step, k):
        self.pair_copy(step, k).wait_recv()
        self.mine_copy(step, k).wait()
        return self.mine[step, k].astype(jnp.float32) + self.pair_in[step, k].astype(jnp.float32)

    def middle(self, k):
        for step in range(1, self.spot.half):
            self.across_out[step, k] = self.pair_sum(step, k).astype(jnp.bfloat16)
            self.across_copy(step, k).start()

    def last(self, k):
        total = self.pair_sum(0, k)
        for step in range(1, self.spot.half):
            self.across_copy(step, k).wait_recv()
            total = total + self.across_in[step, k].astype(jnp.float32)
        return total.astype(jnp.bfloat16)

    def finish(self):
        for k in range(self.chunks):
            for step in range(self.spot.half):
                self.pair_copy(step, k).wait_send()
                if step:
                    self.across_copy(step, k).wait_send()


class Collect:
    def __init__(self, spot, part, out, scratch):
        self.spot, self.total = spot, scratch[9]
        self.keys = far_keys(spot.groups) + near_keys(spot.groups) + [0]
        self.sums = ColumnSum(
            spot,
            spot.groups,
            lambda k: flip(spot.place, self.keys[k]),
            part,
            scratch[:4],
            scratch[4:9],
        )
        self.out = out
        self.local, self.send, self.recv = scratch[10:]

    @staticmethod
    def scratch(columns, groups, block):
        return (
            ColumnSum.scratch(columns, groups, block)
            + [pltpu.VMEM((groups,) + block, jnp.bfloat16)]
            + [pltpu.SemaphoreType.DMA(())]
            + [pltpu.SemaphoreType.DMA((groups,))] * 2
        )

    def copy(self, k):
        spot, key = self.spot, self.keys[k]
        target = self.out.at[spot.place]
        if key == 0:
            return pltpu.make_async_copy(self.total.at[k], target, self.local)
        peer = flip(spot.place, key)
        return remote(
            self.total.at[k], target, self.send.at[k], self.recv.at[k], (peer, spot.lane)
        )

    def begin(self):
        self.sums.begin()

    def middle(self, key):
        self.sums.middle(key)

    def last(self, key):
        self.total[key] = self.sums.last(key)
        self.copy(key).start()

    def finish(self):
        last = self.spot.groups - 1
        for k in range(last):
            self.copy(k).wait_recv()
        for k in range(last):
            self.copy(k).wait_send()
        self.copy(last).wait()
        self.sums.finish()


def collect_kernel(groups, columns, part, out, *scratch):
    spot = Spot(groups, columns)
    job = Collect(spot, part, out, scratch)
    spot.meet()
    job.begin()
    ahead = 2
    for key in range(ahead):
        job.middle(key)
    for key in range(groups):
        if key + ahead < groups:
            job.middle(key + ahead)
        job.last(key)
    job.finish()


def collect(part, which):
    columns, groups = part.shape[:2]
    block = part.shape[2:]
    return pl.pallas_call(
        functools.partial(collect_kernel, groups, columns),
        out_shape=jax.ShapeDtypeStruct((groups,) + block, part.dtype),
        in_specs=[anywhere],
        out_specs=anywhere,
        scratch_shapes=Collect.scratch(columns, groups, block),
        compiler_params=comm_params(which),
        name="collect_rows",
    )(part)


def lanes_at(place, width):
    return pl.ds(pl.multiple_of(place * width, 128), width)


def mixed_kernel(groups, columns, mixed, attended, *sems):
    spot = Spot(groups, columns)
    width = mixed.shape[2]

    def blocks(at, third):
        if width % 128:
            return mixed.at[at], attended.at[spot.place]
        return mixed.at[at], attended.at[:, lanes_at(spot.place, width)]

    job = Exchange(spot, blocks, 1, *sems)
    spot.meet()
    job.begin()
    job.arrive()
    job.finish()


def exchange_mixed(mixed, columns, which):
    groups, rows, width = mixed.shape
    shape = mixed.shape if width % 128 else (rows, groups * width)
    out = pl.pallas_call(
        functools.partial(mixed_kernel, groups, columns),
        out_shape=jax.ShapeDtypeStruct(shape, mixed.dtype),
        in_specs=[anywhere],
        out_specs=anywhere,
        scratch_shapes=Exchange.sems(groups, 1),
        compiler_params=comm_params(which),
        name="exchange_mixed",
    )(mixed)
    if width % 128:
        out = jnp.transpose(out, (1, 0, 2)).reshape(rows, groups * width)
    return out


class Tail:
    def __init__(self, spot, chunks, refs, scratch):
        grads, part, piece, weight, grads_out, sum_all, piece_all, weight_all = refs
        groups = spot.groups
        width = grads.shape[2] // 3
        thirds = 3 if width % 128 == 0 else 1

        def blocks(at, third):
            if thirds == 1:
                return grads.at[at], grads_out.at[spot.place]
            columns_to = pl.ds(pl.multiple_of(third * D + spot.place * width, 128), width)
            return grads.at[at, :, pl.ds(third * width, width)], grads_out.at[:, columns_to]

        self.chunks = chunks
        self.sums = ColumnSum(spot, chunks, lambda k: k, part, scratch[:4], scratch[4:9])
        self.own_sum = scratch[9]
        self.swap = Exchange(spot, blocks, thirds, *scratch[10:13])
        self.line = LineGather(spot, self.own_sum, sum_all, *scratch[13:16])
        self.side = LineGather(spot, piece, piece_all, *scratch[16:19])
        self.column = ColumnGather(spot, weight, weight_all, *scratch[19:24])

    @staticmethod
    def scratch(columns, groups, chunks, block, thirds):
        return (
            ColumnSum.scratch(columns, chunks, block)
            + [pltpu.VMEM((chunks,) + block, jnp.bfloat16)]
            + Exchange.sems(groups, thirds)
            + LineGather.sems(groups) * 2
            + ColumnGather.sems(columns)
        )


def tail_kernel(
    groups,
    columns,
    chunks,
    grads,
    normed,
    own_weight,
    gains,
    extra,
    piece,
    weight,
    grads_out,
    sum_all,
    piece_all,
    weight_all,
    grads_sc,
    normed_sc,
    load_sems,
    part,
    *scratch,
):
    spot = Spot(groups, columns)
    refs = (grads, part, piece, weight, grads_out, sum_all, piece_all, weight_all)
    tail = Tail(spot, chunks, refs, scratch)
    wide = grads.shape[2]
    block_rows = D // (columns * chunks)
    loads = [
        pltpu.make_async_copy(grads, grads_sc, load_sems.at[0]),
        pltpu.make_async_copy(normed, normed_sc, load_sems.at[1]),
    ]
    for load in loads:
        load.start()
    far = far_keys(groups)
    early, late = far[: len(far) // 2], far[len(far) // 2 :]
    spot.meet()
    tail.side.begin()
    for key in early + near_keys(groups) + [0]:
        tail.swap.start(key)
    for load in loads:
        load.wait()
    all_grads = grads_sc[...].reshape(-1, wide)

    for at in range(columns * chunks):
        rows = pl.ds(at * block_rows, block_rows)
        grad = tn_dot(normed_sc[:, rows], all_grads)
        gain = jnp.sum(grad * own_weight[rows, :].astype(jnp.float32), axis=1, keepdims=True)
        gain = gain / gains[rows, :]
        lanes = lax.broadcasted_iota(jnp.int32, (block_rows, spare), 1)
        side = jnp.where(lanes == 0, gain, extra[rows, :].astype(jnp.float32))
        part[at // chunks, at % chunks] = jnp.concatenate([grad, side], axis=1).astype(jnp.bfloat16)
    tail.sums.begin()
    for k in range(chunks):
        tail.sums.middle(k)
    tail.column.begin()
    tail.side.hop(1)
    for k in range(chunks):
        tail.own_sum[k] = tail.sums.last(k)
    tail.line.begin()
    tail.side.hop(2)
    tail.line.hop(1)
    tail.side.hop(3)
    tail.line.hop(2)
    for key in late:
        tail.swap.start(key)
    tail.line.hop(3)
    tail.column.forward()
    tail.side.finish()
    tail.swap.arrive()
    tail.line.finish()
    tail.column.finish()
    tail.swap.finish()
    tail.sums.finish()


def tail_exchange(grads, normed, own_weight, gains, extra, piece, weight, columns, which):
    groups, row_count, wide = grads.shape
    apart = wide // 3 % 128 != 0
    grads_shape = grads.shape if apart else (row_count, wide * groups)
    chunks = 2
    block = (D // columns // chunks, wide + spare)
    shape_of = lambda shape: jax.ShapeDtypeStruct(shape, jnp.bfloat16)
    inside = pl.BlockSpec(memory_space=pltpu.VMEM)
    return pl.pallas_call(
        functools.partial(tail_kernel, groups, columns, chunks),
        out_shape=(
            shape_of(grads_shape),
            shape_of((groups, chunks) + block),
            shape_of((groups,) + piece.shape),
            shape_of((columns,) + weight.shape),
        ),
        in_specs=[anywhere, anywhere, inside, inside, inside, anywhere, anywhere],
        out_specs=(anywhere,) * 4,
        scratch_shapes=[
            pltpu.VMEM(grads.shape, jnp.bfloat16),
            pltpu.VMEM(normed.shape, jnp.bfloat16),
            pltpu.SemaphoreType.DMA((2,)),
            pltpu.VMEM((columns, chunks) + block, jnp.bfloat16),
        ]
        + Tail.scratch(columns, groups, chunks, block, 1 if apart else 3),
        compiler_params=comm_params(which),
        name="tail_exchange",
    )(grads, normed, own_weight, gains, extra, piece, weight)


def finish_kernel(
    width,
    grads,
    weight,
    packed,
    packed_extra,
    tokens,
    gain,
    grad_middle,
    out_low,
    input_grad,
    qkv_grad,
    out_grad,
    extra,
    total_sc,
):
    third = pl.program_id(0)
    for group in range(packed.shape[0]):
        qkv_grad[:, group * width : (group + 1) * width] = packed[group].astype(jnp.float32)
    part = nt_dot(grads[...], weight[...].reshape(D, -1))

    @pl.when(third == 0)
    def _():
        total_sc[...] = part

    @pl.when(third > 0)
    def _():
        total_sc[...] += part

    @pl.when(third == 2)
    def _():
        features = tokens[...].astype(jnp.float32)
        factor = lax.rsqrt(jnp.mean(features * features, axis=-1, keepdims=True) + epsilon)
        unit = features * factor
        scaled = total_sc[...] * gain[...]
        inner = jnp.mean(scaled * unit, axis=-1, keepdims=True)
        input_grad[...] = grad_middle[...] + factor * (scaled - unit * inner)
        out_grad[...] = out_low[...].astype(jnp.float32)
        extra[...] = jnp.sum(packed_extra[...].astype(jnp.float32), axis=0)


def finish(grads, weight, packed, tokens, gain, grad_middle, out_low, width):
    groups, shard_rows = packed.shape[:2]
    columns = weight.shape[0]
    rows = grads.shape[0]
    whole = lambda t: (0, 0)
    full = jax.ShapeDtypeStruct((rows, D), jnp.float32)
    return pl.pallas_call(
        functools.partial(finish_kernel, width),
        grid=(3,),
        out_shape=(
            full,
            jax.ShapeDtypeStruct((shard_rows, 3 * D), jnp.float32),
            jax.ShapeDtypeStruct((shard_rows, D), jnp.float32),
            jax.ShapeDtypeStruct((shard_rows, spare), jnp.float32),
        ),
        in_specs=[
            pl.BlockSpec((rows, D), lambda t: (0, t)),
            pl.BlockSpec((columns, shard_rows, D), lambda t: (0, 0, t)),
            pl.BlockSpec((groups, shard_rows, width), lambda t: (0, 0, t)),
            pl.BlockSpec((groups, shard_rows, spare), lambda t: (0, 0, 3 * width // spare)),
            pl.BlockSpec((rows, D), whole),
            pl.BlockSpec((1, D), whole),
            pl.BlockSpec((rows, D), whole),
            pl.BlockSpec((shard_rows, D), whole),
        ],
        out_specs=(
            pl.BlockSpec((rows, D), whole),
            pl.BlockSpec((shard_rows, D), lambda t: (0, t)),
            pl.BlockSpec((shard_rows, D), whole),
            pl.BlockSpec((shard_rows, spare), whole),
        ),
        scratch_shapes=[pltpu.VMEM((rows, D), jnp.float32)],
        compiler_params=pltpu.CompilerParams(vmem_limit_bytes=60 * mega),
        name="finish",
    )(grads, weight, packed, packed, tokens, gain, grad_middle, out_low)


def rms_norm(features, scales):
    factor = lax.rsqrt(jnp.mean(features * features, axis=-1, keepdims=True) + epsilon)
    return features * factor * scales


def buckets_of(offsets):
    distance = np.abs(offsets)
    beyond = 8 + np.sum(distance[..., None] >= np.array(far_bounds), axis=-1)
    return np.where(distance < 8, distance, beyond) + 16 * (offsets > 0)


def skew_buckets():
    lanes = np.arange(2 * tile)
    from_query = np.where(lanes < tile, -lanes, 2 * tile - lanes)
    return np.concatenate([buckets_of(near * tile + from_query) for near in (-1, 0, 1)])


def lane_row_mask(head, width, rows):
    lanes = lax.broadcasted_iota(jnp.int32, (rows, width), 1)
    return (lanes >= head * HEAD) & (lanes < (head + 1) * HEAD)


def fold_rows(block, op):
    return op(block.reshape(block.shape[0] // 8, 8, block.shape[1]), axis=0)


def nt_dot(left, right):
    return lax.dot_general(left, right, (((1,), (1,)), ((), ())), preferred_element_type=jnp.float32)


def tn_dot(left, right):
    return lax.dot_general(left, right, (((0,), (0,)), ((), ())), preferred_element_type=jnp.float32)


def nn_dot(left, right):
    return jnp.dot(left, right, preferred_element_type=jnp.float32)


def build_bias(base_ref, far_ref, bias_sc, heads_here):
    for head in range(heads_here):
        for near in range(3):
            row = base_ref[pl.ds(head * 3 + near, 1), :]
            wide = jnp.broadcast_to(row, (tile, 2 * tile))
            skewed = pltpu.roll(wide, 0, 1, stride=1, stride_axis=0)
            bias_sc[head, near] = skewed[:, :tile]
        bias_sc[head, 3] = jnp.full((tile, tile), far_ref[head, 1], jnp.float32)


def unskew_sum(wide):
    lanes = wide.shape[1]
    half = wide.shape[0] // 2
    while half >= 8:
        wide = wide[:half] + pltpu.roll(wide[half:], lanes - half, 1)
        half //= 2
    total = wide[0:1]
    for row in range(1, 8):
        total = total + pltpu.roll(wide[row : row + 1], lanes - row, 1)
    return total


def rows_at(index):
    return pl.ds(pl.multiple_of(index * tile, tile), tile)


def visible_tile(key_tile, query_tile, prefix_length):
    key_pos = key_tile * tile + lax.broadcasted_iota(jnp.int32, (tile, tile), 0)
    query_pos = query_tile * tile + lax.broadcasted_iota(jnp.int32, (tile, tile), 1)
    return (key_pos <= query_pos) | (key_pos < prefix_length)


class Spread:
    def __init__(self, spot, rows, far_rows, full, sems):
        self.spot, self.rows, self.far_rows, self.full = spot, rows, far_rows, full
        self.local, self.send, self.recv = sems[:3]
        self.across_send, self.across_recv, self.core_send, self.core_recv = sems[3:]
        self.early = early_keys(spot.groups)
        self.rest = [key for key in far_keys(spot.groups) if key not in self.early]
        self.near = near_keys(spot.groups)

    @staticmethod
    def sems(groups, columns):
        return [pltpu.SemaphoreType.DMA((groups,))] * 3 + [
            pltpu.SemaphoreType.DMA((groups, columns // 2))
        ] * 4

    def source(self, key):
        spot = self.spot
        if key == 0:
            return self.rows.at[spot.place]
        at = flip(spot.place, key)
        return self.far_rows.at[at] if key in self.early else self.full.at[spot.lane, at]

    def local_copy(self, key):
        spot = self.spot
        target = self.full.at[spot.lane, flip(spot.place, key)]
        return pltpu.make_async_copy(self.source(key), target, self.local.at[key])

    def swap(self, key):
        spot = self.spot
        peer = flip(spot.place, key)
        return remote(
            self.rows.at[peer],
            self.full.at[spot.lane, spot.place],
            self.send.at[key],
            self.recv.at[key],
            (peer, spot.lane),
        )

    def across(self, key, step):
        spot = self.spot
        return remote(
            self.source(key),
            self.full.at[spot.lane, flip(spot.place, key)],
            self.across_send.at[key, step],
            self.across_recv.at[key, step],
            (spot.place, spot.across(step)),
        )

    def core(self, key, step):
        spot = self.spot
        lane = spot.behind(step)
        target = self.full.at[lane, flip(spot.place, key)]
        return remote(
            target if step else self.source(key),
            target,
            self.core_send.at[key, step],
            self.core_recv.at[key, step],
            (spot.place, spot.partner),
        )

    def send_on(self, key):
        for step in range(1, self.spot.half):
            self.across(key, step).start()
        self.core(key, 0).start()

    def begin(self):
        for key in self.rest + self.near:
            self.swap(key).start()
        for key in [0] + self.early:
            self.send_on(key)
            self.local_copy(key).start()

    def advance(self, key):
        self.swap(key).wait_recv()
        self.send_on(key)

    def pass_on(self, key):
        for step in range(1, self.spot.half):
            self.across(key, step).wait_recv()
            self.core(key, step).start()

    def finish(self):
        half = self.spot.half
        keys = range(self.spot.groups)
        for key in keys:
            for step in range(half):
                self.core(key, step).wait_recv()
        for key in keys:
            if key in self.near + self.rest:
                self.swap(key).wait_send()
            else:
                self.local_copy(key).wait()
            for step in range(half):
                self.core(key, step).wait_send()
                if step:
                    self.across(key, step).wait_send()


def attend_forward_kernel(
    heads_here,
    groups,
    columns,
    prefix_ref,
    far_ref,
    base_ref,
    qkv_ref,
    rows_ref,
    far_rows_ref,
    mixed_ref,
    totals_ref,
    full_ref,
    bias_sc,
    score_sc,
    value_sc,
    *sems,
):
    width = heads_here * HEAD
    query_tile = pl.program_id(0)
    tiles = qkv_ref.shape[0] // tile
    spot = Spot(groups, columns)
    job = Spread(spot, rows_ref, far_rows_ref, full_ref, sems)

    @pl.when(query_tile == 0)
    def _():
        spot.meet()
        job.begin()

    prefix_length = prefix_ref[0]
    heads = range(heads_here)

    @pl.when(query_tile == 0)
    def _():
        build_bias(base_ref, far_ref, bias_sc, heads_here)
        for key_tile in range(value_sc.shape[1] // tile):
            rows = pl.ds(key_tile * tile, tile)
            values = qkv_ref[rows, 2 * width : 3 * width].astype(jnp.float32)
            value_sc[:, rows] = jnp.transpose(values).astype(jnp.bfloat16)

    queries = qkv_ref[rows_at(query_tile), :width]
    head_queries = [
        jnp.where(lane_row_mask(head, width, tile), queries, jnp.zeros_like(queries)) for head in heads
    ]

    def score_tiles(key_tile, tops, finish):
        keys = qkv_ref[rows_at(key_tile), width : 2 * width]
        out = []
        for head in heads:
            scores = finish(head, nt_dot(keys, head_queries[head]) * (score_scale * log2e))
            score_sc[head, rows_at(key_tile), :] = scores
            out.append(jnp.maximum(tops[head], fold_rows(scores, jnp.max)))
        return tuple(out)

    def far_body(key_tile, tops):
        return score_tiles(key_tile, tops, lambda head, raw: raw + far_ref[head, 0])

    def near_body(key_tile, tops):
        return score_tiles(key_tile, tops, lambda head, raw: raw + bias_sc[head, 0])

    def tail_body(key_tile, tops):
        shown = visible_tile(key_tile, query_tile, prefix_length)
        which = 1 + jnp.minimum(key_tile - query_tile, 2)
        return score_tiles(
            key_tile, tops, lambda head, raw: jnp.where(shown, raw + bias_sc[head, which], masked_score)
        )

    tile_count = jnp.maximum(query_tile + 1, tiles // 2)
    near_start = jnp.maximum(query_tile - 1, 0)
    tops = tuple(jnp.full((8, tile), masked_score, jnp.float32) for _ in heads)
    tops = lax.fori_loop(0, near_start, far_body, tops)
    tops = lax.fori_loop(near_start, query_tile, near_body, tops)
    tops = lax.fori_loop(query_tile, tile_count, tail_body, tops)
    tops = [jnp.max(top, axis=0, keepdims=True) for top in tops]

    def mix_body(key_tile, carry):
        sums, mixes = carry
        new_sums, new_mixes = [], []
        for head in heads:
            expos = jnp.exp2(score_sc[head, rows_at(key_tile), :] - tops[head])
            new_sums.append(sums[head] + fold_rows(expos, jnp.sum))
            values = value_sc[head * HEAD : (head + 1) * HEAD, rows_at(key_tile)]
            new_mixes.append(mixes[head] + nn_dot(values, expos.astype(jnp.bfloat16)))
        return (tuple(new_sums), tuple(new_mixes))

    sums, mixes = lax.fori_loop(
        0,
        tile_count,
        mix_body,
        (
            tuple(jnp.zeros((8, tile), jnp.float32) for _ in heads),
            tuple(jnp.zeros((HEAD, tile), jnp.float32) for _ in heads),
        ),
    )
    parts = []
    for head in heads:
        total = jnp.sum(sums[head], axis=0, keepdims=True)
        parts.append(mixes[head] / total)
        totals_ref[0, pl.ds(head, 1), :] = tops[head] + jnp.log2(total)
    mixed_ref[...] = jnp.transpose(jnp.concatenate(parts, axis=0)).astype(jnp.bfloat16)

    @pl.when(query_tile == tiles // 4)
    def _():
        for key in job.near:
            job.advance(key)

    @pl.when(query_tile == tiles // 2)
    def _():
        job.pass_on(0)
        for key in job.early:
            job.pass_on(key)

    @pl.when(query_tile == tiles - 3)
    def _():
        for key in job.rest:
            job.advance(key)

    @pl.when(query_tile == tiles - 1)
    def _():
        for key in job.near + job.rest:
            job.pass_on(key)
        job.finish()


def attend_forward(prefix, far_bias, base_bias, qkv, rows, far_rows, columns):
    length = qkv.shape[0]
    groups = rows.shape[0]
    width = qkv.shape[1] // 3
    heads_here = width // HEAD
    tiles = length // tile
    return pl.pallas_call(
        functools.partial(attend_forward_kernel, heads_here, groups, columns),
        grid=(tiles,),
        out_shape=(
            jax.ShapeDtypeStruct((length, width), jnp.bfloat16),
            jax.ShapeDtypeStruct((tiles, heads_here, tile), jnp.float32),
            jax.ShapeDtypeStruct((columns,) + rows.shape, rows.dtype),
        ),
        in_specs=[
            pl.BlockSpec(memory_space=pltpu.SMEM),
            pl.BlockSpec(memory_space=pltpu.SMEM),
            pl.BlockSpec(base_bias.shape, lambda i: (0, 0)),
            pl.BlockSpec(qkv.shape, lambda i: (0, 0)),
            anywhere,
            anywhere,
        ],
        out_specs=(
            pl.BlockSpec((tile, width), lambda i: (i, 0)),
            pl.BlockSpec((1, heads_here, tile), lambda i: (i, 0, 0)),
            anywhere,
        ),
        scratch_shapes=[
            pltpu.VMEM((heads_here, 4, tile, tile), jnp.float32),
            pltpu.VMEM((heads_here, length, tile), jnp.float32),
            pltpu.VMEM((width, length), jnp.bfloat16),
        ]
        + Spread.sems(groups, columns),
        compiler_params=comm_params(5),
        cost_estimate=pl.CostEstimate(
            flops=40 * length * length * width, transcendentals=length * length * heads_here,
            bytes_accessed=8 * length * width,
        ),
        name="attend_forward",
    )(prefix, far_bias, base_bias, qkv, rows, far_rows)


def attend_backward_kernel(
    heads_here,
    groups,
    columns,
    prefix_ref,
    far_ref,
    base_ref,
    qkv_ref,
    mixed_ref,
    grad_ref,
    totals_ref,
    part_ref,
    sums_ref,
    out_ref,
    near_ref,
    side_ref,
    result_ref,
    piece_ref,
    bias_sc,
    key_sc,
    grad_key_sc,
    grad_value_sc,
    near_sc,
    *scratch,
):
    width = heads_here * HEAD
    query_tile = pl.program_id(0)
    tiles = qkv_ref.shape[0] // tile
    spot = Spot(groups, columns)
    pieces = scratch[0]
    swap = Exchange(
        spot, lambda at, third: (sums_ref.at[at], pieces.at[spot.place]), 1, *scratch[1:4]
    )
    job = Collect(spot, part_ref, result_ref, scratch[4:])

    @pl.when(query_tile == 0)
    def _():
        spot.meet()
        job.begin()
        swap.begin()

    prefix_length = prefix_ref[0]
    heads = range(heads_here)

    @pl.when(query_tile == 0)
    def _():
        build_bias(base_ref, far_ref, bias_sc, heads_here)
        for key_tile in range(key_sc.shape[1] // tile):
            rows = pl.ds(key_tile * tile, tile)
            keys = qkv_ref[rows, width : 2 * width].astype(jnp.float32)
            key_sc[:, rows] = jnp.transpose(keys).astype(jnp.bfloat16)
        grad_key_sc[...] = jnp.zeros_like(grad_key_sc)
        grad_value_sc[...] = jnp.zeros_like(grad_value_sc)
        near_sc[...] = jnp.zeros_like(near_sc)
        side_ref[...] = jnp.zeros_like(side_ref)

    queries = qkv_ref[rows_at(query_tile), :width]
    grads = grad_ref[rows_at(query_tile), :]
    products = grads.astype(jnp.float32) * mixed_ref[rows_at(query_tile), :].astype(jnp.float32)
    head_queries, head_grads, inners, totals = [], [], [], []
    for head in heads:
        mask = lane_row_mask(head, width, tile)
        head_queries.append(jnp.where(mask, queries, jnp.zeros_like(queries)))
        head_grads.append(jnp.where(mask, grads, jnp.zeros_like(grads)))
        ones = jnp.where(lane_row_mask(head, width, 8), 1.0, 0.0)
        inner = lax.dot_general(
            ones,
            products,
            (((1,), (1,)), ((), ())),
            precision=lax.Precision.HIGHEST,
            preferred_element_type=jnp.float32,
        )
        inners.append(inner[0:1, :])
        totals.append(totals_ref[0, pl.ds(head, 1), :])

    def step(key_tile, carry, finish, keep):
        sides, grad_queries = carry
        keys = qkv_ref[rows_at(key_tile), width : 2 * width]
        values = qkv_ref[rows_at(key_tile), 2 * width : 3 * width]
        new_sides, new_queries = [], []
        key_part, value_part = None, None
        for head in heads:
            raw = nt_dot(keys, head_queries[head]) * (score_scale * log2e)
            attention = jnp.exp2(finish(head, raw))
            grad_weights = nt_dot(values, head_grads[head])
            grad_scores = attention * (grad_weights - inners[head])
            new_sides.append(keep(head, grad_scores, sides[head]))
            low_scores = grad_scores.astype(jnp.bfloat16)
            keys_across = key_sc[head * HEAD : (head + 1) * HEAD, rows_at(key_tile)]
            new_queries.append(grad_queries[head] + nn_dot(keys_across, low_scores))
            value_one = nn_dot(attention.astype(jnp.bfloat16), head_grads[head])
            key_one = nn_dot(low_scores, head_queries[head])
            value_part = value_one if value_part is None else value_part + value_one
            key_part = key_one if key_part is None else key_part + key_one
        grad_key_sc[rows_at(key_tile), :] += key_part
        grad_value_sc[rows_at(key_tile), :] += value_part
        return (tuple(new_sides), tuple(new_queries))

    def add_side(head, grad_scores, side):
        return side + fold_rows(grad_scores, jnp.sum)

    def far_body(key_tile, carry):
        return step(
            key_tile, carry, lambda head, raw: raw + (far_ref[head, 0] - totals[head]), add_side
        )

    def near_body(key_tile, carry):
        def keep(head, grad_scores, side):
            near_sc[head, 0] += grad_scores
            return side

        return step(
            key_tile, carry, lambda head, raw: raw + bias_sc[head, 0] - totals[head], keep
        )

    def tail_body(key_tile, carry):
        shown = visible_tile(key_tile, query_tile, prefix_length)
        which = 1 + jnp.minimum(key_tile - query_tile, 2)

        def keep(head, grad_scores, side):
            near_sc[head, which] += grad_scores
            return side

        return step(
            key_tile,
            carry,
            lambda head, raw: jnp.where(
                shown, raw + bias_sc[head, which] - totals[head], masked_score
            ),
            keep,
        )

    tile_count = jnp.maximum(query_tile + 1, tiles // 2)
    near_start = jnp.maximum(query_tile - 1, 0)
    carry = (
        tuple(jnp.zeros((8, tile), jnp.float32) for _ in heads),
        tuple(jnp.zeros((HEAD, tile), jnp.float32) for _ in heads),
    )
    carry = lax.fori_loop(0, near_start, far_body, carry)
    carry = lax.fori_loop(near_start, query_tile, near_body, carry)
    carry = lax.fori_loop(query_tile, tile_count, tail_body, carry)
    sides, grad_queries = carry
    for head in heads:
        side_ref[head, 0] += sides[head]
    across = jnp.concatenate(grad_queries, axis=0) * score_scale
    out_ref[rows_at(query_tile), :width] = jnp.transpose(across).astype(jnp.bfloat16)

    @pl.when(query_tile == tiles - 1)
    def _():
        out_ref[:, width : 2 * width] = (grad_key_sc[...] * score_scale).astype(jnp.bfloat16)
        out_ref[:, 2 * width : 3 * width] = grad_value_sc[...].astype(jnp.bfloat16)
        for head in heads:
            side_ref[head, 1] = fold_rows(near_sc[head, 3], jnp.sum)
            for near in range(3):
                wide = jnp.concatenate(
                    [near_sc[head, near], jnp.zeros((tile, tile), jnp.float32)], axis=1
                )
                near_ref[pl.ds(head * 3 + near, 1), :] = unskew_sum(wide)

    for step in range(tiles):
        middles = [key for key in range(groups) if key * 2 // groups == step]
        lasts = [key for key in range(groups) if min(tiles - 1, 2 + key * 3 // 4) == step]

        @pl.when(query_tile == step)
        def _():
            for key in middles:
                job.middle(key)
            for key in lasts:
                job.last(key)

    @pl.when(query_tile == tiles - 1)
    def _():
        swap.arrive()
        piece_ref[...] = jnp.sum(pieces[...].astype(jnp.float32), axis=0).astype(jnp.bfloat16)
        job.finish()
        swap.finish()


def attend_backward(
    prefix, far_bias, base_bias, qkv, mixed, grad_mixed, totals, part, sums, columns
):
    length = qkv.shape[0]
    groups, piece_rows, piece_width = sums.shape
    block = part.shape[2:]
    width = qkv.shape[1] // 3
    heads_here = width // HEAD
    tiles = length // tile
    whole = lambda i: (0, 0)
    return pl.pallas_call(
        functools.partial(attend_backward_kernel, heads_here, groups, columns),
        grid=(tiles,),
        out_shape=(
            jax.ShapeDtypeStruct((length, 3 * width), jnp.bfloat16),
            jax.ShapeDtypeStruct((heads_here * 3, 2 * tile), jnp.float32),
            jax.ShapeDtypeStruct((heads_here, 2, 8, tile), jnp.float32),
            jax.ShapeDtypeStruct((groups,) + block, jnp.bfloat16),
            jax.ShapeDtypeStruct((piece_rows, piece_width), jnp.bfloat16),
        ),
        in_specs=[
            pl.BlockSpec(memory_space=pltpu.SMEM),
            pl.BlockSpec(memory_space=pltpu.SMEM),
            pl.BlockSpec(base_bias.shape, whole),
            pl.BlockSpec(qkv.shape, whole),
            pl.BlockSpec(mixed.shape, whole),
            pl.BlockSpec(mixed.shape, whole),
            pl.BlockSpec((1, heads_here, tile), lambda i: (i, 0, 0)),
            anywhere,
            anywhere,
        ],
        out_specs=(
            pl.BlockSpec((length, 3 * width), whole),
            pl.BlockSpec((heads_here * 3, 2 * tile), whole),
            pl.BlockSpec((heads_here, 2, 8, tile), lambda i: (0, 0, 0, 0)),
            anywhere,
            pl.BlockSpec((piece_rows, piece_width), whole),
        ),
        scratch_shapes=[
            pltpu.VMEM((heads_here, 4, tile, tile), jnp.float32),
            pltpu.VMEM((width, length), jnp.bfloat16),
            pltpu.VMEM((length, width), jnp.float32),
            pltpu.VMEM((length, width), jnp.float32),
            pltpu.VMEM((heads_here, 4, tile, tile), jnp.float32),
            pltpu.VMEM(sums.shape, jnp.bfloat16),
        ]
        + Exchange.sems(groups, 1)
        + Collect.scratch(columns, groups, block),
        compiler_params=comm_params(6, 60),
        cost_estimate=pl.CostEstimate(
            flops=70 * length * length * width, transcendentals=length * length * heads_here,
            bytes_accessed=16 * length * width,
        ),
        name="attend_backward",
    )(prefix, far_bias, base_bias, qkv, mixed, grad_mixed, totals, part, sums)


def gelu_parts(act):
    inner = math.sqrt(2.0 / math.pi) * (act + 0.044715 * act * act * act)
    tanh = jnp.tanh(inner)
    half = 0.5 * (1.0 + tanh)
    slope = math.sqrt(2.0 / math.pi) * (1.0 + 3.0 * 0.044715 * act * act)
    return act * half, half + 0.5 * act * (1.0 - tanh * tanh) * slope


def slot_rows(experts_here):
    return experts_here * main_slots + -(-experts_here * tail_slots // 8) * 8


def tail_select(expert, sources, tail_height):
    rows = lax.broadcasted_iota(jnp.int32, (sources * tail_slots, sources * tail_height), 0)
    columns = lax.broadcasted_iota(jnp.int32, (sources * tail_slots, sources * tail_height), 1)
    wanted = (rows // tail_slots) * tail_height + expert * tail_slots + rows % tail_slots
    return jnp.where(columns == wanted, 1.0, 0.0).astype(jnp.bfloat16)


def expert_input(main_ref, tail_ref, select):
    width = main_ref.shape[-1]
    main = main_ref[...].reshape(-1, width)
    tail = nn_dot(select, tail_ref[...].reshape(-1, width)).astype(jnp.bfloat16)
    return jnp.concatenate([main, tail], axis=0)


def gates_of(wide_rows):
    return wide_rows[:, D : D + 1].astype(jnp.float32) + wide_rows[:, D + 1 : D + 2].astype(
        jnp.float32
    )


def expert_output(value, select, expert, main_sc, tail_sc):
    low = value.astype(jnp.bfloat16)
    main_count = main_sc.shape[0] * main_sc.shape[1] * main_slots
    main_sc[...] = low[:main_count].reshape(main_sc.shape)
    spread = tn_dot(select, low[main_count:]).astype(jnp.bfloat16).reshape(tail_sc.shape)

    @pl.when(expert == 0)
    def _():
        tail_sc[...] = spread

    @pl.when(expert > 0)
    def _():
        tail_sc[...] += spread


def expert_math(wide_rows, raw_hidden, gate_weight, up_weight, down_weight):
    rows, gates = wide_rows[:, :D], gates_of(wide_rows)
    gate_act = nt_dot(rows, gate_weight)
    up_act = nt_dot(rows, up_weight)
    gelu, slope = gelu_parts(gate_act)
    hidden = (gelu * up_act).astype(jnp.bfloat16)
    grad_gates = jnp.sum(raw_hidden * hidden.astype(jnp.float32), axis=1, keepdims=True)
    grad_hidden = raw_hidden * gates
    grad_gate = (grad_hidden * up_act * slope).astype(jnp.bfloat16)
    grad_up = (grad_hidden * gelu).astype(jnp.bfloat16)
    back = nn_dot(grad_gate, gate_weight) + nn_dot(grad_up, up_weight)
    lanes = lax.broadcasted_iota(jnp.int32, (back.shape[0], spare), 1)
    back = jnp.concatenate([back, jnp.where(lanes == 0, grad_gates, 0.0)], axis=1)
    return hidden, grad_gate, grad_up, back, nn_dot(hidden, down_weight)


def expert_act_kernel(
    experts_here,
    row_main,
    row_tail,
    grad_main,
    grad_tail,
    gate_weight,
    up_weight,
    down_weight,
    hidden_ref,
    grad_gate_ref,
    grad_up_ref,
    result_ref,
    back_ref,
    result_main,
    result_tail,
    back_main,
    back_tail,
    sems,
):
    part, expert = pl.program_id(0), pl.program_id(1)
    shards_part = row_main.shape[0]
    sources = shards_part * row_main.shape[1]
    tail_height = row_tail.shape[2]
    sources_at = pl.ds(part * shards_part, shards_part)
    select = tail_select(expert, sources, tail_height)
    wide_rows = expert_input(row_main, row_tail, select)
    grads = expert_input(grad_main, grad_tail, select)
    hidden, grad_gate, grad_up, back, result = expert_math(
        wide_rows,
        nt_dot(grads, down_weight[0]),
        gate_weight[0],
        up_weight[0],
        down_weight[0],
    )
    hidden_ref[0] = hidden
    grad_gate_ref[0] = grad_gate
    grad_up_ref[0] = grad_up

    def main_copies(at):
        place = pl.ds(pl.multiple_of(at * main_slots, main_slots), main_slots)
        return (
            pltpu.make_async_copy(result_main, result_ref.at[sources_at, :, place, :], sems.at[0]),
            pltpu.make_async_copy(back_main, back_ref.at[sources_at, :, place, :], sems.at[1]),
        )

    @pl.when(expert > 0)
    def _():
        for copy in main_copies(expert - 1):
            copy.wait()

    expert_output(result, select, expert, result_main, result_tail)
    expert_output(back, select, expert, back_main, back_tail)
    for copy in main_copies(expert):
        copy.start()

    @pl.when(expert == experts_here - 1)
    def _():
        place = pl.ds(experts_here * main_slots, tail_height)
        tails = (
            pltpu.make_async_copy(result_tail, result_ref.at[sources_at, :, place, :], sems.at[2]),
            pltpu.make_async_copy(back_tail, back_ref.at[sources_at, :, place, :], sems.at[3]),
        )
        for copy in tails:
            copy.start()
        for copy in main_copies(expert):
            copy.wait()
        for copy in tails:
            copy.wait()


def parts_of(rows):
    shards, groups = rows.shape[:2]
    return max(1, shards * groups // part_sources)


def row_specs(rows, experts_here, order):
    shards, groups, height, width = rows.shape
    shards_part = shards // parts_of(rows)
    tail_height = slot_rows(experts_here) - experts_here * main_slots
    tail_at = experts_here * main_slots // tail_height
    main_at = lambda e, c: (c, 0, e, 0)
    side_at = lambda e, c: (c, 0, tail_at, 0)
    return [
        pl.BlockSpec((shards_part, groups, main_slots, width), order(main_at)),
        pl.BlockSpec((shards_part, groups, tail_height, width), order(side_at)),
    ]


def expert_act(rows, grads, gate_weight, up_weight, down_weight):
    experts_here, units, width = gate_weight.shape
    shards, groups = rows.shape[:2]
    count = shards * groups * CAP
    parts = parts_of(rows)
    height = slot_rows(experts_here)
    tail_height = height - experts_here * main_slots
    order = lambda index: lambda c, e: index(e, c)
    weight_spec = pl.BlockSpec((1, units, width), lambda c, e: (e, 0, 0))
    act_spec = pl.BlockSpec((1, count // parts, units), lambda c, e: (e, c, 0))
    act_shape = jax.ShapeDtypeStruct((experts_here, count, units), jnp.bfloat16)
    slot_shape = lambda lanes: jax.ShapeDtypeStruct(
        (shards, groups, height, lanes), jnp.bfloat16
    )
    scratch = [
        pltpu.VMEM((shards // parts, groups, rows_of, lanes), jnp.bfloat16)
        for lanes in (width, width + spare)
        for rows_of in (main_slots, tail_height)
    ]
    return pl.pallas_call(
        functools.partial(expert_act_kernel, experts_here),
        grid=(parts, experts_here),
        out_shape=(act_shape, act_shape, act_shape, slot_shape(width), slot_shape(width + spare)),
        in_specs=row_specs(rows, experts_here, order)
        + row_specs(grads, experts_here, order)
        + [weight_spec] * 3,
        out_specs=(
            act_spec,
            act_spec,
            act_spec,
            pl.BlockSpec(memory_space=pl.ANY),
            pl.BlockSpec(memory_space=pl.ANY),
        ),
        scratch_shapes=scratch + [pltpu.SemaphoreType.DMA((4,))],
        compiler_params=pltpu.CompilerParams(vmem_limit_bytes=60 * mega),
        cost_estimate=pl.CostEstimate(
            flops=12 * experts_here * count * width * units,
            transcendentals=experts_here * count * units,
            bytes_accessed=6 * experts_here * width * units + 8 * experts_here * count * width,
        ),
        name="expert_act",
    )(rows, rows, grads, grads, gate_weight, up_weight, down_weight)


class RowChunk:
    def __init__(self, spot, number, place_rows, rows_in, rows_all, back_out, bufs, sems):
        self.spot, self.number, self.place_rows = spot, number, place_rows
        self.rows_in, self.rows_all, self.back_out = rows_in, rows_all, back_out
        self.rows, self.back, self.pair_in, self.across_out, self.across_in, self.total = bufs
        (
            self.local,
            self.send,
            self.recv,
            self.across_send,
            self.across_recv,
            self.core_send,
            self.core_recv,
            self.pair_send,
            self.pair_recv,
            self.sum_send,
            self.sum_recv,
            self.back_send,
            self.back_recv,
        ) = sems

    @staticmethod
    def sems(groups, columns, chunks):
        half = columns // 2
        dma = pltpu.SemaphoreType.DMA
        return (
            [dma((chunks, 3))]
            + [dma((chunks, groups))] * 2
            + [dma((chunks, groups, half))] * 4
            + [dma((chunks, half))] * 2
            + [dma((chunks, half, 2))] * 2
            + [dma((chunks, groups))] * 2
        )

    def own(self):
        spot = self.spot
        return pltpu.make_async_copy(
            self.rows_in.at[spot.place, self.place_rows],
            self.rows.at[spot.lane, spot.place],
            self.local.at[self.number, 0],
        )

    def keep(self):
        return pltpu.make_async_copy(
            self.rows, self.rows_all.at[:, :, self.place_rows], self.local.at[self.number, 1]
        )

    def swap(self, key):
        spot, at = self.spot, self.number
        peer = flip(spot.place, key)
        return remote(
            self.rows_in.at[peer, self.place_rows],
            self.rows.at[spot.lane, spot.place],
            self.send.at[at, key],
            self.recv.at[at, key],
            (peer, spot.lane),
        )

    def across(self, key, step):
        spot, at = self.spot, self.number
        block = self.rows.at[spot.lane, flip(spot.place, key)]
        return remote(
            block,
            block,
            self.across_send.at[at, key, step],
            self.across_recv.at[at, key, step],
            (spot.place, spot.across(step)),
        )

    def core(self, key, step):
        spot, at = self.spot, self.number
        block = self.rows.at[spot.behind(step), flip(spot.place, key)]
        return remote(
            block,
            block,
            self.core_send.at[at, key, step],
            self.core_recv.at[at, key, step],
            (spot.place, spot.partner),
        )

    def begin(self):
        groups = self.spot.groups
        self.own().start()
        for key in far_keys(groups) + near_keys(groups):
            self.swap(key).start()

    def advance(self):
        for key in range(self.spot.groups):
            if key == 0:
                self.own().wait()
            else:
                self.swap(key).wait_recv()
            for step in range(1, self.spot.half):
                self.across(key, step).start()
            self.core(key, 0).start()

    def complete(self):
        groups, half = self.spot.groups, self.spot.half
        for key in range(groups):
            for step in range(1, half):
                self.across(key, step).wait_recv()
                self.core(key, step).start()
        for key in range(groups):
            for step in range(half):
                self.core(key, step).wait_recv()
        self.keep().start()

    def pair_copy(self, step):
        spot, at = self.spot, self.number
        return remote(
            self.back.at[spot.lane_at(step, True)],
            self.pair_in.at[step],
            self.pair_send.at[at, step],
            self.pair_recv.at[at, step],
            (spot.place, spot.partner),
        )

    def side(self, near):
        half = self.spot.groups // 2
        here = self.spot.place // half
        return pl.ds((here if near else 1 - here) * half, half)

    def sum_copy(self, step, near):
        spot, at = self.spot, self.number
        groups = self.side(near)
        return remote(
            self.across_out.at[step, groups],
            self.across_in.at[step, groups],
            self.sum_send.at[at, step, near],
            self.sum_recv.at[at, step, near],
            (spot.place, spot.across(step)),
        )

    def back_copy(self, key):
        spot, at = self.spot, self.number
        peer = flip(spot.place, key)
        target = self.back_out.at[spot.place, self.place_rows]
        if key == 0:
            return pltpu.make_async_copy(self.total.at[peer], target, self.local.at[at, 2])
        return remote(
            self.total.at[peer],
            target,
            self.back_send.at[at, key],
            self.back_recv.at[at, key],
            (peer, spot.lane),
        )

    def pair(self):
        for step in list(range(1, self.spot.half)) + [0]:
            self.pair_copy(step).start()

    def pair_sum(self, step, near):
        groups = self.side(near)
        mine = self.back[self.spot.lane_at(step, False), groups].astype(jnp.float32)
        return mine + self.pair_in[step, groups].astype(jnp.float32)

    def middle(self):
        for step in range(1, self.spot.half):
            self.pair_copy(step).wait_recv()
        for near in range(2):
            for step in range(1, self.spot.half):
                total = self.pair_sum(step, near)
                self.across_out[step, self.side(near)] = total.astype(jnp.bfloat16)
                self.sum_copy(step, near).start()
        self.pair_copy(0).wait_recv()

    def last(self, near):
        total = self.pair_sum(0, near)
        for step in range(1, self.spot.half):
            self.sum_copy(step, near).wait_recv()
            total = total + self.across_in[step, self.side(near)].astype(jnp.float32)
        self.total[self.side(near)] = total.astype(jnp.bfloat16)
        groups = self.spot.groups
        for key in near_keys(groups) + [0] if near else far_keys(groups):
            self.back_copy(key).start()

    def finish(self):
        groups, half = self.spot.groups, self.spot.half
        for key in range(1, groups):
            self.back_copy(key).wait_recv()
        self.back_copy(0).wait()
        self.keep().wait()
        for key in range(groups):
            if key:
                self.swap(key).wait_send()
                self.back_copy(key).wait_send()
            for step in range(half):
                self.core(key, step).wait_send()
                if step:
                    self.across(key, step).wait_send()
        for step in range(half):
            self.pair_copy(step).wait_send()
            if step:
                self.sum_copy(step, 0).wait_send()
                self.sum_copy(step, 1).wait_send()


def experts_kernel(
    experts_here,
    groups,
    columns,
    rows_in,
    grad_main,
    grad_tail,
    gate_weight,
    up_weight,
    down_weight,
    hidden_ref,
    grad_gate_ref,
    grad_up_ref,
    result_ref,
    rows_all,
    back_out,
    result_main,
    result_tail,
    result_sems,
    *scratch,
):
    expert = pl.program_id(0)
    tail_height = result_tail.shape[2]
    spot = Spot(groups, columns)
    mains, tails, sems = scratch[:6], scratch[6:12], scratch[12:]
    chunks = [
        RowChunk(
            spot,
            at,
            pl.ds(at * main_slots, main_slots),
            rows_in,
            rows_all,
            back_out,
            [buf.at[at] for buf in mains],
            sems,
        )
        for at in range(experts_here)
    ]
    tail = RowChunk(
        spot,
        experts_here,
        pl.ds(experts_here * main_slots, tail_height),
        rows_in,
        rows_all,
        back_out,
        tails,
        sems,
    )

    @pl.when(expert == 0)
    def _():
        spot.meet()
        tail.begin()
        chunks[0].begin()
    select = tail_select(expert, groups * columns, tail_height)
    raw_hidden = nt_dot(expert_input(grad_main, grad_tail, select), down_weight[0])

    @pl.when(expert == 0)
    def _():
        tail.advance()
        chunks[0].advance()
        chunks[1].begin()

    for at in range(experts_here):

        @pl.when(expert == at)
        def _():
            if at + 1 < experts_here:
                chunks[at + 1].advance()
            if at + 2 < experts_here:
                chunks[at + 2].begin()
            if at == 0:
                tail.complete()
            chunks[at].complete()
            if at:
                chunks[at - 1].middle()

    main_rows, tail_rows, main_back, tail_back = mains[0], tails[0], mains[1], tails[1]
    wide_rows = expert_input(main_rows.at[expert], tail_rows, select)
    hidden, grad_gate, grad_up, back, result = expert_math(
        wide_rows, raw_hidden, gate_weight[0], up_weight[0], down_weight[0]
    )
    hidden_ref[0] = hidden
    grad_gate_ref[0] = grad_gate
    grad_up_ref[0] = grad_up
    expert_output(back, select, expert, main_back.at[expert], tail_back)

    for at in range(experts_here):

        @pl.when(expert == at)
        def _():
            chunks[at].pair()
            if at == experts_here - 1:
                tail.pair()
                chunks[at].middle()
                tail.middle()
            if at:
                chunks[at - 1].last(0)
                chunks[at - 1].last(1)

    def result_copy(at):
        place = pl.ds(pl.multiple_of(at * main_slots, main_slots), main_slots)
        return pltpu.make_async_copy(result_main, result_ref.at[:, :, place], result_sems.at[0])

    @pl.when(expert > 0)
    def _():
        result_copy(expert - 1).wait()

    expert_output(result, select, expert, result_main, result_tail)
    result_copy(expert).start()

    @pl.when(expert == experts_here - 1)
    def _():
        place = pl.ds(experts_here * main_slots, tail_height)
        side = pltpu.make_async_copy(result_tail, result_ref.at[:, :, place], result_sems.at[1])
        side.start()
        for near in range(2):
            chunks[-1].last(near)
            tail.last(near)
        for chunk in chunks + [tail]:
            chunk.finish()
        result_copy(expert).wait()
        side.wait()


def experts(rows, grads, gate_weight, up_weight, down_weight, columns):
    experts_here, units, width = gate_weight.shape
    groups, height, wide = rows.shape
    half = columns // 2
    count = columns * groups * CAP
    tail_height = height - experts_here * main_slots
    weight_spec = pl.BlockSpec((1, units, width), lambda e: (e, 0, 0))
    act_spec = pl.BlockSpec((1, count, units), lambda e: (e, 0, 0))
    act_shape = jax.ShapeDtypeStruct((experts_here, count, units), jnp.bfloat16)
    low = lambda *shape: pltpu.VMEM(shape, jnp.bfloat16)
    bufs = lambda lead, rows_of: [
        low(*lead, columns, groups, rows_of, wide),
        low(*lead, columns, groups, rows_of, wide),
        low(*lead, half, groups, rows_of, wide),
        low(*lead, half, groups, rows_of, wide),
        low(*lead, half, groups, rows_of, wide),
        low(*lead, groups, rows_of, wide),
    ]
    return pl.pallas_call(
        functools.partial(experts_kernel, experts_here, groups, columns),
        grid=(experts_here,),
        out_shape=(
            act_shape,
            act_shape,
            act_shape,
            jax.ShapeDtypeStruct((columns, groups, height, width), jnp.bfloat16),
            jax.ShapeDtypeStruct((columns,) + rows.shape, jnp.bfloat16),
            jax.ShapeDtypeStruct(rows.shape, jnp.bfloat16),
        ),
        in_specs=[anywhere]
        + row_specs(grads, experts_here, lambda index: lambda e: index(e, 0))
        + [weight_spec] * 3,
        out_specs=(act_spec, act_spec, act_spec, anywhere, anywhere, anywhere),
        scratch_shapes=[
            low(columns, groups, main_slots, width),
            low(columns, groups, tail_height, width),
            pltpu.SemaphoreType.DMA((2,)),
        ]
        + bufs((experts_here,), main_slots)
        + bufs((), tail_height)
        + RowChunk.sems(groups, columns, experts_here + 1),
        compiler_params=comm_params(10),
        cost_estimate=pl.CostEstimate(
            flops=12 * experts_here * count * width * units,
            transcendentals=experts_here * count * units,
            bytes_accessed=6 * experts_here * width * units + 8 * experts_here * count * width,
        ),
        name="experts",
    )(rows, grads, grads, gate_weight, up_weight, down_weight)


def expert_weight_kernel(
    parts,
    row_main,
    row_tail,
    grad_main,
    grad_tail,
    hidden_ref,
    grad_gate_ref,
    grad_up_ref,
    gate_out,
    up_out,
    down_out,
):
    expert, part = pl.program_id(0), pl.program_id(1)
    sources = row_main.shape[0] * row_main.shape[1]
    select = tail_select(expert, sources, row_tail.shape[2])
    wide_rows = expert_input(row_main, row_tail, select)
    rows = wide_rows[:, :D]
    grads = expert_input(grad_main, grad_tail, select)
    grad_low = (grads.astype(jnp.float32) * gates_of(wide_rows)).astype(jnp.bfloat16)

    @pl.when(part == 0)
    def _():
        gate_out[0] = tn_dot(grad_gate_ref[0], rows)
        up_out[0] = tn_dot(grad_up_ref[0], rows)
        down_out[0] = tn_dot(hidden_ref[0], grad_low)

    if parts > 1:

        @pl.when(part > 0)
        def _():
            gate_out[0] += tn_dot(grad_gate_ref[0], rows)
            up_out[0] += tn_dot(grad_up_ref[0], rows)
            down_out[0] += tn_dot(hidden_ref[0], grad_low)


def expert_weight_grads(rows, grads, hidden, grad_gate, grad_up):
    experts_here, count, units = hidden.shape
    width = grads.shape[-1]
    parts = parts_of(rows)
    order = lambda index: index
    act_spec = pl.BlockSpec((1, count // parts, units), lambda e, c: (e, c, 0))
    out_spec = pl.BlockSpec((1, units, width), lambda e, c: (e, 0, 0))
    out_shape = jax.ShapeDtypeStruct((experts_here, units, width), jnp.float32)
    return pl.pallas_call(
        functools.partial(expert_weight_kernel, parts),
        grid=(experts_here, parts),
        out_shape=(out_shape, out_shape, out_shape),
        in_specs=row_specs(rows, experts_here, order)
        + row_specs(grads, experts_here, order)
        + [act_spec] * 3,
        out_specs=(out_spec, out_spec, out_spec),
        compiler_params=pltpu.CompilerParams(vmem_limit_bytes=60 * mega),
        cost_estimate=pl.CostEstimate(
            flops=6 * experts_here * count * width * units,
            transcendentals=0,
            bytes_accessed=12 * experts_here * width * units + 10 * experts_here * count * width,
        ),
        name="expert_weight_grads",
    )(rows, rows, grads, grads, hidden, grad_gate, grad_up)


def pair_slots(token_routes, ranks, experts_here):
    row_count = token_routes.shape[0]
    expert_pair = jnp.concatenate([token_routes[:, 0], token_routes[:, 1]])
    rank_pair = jnp.concatenate([ranks, ranks + row_count])
    earlier = (expert_pair[None, :] == expert_pair[:, None]) & (
        rank_pair[None, :] < rank_pair[:, None]
    )
    slot_index = jnp.sum(earlier.astype(jnp.int32), axis=1)
    height = slot_rows(experts_here)
    local = expert_pair % experts_here
    main_at = local * main_slots + slot_index
    tail_at = experts_here * main_slots + local * tail_slots + slot_index - main_slots
    row = jnp.where(slot_index < main_slots, main_at, tail_at)
    slots = (expert_pair // experts_here) * height + row
    return jnp.where(slot_index < CAP, slots, -1)


def router_head(logits, token_routes, weights):
    token_count = logits.shape[0]
    probabilities = jax.nn.softmax(logits, axis=-1)
    log_totals = jax.nn.logsumexp(logits, axis=-1)
    picked = (token_routes[:, :, None] == jnp.arange(EXPERTS, dtype=jnp.int32)).astype(jnp.float32)
    chosen = jnp.sum(picked * probabilities[:, None, :], axis=-1)
    gate_values = chosen / jnp.sum(chosen, axis=1, keepdims=True)
    shares = jnp.sum(picked, axis=(0, 1)) / (token_count * TOP)
    balance = EXPERTS * jnp.sum(shares * jnp.sum(probabilities, axis=0))
    return (gate_values, weights[0] * jnp.sum(log_totals * log_totals) + weights[1] * balance)


def column(values, rows):
    return jnp.pad(values, (0, rows - values.shape[0]))[:, None]


def shards(
    inputs,
    grad_out,
    prefix,
    routes,
    priority,
    loss_weights,
    norm_attn,
    norm_moe,
    qkv_weight,
    out_weight,
    bias_table,
    router_weight,
    gate_weight,
    up_weight,
    down_weight,
):
    row_count = inputs.shape[0]
    groups = lax.axis_size("expert")
    columns_of = lax.axis_size("shard")
    place = lax.axis_index("expert")
    length = row_count * groups
    heads_here = HEADS // groups
    width = heads_here * HEAD
    experts_here = EXPERTS // groups
    shard_rows = D // columns_of
    height = slot_rows(experts_here)

    own_columns = lax.dynamic_slice_in_dim(
        qkv_weight.reshape(shard_rows, 3, groups, width), place, 1, 2
    ).reshape(shard_rows, 3 * width)
    packed_small = jnp.concatenate(
        [
            own_columns,
            router_weight,
            norm_attn[:, None],
            norm_moe[:, None],
            column(bias_table.reshape(-1), shard_rows),
            jnp.zeros((shard_rows, spare - EXPERTS - 3), jnp.bfloat16),
        ],
        axis=1,
    )
    token_routes = routes.reshape(row_count, TOP)
    slots = pair_slots(token_routes, priority.reshape(row_count), experts_here)
    slot_map = (
        jnp.arange(groups * height, dtype=jnp.int32)[:, None] == slots[None, :]
    ).reshape(groups * height, TOP, row_count)
    slot_any = jnp.any(slot_map, axis=1).astype(jnp.bfloat16)
    slot_pairs = slot_map.astype(jnp.bfloat16).reshape(groups * height, TOP * row_count)
    grad_low = grad_out.reshape(row_count, D)
    grad_slots = nn_dot(slot_any, grad_low).astype(jnp.bfloat16).reshape(groups, height, D)
    _, normed_all, qkv_own, small_full, out_full, far_slots = entry_gather(
        inputs.reshape(row_count, D),
        jnp.broadcast_to(norm_attn.astype(jnp.float32)[None], (8, shard_rows)),
        packed_small,
        out_weight,
        grad_slots,
        3 * width,
        1,
    )
    normed_all = normed_all.reshape(length, D)
    qkv_own = qkv_own.reshape(length, 3 * width)
    small_full = small_full.reshape(D, 3 * width + spare)
    out_full = out_full.reshape(D, D)
    own_weight = small_full[:, : 3 * width]
    extra = small_full[:, 3 * width :]
    router_full = extra[:, :EXPERTS]
    gain_attn = extra[:, EXPERTS].astype(jnp.float32)
    gain_moe = extra[:, EXPERTS + 1].astype(jnp.float32)
    table_rows = BUCKETS // columns_of
    table_full = (
        extra[:, EXPERTS + 2].reshape(columns_of, shard_rows)[:, : table_rows * HEADS]
    ).reshape(BUCKETS, HEADS)
    table_own = lax.dynamic_slice_in_dim(
        table_full.astype(jnp.float32), place * heads_here, heads_here, 1
    )
    near_ids = jnp.asarray(skew_buckets(), jnp.int32)
    near_hot = (near_ids[:, None] == jnp.arange(BUCKETS, dtype=jnp.int32)).astype(jnp.float32)
    base_bias = (
        jnp.dot(near_hot, table_own, precision=lax.Precision.HIGHEST).reshape(3, 2 * tile, heads_here)
        * log2e
    )
    base_bias = jnp.transpose(base_bias, (2, 0, 1)).reshape(heads_here * 3, 2 * tile)
    far_bias = jnp.stack([table_own[15], table_own[31]], axis=1) * log2e

    mixed_own, totals, grads_received = attend_forward(
        prefix, far_bias, base_bias, qkv_own, grad_slots, far_slots, columns_of
    )
    attended = exchange_mixed(mixed_own.reshape(groups, row_count, width), columns_of, 8)

    tokens_in = inputs.reshape(row_count, D).astype(jnp.float32)
    middle = tokens_in + nn_dot(attended, out_full)
    normed_two, norm_two_back = jax.vjp(rms_norm, middle, gain_moe)
    low_two = normed_two.astype(jnp.bfloat16)
    logits = nn_dot(low_two, router_full)
    router_out, router_back = jax.vjp(
        lambda logit_in: router_head(logit_in, token_routes, loss_weights), logits
    )
    gate_values = router_out[0]
    gate_high = lax.reduce_precision(gate_values, 8, 7)
    gate_parts = jnp.stack([gate_high, gate_values - gate_high], axis=-1).astype(jnp.bfloat16)
    wide_rows = jnp.concatenate(
        [
            jnp.broadcast_to(low_two[None], (TOP, row_count, D)),
            jnp.pad(jnp.transpose(gate_parts, (1, 0, 2)), ((0, 0), (0, 0), (0, spare - 2))),
        ],
        axis=2,
    ).reshape(TOP * row_count, D + spare)
    outgoing = nn_dot(slot_pairs, wide_rows).astype(jnp.bfloat16)
    outgoing = outgoing.reshape(groups, height, D + spare)
    gate_across, up_across, down_across = (
        jnp.transpose(weight, (0, 2, 1)) for weight in (gate_weight, up_weight, down_weight)
    )
    if columns_of * groups <= part_sources:
        hidden, grad_gate, grad_up, result_part, rows_received, grad_returned = experts(
            outgoing, grads_received, gate_across, up_across, down_across, columns_of
        )
    else:
        rows_received = dispatch(outgoing, columns_of, 2)
        hidden, grad_gate, grad_up, result_part, back_part = expert_act(
            rows_received, grads_received, gate_across, up_across, down_across
        )
        grad_returned = collect(back_part, 3)
    grad_returned = grad_returned.reshape(groups * height, D + spare)
    grad_low_two = tn_dot(slot_any, grad_returned[:, :D])
    grad_gates = jnp.transpose(
        tn_dot(slot_pairs, grad_returned[:, D:])[:, 0].reshape(TOP, row_count)
    )
    grad_top = grad_low.astype(jnp.float32)
    grad_logits = router_back((grad_gates, jnp.ones((), jnp.float32)))[0]
    low_logits = grad_logits.astype(jnp.bfloat16)
    router_grad = tn_dot(low_two, low_logits)
    grad_low_two = grad_low_two + nt_dot(low_logits, router_full)
    grad_middle_norm, gain_moe_grad = norm_two_back(grad_low_two)
    grad_middle = grad_top + grad_middle_norm
    low_middle = grad_middle.astype(jnp.bfloat16)
    out_grad = tn_dot(attended, low_middle)
    grad_attended = nt_dot(low_middle, out_full).astype(jnp.bfloat16)
    grad_attended = jnp.transpose(grad_attended.reshape(row_count, groups, width), (1, 0, 2))
    grad_mixed = lax.all_to_all(
        grad_attended, "expert", split_axis=0, concat_axis=0, tiled=True
    )
    gate_grad, up_grad, down_grad = expert_weight_grads(
        rows_received, grads_received, hidden, grad_gate, grad_up
    )
    out_sums = lax.psum_scatter(
        out_grad.astype(jnp.bfloat16), "shard", scatter_dimension=0, tiled=True
    ).reshape(groups, shard_rows // groups, D)
    grad_qkv, near_sums, side_sums, returned, out_piece = attend_backward(
        prefix,
        far_bias,
        base_bias,
        qkv_own,
        mixed_own,
        grad_mixed.reshape(length, width),
        totals,
        result_part,
        out_sums,
        columns_of,
    )
    slot_gates = jnp.sum(
        slot_map.astype(jnp.float32) * jnp.transpose(gate_values)[None], axis=1
    )
    slot_high = lax.reduce_precision(slot_gates, 8, 7)
    slot_parts = jnp.concatenate([slot_high, slot_gates - slot_high], axis=1).astype(jnp.bfloat16)
    mixture = tn_dot(slot_parts, returned.reshape(groups * height, D))
    mixture = mixture[:row_count] + mixture[row_count:]
    output = (middle + mixture).astype(jnp.bfloat16)

    table_grad = jnp.einsum(
        "hil,ilb->bh",
        near_sums.reshape(heads_here, 3, 2 * tile),
        near_hot.reshape(3, 2 * tile, BUCKETS),
        precision=lax.Precision.HIGHEST,
    )
    far_sums = jnp.sum(side_sums, axis=(2, 3))
    bucket_ids = jnp.arange(BUCKETS, dtype=jnp.int32)[:, None]
    table_grad = table_grad + jnp.where(bucket_ids == 15, far_sums[:, 0][None], 0.0)
    table_grad = table_grad + jnp.where(bucket_ids == 31, far_sums[:, 1][None], 0.0)
    table_column = jnp.pad(
        table_grad.reshape(columns_of, table_rows * heads_here),
        ((0, 0), (0, shard_rows - table_rows * heads_here)),
    ).reshape(D, 1)

    extra = jnp.concatenate(
        [
            jnp.zeros((D, 1), jnp.float32),
            table_column,
            gain_moe_grad[:, None],
            router_grad,
            jnp.zeros((D, spare - 3 - EXPERTS), jnp.float32),
        ],
        axis=1,
    ).astype(jnp.bfloat16)
    grad_projected, last_all, out_all, qkv_full = tail_exchange(
        grad_qkv.reshape(groups, row_count, 3 * width),
        normed_all,
        own_weight,
        gain_attn[:, None],
        extra,
        out_piece,
        qkv_weight,
        columns_of,
        7,
    )
    last_all = last_all.reshape(groups, shard_rows, 3 * width + spare)
    out_all = out_all.reshape(shard_rows, D)
    if width % 128 == 0:
        input_grad, qkv_total, out_total, extra_total = finish(
            grad_projected,
            qkv_full,
            last_all,
            inputs.reshape(row_count, D),
            gain_attn[None],
            grad_middle,
            out_all,
            width,
        )
    else:
        grad_projected = jnp.transpose(
            grad_projected.reshape(groups, row_count, 3, width), (1, 2, 0, 3)
        ).reshape(row_count, 3 * D)
        grad_low_one = nt_dot(grad_projected, qkv_full.reshape(D, 3 * D))
        _, norm_one_back = jax.vjp(lambda features: rms_norm(features, gain_attn), tokens_in)
        input_grad = grad_middle + norm_one_back(grad_low_one)[0]
        qkv_total = jnp.transpose(
            last_all[:, :, : 3 * width].reshape(groups, shard_rows, 3, width), (1, 2, 0, 3)
        ).reshape(shard_rows, 3 * D).astype(jnp.float32)
        out_total = out_all.astype(jnp.float32)
        extra_total = jnp.sum(last_all[:, :, 3 * width :].astype(jnp.float32), axis=0)
    table_part = last_all[:, : table_rows * heads_here, 3 * width + 1].astype(jnp.float32)
    table_total = jnp.transpose(
        table_part.reshape(groups, table_rows, heads_here), (1, 0, 2)
    ).reshape(table_rows, HEADS)
    return (
        output.reshape(row_count, 1, D),
        input_grad.reshape(row_count, 1, D),
        extra_total[:, 0],
        extra_total[:, 2],
        qkv_total,
        out_total,
        table_total,
        extra_total[:, 3 : 3 + EXPERTS],
        jnp.transpose(gate_grad, (0, 2, 1)),
        jnp.transpose(up_grad, (0, 2, 1)),
        jnp.transpose(down_grad, (0, 2, 1)),
    )


def solution(mesh):
    placed = (
        P("expert", "shard", None),
        P("expert", "shard", None),
        P("shard"),
        P("expert", "shard", None),
        P("expert", "shard", None),
        P(),
        P("shard"),
        P("shard"),
        P("shard", None),
        P("shard", None),
        P("shard", None),
        P("shard", None),
        P("expert", None, "shard"),
        P("expert", None, "shard"),
        P("expert", None, "shard"),
    )
    return jax.shard_map(
        shards,
        mesh=mesh,
        in_specs=placed,
        out_specs=(
            P("expert", "shard", None),
            P("expert", "shard", None),
            P("shard"),
            P("shard"),
            P("shard", None),
            P("shard", None),
            P("shard", None),
            P("shard", None),
            P("expert", None, "shard"),
            P("expert", None, "shard"),
            P("expert", None, "shard"),
        ),
        check_vma=False,
    )
```

```python
import functools
import math

import jax
import jax.numpy as jnp
import numpy as np
from jax import lax
from jax.experimental import pallas as pl
from jax.experimental.pallas import tpu as pltpu
from jax.sharding import PartitionSpec as P

D = 1024
HEADS = 16
HEAD = 64
FF = 2816
EXPERTS = 32
TOP = 2
BUCKETS = 32
CAP = 18

epsilon = 1e-06
masked_score = -1e30
far_bounds = (12, 16, 23, 32, 46, 64, 91)
tile = 256
main_slots = 16
tail_slots = CAP - main_slots
log2e = math.log2(math.e)
score_scale = HEAD ** (-0.5)
mega = 1024 * 1024
part_sources = 32
spare = 128


MESH = pl.DeviceIdType.MESH


def flip(index, key):
    out, bit = index, 1
    while bit <= key:
        if key & bit:
            out = out + bit * (1 - 2 * ((index // bit) % 2))
        bit *= 2
    return out


def near_keys(groups):
    return list(range(1, groups // 2))


def far_keys(groups):
    return list(range(groups // 2, groups))


def early_keys(groups):
    return [key for key in far_keys(groups) if key % line_shape(groups)[1] == 0]


class Spot:
    def __init__(self, groups, columns):
        self.groups, self.columns = groups, columns
        self.place = lax.axis_index("expert")
        self.lane = lax.axis_index("shard")
        self.half = columns // 2
        self.chip = self.lane // 2
        self.core = self.lane % 2
        self.partner = self.chip * 2 + 1 - self.core

    def across(self, step):
        return ((self.chip + step) % self.half) * 2 + self.core

    def behind(self, step):
        return ((self.chip + self.half - step) % self.half) * 2 + self.core

    def lane_at(self, step, other):
        chip = (self.chip + step) % self.half
        return chip * 2 + ((1 - self.core) if other else self.core)

    def meet(self):
        barrier = pltpu.get_barrier_semaphore()
        for key in range(1, self.groups):
            peer = (flip(self.place, key), self.lane)
            pl.semaphore_signal(barrier, inc=1, device_id=peer, device_id_type=MESH)
        for step in range(1, self.columns):
            peer = (self.place, (self.lane + step) % self.columns)
            pl.semaphore_signal(barrier, inc=1, device_id=peer, device_id_type=MESH)
        pl.semaphore_wait(barrier, self.groups + self.columns - 2)


def remote(source, target, send_sem, recv_sem, peer):
    return pltpu.make_async_remote_copy(
        src_ref=source,
        dst_ref=target,
        send_sem=send_sem,
        recv_sem=recv_sem,
        device_id=peer,
        device_id_type=MESH,
    )


def line_shape(groups):
    across = groups // 4
    return 4, across


class LineGather:
    def __init__(self, spot, own, full, local_sem, send_sems, recv_sems):
        self.spot, self.own, self.full = spot, own, full
        self.local_sem, self.send_sems, self.recv_sems = local_sem, send_sems, recv_sems
        self.long, self.wide = line_shape(spot.groups)
        self.z = spot.place // self.wide
        self.y = spot.place % self.wide

    @staticmethod
    def sems(groups):
        long, wide = line_shape(groups)
        return [
            pltpu.SemaphoreType.DMA(()),
            pltpu.SemaphoreType.DMA((2 * long - 1, wide + 1)),
            pltpu.SemaphoreType.DMA((groups,)),
        ]

    def copy(self, job, way, origin, source, target):
        return remote(
            source,
            self.full.at[origin],
            self.send_sems.at[job, way],
            self.recv_sems.at[origin],
            (target, self.spot.lane),
        )

    def each(self, job, origin, source, up, down, act):
        place, wide = self.spot.place, self.wide
        if up:

            @pl.when(self.z + 1 < self.long)
            def _():
                act(self.copy(job, 0, origin, source, place + wide))

        if down:

            @pl.when(self.z >= 1)
            def _():
                act(self.copy(job, 1, origin, source, place - wide))

        for step in range(1, wide):
            target = self.z * wide + (self.y + step) % wide
            act(self.copy(job, 1 + step, origin, source, target))

    def begin(self):
        place = self.spot.place
        self.each(0, place, self.own, True, True, lambda copy: copy.start())
        pltpu.make_async_copy(self.own, self.full.at[place], self.local_sem).start()

    def arrive(self, origin):
        self.copy(0, 0, origin, self.own, self.spot.place).wait_recv()

    def hop(self, k):
        place, wide = self.spot.place, self.wide

        @pl.when(self.z >= k)
        def _():
            origin = place - k * wide
            self.arrive(origin)
            self.each(k, origin, self.full.at[origin], True, False, lambda copy: copy.start())

        @pl.when(self.z + k < self.long)
        def _():
            origin = place + k * wide
            self.arrive(origin)
            job = self.long - 1 + k
            self.each(job, origin, self.full.at[origin], False, True, lambda copy: copy.start())

    def finish(self):
        for row in range(self.long):
            for step in range(1, self.wide):
                self.arrive(row * self.wide + (self.y + step) % self.wide)
        self.settle()

    def settle(self):
        place, wide = self.spot.place, self.wide
        stop = lambda copy: copy.wait_send()
        self.each(0, place, self.own, True, True, stop)
        for k in range(1, self.long):

            @pl.when(self.z >= k)
            def _():
                origin = place - k * wide
                self.each(k, origin, self.full.at[origin], True, False, stop)

            @pl.when(self.z + k < self.long)
            def _():
                origin = place + k * wide
                job = self.long - 1 + k
                self.each(job, origin, self.full.at[origin], False, True, stop)

        pltpu.make_async_copy(self.own, self.full.at[place], self.local_sem).wait()


class ColumnGather:
    def __init__(self, spot, own, full, local_sem, across_send, across_recv, core_send, core_recv):
        self.spot, self.own, self.full = spot, own, full
        self.local_sem = local_sem
        self.across_send, self.across_recv = across_send, across_recv
        self.core_send, self.core_recv = core_send, core_recv

    @staticmethod
    def sems(columns):
        return [pltpu.SemaphoreType.DMA(())] + [pltpu.SemaphoreType.DMA((columns // 2,))] * 4

    def across_copy(self, step):
        spot = self.spot
        return remote(
            self.own,
            self.full.at[spot.lane],
            self.across_send.at[step],
            self.across_recv.at[step],
            (spot.place, spot.across(step)),
        )

    def core_copy(self, step):
        spot = self.spot
        source = self.own if step == 0 else self.full.at[spot.behind(step)]
        target = spot.lane if step == 0 else spot.behind(step)
        return remote(
            source,
            self.full.at[target],
            self.core_send.at[step],
            self.core_recv.at[step],
            (spot.place, spot.partner),
        )

    def begin(self):
        for step in range(1, self.spot.half):
            self.across_copy(step).start()
        self.core_copy(0).start()
        pltpu.make_async_copy(self.own, self.full.at[self.spot.lane], self.local_sem).start()

    def forward(self):
        for step in range(1, self.spot.half):
            self.across_copy(step).wait_recv()
            self.core_copy(step).start()

    def finish(self):
        for step in range(self.spot.half):
            self.core_copy(step).wait_recv()
        for step in range(self.spot.half):
            self.core_copy(step).wait_send()
        for step in range(1, self.spot.half):
            self.across_copy(step).wait_send()
        pltpu.make_async_copy(self.own, self.full.at[self.spot.lane], self.local_sem).wait()


def comm_params(which, limit=60):
    return pltpu.CompilerParams(
        collective_id=which, has_side_effects=True, vmem_limit_bytes=limit * mega
    )


anywhere = pl.BlockSpec(memory_space=pl.ANY)


def entry_kernel(
    groups,
    columns,
    tokens,
    gain,
    pack,
    out_weight,
    rows,
    tokens_all,
    normed_all,
    qkv_all,
    pack_all,
    out_all,
    far_rows,
    side_rows,
    gain_all,
    token_sc,
    normed_sc,
    qkv_sc,
    gain_sc,
    pack_sc,
    token_sem,
    normed_sems,
    qkv_sems,
    pack_sem,
    gain_sem,
    *sems,
):
    spot = Spot(groups, columns)
    line = LineGather(spot, tokens, tokens_all, *sems[:3])
    gains = ColumnGather(spot, gain, gain_sc, *sems[3:8])
    packs = ColumnGather(spot, pack, pack_sc, *sems[8:13])
    outs = ColumnGather(spot, out_weight, out_all, *sems[13:18])
    far_send, far_recv, side_send, side_recv = sems[18:]
    wide = qkv_sc.shape[2]

    def far_copy(key):
        peer = flip(spot.place, key)
        return remote(
            rows.at[peer],
            far_rows.at[spot.place],
            far_send.at[key],
            far_recv.at[key],
            (peer, spot.lane),
        )

    def side_copy(key, step):
        at = flip(spot.place, key)
        return remote(
            far_rows.at[at] if key else rows.at[at],
            side_rows.at[step - 1, at],
            side_send.at[key, step],
            side_recv.at[key, step],
            (spot.place, spot.across(step)),
        )

    def stores(origin):
        return (
            pltpu.make_async_copy(
                normed_sc.at[origin], normed_all.at[origin], normed_sems.at[origin]
            ),
            pltpu.make_async_copy(qkv_sc.at[origin], qkv_all.at[origin], qkv_sems.at[origin]),
        )

    def project(origin, source):
        load = pltpu.make_async_copy(source, token_sc, token_sem)
        load.start()
        load.wait()
        features = token_sc[...].astype(jnp.float32)
        factor = lax.rsqrt(jnp.mean(features * features, axis=-1, keepdims=True) + epsilon)
        gain_row = jnp.concatenate([gain_sc[at, 0:1, :] for at in range(columns)], axis=1)
        normed = (features * factor * gain_row).astype(jnp.bfloat16)
        normed_sc[origin] = normed
        weight = pack_sc[...].reshape(D, -1)[:, :wide]
        qkv_sc[origin] = nn_dot(normed, weight).astype(jnp.bfloat16)
        for store in stores(origin):
            store.start()

    spot.meet()
    line.begin()
    gains.begin()
    packs.begin()
    outs.begin()
    gains.forward()
    packs.forward()
    gains.finish()
    packs.finish()
    keep = pltpu.make_async_copy(pack_sc, pack_all, pack_sem)
    keep.start()
    keep_gain = pltpu.make_async_copy(gain_sc, gain_all, gain_sem)
    keep_gain.start()
    project(spot.place, tokens)
    line.hop(1)
    outs.forward()
    for step in range(1, spot.half):
        side_copy(0, step).start()
    line.hop(2)
    for key in early_keys(groups):
        far_copy(key).start()
    line.hop(3)

    def own_column(row, carry):
        @pl.when(row != line.z)
        def _():
            origin = row * line.wide + line.y
            project(origin, tokens_all.at[origin])

        return carry

    lax.fori_loop(0, line.long, own_column, 0)

    for key in early_keys(groups):
        far_copy(key).wait_recv()
        for step in range(1, spot.half):
            side_copy(key, step).start()

    def other_column(at, carry):
        row = line.z + ((at + 1) // 2) * (1 - 2 * (at % 2))

        @pl.when((row >= 0) & (row < line.long))
        def _():
            for step in range(1, line.wide):
                origin = row * line.wide + (line.y + step) % line.wide
                line.arrive(origin)
                project(origin, tokens_all.at[origin])

        return carry

    lax.fori_loop(0, 2 * line.long - 1, other_column, 0)
    line.settle()
    for key in early_keys(groups):
        far_copy(key).wait_send()
    for key in [0] + early_keys(groups):
        for step in range(1, spot.half):
            side_copy(key, step).wait_recv()
            side_copy(key, step).wait_send()
    outs.finish()
    keep.wait()
    keep_gain.wait()
    for origin in range(groups):
        for store in stores(origin):
            store.wait()


def entry_gather(tokens, gain, pack, out_weight, rows, wide, which):
    groups = rows.shape[0]
    columns = D // out_weight.shape[0]
    count = tokens.shape[0]
    low = lambda *shape: jax.ShapeDtypeStruct(shape, jnp.bfloat16)
    dma = pltpu.SemaphoreType.DMA
    return pl.pallas_call(
        functools.partial(entry_kernel, groups, columns),
        out_shape=(
            low(groups, *tokens.shape),
            low(groups, *tokens.shape),
            low(groups, count, wide),
            low(columns, *pack.shape),
            low(columns, *out_weight.shape),
            low(*rows.shape),
            low(columns // 2 - 1, *rows.shape),
            jax.ShapeDtypeStruct((columns,) + gain.shape, jnp.float32),
        ),
        in_specs=[anywhere] * 5,
        out_specs=(anywhere,) * 8,
        scratch_shapes=[
            pltpu.VMEM(tokens.shape, jnp.bfloat16),
            pltpu.VMEM((groups,) + tokens.shape, jnp.bfloat16),
            pltpu.VMEM((groups, count, wide), jnp.bfloat16),
            pltpu.VMEM((columns,) + gain.shape, jnp.float32),
            pltpu.VMEM((columns,) + pack.shape, jnp.bfloat16),
            dma(()),
            dma((groups,)),
            dma((groups,)),
            dma(()),
            dma(()),
        ]
        + LineGather.sems(groups)
        + ColumnGather.sems(columns) * 3
        + [dma((groups,))] * 2
        + [dma((groups, columns // 2))] * 2,
        compiler_params=comm_params(which),
        name="entry_gather",
    )(tokens, gain, pack, out_weight, rows)


class Dispatch:
    def __init__(self, spot, rows, full, sems):
        self.spot, self.rows, self.full = spot, rows, full
        self.local, self.send, self.recv = sems[:3]
        self.across_send, self.across_recv, self.core_send, self.core_recv = sems[3:]

    @staticmethod
    def sems(groups, columns):
        return (
            [pltpu.SemaphoreType.DMA(())]
            + [pltpu.SemaphoreType.DMA((groups,))] * 2
            + [pltpu.SemaphoreType.DMA((groups, columns // 2))] * 4
        )

    def own(self):
        spot = self.spot
        return pltpu.make_async_copy(
            self.rows.at[spot.place], self.full.at[spot.lane, spot.place], self.local
        )

    def swap(self, key):
        spot = self.spot
        peer = flip(spot.place, key)
        return remote(
            self.rows.at[peer],
            self.full.at[spot.lane, spot.place],
            self.send.at[key],
            self.recv.at[key],
            (peer, spot.lane),
        )

    def across(self, key, step):
        spot = self.spot
        block = self.full.at[spot.lane, flip(spot.place, key)]
        return remote(
            block,
            block,
            self.across_send.at[key, step],
            self.across_recv.at[key, step],
            (spot.place, spot.across(step)),
        )

    def core(self, key, step):
        spot = self.spot
        block = self.full.at[spot.behind(step), flip(spot.place, key)]
        return remote(
            block,
            block,
            self.core_send.at[key, step],
            self.core_recv.at[key, step],
            (spot.place, spot.partner),
        )

    def begin(self):
        groups = self.spot.groups
        self.own().start()
        for key in far_keys(groups) + near_keys(groups):
            self.swap(key).start()

    def advance(self, key):
        if key == 0:
            self.own().wait()
        else:
            self.swap(key).wait_recv()
        for step in range(1, self.spot.half):
            self.across(key, step).start()
        self.core(key, 0).start()

    def pass_on(self, key):
        for step in range(1, self.spot.half):
            self.across(key, step).wait_recv()
            self.core(key, step).start()

    def finish(self):
        groups, half = self.spot.groups, self.spot.half
        for key in range(groups):
            for step in range(half):
                self.core(key, step).wait_recv()
        for key in range(groups):
            if key > 0:
                self.swap(key).wait_send()
            for step in range(1, half):
                self.across(key, step).wait_send()
            for step in range(half):
                self.core(key, step).wait_send()


def dispatch_kernel(groups, columns, rows, full, *sems):
    spot = Spot(groups, columns)
    job = Dispatch(spot, rows, full, sems)
    spot.meet()
    job.begin()
    for key in range(groups):
        job.advance(key)
        if key:
            job.pass_on(key - 1)
    job.pass_on(groups - 1)
    job.finish()


def dispatch(rows, columns, which):
    groups = rows.shape[0]
    return pl.pallas_call(
        functools.partial(dispatch_kernel, groups, columns),
        out_shape=jax.ShapeDtypeStruct((columns,) + rows.shape, rows.dtype),
        in_specs=[anywhere],
        out_specs=anywhere,
        scratch_shapes=Dispatch.sems(groups, columns),
        compiler_params=comm_params(which),
        name="dispatch_rows",
    )(rows)


class Exchange:
    def __init__(self, spot, blocks, thirds, local, send, recv):
        self.spot, self.blocks, self.thirds = spot, blocks, range(thirds)
        self.local, self.send, self.recv = local, send, recv

    @staticmethod
    def sems(groups, thirds):
        return [pltpu.SemaphoreType.DMA((thirds,))] + [
            pltpu.SemaphoreType.DMA((groups, thirds))
        ] * 2

    def copy(self, key, third):
        spot = self.spot
        peer = flip(spot.place, key)
        source, target = self.blocks(peer, third)
        if key == 0:
            return pltpu.make_async_copy(source, target, self.local.at[third])
        return remote(
            source,
            target,
            self.send.at[key, third],
            self.recv.at[key, third],
            (peer, spot.lane),
        )

    def start(self, key):
        for third in self.thirds:
            self.copy(key, third).start()

    def begin(self):
        groups = self.spot.groups
        for key in far_keys(groups) + near_keys(groups) + [0]:
            self.start(key)

    def arrive(self):
        for key in range(self.spot.groups):
            for third in self.thirds:
                copy = self.copy(key, third)
                copy.wait() if key == 0 else copy.wait_recv()

    def finish(self):
        for key in range(1, self.spot.groups):
            for third in self.thirds:
                self.copy(key, third).wait_send()


class ColumnSum:
    def __init__(self, spot, chunks, order, part, bufs, sems):
        self.spot, self.chunks, self.order, self.part = spot, chunks, order, part
        self.pair_in, self.mine, self.across_out, self.across_in = bufs
        self.local, self.pair_send, self.pair_recv, self.across_send, self.across_recv = sems

    @staticmethod
    def scratch(columns, chunks, block):
        half = columns // 2
        return [pltpu.VMEM((half, chunks) + block, jnp.bfloat16)] * 4 + [
            pltpu.SemaphoreType.DMA((half, chunks))
        ] * 5

    def pair_copy(self, step, k):
        spot = self.spot
        return remote(
            self.part.at[spot.lane_at(step, True), self.order(k)],
            self.pair_in.at[step, k],
            self.pair_send.at[step, k],
            self.pair_recv.at[step, k],
            (spot.place, spot.partner),
        )

    def mine_copy(self, step, k):
        return pltpu.make_async_copy(
            self.part.at[self.spot.lane_at(step, False), self.order(k)],
            self.mine.at[step, k],
            self.local.at[step, k],
        )

    def across_copy(self, step, k):
        spot = self.spot
        return remote(
            self.across_out.at[step, k],
            self.across_in.at[step, k],
            self.across_send.at[step, k],
            self.across_recv.at[step, k],
            (spot.place, spot.across(step)),
        )

    def begin(self):
        half = self.spot.half
        for k in range(self.chunks):
            for step in list(range(1, half)) + [0]:
                self.pair_copy(step, k).start()
                self.mine_copy(step, k).start()

    def pair_sum(self, step, k):
        self.pair_copy(step, k).wait_recv()
        self.mine_copy(step, k).wait()
        return self.mine[step, k].astype(jnp.float32) + self.pair_in[step, k].astype(jnp.float32)

    def middle(self, k):
        for step in range(1, self.spot.half):
            self.across_out[step, k] = self.pair_sum(step, k).astype(jnp.bfloat16)
            self.across_copy(step, k).start()

    def last(self, k):
        total = self.pair_sum(0, k)
        for step in range(1, self.spot.half):
            self.across_copy(step, k).wait_recv()
            total = total + self.across_in[step, k].astype(jnp.float32)
        return total.astype(jnp.bfloat16)

    def finish(self):
        for k in range(self.chunks):
            for step in range(self.spot.half):
                self.pair_copy(step, k).wait_send()
                if step:
                    self.across_copy(step, k).wait_send()


class Collect:
    def __init__(self, spot, part, out, scratch):
        self.spot, self.total = spot, scratch[9]
        self.keys = far_keys(spot.groups) + near_keys(spot.groups) + [0]
        self.sums = ColumnSum(
            spot,
            spot.groups,
            lambda k: flip(spot.place, self.keys[k]),
            part,
            scratch[:4],
            scratch[4:9],
        )
        self.out = out
        self.local, self.send, self.recv = scratch[10:]

    @staticmethod
    def scratch(columns, groups, block):
        return (
            ColumnSum.scratch(columns, groups, block)
            + [pltpu.VMEM((groups,) + block, jnp.bfloat16)]
            + [pltpu.SemaphoreType.DMA(())]
            + [pltpu.SemaphoreType.DMA((groups,))] * 2
        )

    def copy(self, k):
        spot, key = self.spot, self.keys[k]
        target = self.out.at[spot.place]
        if key == 0:
            return pltpu.make_async_copy(self.total.at[k], target, self.local)
        peer = flip(spot.place, key)
        return remote(
            self.total.at[k], target, self.send.at[k], self.recv.at[k], (peer, spot.lane)
        )

    def begin(self):
        self.sums.begin()

    def middle(self, key):
        self.sums.middle(key)

    def last(self, key):
        self.total[key] = self.sums.last(key)
        self.copy(key).start()

    def finish(self):
        last = self.spot.groups - 1
        for k in range(last):
            self.copy(k).wait_recv()
        for k in range(last):
            self.copy(k).wait_send()
        self.copy(last).wait()
        self.sums.finish()


def collect_kernel(groups, columns, part, out, *scratch):
    spot = Spot(groups, columns)
    job = Collect(spot, part, out, scratch)
    spot.meet()
    job.begin()
    ahead = 2
    for key in range(ahead):
        job.middle(key)
    for key in range(groups):
        if key + ahead < groups:
            job.middle(key + ahead)
        job.last(key)
    job.finish()


def collect(part, which):
    columns, groups = part.shape[:2]
    block = part.shape[2:]
    return pl.pallas_call(
        functools.partial(collect_kernel, groups, columns),
        out_shape=jax.ShapeDtypeStruct((groups,) + block, part.dtype),
        in_specs=[anywhere],
        out_specs=anywhere,
        scratch_shapes=Collect.scratch(columns, groups, block),
        compiler_params=comm_params(which),
        name="collect_rows",
    )(part)


def lanes_at(place, width):
    return pl.ds(pl.multiple_of(place * width, 128), width)


def mixed_kernel(groups, columns, mixed, attended, *sems):
    spot = Spot(groups, columns)
    width = mixed.shape[2]

    def blocks(at, third):
        if width % 128:
            return mixed.at[at], attended.at[spot.place]
        return mixed.at[at], attended.at[:, lanes_at(spot.place, width)]

    job = Exchange(spot, blocks, 1, *sems)
    spot.meet()
    job.begin()
    job.arrive()
    job.finish()


def exchange_mixed(mixed, columns, which):
    groups, rows, width = mixed.shape
    shape = mixed.shape if width % 128 else (rows, groups * width)
    out = pl.pallas_call(
        functools.partial(mixed_kernel, groups, columns),
        out_shape=jax.ShapeDtypeStruct(shape, mixed.dtype),
        in_specs=[anywhere],
        out_specs=anywhere,
        scratch_shapes=Exchange.sems(groups, 1),
        compiler_params=comm_params(which),
        name="exchange_mixed",
    )(mixed)
    if width % 128:
        out = jnp.transpose(out, (1, 0, 2)).reshape(rows, groups * width)
    return out


class Tail:
    def __init__(self, spot, chunks, refs, scratch):
        grads, part, piece, weight, grads_out, sum_all, piece_all, weight_all = refs
        groups = spot.groups
        width = grads.shape[2] // 3
        thirds = 3 if width % 128 == 0 else 1

        def blocks(at, third):
            if thirds == 1:
                return grads.at[at], grads_out.at[spot.place]
            columns_to = pl.ds(pl.multiple_of(third * D + spot.place * width, 128), width)
            return grads.at[at, :, pl.ds(third * width, width)], grads_out.at[:, columns_to]

        self.chunks = chunks
        self.sums = ColumnSum(spot, chunks, lambda k: k, part, scratch[:4], scratch[4:9])
        self.own_sum = scratch[9]
        self.swap = Exchange(spot, blocks, thirds, *scratch[10:13])
        self.line = LineGather(spot, self.own_sum, sum_all, *scratch[13:16])
        self.side = LineGather(spot, piece, piece_all, *scratch[16:19])
        self.column = ColumnGather(spot, weight, weight_all, *scratch[19:24])

    @staticmethod
    def scratch(columns, groups, chunks, block, thirds):
        return (
            ColumnSum.scratch(columns, chunks, block)
            + [pltpu.VMEM((chunks,) + block, jnp.bfloat16)]
            + Exchange.sems(groups, thirds)
            + LineGather.sems(groups) * 2
            + ColumnGather.sems(columns)
        )


def tail_kernel(
    groups,
    columns,
    chunks,
    grads,
    normed,
    own_weight,
    extra,
    piece,
    weight,
    grads_out,
    sum_all,
    piece_all,
    weight_all,
    grads_sc,
    normed_sc,
    load_sems,
    part,
    *scratch,
):
    spot = Spot(groups, columns)
    refs = (grads, part, piece, weight, grads_out, sum_all, piece_all, weight_all)
    tail = Tail(spot, chunks, refs, scratch)
    wide = grads.shape[2]
    block_rows = D // (columns * chunks)
    loads = [
        pltpu.make_async_copy(grads, grads_sc, load_sems.at[0]),
        pltpu.make_async_copy(normed, normed_sc, load_sems.at[1]),
    ]
    for load in loads:
        load.start()
    far = far_keys(groups)
    early, late = far[: len(far) // 2], far[len(far) // 2 :]
    spot.meet()
    tail.side.begin()
    for key in early + near_keys(groups) + [0]:
        tail.swap.start(key)
    for load in loads:
        load.wait()
    all_grads = grads_sc[...].reshape(-1, wide)

    for at in range(columns * chunks):
        rows = pl.ds(at * block_rows, block_rows)
        grad = tn_dot(normed_sc[:, rows], all_grads)
        weights = own_weight[rows, :][:, :wide].astype(jnp.float32)
        gain = jnp.sum(grad * weights, axis=1, keepdims=True)
        lanes = lax.broadcasted_iota(jnp.int32, (block_rows, spare), 1)
        side = jnp.where(lanes == 0, gain, extra[rows, :].astype(jnp.float32))
        part[at // chunks, at % chunks] = jnp.concatenate([grad, side], axis=1).astype(jnp.bfloat16)
    tail.sums.begin()
    for k in range(chunks):
        tail.sums.middle(k)
    tail.column.begin()
    tail.side.hop(1)
    for k in range(chunks):
        tail.own_sum[k] = tail.sums.last(k)
    tail.line.begin()
    tail.side.hop(2)
    tail.line.hop(1)
    tail.side.hop(3)
    tail.line.hop(2)
    for key in late:
        tail.swap.start(key)
    tail.line.hop(3)
    tail.column.forward()
    tail.side.finish()
    tail.swap.arrive()
    tail.line.finish()
    tail.column.finish()
    tail.swap.finish()
    tail.sums.finish()


def tail_exchange(grads, normed, own_weight, extra, piece, weight, columns, which):
    groups, row_count, wide = grads.shape
    apart = wide // 3 % 128 != 0
    grads_shape = grads.shape if apart else (row_count, wide * groups)
    chunks = 2
    block = (D // columns // chunks, wide + spare)
    shape_of = lambda shape: jax.ShapeDtypeStruct(shape, jnp.bfloat16)
    inside = pl.BlockSpec(memory_space=pltpu.VMEM)
    return pl.pallas_call(
        functools.partial(tail_kernel, groups, columns, chunks),
        out_shape=(
            shape_of(grads_shape),
            shape_of((groups, chunks) + block),
            shape_of((groups,) + piece.shape),
            shape_of((columns,) + weight.shape),
        ),
        in_specs=[anywhere, anywhere, inside, inside, anywhere, anywhere],
        out_specs=(anywhere,) * 4,
        scratch_shapes=[
            pltpu.VMEM(grads.shape, jnp.bfloat16),
            pltpu.VMEM(normed.shape, jnp.bfloat16),
            pltpu.SemaphoreType.DMA((2,)),
            pltpu.VMEM((columns, chunks) + block, jnp.bfloat16),
        ]
        + Tail.scratch(columns, groups, chunks, block, 1 if apart else 3),
        compiler_params=comm_params(which),
        name="tail_exchange",
    )(grads, normed, own_weight, extra, piece, weight)


def finish_kernel(
    width,
    grads,
    weight,
    packed,
    packed_extra,
    tokens,
    gain,
    grad_middle,
    out_low,
    input_grad,
    qkv_grad,
    out_grad,
    extra,
    total_sc,
):
    third = pl.program_id(0)
    for group in range(packed.shape[0]):
        qkv_grad[:, group * width : (group + 1) * width] = packed[group].astype(jnp.float32)
    part = nt_dot(grads[...], weight[...].reshape(D, -1))

    @pl.when(third == 0)
    def _():
        total_sc[...] = part

    @pl.when(third > 0)
    def _():
        total_sc[...] += part

    @pl.when(third == 2)
    def _():
        features = tokens[...].astype(jnp.float32)
        factor = lax.rsqrt(jnp.mean(features * features, axis=-1, keepdims=True) + epsilon)
        unit = features * factor
        scaled = total_sc[...] * gain[...]
        inner = jnp.mean(scaled * unit, axis=-1, keepdims=True)
        input_grad[...] = grad_middle[...] + factor * (scaled - unit * inner)
        out_grad[...] = out_low[...].astype(jnp.float32)
        extra[...] = jnp.transpose(jnp.sum(packed_extra[...].astype(jnp.float32), axis=0))


def finish(grads, weight, packed, tokens, gain, grad_middle, out_low, width):
    groups, shard_rows = packed.shape[:2]
    columns = weight.shape[0]
    rows = grads.shape[0]
    whole = lambda t: (0, 0)
    full = jax.ShapeDtypeStruct((rows, D), jnp.float32)
    return pl.pallas_call(
        functools.partial(finish_kernel, width),
        grid=(3,),
        out_shape=(
            full,
            jax.ShapeDtypeStruct((shard_rows, 3 * D), jnp.float32),
            jax.ShapeDtypeStruct((shard_rows, D), jnp.float32),
            jax.ShapeDtypeStruct((spare, shard_rows), jnp.float32),
        ),
        in_specs=[
            pl.BlockSpec((rows, D), lambda t: (0, t)),
            pl.BlockSpec((columns, shard_rows, D), lambda t: (0, 0, t)),
            pl.BlockSpec((groups, shard_rows, width), lambda t: (0, 0, t)),
            pl.BlockSpec((groups, shard_rows, spare), lambda t: (0, 0, 3 * width // spare)),
            pl.BlockSpec((rows, D), whole),
            pl.BlockSpec((1, D), whole),
            pl.BlockSpec((rows, D), whole),
            pl.BlockSpec((shard_rows, D), whole),
        ],
        out_specs=(
            pl.BlockSpec((rows, D), whole),
            pl.BlockSpec((shard_rows, D), lambda t: (0, t)),
            pl.BlockSpec((shard_rows, D), whole),
            pl.BlockSpec((spare, shard_rows), whole),
        ),
        scratch_shapes=[pltpu.VMEM((rows, D), jnp.float32)],
        compiler_params=pltpu.CompilerParams(vmem_limit_bytes=60 * mega),
        name="finish",
    )(grads, weight, packed, packed, tokens, gain, grad_middle, out_low)


def rms_norm(features, scales):
    factor = lax.rsqrt(jnp.mean(features * features, axis=-1, keepdims=True) + epsilon)
    return features * factor * scales


def buckets_of(offsets):
    distance = np.abs(offsets)
    beyond = 8 + np.sum(distance[..., None] >= np.array(far_bounds), axis=-1)
    return np.where(distance < 8, distance, beyond) + 16 * (offsets > 0)


def skew_buckets():
    lanes = np.arange(2 * tile)
    from_query = np.where(lanes < tile, -lanes, 2 * tile - lanes)
    return np.concatenate([buckets_of(near * tile + from_query) for near in (-1, 0, 1)])


def lane_row_mask(head, width, rows):
    lanes = lax.broadcasted_iota(jnp.int32, (rows, width), 1)
    return (lanes >= head * HEAD) & (lanes < (head + 1) * HEAD)


def fold_rows(block, op):
    return op(block.reshape(block.shape[0] // 8, 8, block.shape[1]), axis=0)


def nt_dot(left, right):
    return lax.dot_general(left, right, (((1,), (1,)), ((), ())), preferred_element_type=jnp.float32)


def tn_dot(left, right):
    return lax.dot_general(left, right, (((0,), (0,)), ((), ())), preferred_element_type=jnp.float32)


def nn_dot(left, right):
    return jnp.dot(left, right, preferred_element_type=jnp.float32)


def build_bias(base_ref, far_ref, bias_sc, heads_here):
    for head in range(heads_here):
        for near in range(3):
            row = base_ref[pl.ds(head * 3 + near, 1), :]
            wide = jnp.broadcast_to(row, (tile, 2 * tile))
            skewed = pltpu.roll(wide, 0, 1, stride=1, stride_axis=0)
            bias_sc[head, near] = skewed[:, :tile]
        bias_sc[head, 3] = jnp.full((tile, tile), far_ref[head, 1], jnp.float32)


def unskew_sum(wide):
    lanes = wide.shape[1]
    half = wide.shape[0] // 2
    while half >= 8:
        wide = wide[:half] + pltpu.roll(wide[half:], lanes - half, 1)
        half //= 2
    total = wide[0:1]
    for row in range(1, 8):
        total = total + pltpu.roll(wide[row : row + 1], lanes - row, 1)
    return total


def rows_at(index):
    return pl.ds(pl.multiple_of(index * tile, tile), tile)


def visible_tile(key_tile, query_tile, prefix_length):
    key_pos = key_tile * tile + lax.broadcasted_iota(jnp.int32, (tile, tile), 0)
    query_pos = query_tile * tile + lax.broadcasted_iota(jnp.int32, (tile, tile), 1)
    return (key_pos <= query_pos) | (key_pos < prefix_length)


class Spread:
    def __init__(self, spot, rows, far_rows, side_rows, full, sems):
        self.spot, self.rows, self.full = spot, rows, full
        self.far_rows, self.side_rows = far_rows, side_rows
        self.send, self.recv, self.local = sems[:3]
        self.across_send, self.across_recv, self.core_send, self.core_recv = sems[3:]
        self.early = early_keys(spot.groups)
        self.rest = [key for key in far_keys(spot.groups) if key not in self.early]
        self.near = near_keys(spot.groups)

    @staticmethod
    def sems(groups, columns):
        half = columns // 2
        return [pltpu.SemaphoreType.DMA((groups,))] * 2 + [
            pltpu.SemaphoreType.DMA((groups, half))
        ] * 5

    def source(self, key, step):
        spot = self.spot
        at = flip(spot.place, key)
        if key and key not in self.early:
            return self.full.at[spot.behind(step), at]
        if step:
            return self.side_rows.at[step - 1, at]
        return self.far_rows.at[at] if key else self.rows.at[at]

    def local_copy(self, key, step):
        spot = self.spot
        target = self.full.at[spot.behind(step), flip(spot.place, key)]
        return pltpu.make_async_copy(self.source(key, step), target, self.local.at[key, step])

    def swap(self, key):
        spot = self.spot
        peer = flip(spot.place, key)
        return remote(
            self.rows.at[peer],
            self.full.at[spot.lane, spot.place],
            self.send.at[key],
            self.recv.at[key],
            (peer, spot.lane),
        )

    def across(self, key, step):
        spot = self.spot
        block = self.full.at[spot.lane, flip(spot.place, key)]
        return remote(
            block,
            block,
            self.across_send.at[key, step],
            self.across_recv.at[key, step],
            (spot.place, spot.across(step)),
        )

    def core(self, key, step):
        spot = self.spot
        return remote(
            self.source(key, step),
            self.full.at[spot.behind(step), flip(spot.place, key)],
            self.core_send.at[key, step],
            self.core_recv.at[key, step],
            (spot.place, spot.partner),
        )

    def begin(self):
        for key in self.rest + self.near:
            self.swap(key).start()
        for key in [0] + self.early:
            for step in range(self.spot.half):
                self.core(key, step).start()
                self.local_copy(key, step).start()

    def advance(self, key):
        self.swap(key).wait_recv()
        for step in range(1, self.spot.half):
            self.across(key, step).start()
        self.core(key, 0).start()

    def pass_on(self, key):
        for step in range(1, self.spot.half):
            self.across(key, step).wait_recv()
            self.core(key, step).start()

    def finish(self):
        half = self.spot.half
        keys = range(self.spot.groups)
        for key in keys:
            for step in range(half):
                self.core(key, step).wait_recv()
        for key in keys:
            moved = key in self.near + self.rest
            if moved:
                self.swap(key).wait_send()
            for step in range(half):
                self.core(key, step).wait_send()
                if not moved:
                    self.local_copy(key, step).wait()
                elif step:
                    self.across(key, step).wait_send()


def attend_forward_kernel(
    heads_here,
    groups,
    columns,
    prefix_ref,
    far_ref,
    base_ref,
    qkv_ref,
    rows_ref,
    far_rows_ref,
    side_rows_ref,
    mixed_ref,
    totals_ref,
    full_ref,
    bias_sc,
    score_sc,
    value_sc,
    *sems,
):
    width = heads_here * HEAD
    query_tile = pl.program_id(0)
    tiles = qkv_ref.shape[0] // tile
    spot = Spot(groups, columns)
    job = Spread(spot, rows_ref, far_rows_ref, side_rows_ref, full_ref, sems)

    @pl.when(query_tile == 0)
    def _():
        spot.meet()
        job.begin()

    prefix_length = prefix_ref[0]
    heads = range(heads_here)

    @pl.when(query_tile == 0)
    def _():
        build_bias(base_ref, far_ref, bias_sc, heads_here)
        for key_tile in range(value_sc.shape[1] // tile):
            rows = pl.ds(key_tile * tile, tile)
            values = qkv_ref[rows, 2 * width : 3 * width].astype(jnp.float32)
            value_sc[:, rows] = jnp.transpose(values).astype(jnp.bfloat16)

    queries = qkv_ref[rows_at(query_tile), :width]
    head_queries = [
        jnp.where(lane_row_mask(head, width, tile), queries, jnp.zeros_like(queries)) for head in heads
    ]

    def score_tiles(key_tile, tops, finish):
        keys = qkv_ref[rows_at(key_tile), width : 2 * width]
        out = []
        for head in heads:
            scores = finish(head, nt_dot(keys, head_queries[head]) * (score_scale * log2e))
            score_sc[head, rows_at(key_tile), :] = scores
            out.append(jnp.maximum(tops[head], fold_rows(scores, jnp.max)))
        return tuple(out)

    def far_body(key_tile, tops):
        return score_tiles(key_tile, tops, lambda head, raw: raw + far_ref[head, 0])

    def near_body(key_tile, tops):
        return score_tiles(key_tile, tops, lambda head, raw: raw + bias_sc[head, 0])

    def tail_body(key_tile, tops):
        shown = visible_tile(key_tile, query_tile, prefix_length)
        which = 1 + jnp.minimum(key_tile - query_tile, 2)
        return score_tiles(
            key_tile, tops, lambda head, raw: jnp.where(shown, raw + bias_sc[head, which], masked_score)
        )

    tile_count = jnp.maximum(query_tile + 1, tiles // 2)
    near_start = jnp.maximum(query_tile - 1, 0)
    tops = tuple(jnp.full((8, tile), masked_score, jnp.float32) for _ in heads)
    tops = lax.fori_loop(0, near_start, far_body, tops)
    tops = lax.fori_loop(near_start, query_tile, near_body, tops)
    tops = lax.fori_loop(query_tile, tile_count, tail_body, tops)
    tops = [jnp.max(top, axis=0, keepdims=True) for top in tops]

    def mix_body(key_tile, carry):
        sums, mixes = carry
        new_sums, new_mixes = [], []
        for head in heads:
            expos = jnp.exp2(score_sc[head, rows_at(key_tile), :] - tops[head])
            new_sums.append(sums[head] + fold_rows(expos, jnp.sum))
            values = value_sc[head * HEAD : (head + 1) * HEAD, rows_at(key_tile)]
            new_mixes.append(mixes[head] + nn_dot(values, expos.astype(jnp.bfloat16)))
        return (tuple(new_sums), tuple(new_mixes))

    sums, mixes = lax.fori_loop(
        0,
        tile_count,
        mix_body,
        (
            tuple(jnp.zeros((8, tile), jnp.float32) for _ in heads),
            tuple(jnp.zeros((HEAD, tile), jnp.float32) for _ in heads),
        ),
    )
    parts = []
    for head in heads:
        total = jnp.sum(sums[head], axis=0, keepdims=True)
        parts.append(mixes[head] / total)
        totals_ref[0, pl.ds(head, 1), :] = tops[head] + jnp.log2(total)
    mixed_ref[...] = jnp.transpose(jnp.concatenate(parts, axis=0)).astype(jnp.bfloat16)

    @pl.when(query_tile == tiles // 4)
    def _():
        for key in job.near:
            job.advance(key)

    @pl.when(query_tile == tiles // 2)
    def _():
        for key in job.near[:1]:
            job.pass_on(key)

    @pl.when(query_tile == tiles - 3)
    def _():
        for key in job.rest:
            job.advance(key)

    @pl.when(query_tile == tiles - 1)
    def _():
        for key in job.near[1:] + job.rest:
            job.pass_on(key)
        job.finish()


def attend_forward(prefix, far_bias, base_bias, qkv, rows, far_rows, side_rows, columns):
    length = qkv.shape[0]
    groups = rows.shape[0]
    width = qkv.shape[1] // 3
    heads_here = width // HEAD
    tiles = length // tile
    return pl.pallas_call(
        functools.partial(attend_forward_kernel, heads_here, groups, columns),
        grid=(tiles,),
        out_shape=(
            jax.ShapeDtypeStruct((length, width), jnp.bfloat16),
            jax.ShapeDtypeStruct((tiles, heads_here, tile), jnp.float32),
            jax.ShapeDtypeStruct((columns,) + rows.shape, rows.dtype),
        ),
        in_specs=[
            pl.BlockSpec(memory_space=pltpu.SMEM),
            pl.BlockSpec(memory_space=pltpu.SMEM),
            pl.BlockSpec(base_bias.shape, lambda i: (0, 0)),
            pl.BlockSpec(qkv.shape, lambda i: (0, 0)),
            anywhere,
            anywhere,
            anywhere,
        ],
        out_specs=(
            pl.BlockSpec((tile, width), lambda i: (i, 0)),
            pl.BlockSpec((1, heads_here, tile), lambda i: (i, 0, 0)),
            anywhere,
        ),
        scratch_shapes=[
            pltpu.VMEM((heads_here, 4, tile, tile), jnp.float32),
            pltpu.VMEM((heads_here, length, tile), jnp.float32),
            pltpu.VMEM((width, length), jnp.bfloat16),
        ]
        + Spread.sems(groups, columns),
        compiler_params=comm_params(5),
        cost_estimate=pl.CostEstimate(
            flops=40 * length * length * width, transcendentals=length * length * heads_here,
            bytes_accessed=8 * length * width,
        ),
        name="attend_forward",
    )(prefix, far_bias, base_bias, qkv, rows, far_rows, side_rows)


def attend_backward_kernel(
    heads_here,
    groups,
    columns,
    prefix_ref,
    far_ref,
    base_ref,
    qkv_ref,
    mixed_ref,
    grad_ref,
    totals_ref,
    part_ref,
    sums_ref,
    out_ref,
    near_ref,
    side_ref,
    result_ref,
    piece_ref,
    bias_sc,
    key_sc,
    grad_key_sc,
    grad_value_sc,
    near_sc,
    *scratch,
):
    width = heads_here * HEAD
    query_tile = pl.program_id(0)
    tiles = qkv_ref.shape[0] // tile
    spot = Spot(groups, columns)
    pieces = scratch[0]
    swap = Exchange(
        spot, lambda at, third: (sums_ref.at[at], pieces.at[spot.place]), 1, *scratch[1:4]
    )
    job = Collect(spot, part_ref, result_ref, scratch[4:])

    @pl.when(query_tile == 0)
    def _():
        spot.meet()
        job.begin()
        swap.begin()

    prefix_length = prefix_ref[0]
    heads = range(heads_here)

    @pl.when(query_tile == 0)
    def _():
        build_bias(base_ref, far_ref, bias_sc, heads_here)
        for key_tile in range(key_sc.shape[1] // tile):
            rows = pl.ds(key_tile * tile, tile)
            keys = qkv_ref[rows, width : 2 * width].astype(jnp.float32)
            key_sc[:, rows] = jnp.transpose(keys).astype(jnp.bfloat16)
        grad_key_sc[...] = jnp.zeros_like(grad_key_sc)
        grad_value_sc[...] = jnp.zeros_like(grad_value_sc)
        near_sc[...] = jnp.zeros_like(near_sc)
        side_ref[...] = jnp.zeros_like(side_ref)

    queries = qkv_ref[rows_at(query_tile), :width]
    grads = grad_ref[rows_at(query_tile), :]
    products = grads.astype(jnp.float32) * mixed_ref[rows_at(query_tile), :].astype(jnp.float32)
    head_queries, head_grads, inners, totals = [], [], [], []
    for head in heads:
        mask = lane_row_mask(head, width, tile)
        head_queries.append(jnp.where(mask, queries, jnp.zeros_like(queries)))
        head_grads.append(jnp.where(mask, grads, jnp.zeros_like(grads)))
        ones = jnp.where(lane_row_mask(head, width, 8), 1.0, 0.0)
        inner = lax.dot_general(
            ones,
            products,
            (((1,), (1,)), ((), ())),
            precision=lax.Precision.HIGHEST,
            preferred_element_type=jnp.float32,
        )
        inners.append(inner[0:1, :])
        totals.append(totals_ref[0, pl.ds(head, 1), :])

    def step(key_tile, carry, finish, keep):
        sides, grad_queries = carry
        keys = qkv_ref[rows_at(key_tile), width : 2 * width]
        values = qkv_ref[rows_at(key_tile), 2 * width : 3 * width]
        new_sides, new_queries = [], []
        key_part, value_part = None, None
        for head in heads:
            raw = nt_dot(keys, head_queries[head]) * (score_scale * log2e)
            attention = jnp.exp2(finish(head, raw))
            grad_weights = nt_dot(values, head_grads[head])
            grad_scores = attention * (grad_weights - inners[head])
            new_sides.append(keep(head, grad_scores, sides[head]))
            low_scores = grad_scores.astype(jnp.bfloat16)
            keys_across = key_sc[head * HEAD : (head + 1) * HEAD, rows_at(key_tile)]
            new_queries.append(grad_queries[head] + nn_dot(keys_across, low_scores))
            value_one = nn_dot(attention.astype(jnp.bfloat16), head_grads[head])
            key_one = nn_dot(low_scores, head_queries[head])
            value_part = value_one if value_part is None else value_part + value_one
            key_part = key_one if key_part is None else key_part + key_one
        grad_key_sc[rows_at(key_tile), :] += key_part
        grad_value_sc[rows_at(key_tile), :] += value_part
        return (tuple(new_sides), tuple(new_queries))

    def add_side(head, grad_scores, side):
        return side + fold_rows(grad_scores, jnp.sum)

    def far_body(key_tile, carry):
        return step(
            key_tile, carry, lambda head, raw: raw + (far_ref[head, 0] - totals[head]), add_side
        )

    def near_body(key_tile, carry):
        def keep(head, grad_scores, side):
            near_sc[head, 0] += grad_scores
            return side

        return step(
            key_tile, carry, lambda head, raw: raw + bias_sc[head, 0] - totals[head], keep
        )

    def tail_body(key_tile, carry):
        shown = visible_tile(key_tile, query_tile, prefix_length)
        which = 1 + jnp.minimum(key_tile - query_tile, 2)

        def keep(head, grad_scores, side):
            near_sc[head, which] += grad_scores
            return side

        return step(
            key_tile,
            carry,
            lambda head, raw: jnp.where(
                shown, raw + bias_sc[head, which] - totals[head], masked_score
            ),
            keep,
        )

    tile_count = jnp.maximum(query_tile + 1, tiles // 2)
    near_start = jnp.maximum(query_tile - 1, 0)
    carry = (
        tuple(jnp.zeros((8, tile), jnp.float32) for _ in heads),
        tuple(jnp.zeros((HEAD, tile), jnp.float32) for _ in heads),
    )
    carry = lax.fori_loop(0, near_start, far_body, carry)
    carry = lax.fori_loop(near_start, query_tile, near_body, carry)
    carry = lax.fori_loop(query_tile, tile_count, tail_body, carry)
    sides, grad_queries = carry
    for head in heads:
        side_ref[head, 0] += sides[head]
    across = jnp.concatenate(grad_queries, axis=0) * score_scale
    out_ref[rows_at(query_tile), :width] = jnp.transpose(across).astype(jnp.bfloat16)

    @pl.when(query_tile == tiles - 1)
    def _():
        out_ref[:, width : 2 * width] = (grad_key_sc[...] * score_scale).astype(jnp.bfloat16)
        out_ref[:, 2 * width : 3 * width] = grad_value_sc[...].astype(jnp.bfloat16)
        for head in heads:
            side_ref[head, 1] = fold_rows(near_sc[head, 3], jnp.sum)
            for near in range(3):
                wide = jnp.concatenate(
                    [near_sc[head, near], jnp.zeros((tile, tile), jnp.float32)], axis=1
                )
                near_ref[pl.ds(head * 3 + near, 1), :] = unskew_sum(wide)

    for step in range(tiles):
        middles = [key for key in range(groups) if key * 2 // groups == step]
        lasts = [key for key in range(groups) if min(tiles - 1, 2 + key * 3 // 4) == step]

        @pl.when(query_tile == step)
        def _():
            for key in middles:
                job.middle(key)
            for key in lasts:
                job.last(key)

    @pl.when(query_tile == tiles - 1)
    def _():
        swap.arrive()
        piece_ref[...] = jnp.sum(pieces[...].astype(jnp.float32), axis=0).astype(jnp.bfloat16)
        job.finish()
        swap.finish()


def attend_backward(
    prefix, far_bias, base_bias, qkv, mixed, grad_mixed, totals, part, sums, columns
):
    length = qkv.shape[0]
    groups, piece_rows, piece_width = sums.shape
    block = part.shape[2:]
    width = qkv.shape[1] // 3
    heads_here = width // HEAD
    tiles = length // tile
    whole = lambda i: (0, 0)
    return pl.pallas_call(
        functools.partial(attend_backward_kernel, heads_here, groups, columns),
        grid=(tiles,),
        out_shape=(
            jax.ShapeDtypeStruct((length, 3 * width), jnp.bfloat16),
            jax.ShapeDtypeStruct((heads_here * 3, 2 * tile), jnp.float32),
            jax.ShapeDtypeStruct((heads_here, 2, 8, tile), jnp.float32),
            jax.ShapeDtypeStruct((groups,) + block, jnp.bfloat16),
            jax.ShapeDtypeStruct((piece_rows, piece_width), jnp.bfloat16),
        ),
        in_specs=[
            pl.BlockSpec(memory_space=pltpu.SMEM),
            pl.BlockSpec(memory_space=pltpu.SMEM),
            pl.BlockSpec(base_bias.shape, whole),
            pl.BlockSpec(qkv.shape, whole),
            pl.BlockSpec(mixed.shape, whole),
            pl.BlockSpec(mixed.shape, whole),
            pl.BlockSpec((1, heads_here, tile), lambda i: (i, 0, 0)),
            anywhere,
            anywhere,
        ],
        out_specs=(
            pl.BlockSpec((length, 3 * width), whole),
            pl.BlockSpec((heads_here * 3, 2 * tile), whole),
            pl.BlockSpec((heads_here, 2, 8, tile), lambda i: (0, 0, 0, 0)),
            anywhere,
            pl.BlockSpec((piece_rows, piece_width), whole),
        ),
        scratch_shapes=[
            pltpu.VMEM((heads_here, 4, tile, tile), jnp.float32),
            pltpu.VMEM((width, length), jnp.bfloat16),
            pltpu.VMEM((length, width), jnp.float32),
            pltpu.VMEM((length, width), jnp.float32),
            pltpu.VMEM((heads_here, 4, tile, tile), jnp.float32),
            pltpu.VMEM(sums.shape, jnp.bfloat16),
        ]
        + Exchange.sems(groups, 1)
        + Collect.scratch(columns, groups, block),
        compiler_params=comm_params(6, 60),
        cost_estimate=pl.CostEstimate(
            flops=70 * length * length * width, transcendentals=length * length * heads_here,
            bytes_accessed=16 * length * width,
        ),
        name="attend_backward",
    )(prefix, far_bias, base_bias, qkv, mixed, grad_mixed, totals, part, sums)


def gelu_parts(act):
    inner = math.sqrt(2.0 / math.pi) * (act + 0.044715 * act * act * act)
    tanh = jnp.tanh(inner)
    half = 0.5 * (1.0 + tanh)
    slope = math.sqrt(2.0 / math.pi) * (1.0 + 3.0 * 0.044715 * act * act)
    return act * half, half + 0.5 * act * (1.0 - tanh * tanh) * slope


def slot_rows(experts_here):
    return experts_here * main_slots + -(-experts_here * tail_slots // 8) * 8


def tail_select(expert, sources, tail_height):
    rows = lax.broadcasted_iota(jnp.int32, (sources * tail_slots, sources * tail_height), 0)
    columns = lax.broadcasted_iota(jnp.int32, (sources * tail_slots, sources * tail_height), 1)
    wanted = (rows // tail_slots) * tail_height + expert * tail_slots + rows % tail_slots
    return jnp.where(columns == wanted, 1.0, 0.0).astype(jnp.bfloat16)


def expert_input(main_ref, tail_ref, select):
    width = main_ref.shape[-1]
    main = main_ref[...].reshape(-1, width)
    tail = nn_dot(select, tail_ref[...].reshape(-1, width)).astype(jnp.bfloat16)
    return jnp.concatenate([main, tail], axis=0)


def gates_of(wide_rows):
    return wide_rows[:, D : D + 1].astype(jnp.float32) + wide_rows[:, D + 1 : D + 2].astype(
        jnp.float32
    )


def expert_output(value, select, expert, main_sc, tail_sc):
    low = value.astype(jnp.bfloat16)
    main_count = main_sc.shape[0] * main_sc.shape[1] * main_slots
    main_sc[...] = low[:main_count].reshape(main_sc.shape)
    spread = tn_dot(select, low[main_count:]).astype(jnp.bfloat16).reshape(tail_sc.shape)

    @pl.when(expert == 0)
    def _():
        tail_sc[...] = spread

    @pl.when(expert > 0)
    def _():
        tail_sc[...] += spread


def expert_math(rows, gates, raw_hidden, gate_weight, up_weight, down_weight):
    gate_act = nt_dot(rows, gate_weight)
    up_act = nt_dot(rows, up_weight)
    gelu, slope = gelu_parts(gate_act)
    hidden = gelu * up_act
    low_hidden = hidden.astype(jnp.bfloat16)
    grad_gates = jnp.sum(raw_hidden * low_hidden.astype(jnp.float32), axis=1, keepdims=True)
    grad_hidden = raw_hidden * gates
    grad_gate = (grad_hidden * up_act * slope).astype(jnp.bfloat16)
    grad_up = (grad_hidden * gelu).astype(jnp.bfloat16)
    back = nn_dot(grad_gate, gate_weight) + nn_dot(grad_up, up_weight)
    gated = (hidden * gates).astype(jnp.bfloat16)
    return gated, grad_gate, grad_up, back, grad_gates, nn_dot(low_hidden, down_weight)


def slot_lanes(expert, experts_here, sources):
    main = sources * main_slots
    count = sources * CAP
    rows = lax.broadcasted_iota(jnp.int32, (count, sources), 0)
    source = jnp.where(rows < main, rows // main_slots, (rows - main) // tail_slots)
    hot = jnp.where(lax.broadcasted_iota(jnp.int32, (count, sources), 1) == source, 1.0, 0.0)
    rows = lax.broadcasted_iota(jnp.int32, (count, spare), 0)
    lane = jnp.where(
        rows < main,
        expert * main_slots + rows % main_slots,
        experts_here * main_slots + expert * tail_slots + (rows - main) % tail_slots,
    )
    return hot.astype(jnp.bfloat16), lax.broadcasted_iota(jnp.int32, (count, spare), 1) == lane


def split_low(values):
    high = values.astype(jnp.bfloat16)
    return high, (values - high.astype(jnp.float32)).astype(jnp.bfloat16)


def expert_act_kernel(
    experts_here,
    row_main,
    row_tail,
    grad_main,
    grad_tail,
    gate_weight,
    up_weight,
    down_weight,
    hidden_ref,
    grad_gate_ref,
    grad_up_ref,
    result_ref,
    back_ref,
    result_main,
    result_tail,
    back_main,
    back_tail,
    sems,
):
    part, expert = pl.program_id(0), pl.program_id(1)
    shards_part = row_main.shape[0]
    sources = shards_part * row_main.shape[1]
    tail_height = row_tail.shape[2]
    sources_at = pl.ds(part * shards_part, shards_part)
    select = tail_select(expert, sources, tail_height)
    wide_rows = expert_input(row_main, row_tail, select)
    grads = expert_input(grad_main, grad_tail, select)
    hidden, grad_gate, grad_up, back, grad_gates, result = expert_math(
        wide_rows[:, :D],
        gates_of(wide_rows),
        nt_dot(grads, down_weight[0]),
        gate_weight[0],
        up_weight[0],
        down_weight[0],
    )
    lanes = lax.broadcasted_iota(jnp.int32, (back.shape[0], spare), 1)
    back = jnp.concatenate([back, jnp.where(lanes == 0, grad_gates, 0.0)], axis=1)
    hidden_ref[0] = hidden
    grad_gate_ref[0] = grad_gate
    grad_up_ref[0] = grad_up

    def main_copies(at):
        place = pl.ds(pl.multiple_of(at * main_slots, main_slots), main_slots)
        return (
            pltpu.make_async_copy(result_main, result_ref.at[sources_at, :, place, :], sems.at[0]),
            pltpu.make_async_copy(back_main, back_ref.at[sources_at, :, place, :], sems.at[1]),
        )

    @pl.when(expert > 0)
    def _():
        for copy in main_copies(expert - 1):
            copy.wait()

    expert_output(result, select, expert, result_main, result_tail)
    expert_output(back, select, expert, back_main, back_tail)
    for copy in main_copies(expert):
        copy.start()

    @pl.when(expert == experts_here - 1)
    def _():
        place = pl.ds(experts_here * main_slots, tail_height)
        tails = (
            pltpu.make_async_copy(result_tail, result_ref.at[sources_at, :, place, :], sems.at[2]),
            pltpu.make_async_copy(back_tail, back_ref.at[sources_at, :, place, :], sems.at[3]),
        )
        for copy in tails:
            copy.start()
        for copy in main_copies(expert):
            copy.wait()
        for copy in tails:
            copy.wait()


def parts_of(rows):
    shards, groups = rows.shape[:2]
    return max(1, shards * groups // part_sources)


def row_specs(rows, experts_here, order):
    shards, groups, height, width = rows.shape
    shards_part = shards // parts_of(rows)
    tail_height = slot_rows(experts_here) - experts_here * main_slots
    tail_at = experts_here * main_slots // tail_height
    main_at = lambda e, c: (c, 0, e, 0)
    side_at = lambda e, c: (c, 0, tail_at, 0)
    return [
        pl.BlockSpec((shards_part, groups, main_slots, width), order(main_at)),
        pl.BlockSpec((shards_part, groups, tail_height, width), order(side_at)),
    ]


def expert_act(rows, grads, gate_weight, up_weight, down_weight):
    experts_here, units, width = gate_weight.shape
    shards, groups = rows.shape[:2]
    count = shards * groups * CAP
    parts = parts_of(rows)
    height = slot_rows(experts_here)
    tail_height = height - experts_here * main_slots
    order = lambda index: lambda c, e: index(e, c)
    weight_spec = pl.BlockSpec((1, units, width), lambda c, e: (e, 0, 0))
    act_spec = pl.BlockSpec((1, count // parts, units), lambda c, e: (e, c, 0))
    act_shape = jax.ShapeDtypeStruct((experts_here, count, units), jnp.bfloat16)
    slot_shape = lambda lanes: jax.ShapeDtypeStruct(
        (shards, groups, height, lanes), jnp.bfloat16
    )
    scratch = [
        pltpu.VMEM((shards // parts, groups, rows_of, lanes), jnp.bfloat16)
        for lanes in (width, width + spare)
        for rows_of in (main_slots, tail_height)
    ]
    return pl.pallas_call(
        functools.partial(expert_act_kernel, experts_here),
        grid=(parts, experts_here),
        out_shape=(act_shape, act_shape, act_shape, slot_shape(width), slot_shape(width + spare)),
        in_specs=row_specs(rows, experts_here, order)
        + row_specs(grads, experts_here, order)
        + [weight_spec] * 3,
        out_specs=(
            act_spec,
            act_spec,
            act_spec,
            pl.BlockSpec(memory_space=pl.ANY),
            pl.BlockSpec(memory_space=pl.ANY),
        ),
        scratch_shapes=scratch + [pltpu.SemaphoreType.DMA((4,))],
        compiler_params=pltpu.CompilerParams(vmem_limit_bytes=60 * mega),
        cost_estimate=pl.CostEstimate(
            flops=12 * experts_here * count * width * units,
            transcendentals=experts_here * count * units,
            bytes_accessed=6 * experts_here * width * units + 8 * experts_here * count * width,
        ),
        name="expert_act",
    )(rows, rows, grads, grads, gate_weight, up_weight, down_weight)


class RowChunk:
    def __init__(self, spot, number, place_rows, rows_in, rows_all, back_out, bufs, sems):
        self.spot, self.number, self.place_rows = spot, number, place_rows
        self.rows_in, self.rows_all, self.back_out = rows_in, rows_all, back_out
        self.rows, self.back, self.pair_in, self.across_out, self.across_in, self.total = bufs
        (
            self.local,
            self.send,
            self.recv,
            self.across_send,
            self.across_recv,
            self.core_send,
            self.core_recv,
            self.pair_send,
            self.pair_recv,
            self.sum_send,
            self.sum_recv,
            self.back_send,
            self.back_recv,
        ) = sems

    @staticmethod
    def sems(groups, columns, chunks):
        half = columns // 2
        dma = pltpu.SemaphoreType.DMA
        return (
            [dma((chunks, 4))]
            + [dma((chunks, groups))] * 2
            + [dma((chunks, half, 2))] * 8
            + [dma((chunks, groups))] * 2
        )

    def keys(self, near):
        groups = self.spot.groups
        return [0] + near_keys(groups) if near else far_keys(groups)

    def side(self, near):
        half = self.spot.groups // 2
        here = self.spot.place // half
        return pl.ds((here if near else 1 - here) * half, half)

    def swap(self, key):
        spot, at = self.spot, self.number
        peer = flip(spot.place, key)
        source = self.rows_in.at[peer, self.place_rows]
        target = self.rows.at[spot.lane, spot.place]
        if key == 0:
            return pltpu.make_async_copy(source, target, self.local.at[at, 0])
        return remote(
            source, target, self.send.at[at, key], self.recv.at[at, key], (peer, spot.lane)
        )

    def keep(self, near):
        side = self.side(near)
        return pltpu.make_async_copy(
            self.rows.at[:, side],
            self.rows_all.at[:, side, self.place_rows],
            self.local.at[self.number, 1 + near],
        )

    def across(self, near, step):
        spot, at = self.spot, self.number
        block = self.rows.at[spot.lane, self.side(near)]
        return remote(
            block,
            block,
            self.across_send.at[at, step, near],
            self.across_recv.at[at, step, near],
            (spot.place, spot.across(step)),
        )

    def core(self, near, step):
        spot, at = self.spot, self.number
        block = self.rows.at[spot.behind(step), self.side(near)]
        return remote(
            block,
            block,
            self.core_send.at[at, step, near],
            self.core_recv.at[at, step, near],
            (spot.place, spot.partner),
        )

    def begin(self, near):
        for key in self.keys(near):
            self.swap(key).start()

    def advance(self, near):
        for key in self.keys(near):
            self.swap(key).wait_recv() if key else self.swap(key).wait()
        for step in range(1, self.spot.half):
            self.across(near, step).start()
        self.core(near, 0).start()

    def complete(self, near):
        half = self.spot.half
        for step in range(1, half):
            self.across(near, step).wait_recv()
            self.core(near, step).start()
        for step in range(half):
            self.core(near, step).wait_recv()
        if self.rows_all is not None:
            self.keep(near).start()

    def pair_copy(self, step, near):
        spot, at = self.spot, self.number
        side = self.side(near)
        return remote(
            self.back.at[spot.lane_at(step, True), side],
            self.pair_in.at[step, side],
            self.pair_send.at[at, step, near],
            self.pair_recv.at[at, step, near],
            (spot.place, spot.partner),
        )

    def sum_copy(self, step, near):
        spot, at = self.spot, self.number
        side = self.side(near)
        return remote(
            self.across_out.at[step, side],
            self.across_in.at[step, side],
            self.sum_send.at[at, step, near],
            self.sum_recv.at[at, step, near],
            (spot.place, spot.across(step)),
        )

    def back_copy(self, key):
        spot, at = self.spot, self.number
        peer = flip(spot.place, key)
        target = self.back_out.at[spot.place, self.place_rows]
        if key == 0:
            return pltpu.make_async_copy(self.total.at[peer], target, self.local.at[at, 3])
        return remote(
            self.total.at[peer],
            target,
            self.back_send.at[at, key],
            self.back_recv.at[at, key],
            (peer, spot.lane),
        )

    def pair(self, near):
        for step in list(range(1, self.spot.half)) + [0]:
            self.pair_copy(step, near).start()

    def pair_sum(self, step, near):
        side = self.side(near)
        mine = self.back[self.spot.lane_at(step, False), side].astype(jnp.float32)
        return mine + self.pair_in[step, side].astype(jnp.float32)

    def middle(self, near):
        for step in range(1, self.spot.half):
            self.pair_copy(step, near).wait_recv()
            total = self.pair_sum(step, near)
            self.across_out[step, self.side(near)] = total.astype(self.total.dtype)
            self.sum_copy(step, near).start()
        self.pair_copy(0, near).wait_recv()

    def last(self, near):
        total = self.pair_sum(0, near)
        for step in range(1, self.spot.half):
            self.sum_copy(step, near).wait_recv()
            total = total + self.across_in[step, self.side(near)].astype(jnp.float32)
        self.total[self.side(near)] = total.astype(self.total.dtype)
        for key in self.keys(near):
            self.back_copy(key).start()

    def finish(self):
        groups, half = self.spot.groups, self.spot.half
        for key in range(1, groups):
            self.back_copy(key).wait_recv()
        self.back_copy(0).wait()
        for near in range(2):
            if self.rows_all is not None:
                self.keep(near).wait()
            for step in range(half):
                self.core(near, step).wait_send()
                self.pair_copy(step, near).wait_send()
                if step:
                    self.across(near, step).wait_send()
                    self.sum_copy(step, near).wait_send()
        for key in range(groups):
            if key:
                self.swap(key).wait_send()
                self.back_copy(key).wait_send()


half_chunks = ((1, 0), (1, 1), (0, 0), (0, 1), (0, 2), (0, 3), (1, 2), (1, 3))


def half_expert(step):
    return step - 2 * ((step // 2 + 1) // 2)


def half_far(step):
    return (step // 2 + 1) // 2 % 2


def experts_kernel(
    experts_here,
    groups,
    columns,
    rows_in,
    gates_in,
    grad_main,
    grad_tail,
    gate_weight,
    up_weight,
    down_weight,
    hidden_ref,
    grad_gate_ref,
    grad_up_ref,
    result_ref,
    rows_all,
    back_out,
    gates_out,
    act_sc,
    act_sems,
    result_main,
    result_tail,
    result_sems,
    *scratch,
):
    now = pl.program_id(0)
    expert = half_expert(now)
    tail_height = result_tail.shape[2]
    half_groups = groups // 2
    sources = half_groups * columns
    main_count, count = sources * main_slots, sources * CAP
    spot = Spot(groups, columns)
    here = spot.place // half_groups
    side_at = here + half_far(now) * (1 - 2 * here)
    side = pl.ds(side_at * half_groups, half_groups)
    mains, tails, sides, sems = scratch[:6], scratch[6:12], scratch[12:18], scratch[18:]
    chunks = [
        RowChunk(
            spot,
            at,
            pl.ds(at * main_slots, main_slots),
            rows_in,
            rows_all,
            back_out,
            [buf.at[at] for buf in mains],
            sems,
        )
        for at in range(experts_here)
    ]
    tail = RowChunk(
        spot,
        experts_here,
        pl.ds(experts_here * main_slots, tail_height),
        rows_in,
        rows_all,
        back_out,
        tails,
        sems,
    )
    scalars = RowChunk(
        spot, experts_here + 1, pl.ds(0, 8), gates_in, None, gates_out, sides, sems
    )

    @pl.when(now == 0)
    def _():
        spot.meet()
        scalars.begin(1)
        tail.begin(1)
        chunks[0].begin(1)
        chunks[1].begin(1)
        scalars.begin(0)
        tail.begin(0)
        chunks[0].begin(0)
        sides[1][...] = jnp.zeros_like(sides[1])

    select = tail_select(expert, sources, tail_height)

    def joined(main, low):
        width = main.shape[-1]
        low = nn_dot(select, low.reshape(-1, width)).astype(jnp.bfloat16)
        return jnp.concatenate([main.reshape(-1, width), low], axis=0)

    raw_hidden = nt_dot(joined(grad_main[:, side], grad_tail[:, side]), down_weight[0])

    def before(step):
        if step == 0:
            scalars.advance(1)
            tail.advance(1)
            chunks[0].advance(1)
            chunks[1].begin(0)
            chunks[1].advance(1)
            scalars.complete(1)
            tail.complete(1)
        elif step == 1:
            scalars.advance(0)
            tail.advance(0)
            chunks[0].advance(0)
            chunks[2].begin(0)
        elif step == 2:
            chunks[1].advance(0)
            chunks[3].begin(0)
            scalars.complete(0)
            tail.complete(0)
        elif step == 3:
            chunks[2].advance(0)
            chunks[2].begin(1)
            chunks[3].begin(1)
        elif step == 4:
            chunks[3].advance(0)
        elif step == 5:
            chunks[2].advance(1)
        elif step == 6:
            chunks[3].advance(1)
        near, at = half_chunks[step]
        chunks[at].complete(near)
        if step:
            near, at = half_chunks[step - 1]
            chunks[at].middle(near)
        if step == 6:
            tail.middle(0)
            scalars.middle(0)

    for step in range(len(half_chunks)):

        @pl.when(now == step)
        def _():
            before(step)

    rows = joined(mains[0][expert, :, side], tails[0][:, side])
    hot, of_slot = slot_lanes(expert, experts_here, sources)
    gate_high, gate_rest = split_low(sides[0][:, side, 0, :].reshape(sources, spare))
    gates = nn_dot(hot, gate_high) + nn_dot(hot, gate_rest)
    gates = jnp.sum(jnp.where(of_slot, gates, 0.0), axis=1, keepdims=True)
    hidden, grad_gate, grad_up, back, grad_gates, result = expert_math(
        rows, gates, raw_hidden, gate_weight[0], up_weight[0], down_weight[0]
    )

    def spread(value, main_target, tail_target):
        low = value.astype(jnp.bfloat16)
        main_target(low[:main_count].reshape(columns, half_groups, main_slots, -1))
        part = tn_dot(select, low[main_count:]).astype(jnp.bfloat16)
        part = part.reshape(columns, half_groups, tail_height, -1)

        @pl.when(expert == 0)
        def _():
            tail_target[:, side] = part

        @pl.when(expert > 0)
        def _():
            tail_target[:, side] += part

    def store_back(value):
        mains[1][expert, :, side] = value

    spread(back, store_back, tails[1])
    side_high, side_rest = split_low(jnp.where(of_slot, grad_gates, 0.0))
    lanes = (tn_dot(hot, side_high) + tn_dot(hot, side_rest)).reshape(columns, half_groups, spare)
    sides[1][:, side, 0, :] += lanes

    def after(step):
        near, at = half_chunks[step]
        chunks[at].pair(near)
        if step == 5:
            tail.pair(0)
            scalars.pair(0)
        if step == 7:
            tail.pair(1)
            scalars.pair(1)
            chunks[at].middle(1)
            tail.middle(1)
            scalars.middle(1)
        if step:
            near, at = half_chunks[step - 1]
            chunks[at].last(near)
        if step == 6:
            tail.last(0)
            scalars.last(0)

    for step in range(len(half_chunks)):

        @pl.when(now == step)
        def _():
            after(step)

    act_rows = pl.ds(pl.multiple_of(side_at * count, 32), count)

    def act_copies():
        outs = (hidden_ref, grad_gate_ref, grad_up_ref)
        return [
            pltpu.make_async_copy(act_sc.at[k], out.at[expert, act_rows], act_sems.at[k])
            for k, out in enumerate(outs)
        ]

    def result_copy():
        place = pl.ds(pl.multiple_of(expert * main_slots, main_slots), main_slots)
        return pltpu.make_async_copy(
            result_main, result_ref.at[:, side, place], result_sems.at[0]
        )

    @pl.when(now > 0)
    def _():
        result_copy().wait()
        for copy in act_copies():
            copy.wait()

    def store_result(value):
        result_main[...] = value

    spread(result, store_result, result_tail)
    act_sc[0] = hidden
    act_sc[1] = grad_gate
    act_sc[2] = grad_up
    result_copy().start()
    for copy in act_copies():
        copy.start()

    @pl.when(now == len(half_chunks) - 1)
    def _():
        place = pl.ds(experts_here * main_slots, tail_height)
        low = pltpu.make_async_copy(result_tail, result_ref.at[:, :, place], result_sems.at[1])
        low.start()
        chunks[-1].last(1)
        tail.last(1)
        scalars.last(1)
        for chunk in chunks + [tail, scalars]:
            chunk.finish()
        result_copy().wait()
        for copy in act_copies():
            copy.wait()
        low.wait()


def experts(rows, gates, grads, gate_weight, up_weight, down_weight, columns):
    experts_here, units, width = gate_weight.shape
    groups, height, wide = rows.shape
    half = columns // 2
    count = columns * groups * CAP
    tail_height = height - experts_here * main_slots
    weight_spec = pl.BlockSpec((1, units, width), lambda t: (half_expert(t), 0, 0))
    act_shape = jax.ShapeDtypeStruct((experts_here, count, units), jnp.bfloat16)
    low = lambda *shape: pltpu.VMEM(shape, jnp.bfloat16)
    bufs = lambda lead, *block, kind=jnp.bfloat16: [
        pltpu.VMEM((*lead, *first, groups, *block), kind)
        for first in ((columns,), (columns,), (half,), (half,), (half,), ())
    ]
    return pl.pallas_call(
        functools.partial(experts_kernel, experts_here, groups, columns),
        grid=(len(half_chunks),),
        out_shape=(
            act_shape,
            act_shape,
            act_shape,
            jax.ShapeDtypeStruct((columns, groups, height, width), jnp.bfloat16),
            jax.ShapeDtypeStruct((columns,) + rows.shape, jnp.bfloat16),
            jax.ShapeDtypeStruct(rows.shape, jnp.bfloat16),
            jax.ShapeDtypeStruct(gates.shape, jnp.float32),
        ),
        in_specs=[anywhere, anywhere]
        + row_specs(grads, experts_here, lambda index: lambda t: index(half_expert(t), 0))
        + [weight_spec] * 3,
        out_specs=(anywhere,) * 7,
        scratch_shapes=[
            low(3, count // 2, units),
            pltpu.SemaphoreType.DMA((3,)),
            low(columns, groups // 2, main_slots, width),
            low(columns, groups, tail_height, width),
            pltpu.SemaphoreType.DMA((2,)),
        ]
        + bufs((experts_here,), main_slots, wide)
        + bufs((), tail_height, wide)
        + bufs((), 8, spare, kind=jnp.float32)
        + RowChunk.sems(groups, columns, experts_here + 2),
        compiler_params=comm_params(10),
        cost_estimate=pl.CostEstimate(
            flops=12 * experts_here * count * width * units,
            transcendentals=experts_here * count * units,
            bytes_accessed=6 * experts_here * width * units + 8 * experts_here * count * width,
        ),
        name="experts",
    )(rows, gates, grads, grads, gate_weight, up_weight, down_weight)


def expert_weight_kernel(
    parts,
    halves,
    row_main,
    row_tail,
    grad_main,
    grad_tail,
    hidden_ref,
    grad_gate_ref,
    grad_up_ref,
    gate_out,
    up_out,
    down_out,
):
    expert, part = pl.program_id(0), pl.program_id(1)
    sources = row_main.shape[0] * row_main.shape[1]
    select = tail_select(expert, sources, row_tail.shape[2])
    if halves == 1:
        rows = expert_input(row_main, row_tail, select)[:, :D]
        grads = expert_input(grad_main, grad_tail, select)
    else:
        groups = row_main.shape[1] // halves
        select = tail_select(expert, sources // halves, row_tail.shape[2])
        sides = [slice(at * groups, (at + 1) * groups) for at in range(halves)]
        both = lambda main, low: jnp.concatenate(
            [expert_input(main[:, side], low[:, side], select) for side in sides], axis=0
        )
        rows, grads = both(row_main, row_tail), both(grad_main, grad_tail)

    @pl.when(part == 0)
    def _():
        gate_out[0] = tn_dot(grad_gate_ref[0], rows)
        up_out[0] = tn_dot(grad_up_ref[0], rows)
        down_out[0] = tn_dot(hidden_ref[0], grads)

    if parts > 1:

        @pl.when(part > 0)
        def _():
            gate_out[0] += tn_dot(grad_gate_ref[0], rows)
            up_out[0] += tn_dot(grad_up_ref[0], rows)
            down_out[0] += tn_dot(hidden_ref[0], grads)


def expert_weight_grads(rows, grads, hidden, grad_gate, grad_up, halves):
    experts_here, count, units = hidden.shape
    width = grads.shape[-1]
    parts = parts_of(rows)
    order = lambda index: index
    act_spec = pl.BlockSpec((1, count // parts, units), lambda e, c: (e, c, 0))
    out_spec = pl.BlockSpec((1, units, width), lambda e, c: (e, 0, 0))
    out_shape = jax.ShapeDtypeStruct((experts_here, units, width), jnp.float32)
    return pl.pallas_call(
        functools.partial(expert_weight_kernel, parts, halves),
        grid=(experts_here, parts),
        out_shape=(out_shape, out_shape, out_shape),
        in_specs=row_specs(rows, experts_here, order)
        + row_specs(grads, experts_here, order)
        + [act_spec] * 3,
        out_specs=(out_spec, out_spec, out_spec),
        compiler_params=pltpu.CompilerParams(vmem_limit_bytes=60 * mega),
        cost_estimate=pl.CostEstimate(
            flops=6 * experts_here * count * width * units,
            transcendentals=0,
            bytes_accessed=12 * experts_here * width * units + 10 * experts_here * count * width,
        ),
        name="expert_weight_grads",
    )(rows, rows, grads, grads, hidden, grad_gate, grad_up)


def pair_slots(token_routes, ranks, experts_here):
    row_count = token_routes.shape[0]
    expert_pair = jnp.concatenate([token_routes[:, 0], token_routes[:, 1]])
    rank_pair = jnp.concatenate([ranks, ranks + row_count])
    earlier = (expert_pair[None, :] == expert_pair[:, None]) & (
        rank_pair[None, :] < rank_pair[:, None]
    )
    slot_index = jnp.sum(earlier.astype(jnp.int32), axis=1)
    height = slot_rows(experts_here)
    local = expert_pair % experts_here
    main_at = local * main_slots + slot_index
    tail_at = experts_here * main_slots + local * tail_slots + slot_index - main_slots
    row = jnp.where(slot_index < main_slots, main_at, tail_at)
    slots = (expert_pair // experts_here) * height + row
    return jnp.where(slot_index < CAP, slots, -1)


def router_head(logits, token_routes, weights):
    token_count = logits.shape[0]
    probabilities = jax.nn.softmax(logits, axis=-1)
    log_totals = jax.nn.logsumexp(logits, axis=-1)
    picked = (token_routes[:, :, None] == jnp.arange(EXPERTS, dtype=jnp.int32)).astype(jnp.float32)
    chosen = jnp.sum(picked * probabilities[:, None, :], axis=-1)
    gate_values = chosen / jnp.sum(chosen, axis=1, keepdims=True)
    shares = jnp.sum(picked, axis=(0, 1)) / (token_count * TOP)
    balance = EXPERTS * jnp.sum(shares * jnp.sum(probabilities, axis=0))
    return (gate_values, weights[0] * jnp.sum(log_totals * log_totals) + weights[1] * balance)


def column(values, rows):
    return jnp.pad(values, (0, rows - values.shape[0]))[:, None]


def shards(
    inputs,
    grad_out,
    prefix,
    routes,
    priority,
    loss_weights,
    norm_attn,
    norm_moe,
    qkv_weight,
    out_weight,
    bias_table,
    router_weight,
    gate_weight,
    up_weight,
    down_weight,
):
    row_count = inputs.shape[0]
    groups = lax.axis_size("expert")
    columns_of = lax.axis_size("shard")
    place = lax.axis_index("expert")
    length = row_count * groups
    heads_here = HEADS // groups
    width = heads_here * HEAD
    experts_here = EXPERTS // groups
    shard_rows = D // columns_of
    height = slot_rows(experts_here)

    packed_small = jnp.concatenate(
        [
            lax.dynamic_slice(
                qkv_weight, (0, third * D + place * width), (shard_rows, width)
            )
            for third in range(3)
        ]
        + [jnp.pad(router_weight, ((0, 0), (0, spare - EXPERTS)))],
        axis=1,
    )
    table_rows = BUCKETS // columns_of
    table_low = bias_table.astype(jnp.float32).reshape(1, table_rows * HEADS)
    gain_rows = jnp.concatenate(
        [
            norm_attn.astype(jnp.float32)[None],
            norm_moe.astype(jnp.float32)[None],
            jnp.pad(table_low, ((0, 0), (0, shard_rows - table_rows * HEADS))),
            jnp.zeros((5, shard_rows), jnp.float32),
        ],
        axis=0,
    )
    token_routes = routes.reshape(row_count, TOP)
    slots = pair_slots(token_routes, priority.reshape(row_count), experts_here)
    slot_map = (
        jnp.arange(groups * height, dtype=jnp.int32)[:, None] == slots[None, :]
    ).reshape(groups * height, TOP, row_count)
    slot_any = jnp.any(slot_map, axis=1).astype(jnp.bfloat16)
    slot_pairs = slot_map.astype(jnp.bfloat16).reshape(groups * height, TOP * row_count)
    grad_low = grad_out.reshape(row_count, D)
    grad_slots = nn_dot(slot_any, grad_low).astype(jnp.bfloat16).reshape(groups, height, D)
    _, normed_all, qkv_own, small_full, out_full, far_slots, side_slots, gains = entry_gather(
        inputs.reshape(row_count, D),
        gain_rows,
        packed_small,
        out_weight,
        grad_slots,
        3 * width,
        1,
    )
    normed_all = normed_all.reshape(length, D)
    qkv_own = qkv_own.reshape(length, 3 * width)
    small_full = small_full.reshape(D, 3 * width + spare)
    out_full = out_full.reshape(D, D)
    router_full = small_full[:, 3 * width : 3 * width + EXPERTS]
    gain_attn = gains[:, 0].reshape(D)
    gain_moe = gains[:, 1].reshape(D)
    table_full = gains[:, 2, : table_rows * HEADS].reshape(BUCKETS, HEADS)
    table_own = lax.dynamic_slice_in_dim(
        table_full, place * heads_here, heads_here, 1
    )
    near_ids = jnp.asarray(skew_buckets(), jnp.int32)
    near_hot = (near_ids[:, None] == jnp.arange(BUCKETS, dtype=jnp.int32)).astype(jnp.float32)
    base_bias = (
        jnp.dot(near_hot, table_own, precision=lax.Precision.HIGHEST).reshape(3, 2 * tile, heads_here)
        * log2e
    )
    base_bias = jnp.transpose(base_bias, (2, 0, 1)).reshape(heads_here * 3, 2 * tile)
    far_bias = jnp.stack([table_own[15], table_own[31]], axis=1) * log2e

    mixed_own, totals, grads_received = attend_forward(
        prefix, far_bias, base_bias, qkv_own, grad_slots, far_slots, side_slots, columns_of
    )
    attended = exchange_mixed(mixed_own.reshape(groups, row_count, width), columns_of, 8)

    tokens_in = inputs.reshape(row_count, D).astype(jnp.float32)
    middle = tokens_in + nn_dot(attended, out_full)
    normed_two, norm_two_back = jax.vjp(rms_norm, middle, gain_moe)
    low_two = normed_two.astype(jnp.bfloat16)
    logits = nn_dot(low_two, router_full)
    router_out, router_back = jax.vjp(
        lambda logit_in: router_head(logit_in, token_routes, loss_weights), logits
    )
    gate_values = router_out[0]
    slot_gates = jnp.sum(
        slot_map.astype(jnp.float32) * jnp.transpose(gate_values)[None], axis=1
    )
    fused = columns_of * groups <= part_sources and experts_here == 4
    if fused:
        outgoing = nn_dot(slot_any, low_two).astype(jnp.bfloat16).reshape(groups, height, D)
        gate_block = jnp.pad(
            jnp.sum(slot_gates, axis=1).reshape(groups, 1, height),
            ((0, 0), (0, 7), (0, spare - height)),
        )
    else:
        gate_high = lax.reduce_precision(gate_values, 8, 7)
        gate_parts = jnp.stack([gate_high, gate_values - gate_high], axis=-1).astype(jnp.bfloat16)
        wide_rows = jnp.concatenate(
            [
                jnp.broadcast_to(low_two[None], (TOP, row_count, D)),
                jnp.pad(jnp.transpose(gate_parts, (1, 0, 2)), ((0, 0), (0, 0), (0, spare - 2))),
            ],
            axis=2,
        ).reshape(TOP * row_count, D + spare)
        outgoing = nn_dot(slot_pairs, wide_rows).astype(jnp.bfloat16)
        outgoing = outgoing.reshape(groups, height, D + spare)
    gate_across, up_across, down_across = (
        jnp.transpose(weight, (0, 2, 1)) for weight in (gate_weight, up_weight, down_weight)
    )
    if fused:
        (
            hidden,
            grad_gate,
            grad_up,
            result_part,
            rows_received,
            grad_returned,
            side_returned,
        ) = experts(
            outgoing, gate_block, grads_received, gate_across, up_across, down_across, columns_of
        )
        slot_grads = side_returned[:, 0, :height].reshape(groups * height)
        grad_gates = jnp.sum(
            jnp.where(slot_map, slot_grads[:, None, None], 0.0), axis=0
        )
        grad_gates = jnp.transpose(grad_gates)
        grad_returned = grad_returned.reshape(groups * height, D)
    else:
        rows_received = dispatch(outgoing, columns_of, 2)
        hidden, grad_gate, grad_up, result_part, back_part = expert_act(
            rows_received, grads_received, gate_across, up_across, down_across
        )
        grad_returned = collect(back_part, 3).reshape(groups * height, D + spare)
        grad_gates = jnp.transpose(
            tn_dot(slot_pairs, grad_returned[:, D:])[:, 0].reshape(TOP, row_count)
        )
    grad_low_two = tn_dot(slot_any, grad_returned[:, :D])
    grad_top = grad_low.astype(jnp.float32)
    grad_logits = router_back((grad_gates, jnp.ones((), jnp.float32)))[0]
    low_logits = grad_logits.astype(jnp.bfloat16)
    router_grad = tn_dot(low_two, low_logits)
    grad_low_two = grad_low_two + nt_dot(low_logits, router_full)
    grad_middle_norm, gain_moe_grad = norm_two_back(grad_low_two)
    grad_middle = grad_top + grad_middle_norm
    low_middle = grad_middle.astype(jnp.bfloat16)
    out_grad = tn_dot(attended, low_middle)
    grad_attended = nt_dot(low_middle, out_full).astype(jnp.bfloat16)
    grad_attended = jnp.transpose(grad_attended.reshape(row_count, groups, width), (1, 0, 2))
    grad_mixed = lax.all_to_all(
        grad_attended, "expert", split_axis=0, concat_axis=0, tiled=True
    )
    gate_grad, up_grad, down_grad = expert_weight_grads(
        rows_received, grads_received, hidden, grad_gate, grad_up, 2 if fused else 1
    )
    out_sums = lax.psum_scatter(
        out_grad.astype(jnp.bfloat16), "shard", scatter_dimension=0, tiled=True
    ).reshape(groups, shard_rows // groups, D)
    grad_qkv, near_sums, side_sums, returned, out_piece = attend_backward(
        prefix,
        far_bias,
        base_bias,
        qkv_own,
        mixed_own,
        grad_mixed.reshape(length, width),
        totals,
        result_part,
        out_sums,
        columns_of,
    )
    slot_high = lax.reduce_precision(slot_gates, 8, 7)
    slot_parts = jnp.concatenate([slot_high, slot_gates - slot_high], axis=1).astype(jnp.bfloat16)
    mixture = tn_dot(slot_parts, returned.reshape(groups * height, D))
    mixture = mixture[:row_count] + mixture[row_count:]
    output = (middle + mixture).astype(jnp.bfloat16)

    table_grad = jnp.einsum(
        "hil,ilb->bh",
        near_sums.reshape(heads_here, 3, 2 * tile),
        near_hot.reshape(3, 2 * tile, BUCKETS),
        precision=lax.Precision.HIGHEST,
    )
    far_sums = jnp.sum(side_sums, axis=(2, 3))
    bucket_ids = jnp.arange(BUCKETS, dtype=jnp.int32)[:, None]
    table_grad = table_grad + jnp.where(bucket_ids == 15, far_sums[:, 0][None], 0.0)
    table_grad = table_grad + jnp.where(bucket_ids == 31, far_sums[:, 1][None], 0.0)
    table_column = jnp.pad(
        table_grad.reshape(columns_of, table_rows * heads_here),
        ((0, 0), (0, shard_rows - table_rows * heads_here)),
    ).reshape(D, 1)

    extra = jnp.concatenate(
        [
            jnp.zeros((D, 1), jnp.float32),
            table_column,
            gain_moe_grad[:, None],
            router_grad,
            jnp.zeros((D, spare - 3 - EXPERTS), jnp.float32),
        ],
        axis=1,
    ).astype(jnp.bfloat16)
    grad_projected, last_all, out_all, qkv_full = tail_exchange(
        grad_qkv.reshape(groups, row_count, 3 * width),
        normed_all,
        small_full,
        extra,
        out_piece,
        qkv_weight,
        columns_of,
        7,
    )
    last_all = last_all.reshape(groups, shard_rows, 3 * width + spare)
    out_all = out_all.reshape(shard_rows, D)
    if width % 128 == 0:
        input_grad, qkv_total, out_total, extra_total = finish(
            grad_projected,
            qkv_full,
            last_all,
            inputs.reshape(row_count, D),
            gain_attn[None],
            grad_middle,
            out_all,
            width,
        )
    else:
        grad_projected = jnp.transpose(
            grad_projected.reshape(groups, row_count, 3, width), (1, 2, 0, 3)
        ).reshape(row_count, 3 * D)
        grad_low_one = nt_dot(grad_projected, qkv_full.reshape(D, 3 * D))
        _, norm_one_back = jax.vjp(lambda features: rms_norm(features, gain_attn), tokens_in)
        input_grad = grad_middle + norm_one_back(grad_low_one)[0]
        qkv_total = jnp.transpose(
            last_all[:, :, : 3 * width].reshape(groups, shard_rows, 3, width), (1, 2, 0, 3)
        ).reshape(shard_rows, 3 * D).astype(jnp.float32)
        out_total = out_all.astype(jnp.float32)
        extra_total = jnp.sum(last_all[:, :, 3 * width :].astype(jnp.float32), axis=0).T
    table_part = last_all[:, : table_rows * heads_here, 3 * width + 1].astype(jnp.float32)
    table_total = jnp.transpose(
        table_part.reshape(groups, table_rows, heads_here), (1, 0, 2)
    ).reshape(table_rows, HEADS)
    return (
        output.reshape(row_count, 1, D),
        input_grad.reshape(row_count, 1, D),
        extra_total[0] / norm_attn.astype(jnp.float32),
        extra_total[2],
        qkv_total,
        out_total,
        table_total,
        extra_total[3 : 3 + EXPERTS].T,
        jnp.transpose(gate_grad, (0, 2, 1)),
        jnp.transpose(up_grad, (0, 2, 1)),
        jnp.transpose(down_grad, (0, 2, 1)),
    )


def solution(mesh):
    placed = (
        P("expert", "shard", None),
        P("expert", "shard", None),
        P("shard"),
        P("expert", "shard", None),
        P("expert", "shard", None),
        P(),
        P("shard"),
        P("shard"),
        P("shard", None),
        P("shard", None),
        P("shard", None),
        P("shard", None),
        P("expert", None, "shard"),
        P("expert", None, "shard"),
        P("expert", None, "shard"),
    )
    return jax.shard_map(
        shards,
        mesh=mesh,
        in_specs=placed,
        out_specs=(
            P("expert", "shard", None),
            P("expert", "shard", None),
            P("shard"),
            P("shard"),
            P("shard", None),
            P("shard", None),
            P("shard", None),
            P("shard", None),
            P("expert", None, "shard"),
            P("expert", None, "shard"),
            P("expert", None, "shard"),
        ),
        check_vma=False,
    )
```

```python
import functools
import math

import jax
import jax.numpy as jnp
import numpy as np
from jax import lax
from jax.experimental import pallas as pl
from jax.experimental.pallas import tpu as pltpu
from jax.sharding import PartitionSpec as P

D = 1024
HEADS = 16
HEAD = 64
FF = 2816
EXPERTS = 32
TOP = 2
BUCKETS = 32
CAP = 18

epsilon = 1e-06
masked_score = -1e30
far_bounds = (12, 16, 23, 32, 46, 64, 91)
tile = 256
main_slots = 16
tail_slots = CAP - main_slots
log2e = math.log2(math.e)
score_scale = HEAD ** (-0.5)
mega = 1024 * 1024
part_sources = 32
spare = 128


MESH = pl.DeviceIdType.MESH


def flip(index, key):
    out, bit = index, 1
    while bit <= key:
        if key & bit:
            out = out + bit * (1 - 2 * ((index // bit) % 2))
        bit *= 2
    return out


def near_keys(groups):
    return list(range(1, groups // 2))


def far_keys(groups):
    return list(range(groups // 2, groups))


def early_keys(groups):
    return [key for key in far_keys(groups) if key % line_shape(groups)[1] == 0]


class Spot:
    def __init__(self, groups, columns):
        self.groups, self.columns = groups, columns
        self.place = lax.axis_index("expert")
        self.lane = lax.axis_index("shard")
        self.half = columns // 2
        self.chip = self.lane // 2
        self.core = self.lane % 2
        self.partner = self.chip * 2 + 1 - self.core

    def across(self, step):
        return ((self.chip + step) % self.half) * 2 + self.core

    def behind(self, step):
        return ((self.chip + self.half - step) % self.half) * 2 + self.core

    def lane_at(self, step, other):
        chip = (self.chip + step) % self.half
        return chip * 2 + ((1 - self.core) if other else self.core)

    def meet(self):
        barrier = pltpu.get_barrier_semaphore()
        for key in range(1, self.groups):
            peer = (flip(self.place, key), self.lane)
            pl.semaphore_signal(barrier, inc=1, device_id=peer, device_id_type=MESH)
        for step in range(1, self.columns):
            peer = (self.place, (self.lane + step) % self.columns)
            pl.semaphore_signal(barrier, inc=1, device_id=peer, device_id_type=MESH)
        pl.semaphore_wait(barrier, self.groups + self.columns - 2)


def remote(source, target, send_sem, recv_sem, peer):
    return pltpu.make_async_remote_copy(
        src_ref=source,
        dst_ref=target,
        send_sem=send_sem,
        recv_sem=recv_sem,
        device_id=peer,
        device_id_type=MESH,
    )


def line_shape(groups):
    across = groups // 4
    return 4, across


class LineGather:
    def __init__(self, spot, own, full, local_sem, send_sems, recv_sems, rows=None):
        self.spot, self.own, self.full, self.rows = spot, own, full, rows
        self.local_sem, self.send_sems, self.recv_sems = local_sem, send_sems, recv_sems
        self.long, self.wide = line_shape(spot.groups)
        self.z = spot.place // self.wide
        self.y = spot.place % self.wide

    @staticmethod
    def sems(groups):
        long, wide = line_shape(groups)
        return [
            pltpu.SemaphoreType.DMA(()),
            pltpu.SemaphoreType.DMA((2 * long - 1, wide + 1)),
            pltpu.SemaphoreType.DMA((groups,)),
        ]

    def block(self, origin):
        return self.full.at[origin] if self.rows is None else self.full.at[origin, self.rows]

    def copy(self, job, way, origin, source, target):
        return remote(
            source,
            self.block(origin),
            self.send_sems.at[job, way],
            self.recv_sems.at[origin],
            (target, self.spot.lane),
        )

    def each(self, job, origin, source, up, down, act):
        place, wide = self.spot.place, self.wide
        if up:

            @pl.when(self.z + 1 < self.long)
            def _():
                act(self.copy(job, 0, origin, source, place + wide))

        if down:

            @pl.when(self.z >= 1)
            def _():
                act(self.copy(job, 1, origin, source, place - wide))

        for step in range(1, wide):
            target = self.z * wide + (self.y + step) % wide
            act(self.copy(job, 1 + step, origin, source, target))

    def begin(self):
        place = self.spot.place
        self.each(0, place, self.own, True, True, lambda copy: copy.start())
        pltpu.make_async_copy(self.own, self.block(place), self.local_sem).start()

    def arrive(self, origin):
        self.copy(0, 0, origin, self.own, self.spot.place).wait_recv()

    def hop(self, k):
        place, wide = self.spot.place, self.wide

        @pl.when(self.z >= k)
        def _():
            origin = place - k * wide
            self.arrive(origin)
            self.each(k, origin, self.block(origin), True, False, lambda copy: copy.start())

        @pl.when(self.z + k < self.long)
        def _():
            origin = place + k * wide
            self.arrive(origin)
            job = self.long - 1 + k
            self.each(job, origin, self.block(origin), False, True, lambda copy: copy.start())

    def finish(self):
        for row in range(self.long):
            for step in range(1, self.wide):
                self.arrive(row * self.wide + (self.y + step) % self.wide)
        self.settle()

    def settle(self):
        place, wide = self.spot.place, self.wide
        stop = lambda copy: copy.wait_send()
        self.each(0, place, self.own, True, True, stop)
        for k in range(1, self.long):

            @pl.when(self.z >= k)
            def _():
                origin = place - k * wide
                self.each(k, origin, self.block(origin), True, False, stop)

            @pl.when(self.z + k < self.long)
            def _():
                origin = place + k * wide
                job = self.long - 1 + k
                self.each(job, origin, self.block(origin), False, True, stop)

        pltpu.make_async_copy(self.own, self.block(place), self.local_sem).wait()


class ColumnGather:
    def __init__(self, spot, own, full, local_sem, across_send, across_recv, core_send, core_recv):
        self.spot, self.own, self.full = spot, own, full
        self.local_sem = local_sem
        self.across_send, self.across_recv = across_send, across_recv
        self.core_send, self.core_recv = core_send, core_recv

    @staticmethod
    def sems(columns):
        return [pltpu.SemaphoreType.DMA(())] + [pltpu.SemaphoreType.DMA((columns // 2,))] * 4

    def across_copy(self, step):
        spot = self.spot
        return remote(
            self.own,
            self.full.at[spot.lane],
            self.across_send.at[step],
            self.across_recv.at[step],
            (spot.place, spot.across(step)),
        )

    def core_copy(self, step):
        spot = self.spot
        source = self.own if step == 0 else self.full.at[spot.behind(step)]
        target = spot.lane if step == 0 else spot.behind(step)
        return remote(
            source,
            self.full.at[target],
            self.core_send.at[step],
            self.core_recv.at[step],
            (spot.place, spot.partner),
        )

    def begin(self):
        for step in range(1, self.spot.half):
            self.across_copy(step).start()
        self.core_copy(0).start()
        pltpu.make_async_copy(self.own, self.full.at[self.spot.lane], self.local_sem).start()

    def forward(self):
        for step in range(1, self.spot.half):
            self.across_copy(step).wait_recv()
            self.core_copy(step).start()

    def finish(self):
        for step in range(self.spot.half):
            self.core_copy(step).wait_recv()
        for step in range(self.spot.half):
            self.core_copy(step).wait_send()
        for step in range(1, self.spot.half):
            self.across_copy(step).wait_send()
        pltpu.make_async_copy(self.own, self.full.at[self.spot.lane], self.local_sem).wait()


def comm_params(which, limit=60):
    return pltpu.CompilerParams(
        collective_id=which, has_side_effects=True, vmem_limit_bytes=limit * mega
    )


anywhere = pl.BlockSpec(memory_space=pl.ANY)


def entry_kernel(
    groups,
    columns,
    tokens,
    gain,
    pack,
    out_weight,
    rows,
    tokens_all,
    normed_all,
    qkv_all,
    pack_all,
    out_all,
    far_rows,
    side_rows,
    gain_all,
    token_sc,
    normed_sc,
    qkv_sc,
    gain_sc,
    pack_sc,
    token_sem,
    normed_sems,
    qkv_sems,
    pack_sem,
    gain_sem,
    *sems,
):
    spot = Spot(groups, columns)
    half_rows = tokens.shape[0] // 2
    lines = [
        LineGather(spot, tokens.at[rows_at], tokens_all, *line_sems, rows=rows_at)
        for rows_at, line_sems in (
            (pl.ds(0, half_rows), sems[:3]),
            (pl.ds(half_rows, half_rows), sems[3:6]),
        )
    ]
    line, sems = lines[0], sems[3:]
    gains = ColumnGather(spot, gain, gain_sc, *sems[3:8])
    packs = ColumnGather(spot, pack, pack_sc, *sems[8:13])
    outs = ColumnGather(spot, out_weight, out_all, *sems[13:18])
    far_send, far_recv, side_send, side_recv = sems[18:]
    wide = qkv_sc.shape[2]

    def far_copy(key):
        peer = flip(spot.place, key)
        return remote(
            rows.at[peer],
            far_rows.at[spot.place],
            far_send.at[key],
            far_recv.at[key],
            (peer, spot.lane),
        )

    def side_copy(key, step):
        at = flip(spot.place, key)
        return remote(
            far_rows.at[at] if key else rows.at[at],
            side_rows.at[step - 1, at],
            side_send.at[key, step],
            side_recv.at[key, step],
            (spot.place, spot.across(step)),
        )

    def stores(origin):
        return (
            pltpu.make_async_copy(
                normed_sc.at[origin], normed_all.at[origin], normed_sems.at[origin]
            ),
            pltpu.make_async_copy(qkv_sc.at[origin], qkv_all.at[origin], qkv_sems.at[origin]),
        )

    def project(origin, source):
        load = pltpu.make_async_copy(source, token_sc, token_sem)
        load.start()
        load.wait()
        features = token_sc[...].astype(jnp.float32)
        factor = lax.rsqrt(jnp.mean(features * features, axis=-1, keepdims=True) + epsilon)
        gain_row = jnp.concatenate([gain_sc[at, 0:1, :] for at in range(columns)], axis=1)
        normed = (features * factor * gain_row).astype(jnp.bfloat16)
        normed_sc[origin] = normed
        weight = pack_sc[...].reshape(D, -1)[:, :wide]
        qkv_sc[origin] = nn_dot(normed, weight).astype(jnp.bfloat16)
        for store in stores(origin):
            store.start()

    spot.meet()
    for line in lines:
        line.begin()
    gains.begin()
    packs.begin()
    outs.begin()
    gains.forward()
    packs.forward()
    gains.finish()
    packs.finish()
    keep = pltpu.make_async_copy(pack_sc, pack_all, pack_sem)
    keep.start()
    keep_gain = pltpu.make_async_copy(gain_sc, gain_all, gain_sem)
    keep_gain.start()
    project(spot.place, tokens)
    for line in lines:
        line.hop(1)
    outs.forward()
    for step in range(1, spot.half):
        side_copy(0, step).start()
    for line in lines:
        line.hop(2)
    for key in early_keys(groups):
        far_copy(key).start()
    for line in lines:
        line.hop(3)

    def own_column(row, carry):
        @pl.when(row != line.z)
        def _():
            origin = row * line.wide + line.y
            project(origin, tokens_all.at[origin])

        return carry

    lax.fori_loop(0, line.long, own_column, 0)

    for key in early_keys(groups):
        far_copy(key).wait_recv()
        for step in range(1, spot.half):
            side_copy(key, step).start()

    def other_column(at, carry):
        row = line.z + ((at + 1) // 2) * (1 - 2 * (at % 2))

        @pl.when((row >= 0) & (row < line.long))
        def _():
            for step in range(1, line.wide):
                origin = row * line.wide + (line.y + step) % line.wide
                for part in lines:
                    part.arrive(origin)
                project(origin, tokens_all.at[origin])

        return carry

    lax.fori_loop(0, 2 * line.long - 1, other_column, 0)
    for line in lines:
        line.settle()
    for key in early_keys(groups):
        far_copy(key).wait_send()
    for key in [0] + early_keys(groups):
        for step in range(1, spot.half):
            side_copy(key, step).wait_recv()
            side_copy(key, step).wait_send()
    outs.finish()
    keep.wait()
    keep_gain.wait()
    for origin in range(groups):
        for store in stores(origin):
            store.wait()


def entry_gather(tokens, gain, pack, out_weight, rows, wide, which):
    groups = rows.shape[0]
    columns = D // out_weight.shape[0]
    count = tokens.shape[0]
    low = lambda *shape: jax.ShapeDtypeStruct(shape, jnp.bfloat16)
    dma = pltpu.SemaphoreType.DMA
    return pl.pallas_call(
        functools.partial(entry_kernel, groups, columns),
        out_shape=(
            low(groups, *tokens.shape),
            low(groups, *tokens.shape),
            low(groups, count, wide),
            low(columns, *pack.shape),
            low(columns, *out_weight.shape),
            low(*rows.shape),
            low(columns // 2 - 1, *rows.shape),
            jax.ShapeDtypeStruct((columns,) + gain.shape, jnp.float32),
        ),
        in_specs=[anywhere] * 5,
        out_specs=(anywhere,) * 8,
        scratch_shapes=[
            pltpu.VMEM(tokens.shape, jnp.bfloat16),
            pltpu.VMEM((groups,) + tokens.shape, jnp.bfloat16),
            pltpu.VMEM((groups, count, wide), jnp.bfloat16),
            pltpu.VMEM((columns,) + gain.shape, jnp.float32),
            pltpu.VMEM((columns,) + pack.shape, jnp.bfloat16),
            dma(()),
            dma((groups,)),
            dma((groups,)),
            dma(()),
            dma(()),
        ]
        + LineGather.sems(groups) * 2
        + ColumnGather.sems(columns) * 3
        + [dma((groups,))] * 2
        + [dma((groups, columns // 2))] * 2,
        compiler_params=comm_params(which),
        name="entry_gather",
    )(tokens, gain, pack, out_weight, rows)


class Dispatch:
    def __init__(self, spot, rows, full, sems):
        self.spot, self.rows, self.full = spot, rows, full
        self.local, self.send, self.recv = sems[:3]
        self.across_send, self.across_recv, self.core_send, self.core_recv = sems[3:]

    @staticmethod
    def sems(groups, columns):
        return (
            [pltpu.SemaphoreType.DMA(())]
            + [pltpu.SemaphoreType.DMA((groups,))] * 2
            + [pltpu.SemaphoreType.DMA((groups, columns // 2))] * 4
        )

    def own(self):
        spot = self.spot
        return pltpu.make_async_copy(
            self.rows.at[spot.place], self.full.at[spot.lane, spot.place], self.local
        )

    def swap(self, key):
        spot = self.spot
        peer = flip(spot.place, key)
        return remote(
            self.rows.at[peer],
            self.full.at[spot.lane, spot.place],
            self.send.at[key],
            self.recv.at[key],
            (peer, spot.lane),
        )

    def across(self, key, step):
        spot = self.spot
        block = self.full.at[spot.lane, flip(spot.place, key)]
        return remote(
            block,
            block,
            self.across_send.at[key, step],
            self.across_recv.at[key, step],
            (spot.place, spot.across(step)),
        )

    def core(self, key, step):
        spot = self.spot
        block = self.full.at[spot.behind(step), flip(spot.place, key)]
        return remote(
            block,
            block,
            self.core_send.at[key, step],
            self.core_recv.at[key, step],
            (spot.place, spot.partner),
        )

    def begin(self):
        groups = self.spot.groups
        self.own().start()
        for key in far_keys(groups) + near_keys(groups):
            self.swap(key).start()

    def advance(self, key):
        if key == 0:
            self.own().wait()
        else:
            self.swap(key).wait_recv()
        for step in range(1, self.spot.half):
            self.across(key, step).start()
        self.core(key, 0).start()

    def pass_on(self, key):
        for step in range(1, self.spot.half):
            self.across(key, step).wait_recv()
            self.core(key, step).start()

    def finish(self):
        groups, half = self.spot.groups, self.spot.half
        for key in range(groups):
            for step in range(half):
                self.core(key, step).wait_recv()
        for key in range(groups):
            if key > 0:
                self.swap(key).wait_send()
            for step in range(1, half):
                self.across(key, step).wait_send()
            for step in range(half):
                self.core(key, step).wait_send()


def dispatch_kernel(groups, columns, rows, full, *sems):
    spot = Spot(groups, columns)
    job = Dispatch(spot, rows, full, sems)
    spot.meet()
    job.begin()
    for key in range(groups):
        job.advance(key)
        if key:
            job.pass_on(key - 1)
    job.pass_on(groups - 1)
    job.finish()


def dispatch(rows, columns, which):
    groups = rows.shape[0]
    return pl.pallas_call(
        functools.partial(dispatch_kernel, groups, columns),
        out_shape=jax.ShapeDtypeStruct((columns,) + rows.shape, rows.dtype),
        in_specs=[anywhere],
        out_specs=anywhere,
        scratch_shapes=Dispatch.sems(groups, columns),
        compiler_params=comm_params(which),
        name="dispatch_rows",
    )(rows)


class Exchange:
    def __init__(self, spot, blocks, thirds, local, send, recv):
        self.spot, self.blocks, self.thirds = spot, blocks, range(thirds)
        self.local, self.send, self.recv = local, send, recv

    @staticmethod
    def sems(groups, thirds):
        return [pltpu.SemaphoreType.DMA((thirds,))] + [
            pltpu.SemaphoreType.DMA((groups, thirds))
        ] * 2

    def copy(self, key, third):
        spot = self.spot
        peer = flip(spot.place, key)
        source, target = self.blocks(peer, third)
        if key == 0:
            return pltpu.make_async_copy(source, target, self.local.at[third])
        return remote(
            source,
            target,
            self.send.at[key, third],
            self.recv.at[key, third],
            (peer, spot.lane),
        )

    def start(self, key):
        for third in self.thirds:
            self.copy(key, third).start()

    def begin(self):
        groups = self.spot.groups
        for key in far_keys(groups) + near_keys(groups) + [0]:
            self.start(key)

    def arrive(self):
        for key in range(self.spot.groups):
            for third in self.thirds:
                copy = self.copy(key, third)
                copy.wait() if key == 0 else copy.wait_recv()

    def finish(self):
        for key in range(1, self.spot.groups):
            for third in self.thirds:
                self.copy(key, third).wait_send()


class ColumnSum:
    def __init__(self, spot, chunks, order, part, bufs, sems):
        self.spot, self.chunks, self.order, self.part = spot, chunks, order, part
        self.pair_in, self.mine, self.across_out, self.across_in = bufs
        self.local, self.pair_send, self.pair_recv, self.across_send, self.across_recv = sems

    @staticmethod
    def scratch(columns, chunks, block):
        half = columns // 2
        return [pltpu.VMEM((half, chunks) + block, jnp.bfloat16)] * 4 + [
            pltpu.SemaphoreType.DMA((half, chunks))
        ] * 5

    def pair_copy(self, step, k):
        spot = self.spot
        return remote(
            self.part.at[spot.lane_at(step, True), self.order(k)],
            self.pair_in.at[step, k],
            self.pair_send.at[step, k],
            self.pair_recv.at[step, k],
            (spot.place, spot.partner),
        )

    def mine_copy(self, step, k):
        return pltpu.make_async_copy(
            self.part.at[self.spot.lane_at(step, False), self.order(k)],
            self.mine.at[step, k],
            self.local.at[step, k],
        )

    def across_copy(self, step, k):
        spot = self.spot
        return remote(
            self.across_out.at[step, k],
            self.across_in.at[step, k],
            self.across_send.at[step, k],
            self.across_recv.at[step, k],
            (spot.place, spot.across(step)),
        )

    def begin(self):
        half = self.spot.half
        for k in range(self.chunks):
            for step in list(range(1, half)) + [0]:
                self.pair_copy(step, k).start()
                self.mine_copy(step, k).start()

    def pair_sum(self, step, k):
        self.pair_copy(step, k).wait_recv()
        self.mine_copy(step, k).wait()
        return self.mine[step, k].astype(jnp.float32) + self.pair_in[step, k].astype(jnp.float32)

    def middle(self, k):
        for step in range(1, self.spot.half):
            self.across_out[step, k] = self.pair_sum(step, k).astype(jnp.bfloat16)
            self.across_copy(step, k).start()

    def last(self, k):
        total = self.pair_sum(0, k)
        for step in range(1, self.spot.half):
            self.across_copy(step, k).wait_recv()
            total = total + self.across_in[step, k].astype(jnp.float32)
        return total.astype(jnp.bfloat16)

    def finish(self):
        for k in range(self.chunks):
            for step in range(self.spot.half):
                self.pair_copy(step, k).wait_send()
                if step:
                    self.across_copy(step, k).wait_send()


class Collect:
    def __init__(self, spot, part, out, scratch):
        self.spot, self.total = spot, scratch[9]
        self.keys = far_keys(spot.groups) + near_keys(spot.groups) + [0]
        self.sums = ColumnSum(
            spot,
            spot.groups,
            lambda k: flip(spot.place, self.keys[k]),
            part,
            scratch[:4],
            scratch[4:9],
        )
        self.out = out
        self.local, self.send, self.recv = scratch[10:]

    @staticmethod
    def scratch(columns, groups, block):
        return (
            ColumnSum.scratch(columns, groups, block)
            + [pltpu.VMEM((groups,) + block, jnp.bfloat16)]
            + [pltpu.SemaphoreType.DMA(())]
            + [pltpu.SemaphoreType.DMA((groups,))] * 2
        )

    def copy(self, k):
        spot, key = self.spot, self.keys[k]
        target = self.out.at[spot.place]
        if key == 0:
            return pltpu.make_async_copy(self.total.at[k], target, self.local)
        peer = flip(spot.place, key)
        return remote(
            self.total.at[k], target, self.send.at[k], self.recv.at[k], (peer, spot.lane)
        )

    def begin(self):
        self.sums.begin()

    def middle(self, key):
        self.sums.middle(key)

    def last(self, key):
        self.total[key] = self.sums.last(key)
        self.copy(key).start()

    def finish(self):
        last = self.spot.groups - 1
        for k in range(last):
            self.copy(k).wait_recv()
        for k in range(last):
            self.copy(k).wait_send()
        self.copy(last).wait()
        self.sums.finish()


def collect_kernel(groups, columns, part, out, *scratch):
    spot = Spot(groups, columns)
    job = Collect(spot, part, out, scratch)
    spot.meet()
    job.begin()
    ahead = 2
    for key in range(ahead):
        job.middle(key)
    for key in range(groups):
        if key + ahead < groups:
            job.middle(key + ahead)
        job.last(key)
    job.finish()


def collect(part, which):
    columns, groups = part.shape[:2]
    block = part.shape[2:]
    return pl.pallas_call(
        functools.partial(collect_kernel, groups, columns),
        out_shape=jax.ShapeDtypeStruct((groups,) + block, part.dtype),
        in_specs=[anywhere],
        out_specs=anywhere,
        scratch_shapes=Collect.scratch(columns, groups, block),
        compiler_params=comm_params(which),
        name="collect_rows",
    )(part)


def lanes_at(place, width):
    return pl.ds(pl.multiple_of(place * width, 128), width)


def mixed_kernel(groups, columns, mixed, attended, *sems):
    spot = Spot(groups, columns)
    width = mixed.shape[2]

    def blocks(at, third):
        if width % 128:
            return mixed.at[at], attended.at[spot.place]
        return mixed.at[at], attended.at[:, lanes_at(spot.place, width)]

    job = Exchange(spot, blocks, 1, *sems)
    spot.meet()
    job.begin()
    job.arrive()
    job.finish()


def exchange_mixed(mixed, columns, which):
    groups, rows, width = mixed.shape
    shape = mixed.shape if width % 128 else (rows, groups * width)
    out = pl.pallas_call(
        functools.partial(mixed_kernel, groups, columns),
        out_shape=jax.ShapeDtypeStruct(shape, mixed.dtype),
        in_specs=[anywhere],
        out_specs=anywhere,
        scratch_shapes=Exchange.sems(groups, 1),
        compiler_params=comm_params(which),
        name="exchange_mixed",
    )(mixed)
    if width % 128:
        out = jnp.transpose(out, (1, 0, 2)).reshape(rows, groups * width)
    return out


class Tail:
    def __init__(self, spot, chunks, refs, scratch):
        grads, part, piece, weight, grads_out, sum_all, piece_all, weight_all = refs
        groups = spot.groups
        width = grads.shape[2] // 3
        thirds = 3 if width % 128 == 0 else 1

        def blocks(at, third):
            if thirds == 1:
                return grads.at[at], grads_out.at[spot.place]
            columns_to = pl.ds(pl.multiple_of(third * D + spot.place * width, 128), width)
            return grads.at[at, :, pl.ds(third * width, width)], grads_out.at[:, columns_to]

        self.chunks = chunks
        self.sums = ColumnSum(spot, chunks, lambda k: k, part, scratch[:4], scratch[4:9])
        self.own_sum = scratch[9]
        self.swap = Exchange(spot, blocks, thirds, *scratch[10:13])
        self.line = LineGather(spot, self.own_sum, sum_all, *scratch[13:16])
        self.side = LineGather(spot, piece, piece_all, *scratch[16:19])
        self.column = ColumnGather(spot, weight, weight_all, *scratch[19:24])

    @staticmethod
    def scratch(columns, groups, chunks, block, thirds):
        return (
            ColumnSum.scratch(columns, chunks, block)
            + [pltpu.VMEM((chunks,) + block, jnp.bfloat16)]
            + Exchange.sems(groups, thirds)
            + LineGather.sems(groups) * 2
            + ColumnGather.sems(columns)
        )


def tail_kernel(
    groups,
    columns,
    chunks,
    grads,
    normed,
    own_weight,
    extra,
    piece,
    weight,
    grads_out,
    sum_all,
    piece_all,
    weight_all,
    grads_sc,
    normed_sc,
    load_sems,
    part,
    *scratch,
):
    spot = Spot(groups, columns)
    refs = (grads, part, piece, weight, grads_out, sum_all, piece_all, weight_all)
    tail = Tail(spot, chunks, refs, scratch)
    wide = grads.shape[2]
    block_rows = D // (columns * chunks)
    loads = [
        pltpu.make_async_copy(grads, grads_sc, load_sems.at[0]),
        pltpu.make_async_copy(normed, normed_sc, load_sems.at[1]),
    ]
    for load in loads:
        load.start()
    far = far_keys(groups)
    early, late = far[: len(far) // 2], far[len(far) // 2 :]
    spot.meet()
    tail.side.begin()
    for key in early + near_keys(groups) + [0]:
        tail.swap.start(key)
    for load in loads:
        load.wait()
    all_grads = grads_sc[...].reshape(-1, wide)

    for at in range(columns * chunks):
        rows = pl.ds(at * block_rows, block_rows)
        grad = tn_dot(normed_sc[:, rows], all_grads)
        weights = own_weight[rows, :][:, :wide].astype(jnp.float32)
        gain = jnp.sum(grad * weights, axis=1, keepdims=True)
        lanes = lax.broadcasted_iota(jnp.int32, (block_rows, spare), 1)
        side = jnp.where(lanes == 0, gain, extra[rows, :].astype(jnp.float32))
        part[at // chunks, at % chunks] = jnp.concatenate([grad, side], axis=1).astype(jnp.bfloat16)
    tail.sums.begin()
    for k in range(chunks):
        tail.sums.middle(k)
    tail.column.begin()
    tail.side.hop(1)
    for k in range(chunks):
        tail.own_sum[k] = tail.sums.last(k)
    tail.line.begin()
    tail.side.hop(2)
    tail.line.hop(1)
    tail.side.hop(3)
    tail.line.hop(2)
    for key in late:
        tail.swap.start(key)
    tail.line.hop(3)
    tail.column.forward()
    tail.side.finish()
    tail.swap.arrive()
    tail.line.finish()
    tail.column.finish()
    tail.swap.finish()
    tail.sums.finish()


def tail_exchange(grads, normed, own_weight, extra, piece, weight, columns, which):
    groups, row_count, wide = grads.shape
    apart = wide // 3 % 128 != 0
    grads_shape = grads.shape if apart else (row_count, wide * groups)
    chunks = 2
    block = (D // columns // chunks, wide + spare)
    shape_of = lambda shape: jax.ShapeDtypeStruct(shape, jnp.bfloat16)
    inside = pl.BlockSpec(memory_space=pltpu.VMEM)
    return pl.pallas_call(
        functools.partial(tail_kernel, groups, columns, chunks),
        out_shape=(
            shape_of(grads_shape),
            shape_of((groups, chunks) + block),
            shape_of((groups,) + piece.shape),
            shape_of((columns,) + weight.shape),
        ),
        in_specs=[anywhere, anywhere, inside, inside, anywhere, anywhere],
        out_specs=(anywhere,) * 4,
        scratch_shapes=[
            pltpu.VMEM(grads.shape, jnp.bfloat16),
            pltpu.VMEM(normed.shape, jnp.bfloat16),
            pltpu.SemaphoreType.DMA((2,)),
            pltpu.VMEM((columns, chunks) + block, jnp.bfloat16),
        ]
        + Tail.scratch(columns, groups, chunks, block, 1 if apart else 3),
        compiler_params=comm_params(which),
        name="tail_exchange",
    )(grads, normed, own_weight, extra, piece, weight)


def finish_kernel(
    width,
    grads,
    weight,
    packed,
    packed_extra,
    tokens,
    gain,
    grad_middle,
    out_low,
    input_grad,
    qkv_grad,
    out_grad,
    extra,
    total_sc,
):
    third = pl.program_id(0)
    for group in range(packed.shape[0]):
        qkv_grad[:, group * width : (group + 1) * width] = packed[group].astype(jnp.float32)
    part = nt_dot(grads[...], weight[...].reshape(D, -1))

    @pl.when(third == 0)
    def _():
        total_sc[...] = part

    @pl.when(third > 0)
    def _():
        total_sc[...] += part

    @pl.when(third == 2)
    def _():
        features = tokens[...].astype(jnp.float32)
        factor = lax.rsqrt(jnp.mean(features * features, axis=-1, keepdims=True) + epsilon)
        unit = features * factor
        scaled = total_sc[...] * gain[...]
        inner = jnp.mean(scaled * unit, axis=-1, keepdims=True)
        input_grad[...] = grad_middle[...] + factor * (scaled - unit * inner)
        out_grad[...] = out_low[...].astype(jnp.float32)
        extra[...] = jnp.transpose(jnp.sum(packed_extra[...].astype(jnp.float32), axis=0))


def finish(grads, weight, packed, tokens, gain, grad_middle, out_low, width):
    groups, shard_rows = packed.shape[:2]
    columns = weight.shape[0]
    rows = grads.shape[0]
    whole = lambda t: (0, 0)
    full = jax.ShapeDtypeStruct((rows, D), jnp.float32)
    return pl.pallas_call(
        functools.partial(finish_kernel, width),
        grid=(3,),
        out_shape=(
            full,
            jax.ShapeDtypeStruct((shard_rows, 3 * D), jnp.float32),
            jax.ShapeDtypeStruct((shard_rows, D), jnp.float32),
            jax.ShapeDtypeStruct((spare, shard_rows), jnp.float32),
        ),
        in_specs=[
            pl.BlockSpec((rows, D), lambda t: (0, t)),
            pl.BlockSpec((columns, shard_rows, D), lambda t: (0, 0, t)),
            pl.BlockSpec((groups, shard_rows, width), lambda t: (0, 0, t)),
            pl.BlockSpec((groups, shard_rows, spare), lambda t: (0, 0, 3 * width // spare)),
            pl.BlockSpec((rows, D), whole),
            pl.BlockSpec((1, D), whole),
            pl.BlockSpec((rows, D), whole),
            pl.BlockSpec((shard_rows, D), whole),
        ],
        out_specs=(
            pl.BlockSpec((rows, D), whole),
            pl.BlockSpec((shard_rows, D), lambda t: (0, t)),
            pl.BlockSpec((shard_rows, D), whole),
            pl.BlockSpec((spare, shard_rows), whole),
        ),
        scratch_shapes=[pltpu.VMEM((rows, D), jnp.float32)],
        compiler_params=pltpu.CompilerParams(vmem_limit_bytes=60 * mega),
        name="finish",
    )(grads, weight, packed, packed, tokens, gain, grad_middle, out_low)


def rms_norm(features, scales):
    factor = lax.rsqrt(jnp.mean(features * features, axis=-1, keepdims=True) + epsilon)
    return features * factor * scales


def buckets_of(offsets):
    distance = np.abs(offsets)
    beyond = 8 + np.sum(distance[..., None] >= np.array(far_bounds), axis=-1)
    return np.where(distance < 8, distance, beyond) + 16 * (offsets > 0)


def skew_buckets():
    lanes = np.arange(2 * tile)
    from_query = np.where(lanes < tile, -lanes, 2 * tile - lanes)
    return np.concatenate([buckets_of(near * tile + from_query) for near in (-1, 0, 1)])


def lane_row_mask(head, width, rows):
    lanes = lax.broadcasted_iota(jnp.int32, (rows, width), 1)
    return (lanes >= head * HEAD) & (lanes < (head + 1) * HEAD)


def fold_rows(block, op):
    return op(block.reshape(block.shape[0] // 8, 8, block.shape[1]), axis=0)


def nt_dot(left, right):
    return lax.dot_general(left, right, (((1,), (1,)), ((), ())), preferred_element_type=jnp.float32)


def tn_dot(left, right):
    return lax.dot_general(left, right, (((0,), (0,)), ((), ())), preferred_element_type=jnp.float32)


def nn_dot(left, right):
    return jnp.dot(left, right, preferred_element_type=jnp.float32)


def build_bias(base_ref, far_ref, bias_sc, heads_here):
    for head in range(heads_here):
        for near in range(3):
            row = base_ref[pl.ds(head * 3 + near, 1), :]
            wide = jnp.broadcast_to(row, (tile, 2 * tile))
            skewed = pltpu.roll(wide, 0, 1, stride=1, stride_axis=0)
            bias_sc[head, near] = skewed[:, :tile]
        bias_sc[head, 3] = jnp.full((tile, tile), far_ref[head, 1], jnp.float32)


def unskew_sum(wide):
    lanes = wide.shape[1]
    half = wide.shape[0] // 2
    while half >= 8:
        wide = wide[:half] + pltpu.roll(wide[half:], lanes - half, 1)
        half //= 2
    total = wide[0:1]
    for row in range(1, 8):
        total = total + pltpu.roll(wide[row : row + 1], lanes - row, 1)
    return total


def rows_at(index):
    return pl.ds(pl.multiple_of(index * tile, tile), tile)


def visible_tile(key_tile, query_tile, prefix_length):
    key_pos = key_tile * tile + lax.broadcasted_iota(jnp.int32, (tile, tile), 0)
    query_pos = query_tile * tile + lax.broadcasted_iota(jnp.int32, (tile, tile), 1)
    return (key_pos <= query_pos) | (key_pos < prefix_length)


class Spread:
    def __init__(self, spot, rows, far_rows, side_rows, full, sems):
        self.spot, self.rows, self.full = spot, rows, full
        self.far_rows, self.side_rows = far_rows, side_rows
        self.send, self.recv, self.local = sems[:3]
        self.across_send, self.across_recv, self.core_send, self.core_recv = sems[3:]
        self.early = early_keys(spot.groups)
        self.rest = [key for key in far_keys(spot.groups) if key not in self.early]
        self.near = near_keys(spot.groups)

    @staticmethod
    def sems(groups, columns):
        half = columns // 2
        return [pltpu.SemaphoreType.DMA((groups,))] * 2 + [
            pltpu.SemaphoreType.DMA((groups, half))
        ] * 5

    def source(self, key, step):
        spot = self.spot
        at = flip(spot.place, key)
        if key and key not in self.early:
            return self.full.at[spot.behind(step), at]
        if step:
            return self.side_rows.at[step - 1, at]
        return self.far_rows.at[at] if key else self.rows.at[at]

    def local_copy(self, key, step):
        spot = self.spot
        target = self.full.at[spot.behind(step), flip(spot.place, key)]
        return pltpu.make_async_copy(self.source(key, step), target, self.local.at[key, step])

    def swap(self, key):
        spot = self.spot
        peer = flip(spot.place, key)
        return remote(
            self.rows.at[peer],
            self.full.at[spot.lane, spot.place],
            self.send.at[key],
            self.recv.at[key],
            (peer, spot.lane),
        )

    def across(self, key, step):
        spot = self.spot
        block = self.full.at[spot.lane, flip(spot.place, key)]
        return remote(
            block,
            block,
            self.across_send.at[key, step],
            self.across_recv.at[key, step],
            (spot.place, spot.across(step)),
        )

    def core(self, key, step):
        spot = self.spot
        return remote(
            self.source(key, step),
            self.full.at[spot.behind(step), flip(spot.place, key)],
            self.core_send.at[key, step],
            self.core_recv.at[key, step],
            (spot.place, spot.partner),
        )

    def begin(self):
        for key in self.rest + self.near:
            self.swap(key).start()
        for key in [0] + self.early:
            for step in range(self.spot.half):
                self.core(key, step).start()
                self.local_copy(key, step).start()

    def advance(self, key):
        self.swap(key).wait_recv()
        for step in range(1, self.spot.half):
            self.across(key, step).start()
        self.core(key, 0).start()

    def pass_on(self, key):
        for step in range(1, self.spot.half):
            self.across(key, step).wait_recv()
            self.core(key, step).start()

    def finish(self):
        half = self.spot.half
        keys = range(self.spot.groups)
        for key in keys:
            for step in range(half):
                self.core(key, step).wait_recv()
        for key in keys:
            moved = key in self.near + self.rest
            if moved:
                self.swap(key).wait_send()
            for step in range(half):
                self.core(key, step).wait_send()
                if not moved:
                    self.local_copy(key, step).wait()
                elif step:
                    self.across(key, step).wait_send()


def attend_forward_kernel(
    heads_here,
    groups,
    columns,
    prefix_ref,
    far_ref,
    base_ref,
    qkv_ref,
    rows_ref,
    far_rows_ref,
    side_rows_ref,
    mixed_ref,
    totals_ref,
    full_ref,
    bias_sc,
    score_sc,
    value_sc,
    *sems,
):
    width = heads_here * HEAD
    query_tile = pl.program_id(0)
    tiles = qkv_ref.shape[0] // tile
    spot = Spot(groups, columns)
    job = Spread(spot, rows_ref, far_rows_ref, side_rows_ref, full_ref, sems)

    @pl.when(query_tile == 0)
    def _():
        spot.meet()
        job.begin()

    prefix_length = prefix_ref[0]
    heads = range(heads_here)

    @pl.when(query_tile == 0)
    def _():
        build_bias(base_ref, far_ref, bias_sc, heads_here)
        for key_tile in range(value_sc.shape[1] // tile):
            rows = pl.ds(key_tile * tile, tile)
            values = qkv_ref[rows, 2 * width : 3 * width].astype(jnp.float32)
            value_sc[:, rows] = jnp.transpose(values).astype(jnp.bfloat16)

    queries = qkv_ref[rows_at(query_tile), :width]
    head_queries = [
        jnp.where(lane_row_mask(head, width, tile), queries, jnp.zeros_like(queries)) for head in heads
    ]

    def score_tiles(key_tile, tops, finish):
        keys = qkv_ref[rows_at(key_tile), width : 2 * width]
        out = []
        for head in heads:
            scores = finish(head, nt_dot(keys, head_queries[head]) * (score_scale * log2e))
            score_sc[head, rows_at(key_tile), :] = scores
            out.append(jnp.maximum(tops[head], fold_rows(scores, jnp.max)))
        return tuple(out)

    def far_body(key_tile, tops):
        return score_tiles(key_tile, tops, lambda head, raw: raw + far_ref[head, 0])

    def near_body(key_tile, tops):
        return score_tiles(key_tile, tops, lambda head, raw: raw + bias_sc[head, 0])

    def tail_body(key_tile, tops):
        shown = visible_tile(key_tile, query_tile, prefix_length)
        which = 1 + jnp.minimum(key_tile - query_tile, 2)
        return score_tiles(
            key_tile, tops, lambda head, raw: jnp.where(shown, raw + bias_sc[head, which], masked_score)
        )

    tile_count = jnp.maximum(query_tile + 1, tiles // 2)
    near_start = jnp.maximum(query_tile - 1, 0)
    tops = tuple(jnp.full((8, tile), masked_score, jnp.float32) for _ in heads)
    tops = lax.fori_loop(0, near_start, far_body, tops)
    tops = lax.fori_loop(near_start, query_tile, near_body, tops)
    tops = lax.fori_loop(query_tile, tile_count, tail_body, tops)
    tops = [jnp.max(top, axis=0, keepdims=True) for top in tops]

    def mix_body(key_tile, carry):
        sums, mixes = carry
        new_sums, new_mixes = [], []
        for head in heads:
            expos = jnp.exp2(score_sc[head, rows_at(key_tile), :] - tops[head])
            new_sums.append(sums[head] + fold_rows(expos, jnp.sum))
            values = value_sc[head * HEAD : (head + 1) * HEAD, rows_at(key_tile)]
            new_mixes.append(mixes[head] + nn_dot(values, expos.astype(jnp.bfloat16)))
        return (tuple(new_sums), tuple(new_mixes))

    sums, mixes = lax.fori_loop(
        0,
        tile_count,
        mix_body,
        (
            tuple(jnp.zeros((8, tile), jnp.float32) for _ in heads),
            tuple(jnp.zeros((HEAD, tile), jnp.float32) for _ in heads),
        ),
    )
    parts = []
    for head in heads:
        total = jnp.sum(sums[head], axis=0, keepdims=True)
        parts.append(mixes[head] / total)
        totals_ref[0, pl.ds(head, 1), :] = tops[head] + jnp.log2(total)
    mixed_ref[...] = jnp.transpose(jnp.concatenate(parts, axis=0)).astype(jnp.bfloat16)

    @pl.when(query_tile == tiles // 2)
    def _():
        for key in job.near:
            job.advance(key)

    @pl.when(query_tile == tiles - 2)
    def _():
        for key in job.near[:1]:
            job.pass_on(key)

    @pl.when(query_tile == tiles - 2)
    def _():
        for key in job.rest:
            job.advance(key)

    @pl.when(query_tile == tiles - 1)
    def _():
        for key in job.near[1:] + job.rest:
            job.pass_on(key)
        job.finish()


def attend_forward(prefix, far_bias, base_bias, qkv, rows, far_rows, side_rows, columns):
    length = qkv.shape[0]
    groups = rows.shape[0]
    width = qkv.shape[1] // 3
    heads_here = width // HEAD
    tiles = length // tile
    return pl.pallas_call(
        functools.partial(attend_forward_kernel, heads_here, groups, columns),
        grid=(tiles,),
        out_shape=(
            jax.ShapeDtypeStruct((length, width), jnp.bfloat16),
            jax.ShapeDtypeStruct((tiles, heads_here, tile), jnp.float32),
            jax.ShapeDtypeStruct((columns,) + rows.shape, rows.dtype),
        ),
        in_specs=[
            pl.BlockSpec(memory_space=pltpu.SMEM),
            pl.BlockSpec(memory_space=pltpu.SMEM),
            pl.BlockSpec(base_bias.shape, lambda i: (0, 0)),
            pl.BlockSpec(qkv.shape, lambda i: (0, 0)),
            anywhere,
            anywhere,
            anywhere,
        ],
        out_specs=(
            pl.BlockSpec((tile, width), lambda i: (i, 0)),
            pl.BlockSpec((1, heads_here, tile), lambda i: (i, 0, 0)),
            anywhere,
        ),
        scratch_shapes=[
            pltpu.VMEM((heads_here, 4, tile, tile), jnp.float32),
            pltpu.VMEM((heads_here, length, tile), jnp.float32),
            pltpu.VMEM((width, length), jnp.bfloat16),
        ]
        + Spread.sems(groups, columns),
        compiler_params=comm_params(5),
        cost_estimate=pl.CostEstimate(
            flops=40 * length * length * width, transcendentals=length * length * heads_here,
            bytes_accessed=8 * length * width,
        ),
        name="attend_forward",
    )(prefix, far_bias, base_bias, qkv, rows, far_rows, side_rows)


def attend_backward_kernel(
    heads_here,
    groups,
    columns,
    prefix_ref,
    far_ref,
    base_ref,
    qkv_ref,
    mixed_ref,
    grad_ref,
    totals_ref,
    part_ref,
    sums_ref,
    out_ref,
    near_ref,
    side_ref,
    result_ref,
    piece_ref,
    bias_sc,
    key_sc,
    grad_key_sc,
    grad_value_sc,
    near_sc,
    *scratch,
):
    width = heads_here * HEAD
    query_tile = pl.program_id(0)
    tiles = qkv_ref.shape[0] // tile
    spot = Spot(groups, columns)
    pieces = scratch[0]
    swap = Exchange(
        spot, lambda at, third: (sums_ref.at[at], pieces.at[spot.place]), 1, *scratch[1:4]
    )
    job = Collect(spot, part_ref, result_ref, scratch[4:])

    @pl.when(query_tile == 0)
    def _():
        spot.meet()
        job.begin()
        swap.begin()

    prefix_length = prefix_ref[0]
    heads = range(heads_here)

    @pl.when(query_tile == 0)
    def _():
        build_bias(base_ref, far_ref, bias_sc, heads_here)
        for key_tile in range(key_sc.shape[1] // tile):
            rows = pl.ds(key_tile * tile, tile)
            keys = qkv_ref[rows, width : 2 * width].astype(jnp.float32)
            key_sc[:, rows] = jnp.transpose(keys).astype(jnp.bfloat16)
        grad_key_sc[...] = jnp.zeros_like(grad_key_sc)
        grad_value_sc[...] = jnp.zeros_like(grad_value_sc)
        near_sc[...] = jnp.zeros_like(near_sc)
        side_ref[...] = jnp.zeros_like(side_ref)

    queries = qkv_ref[rows_at(query_tile), :width]
    grads = grad_ref[rows_at(query_tile), :]
    products = grads.astype(jnp.float32) * mixed_ref[rows_at(query_tile), :].astype(jnp.float32)
    head_queries, head_grads, inners, totals = [], [], [], []
    for head in heads:
        mask = lane_row_mask(head, width, tile)
        head_queries.append(jnp.where(mask, queries, jnp.zeros_like(queries)))
        head_grads.append(jnp.where(mask, grads, jnp.zeros_like(grads)))
        ones = jnp.where(lane_row_mask(head, width, 8), 1.0, 0.0)
        inner = lax.dot_general(
            ones,
            products,
            (((1,), (1,)), ((), ())),
            precision=lax.Precision.HIGHEST,
            preferred_element_type=jnp.float32,
        )
        inners.append(inner[0:1, :])
        totals.append(totals_ref[0, pl.ds(head, 1), :])

    def step(key_tile, carry, finish, keep):
        sides, grad_queries = carry
        keys = qkv_ref[rows_at(key_tile), width : 2 * width]
        values = qkv_ref[rows_at(key_tile), 2 * width : 3 * width]
        new_sides, new_queries = [], []
        key_part, value_part = None, None
        for head in heads:
            raw = nt_dot(keys, head_queries[head]) * (score_scale * log2e)
            attention = jnp.exp2(finish(head, raw))
            grad_weights = nt_dot(values, head_grads[head])
            grad_scores = attention * (grad_weights - inners[head])
            new_sides.append(keep(head, grad_scores, sides[head]))
            low_scores = grad_scores.astype(jnp.bfloat16)
            keys_across = key_sc[head * HEAD : (head + 1) * HEAD, rows_at(key_tile)]
            new_queries.append(grad_queries[head] + nn_dot(keys_across, low_scores))
            value_one = nn_dot(attention.astype(jnp.bfloat16), head_grads[head])
            key_one = nn_dot(low_scores, head_queries[head])
            value_part = value_one if value_part is None else value_part + value_one
            key_part = key_one if key_part is None else key_part + key_one
        grad_key_sc[rows_at(key_tile), :] += key_part
        grad_value_sc[rows_at(key_tile), :] += value_part
        return (tuple(new_sides), tuple(new_queries))

    def add_side(head, grad_scores, side):
        return side + fold_rows(grad_scores, jnp.sum)

    def far_body(key_tile, carry):
        return step(
            key_tile, carry, lambda head, raw: raw + (far_ref[head, 0] - totals[head]), add_side
        )

    def near_body(key_tile, carry):
        def keep(head, grad_scores, side):
            near_sc[head, 0] += grad_scores
            return side

        return step(
            key_tile, carry, lambda head, raw: raw + bias_sc[head, 0] - totals[head], keep
        )

    def tail_body(key_tile, carry):
        shown = visible_tile(key_tile, query_tile, prefix_length)
        which = 1 + jnp.minimum(key_tile - query_tile, 2)

        def keep(head, grad_scores, side):
            near_sc[head, which] += grad_scores
            return side

        return step(
            key_tile,
            carry,
            lambda head, raw: jnp.where(
                shown, raw + bias_sc[head, which] - totals[head], masked_score
            ),
            keep,
        )

    tile_count = jnp.maximum(query_tile + 1, tiles // 2)
    near_start = jnp.maximum(query_tile - 1, 0)
    carry = (
        tuple(jnp.zeros((8, tile), jnp.float32) for _ in heads),
        tuple(jnp.zeros((HEAD, tile), jnp.float32) for _ in heads),
    )
    carry = lax.fori_loop(0, near_start, far_body, carry)
    carry = lax.fori_loop(near_start, query_tile, near_body, carry)
    carry = lax.fori_loop(query_tile, tile_count, tail_body, carry)
    sides, grad_queries = carry
    for head in heads:
        side_ref[head, 0] += sides[head]
    across = jnp.concatenate(grad_queries, axis=0) * score_scale
    out_ref[rows_at(query_tile), :width] = jnp.transpose(across).astype(jnp.bfloat16)

    @pl.when(query_tile == tiles - 1)
    def _():
        out_ref[:, width : 2 * width] = (grad_key_sc[...] * score_scale).astype(jnp.bfloat16)
        out_ref[:, 2 * width : 3 * width] = grad_value_sc[...].astype(jnp.bfloat16)
        for head in heads:
            side_ref[head, 1] = fold_rows(near_sc[head, 3], jnp.sum)
            for near in range(3):
                wide = jnp.concatenate(
                    [near_sc[head, near], jnp.zeros((tile, tile), jnp.float32)], axis=1
                )
                near_ref[pl.ds(head * 3 + near, 1), :] = unskew_sum(wide)

    for step in range(tiles):
        middles = [key for key in range(groups) if key * 2 // groups == step]
        lasts = [key for key in range(groups) if min(tiles - 1, 2 + key * 3 // 4) == step]

        @pl.when(query_tile == step)
        def _():
            for key in middles:
                job.middle(key)
            for key in lasts:
                job.last(key)

    @pl.when(query_tile == tiles - 1)
    def _():
        swap.arrive()
        piece_ref[...] = jnp.sum(pieces[...].astype(jnp.float32), axis=0).astype(jnp.bfloat16)
        job.finish()
        swap.finish()


def attend_backward(
    prefix, far_bias, base_bias, qkv, mixed, grad_mixed, totals, part, sums, columns
):
    length = qkv.shape[0]
    groups, piece_rows, piece_width = sums.shape
    block = part.shape[2:]
    width = qkv.shape[1] // 3
    heads_here = width // HEAD
    tiles = length // tile
    whole = lambda i: (0, 0)
    return pl.pallas_call(
        functools.partial(attend_backward_kernel, heads_here, groups, columns),
        grid=(tiles,),
        out_shape=(
            jax.ShapeDtypeStruct((length, 3 * width), jnp.bfloat16),
            jax.ShapeDtypeStruct((heads_here * 3, 2 * tile), jnp.float32),
            jax.ShapeDtypeStruct((heads_here, 2, 8, tile), jnp.float32),
            jax.ShapeDtypeStruct((groups,) + block, jnp.bfloat16),
            jax.ShapeDtypeStruct((piece_rows, piece_width), jnp.bfloat16),
        ),
        in_specs=[
            pl.BlockSpec(memory_space=pltpu.SMEM),
            pl.BlockSpec(memory_space=pltpu.SMEM),
            pl.BlockSpec(base_bias.shape, whole),
            pl.BlockSpec(qkv.shape, whole),
            pl.BlockSpec(mixed.shape, whole),
            pl.BlockSpec(mixed.shape, whole),
            pl.BlockSpec((1, heads_here, tile), lambda i: (i, 0, 0)),
            anywhere,
            anywhere,
        ],
        out_specs=(
            pl.BlockSpec((length, 3 * width), whole),
            pl.BlockSpec((heads_here * 3, 2 * tile), whole),
            pl.BlockSpec((heads_here, 2, 8, tile), lambda i: (0, 0, 0, 0)),
            anywhere,
            pl.BlockSpec((piece_rows, piece_width), whole),
        ),
        scratch_shapes=[
            pltpu.VMEM((heads_here, 4, tile, tile), jnp.float32),
            pltpu.VMEM((width, length), jnp.bfloat16),
            pltpu.VMEM((length, width), jnp.float32),
            pltpu.VMEM((length, width), jnp.float32),
            pltpu.VMEM((heads_here, 4, tile, tile), jnp.float32),
            pltpu.VMEM(sums.shape, jnp.bfloat16),
        ]
        + Exchange.sems(groups, 1)
        + Collect.scratch(columns, groups, block),
        compiler_params=comm_params(6, 60),
        cost_estimate=pl.CostEstimate(
            flops=70 * length * length * width, transcendentals=length * length * heads_here,
            bytes_accessed=16 * length * width,
        ),
        name="attend_backward",
    )(prefix, far_bias, base_bias, qkv, mixed, grad_mixed, totals, part, sums)


def gelu_parts(act):
    inner = math.sqrt(2.0 / math.pi) * (act + 0.044715 * act * act * act)
    tanh = jnp.tanh(inner)
    half = 0.5 * (1.0 + tanh)
    slope = math.sqrt(2.0 / math.pi) * (1.0 + 3.0 * 0.044715 * act * act)
    return act * half, half + 0.5 * act * (1.0 - tanh * tanh) * slope


def slot_rows(experts_here):
    return experts_here * main_slots + -(-experts_here * tail_slots // 8) * 8


def tail_select(expert, sources, tail_height):
    rows = lax.broadcasted_iota(jnp.int32, (sources * tail_slots, sources * tail_height), 0)
    columns = lax.broadcasted_iota(jnp.int32, (sources * tail_slots, sources * tail_height), 1)
    wanted = (rows // tail_slots) * tail_height + expert * tail_slots + rows % tail_slots
    return jnp.where(columns == wanted, 1.0, 0.0).astype(jnp.bfloat16)


def expert_input(main_ref, tail_ref, select):
    width = main_ref.shape[-1]
    main = main_ref[...].reshape(-1, width)
    tail = nn_dot(select, tail_ref[...].reshape(-1, width)).astype(jnp.bfloat16)
    return jnp.concatenate([main, tail], axis=0)


def gates_of(wide_rows):
    return wide_rows[:, D : D + 1].astype(jnp.float32) + wide_rows[:, D + 1 : D + 2].astype(
        jnp.float32
    )


def expert_output(value, select, expert, main_sc, tail_sc):
    low = value.astype(jnp.bfloat16)
    main_count = main_sc.shape[0] * main_sc.shape[1] * main_slots
    main_sc[...] = low[:main_count].reshape(main_sc.shape)
    spread = tn_dot(select, low[main_count:]).astype(jnp.bfloat16).reshape(tail_sc.shape)

    @pl.when(expert == 0)
    def _():
        tail_sc[...] = spread

    @pl.when(expert > 0)
    def _():
        tail_sc[...] += spread


def expert_math(rows, gates, raw_hidden, gate_weight, up_weight, down_weight):
    gate_act = nt_dot(rows, gate_weight)
    up_act = nt_dot(rows, up_weight)
    gelu, slope = gelu_parts(gate_act)
    hidden = gelu * up_act
    low_hidden = hidden.astype(jnp.bfloat16)
    grad_gates = jnp.sum(raw_hidden * low_hidden.astype(jnp.float32), axis=1, keepdims=True)
    grad_hidden = raw_hidden * gates
    grad_gate = (grad_hidden * up_act * slope).astype(jnp.bfloat16)
    grad_up = (grad_hidden * gelu).astype(jnp.bfloat16)
    back = nn_dot(grad_gate, gate_weight) + nn_dot(grad_up, up_weight)
    gated = (hidden * gates).astype(jnp.bfloat16)
    return gated, grad_gate, grad_up, back, grad_gates, nn_dot(low_hidden, down_weight)


def slot_lanes(expert, experts_here, sources):
    main = sources * main_slots
    count = sources * CAP
    rows = lax.broadcasted_iota(jnp.int32, (count, sources), 0)
    source = jnp.where(rows < main, rows // main_slots, (rows - main) // tail_slots)
    hot = jnp.where(lax.broadcasted_iota(jnp.int32, (count, sources), 1) == source, 1.0, 0.0)
    rows = lax.broadcasted_iota(jnp.int32, (count, spare), 0)
    lane = jnp.where(
        rows < main,
        expert * main_slots + rows % main_slots,
        experts_here * main_slots + expert * tail_slots + (rows - main) % tail_slots,
    )
    return hot.astype(jnp.bfloat16), lax.broadcasted_iota(jnp.int32, (count, spare), 1) == lane


def split_low(values):
    high = values.astype(jnp.bfloat16)
    return high, (values - high.astype(jnp.float32)).astype(jnp.bfloat16)


def expert_act_kernel(
    experts_here,
    row_main,
    row_tail,
    grad_main,
    grad_tail,
    gate_weight,
    up_weight,
    down_weight,
    hidden_ref,
    grad_gate_ref,
    grad_up_ref,
    result_ref,
    back_ref,
    result_main,
    result_tail,
    back_main,
    back_tail,
    sems,
):
    part, expert = pl.program_id(0), pl.program_id(1)
    shards_part = row_main.shape[0]
    sources = shards_part * row_main.shape[1]
    tail_height = row_tail.shape[2]
    sources_at = pl.ds(part * shards_part, shards_part)
    select = tail_select(expert, sources, tail_height)
    wide_rows = expert_input(row_main, row_tail, select)
    grads = expert_input(grad_main, grad_tail, select)
    hidden, grad_gate, grad_up, back, grad_gates, result = expert_math(
        wide_rows[:, :D],
        gates_of(wide_rows),
        nt_dot(grads, down_weight[0]),
        gate_weight[0],
        up_weight[0],
        down_weight[0],
    )
    lanes = lax.broadcasted_iota(jnp.int32, (back.shape[0], spare), 1)
    back = jnp.concatenate([back, jnp.where(lanes == 0, grad_gates, 0.0)], axis=1)
    hidden_ref[0] = hidden
    grad_gate_ref[0] = grad_gate
    grad_up_ref[0] = grad_up

    def main_copies(at):
        place = pl.ds(pl.multiple_of(at * main_slots, main_slots), main_slots)
        return (
            pltpu.make_async_copy(result_main, result_ref.at[sources_at, :, place, :], sems.at[0]),
            pltpu.make_async_copy(back_main, back_ref.at[sources_at, :, place, :], sems.at[1]),
        )

    @pl.when(expert > 0)
    def _():
        for copy in main_copies(expert - 1):
            copy.wait()

    expert_output(result, select, expert, result_main, result_tail)
    expert_output(back, select, expert, back_main, back_tail)
    for copy in main_copies(expert):
        copy.start()

    @pl.when(expert == experts_here - 1)
    def _():
        place = pl.ds(experts_here * main_slots, tail_height)
        tails = (
            pltpu.make_async_copy(result_tail, result_ref.at[sources_at, :, place, :], sems.at[2]),
            pltpu.make_async_copy(back_tail, back_ref.at[sources_at, :, place, :], sems.at[3]),
        )
        for copy in tails:
            copy.start()
        for copy in main_copies(expert):
            copy.wait()
        for copy in tails:
            copy.wait()


def parts_of(rows):
    shards, groups = rows.shape[:2]
    return max(1, shards * groups // part_sources)


def row_specs(rows, experts_here, order):
    shards, groups, height, width = rows.shape
    shards_part = shards // parts_of(rows)
    tail_height = slot_rows(experts_here) - experts_here * main_slots
    tail_at = experts_here * main_slots // tail_height
    main_at = lambda e, c: (c, 0, e, 0)
    side_at = lambda e, c: (c, 0, tail_at, 0)
    return [
        pl.BlockSpec((shards_part, groups, main_slots, width), order(main_at)),
        pl.BlockSpec((shards_part, groups, tail_height, width), order(side_at)),
    ]


def expert_act(rows, grads, gate_weight, up_weight, down_weight):
    experts_here, units, width = gate_weight.shape
    shards, groups = rows.shape[:2]
    count = shards * groups * CAP
    parts = parts_of(rows)
    height = slot_rows(experts_here)
    tail_height = height - experts_here * main_slots
    order = lambda index: lambda c, e: index(e, c)
    weight_spec = pl.BlockSpec((1, units, width), lambda c, e: (e, 0, 0))
    act_spec = pl.BlockSpec((1, count // parts, units), lambda c, e: (e, c, 0))
    act_shape = jax.ShapeDtypeStruct((experts_here, count, units), jnp.bfloat16)
    slot_shape = lambda lanes: jax.ShapeDtypeStruct(
        (shards, groups, height, lanes), jnp.bfloat16
    )
    scratch = [
        pltpu.VMEM((shards // parts, groups, rows_of, lanes), jnp.bfloat16)
        for lanes in (width, width + spare)
        for rows_of in (main_slots, tail_height)
    ]
    return pl.pallas_call(
        functools.partial(expert_act_kernel, experts_here),
        grid=(parts, experts_here),
        out_shape=(act_shape, act_shape, act_shape, slot_shape(width), slot_shape(width + spare)),
        in_specs=row_specs(rows, experts_here, order)
        + row_specs(grads, experts_here, order)
        + [weight_spec] * 3,
        out_specs=(
            act_spec,
            act_spec,
            act_spec,
            pl.BlockSpec(memory_space=pl.ANY),
            pl.BlockSpec(memory_space=pl.ANY),
        ),
        scratch_shapes=scratch + [pltpu.SemaphoreType.DMA((4,))],
        compiler_params=pltpu.CompilerParams(vmem_limit_bytes=60 * mega),
        cost_estimate=pl.CostEstimate(
            flops=12 * experts_here * count * width * units,
            transcendentals=experts_here * count * units,
            bytes_accessed=6 * experts_here * width * units + 8 * experts_here * count * width,
        ),
        name="expert_act",
    )(rows, rows, grads, grads, gate_weight, up_weight, down_weight)


class RowChunk:
    def __init__(self, spot, number, place_rows, rows_in, rows_all, back_out, bufs, sems):
        self.spot, self.number, self.place_rows = spot, number, place_rows
        self.rows_in, self.rows_all, self.back_out = rows_in, rows_all, back_out
        self.rows, self.back, self.pair_in, self.across_out, self.across_in, self.total = bufs
        (
            self.local,
            self.send,
            self.recv,
            self.across_send,
            self.across_recv,
            self.core_send,
            self.core_recv,
            self.pair_send,
            self.pair_recv,
            self.sum_send,
            self.sum_recv,
            self.back_send,
            self.back_recv,
        ) = sems

    @staticmethod
    def sems(groups, columns, chunks):
        half = columns // 2
        dma = pltpu.SemaphoreType.DMA
        return (
            [dma((chunks, 4))]
            + [dma((chunks, groups))] * 2
            + [dma((chunks, half, 2))] * 8
            + [dma((chunks, groups))] * 2
        )

    def keys(self, near):
        groups = self.spot.groups
        return [0] + near_keys(groups) if near else far_keys(groups)

    def side(self, near):
        half = self.spot.groups // 2
        here = self.spot.place // half
        return pl.ds((here if near else 1 - here) * half, half)

    def swap(self, key):
        spot, at = self.spot, self.number
        peer = flip(spot.place, key)
        source = self.rows_in.at[peer, self.place_rows]
        target = self.rows.at[spot.lane, spot.place]
        if key == 0:
            return pltpu.make_async_copy(source, target, self.local.at[at, 0])
        return remote(
            source, target, self.send.at[at, key], self.recv.at[at, key], (peer, spot.lane)
        )

    def keep(self, near):
        side = self.side(near)
        return pltpu.make_async_copy(
            self.rows.at[:, side],
            self.rows_all.at[:, side, self.place_rows],
            self.local.at[self.number, 1 + near],
        )

    def across(self, near, step):
        spot, at = self.spot, self.number
        block = self.rows.at[spot.lane, self.side(near)]
        return remote(
            block,
            block,
            self.across_send.at[at, step, near],
            self.across_recv.at[at, step, near],
            (spot.place, spot.across(step)),
        )

    def core(self, near, step):
        spot, at = self.spot, self.number
        block = self.rows.at[spot.behind(step), self.side(near)]
        return remote(
            block,
            block,
            self.core_send.at[at, step, near],
            self.core_recv.at[at, step, near],
            (spot.place, spot.partner),
        )

    def begin(self, near):
        for key in self.keys(near):
            self.swap(key).start()

    def advance(self, near):
        for key in self.keys(near):
            self.swap(key).wait_recv() if key else self.swap(key).wait()
        for step in range(1, self.spot.half):
            self.across(near, step).start()
        self.core(near, 0).start()

    def complete(self, near):
        half = self.spot.half
        for step in range(1, half):
            self.across(near, step).wait_recv()
            self.core(near, step).start()
        for step in range(half):
            self.core(near, step).wait_recv()
        if self.rows_all is not None:
            self.keep(near).start()

    def pair_copy(self, step, near):
        spot, at = self.spot, self.number
        side = self.side(near)
        return remote(
            self.back.at[spot.lane_at(step, True), side],
            self.pair_in.at[step, side],
            self.pair_send.at[at, step, near],
            self.pair_recv.at[at, step, near],
            (spot.place, spot.partner),
        )

    def sum_copy(self, step, near):
        spot, at = self.spot, self.number
        side = self.side(near)
        return remote(
            self.across_out.at[step, side],
            self.across_in.at[step, side],
            self.sum_send.at[at, step, near],
            self.sum_recv.at[at, step, near],
            (spot.place, spot.across(step)),
        )

    def back_copy(self, key):
        spot, at = self.spot, self.number
        peer = flip(spot.place, key)
        target = self.back_out.at[spot.place, self.place_rows]
        if key == 0:
            return pltpu.make_async_copy(self.total.at[peer], target, self.local.at[at, 3])
        return remote(
            self.total.at[peer],
            target,
            self.back_send.at[at, key],
            self.back_recv.at[at, key],
            (peer, spot.lane),
        )

    def pair(self, near):
        for step in list(range(1, self.spot.half)) + [0]:
            self.pair_copy(step, near).start()

    def pair_sum(self, step, near):
        side = self.side(near)
        mine = self.back[self.spot.lane_at(step, False), side].astype(jnp.float32)
        return mine + self.pair_in[step, side].astype(jnp.float32)

    def middle(self, near):
        for step in range(1, self.spot.half):
            self.pair_copy(step, near).wait_recv()
            total = self.pair_sum(step, near)
            self.across_out[step, self.side(near)] = total.astype(self.total.dtype)
            self.sum_copy(step, near).start()
        self.pair_copy(0, near).wait_recv()

    def last(self, near):
        total = self.pair_sum(0, near)
        for step in range(1, self.spot.half):
            self.sum_copy(step, near).wait_recv()
            total = total + self.across_in[step, self.side(near)].astype(jnp.float32)
        self.total[self.side(near)] = total.astype(self.total.dtype)
        for key in self.keys(near):
            self.back_copy(key).start()

    def finish(self):
        groups, half = self.spot.groups, self.spot.half
        for key in range(1, groups):
            self.back_copy(key).wait_recv()
        self.back_copy(0).wait()
        for near in range(2):
            if self.rows_all is not None:
                self.keep(near).wait()
            for step in range(half):
                self.core(near, step).wait_send()
                self.pair_copy(step, near).wait_send()
                if step:
                    self.across(near, step).wait_send()
                    self.sum_copy(step, near).wait_send()
        for key in range(groups):
            if key:
                self.swap(key).wait_send()
                self.back_copy(key).wait_send()


half_chunks = ((1, 0), (1, 1), (0, 0), (0, 1), (0, 2), (0, 3), (1, 2), (1, 3))


def half_expert(step):
    return step - 2 * ((step // 2 + 1) // 2)


def half_far(step):
    return (step // 2 + 1) // 2 % 2


def experts_kernel(
    experts_here,
    groups,
    columns,
    rows_in,
    gates_in,
    grad_main,
    grad_tail,
    gate_weight,
    up_weight,
    down_weight,
    hidden_ref,
    grad_gate_ref,
    grad_up_ref,
    result_ref,
    rows_all,
    back_out,
    gates_out,
    act_sc,
    act_sems,
    result_main,
    result_tail,
    result_sems,
    *scratch,
):
    now = pl.program_id(0)
    expert = half_expert(now)
    tail_height = result_tail.shape[2]
    half_groups = groups // 2
    sources = half_groups * columns
    main_count, count = sources * main_slots, sources * CAP
    spot = Spot(groups, columns)
    here = spot.place // half_groups
    side_at = here + half_far(now) * (1 - 2 * here)
    side = pl.ds(side_at * half_groups, half_groups)
    mains, tails, sides, sems = scratch[:6], scratch[6:12], scratch[12:18], scratch[18:]
    chunks = [
        RowChunk(
            spot,
            at,
            pl.ds(at * main_slots, main_slots),
            rows_in,
            rows_all,
            back_out,
            [buf.at[at] for buf in mains],
            sems,
        )
        for at in range(experts_here)
    ]
    tail = RowChunk(
        spot,
        experts_here,
        pl.ds(experts_here * main_slots, tail_height),
        rows_in,
        rows_all,
        back_out,
        tails,
        sems,
    )
    scalars = RowChunk(
        spot, experts_here + 1, pl.ds(0, 8), gates_in, None, gates_out, sides, sems
    )

    @pl.when(now == 0)
    def _():
        spot.meet()
        scalars.begin(1)
        tail.begin(1)
        chunks[0].begin(1)
        chunks[1].begin(1)
        scalars.begin(0)
        tail.begin(0)
        chunks[0].begin(0)
        sides[1][...] = jnp.zeros_like(sides[1])

    select = tail_select(expert, sources, tail_height)

    def joined(main, low):
        width = main.shape[-1]
        low = nn_dot(select, low.reshape(-1, width)).astype(jnp.bfloat16)
        return jnp.concatenate([main.reshape(-1, width), low], axis=0)

    raw_hidden = nt_dot(joined(grad_main[:, side], grad_tail[:, side]), down_weight[0])

    def before(step):
        if step == 0:
            scalars.advance(1)
            tail.advance(1)
            chunks[0].advance(1)
            chunks[1].begin(0)
            chunks[1].advance(1)
            scalars.complete(1)
            tail.complete(1)
        elif step == 1:
            scalars.advance(0)
            tail.advance(0)
            chunks[0].advance(0)
            chunks[2].begin(0)
        elif step == 2:
            chunks[1].advance(0)
            chunks[3].begin(0)
            scalars.complete(0)
            tail.complete(0)
        elif step == 3:
            chunks[2].advance(0)
            chunks[2].begin(1)
            chunks[3].begin(1)
        elif step == 4:
            chunks[3].advance(0)
        elif step == 5:
            chunks[2].advance(1)
        elif step == 6:
            chunks[3].advance(1)
        near, at = half_chunks[step]
        chunks[at].complete(near)
        if step:
            near, at = half_chunks[step - 1]
            chunks[at].middle(near)
        if step == 6:
            tail.middle(0)
            scalars.middle(0)

    for step in range(len(half_chunks)):

        @pl.when(now == step)
        def _():
            before(step)

    rows = joined(mains[0][expert, :, side], tails[0][:, side])
    hot, of_slot = slot_lanes(expert, experts_here, sources)
    gate_high, gate_rest = split_low(sides[0][:, side, 0, :].reshape(sources, spare))
    gates = nn_dot(hot, gate_high) + nn_dot(hot, gate_rest)
    gates = jnp.sum(jnp.where(of_slot, gates, 0.0), axis=1, keepdims=True)
    hidden, grad_gate, grad_up, back, grad_gates, result = expert_math(
        rows, gates, raw_hidden, gate_weight[0], up_weight[0], down_weight[0]
    )

    def spread(value, main_target, tail_target):
        low = value.astype(jnp.bfloat16)
        main_target(low[:main_count].reshape(columns, half_groups, main_slots, -1))
        part = tn_dot(select, low[main_count:]).astype(jnp.bfloat16)
        part = part.reshape(columns, half_groups, tail_height, -1)

        @pl.when(expert == 0)
        def _():
            tail_target[:, side] = part

        @pl.when(expert > 0)
        def _():
            tail_target[:, side] += part

    def store_back(value):
        mains[1][expert, :, side] = value

    spread(back, store_back, tails[1])
    side_high, side_rest = split_low(jnp.where(of_slot, grad_gates, 0.0))
    lanes = (tn_dot(hot, side_high) + tn_dot(hot, side_rest)).reshape(columns, half_groups, spare)
    sides[1][:, side, 0, :] += lanes

    def after(step):
        near, at = half_chunks[step]
        chunks[at].pair(near)
        if step == 5:
            tail.pair(0)
            scalars.pair(0)
        if step == 7:
            tail.pair(1)
            scalars.pair(1)
            chunks[at].middle(1)
            tail.middle(1)
            scalars.middle(1)
        if step:
            near, at = half_chunks[step - 1]
            chunks[at].last(near)
        if step == 6:
            tail.last(0)
            scalars.last(0)

    for step in range(len(half_chunks)):

        @pl.when(now == step)
        def _():
            after(step)

    act_rows = pl.ds(pl.multiple_of(side_at * count, 32), count)

    def act_copies():
        outs = (hidden_ref, grad_gate_ref, grad_up_ref)
        return [
            pltpu.make_async_copy(act_sc.at[k], out.at[expert, act_rows], act_sems.at[k])
            for k, out in enumerate(outs)
        ]

    def result_copy():
        place = pl.ds(pl.multiple_of(expert * main_slots, main_slots), main_slots)
        return pltpu.make_async_copy(
            result_main, result_ref.at[:, side, place], result_sems.at[0]
        )

    @pl.when(now > 0)
    def _():
        result_copy().wait()
        for copy in act_copies():
            copy.wait()

    def store_result(value):
        result_main[...] = value

    spread(result, store_result, result_tail)
    act_sc[0] = hidden
    act_sc[1] = grad_gate
    act_sc[2] = grad_up
    result_copy().start()
    for copy in act_copies():
        copy.start()

    @pl.when(now == len(half_chunks) - 1)
    def _():
        place = pl.ds(experts_here * main_slots, tail_height)
        low = pltpu.make_async_copy(result_tail, result_ref.at[:, :, place], result_sems.at[1])
        low.start()
        chunks[-1].last(1)
        tail.last(1)
        scalars.last(1)
        for chunk in chunks + [tail, scalars]:
            chunk.finish()
        result_copy().wait()
        for copy in act_copies():
            copy.wait()
        low.wait()


def experts(rows, gates, grads, gate_weight, up_weight, down_weight, columns):
    experts_here, units, width = gate_weight.shape
    groups, height, wide = rows.shape
    half = columns // 2
    count = columns * groups * CAP
    tail_height = height - experts_here * main_slots
    weight_spec = pl.BlockSpec((1, units, width), lambda t: (half_expert(t), 0, 0))
    act_shape = jax.ShapeDtypeStruct((experts_here, count, units), jnp.bfloat16)
    low = lambda *shape: pltpu.VMEM(shape, jnp.bfloat16)
    bufs = lambda lead, *block, kind=jnp.bfloat16: [
        pltpu.VMEM((*lead, *first, groups, *block), kind)
        for first in ((columns,), (columns,), (half,), (half,), (half,), ())
    ]
    return pl.pallas_call(
        functools.partial(experts_kernel, experts_here, groups, columns),
        grid=(len(half_chunks),),
        out_shape=(
            act_shape,
            act_shape,
            act_shape,
            jax.ShapeDtypeStruct((columns, groups, height, width), jnp.bfloat16),
            jax.ShapeDtypeStruct((columns,) + rows.shape, jnp.bfloat16),
            jax.ShapeDtypeStruct(rows.shape, jnp.bfloat16),
            jax.ShapeDtypeStruct(gates.shape, jnp.float32),
        ),
        in_specs=[anywhere, anywhere]
        + row_specs(grads, experts_here, lambda index: lambda t: index(half_expert(t), 0))
        + [weight_spec] * 3,
        out_specs=(anywhere,) * 7,
        scratch_shapes=[
            low(3, count // 2, units),
            pltpu.SemaphoreType.DMA((3,)),
            low(columns, groups // 2, main_slots, width),
            low(columns, groups, tail_height, width),
            pltpu.SemaphoreType.DMA((2,)),
        ]
        + bufs((experts_here,), main_slots, wide)
        + bufs((), tail_height, wide)
        + bufs((), 8, spare, kind=jnp.float32)
        + RowChunk.sems(groups, columns, experts_here + 2),
        compiler_params=comm_params(10),
        cost_estimate=pl.CostEstimate(
            flops=12 * experts_here * count * width * units,
            transcendentals=experts_here * count * units,
            bytes_accessed=6 * experts_here * width * units + 8 * experts_here * count * width,
        ),
        name="experts",
    )(rows, gates, grads, grads, gate_weight, up_weight, down_weight)


def expert_weight_kernel(
    parts,
    halves,
    row_main,
    row_tail,
    grad_main,
    grad_tail,
    hidden_ref,
    grad_gate_ref,
    grad_up_ref,
    gate_out,
    up_out,
    down_out,
):
    expert, part = pl.program_id(0), pl.program_id(1)
    sources = row_main.shape[0] * row_main.shape[1]
    select = tail_select(expert, sources, row_tail.shape[2])
    if halves == 1:
        rows = expert_input(row_main, row_tail, select)[:, :D]
        grads = expert_input(grad_main, grad_tail, select)
    else:
        groups = row_main.shape[1] // halves
        select = tail_select(expert, sources // halves, row_tail.shape[2])
        sides = [slice(at * groups, (at + 1) * groups) for at in range(halves)]
        both = lambda main, low: jnp.concatenate(
            [expert_input(main[:, side], low[:, side], select) for side in sides], axis=0
        )
        rows, grads = both(row_main, row_tail), both(grad_main, grad_tail)

    @pl.when(part == 0)
    def _():
        gate_out[0] = tn_dot(grad_gate_ref[0], rows)
        up_out[0] = tn_dot(grad_up_ref[0], rows)
        down_out[0] = tn_dot(hidden_ref[0], grads)

    if parts > 1:

        @pl.when(part > 0)
        def _():
            gate_out[0] += tn_dot(grad_gate_ref[0], rows)
            up_out[0] += tn_dot(grad_up_ref[0], rows)
            down_out[0] += tn_dot(hidden_ref[0], grads)


def expert_weight_grads(rows, grads, hidden, grad_gate, grad_up, halves):
    experts_here, count, units = hidden.shape
    width = grads.shape[-1]
    parts = parts_of(rows)
    order = lambda index: index
    act_spec = pl.BlockSpec((1, count // parts, units), lambda e, c: (e, c, 0))
    out_spec = pl.BlockSpec((1, units, width), lambda e, c: (e, 0, 0))
    out_shape = jax.ShapeDtypeStruct((experts_here, units, width), jnp.float32)
    return pl.pallas_call(
        functools.partial(expert_weight_kernel, parts, halves),
        grid=(experts_here, parts),
        out_shape=(out_shape, out_shape, out_shape),
        in_specs=row_specs(rows, experts_here, order)
        + row_specs(grads, experts_here, order)
        + [act_spec] * 3,
        out_specs=(out_spec, out_spec, out_spec),
        compiler_params=pltpu.CompilerParams(vmem_limit_bytes=60 * mega),
        cost_estimate=pl.CostEstimate(
            flops=6 * experts_here * count * width * units,
            transcendentals=0,
            bytes_accessed=12 * experts_here * width * units + 10 * experts_here * count * width,
        ),
        name="expert_weight_grads",
    )(rows, rows, grads, grads, hidden, grad_gate, grad_up)


def pair_slots(token_routes, ranks, experts_here):
    row_count = token_routes.shape[0]
    expert_pair = jnp.concatenate([token_routes[:, 0], token_routes[:, 1]])
    rank_pair = jnp.concatenate([ranks, ranks + row_count])
    earlier = (expert_pair[None, :] == expert_pair[:, None]) & (
        rank_pair[None, :] < rank_pair[:, None]
    )
    slot_index = jnp.sum(earlier.astype(jnp.int32), axis=1)
    height = slot_rows(experts_here)
    local = expert_pair % experts_here
    main_at = local * main_slots + slot_index
    tail_at = experts_here * main_slots + local * tail_slots + slot_index - main_slots
    row = jnp.where(slot_index < main_slots, main_at, tail_at)
    slots = (expert_pair // experts_here) * height + row
    return jnp.where(slot_index < CAP, slots, -1)


def router_head(logits, token_routes, weights):
    token_count = logits.shape[0]
    probabilities = jax.nn.softmax(logits, axis=-1)
    log_totals = jax.nn.logsumexp(logits, axis=-1)
    picked = (token_routes[:, :, None] == jnp.arange(EXPERTS, dtype=jnp.int32)).astype(jnp.float32)
    chosen = jnp.sum(picked * probabilities[:, None, :], axis=-1)
    gate_values = chosen / jnp.sum(chosen, axis=1, keepdims=True)
    shares = jnp.sum(picked, axis=(0, 1)) / (token_count * TOP)
    balance = EXPERTS * jnp.sum(shares * jnp.sum(probabilities, axis=0))
    return (gate_values, weights[0] * jnp.sum(log_totals * log_totals) + weights[1] * balance)


def column(values, rows):
    return jnp.pad(values, (0, rows - values.shape[0]))[:, None]


def shards(
    inputs,
    grad_out,
    prefix,
    routes,
    priority,
    loss_weights,
    norm_attn,
    norm_moe,
    qkv_weight,
    out_weight,
    bias_table,
    router_weight,
    gate_weight,
    up_weight,
    down_weight,
):
    row_count = inputs.shape[0]
    groups = lax.axis_size("expert")
    columns_of = lax.axis_size("shard")
    place = lax.axis_index("expert")
    length = row_count * groups
    heads_here = HEADS // groups
    width = heads_here * HEAD
    experts_here = EXPERTS // groups
    shard_rows = D // columns_of
    height = slot_rows(experts_here)

    packed_small = jnp.concatenate(
        [
            lax.dynamic_slice(
                qkv_weight, (0, third * D + place * width), (shard_rows, width)
            )
            for third in range(3)
        ]
        + [jnp.pad(router_weight, ((0, 0), (0, spare - EXPERTS)))],
        axis=1,
    )
    table_rows = BUCKETS // columns_of
    table_low = bias_table.astype(jnp.float32).reshape(1, table_rows * HEADS)
    gain_rows = jnp.concatenate(
        [
            norm_attn.astype(jnp.float32)[None],
            norm_moe.astype(jnp.float32)[None],
            jnp.pad(table_low, ((0, 0), (0, shard_rows - table_rows * HEADS))),
            jnp.zeros((5, shard_rows), jnp.float32),
        ],
        axis=0,
    )
    token_routes = routes.reshape(row_count, TOP)
    slots = pair_slots(token_routes, priority.reshape(row_count), experts_here)
    slot_map = (
        jnp.arange(groups * height, dtype=jnp.int32)[:, None] == slots[None, :]
    ).reshape(groups * height, TOP, row_count)
    slot_any = jnp.any(slot_map, axis=1).astype(jnp.bfloat16)
    token_slots = jnp.any(
        slots.reshape(TOP, row_count)[:, :, None] == jnp.arange(groups * height, dtype=jnp.int32),
        axis=0,
    ).astype(jnp.bfloat16)
    slot_pairs = slot_map.astype(jnp.bfloat16).reshape(groups * height, TOP * row_count)
    grad_low = grad_out.reshape(row_count, D)
    grad_slots = nn_dot(slot_any, grad_low).astype(jnp.bfloat16).reshape(groups, height, D)
    _, normed_all, qkv_own, small_full, out_full, far_slots, side_slots, gains = entry_gather(
        inputs.reshape(row_count, D),
        gain_rows,
        packed_small,
        out_weight,
        grad_slots,
        3 * width,
        1,
    )
    normed_all = normed_all.reshape(length, D)
    qkv_own = qkv_own.reshape(length, 3 * width)
    small_full = small_full.reshape(D, 3 * width + spare)
    out_full = out_full.reshape(D, D)
    router_full = small_full[:, 3 * width : 3 * width + EXPERTS]
    gain_attn = gains[:, 0].reshape(D)
    gain_moe = gains[:, 1].reshape(D)
    table_full = gains[:, 2, : table_rows * HEADS].reshape(BUCKETS, HEADS)
    table_own = lax.dynamic_slice_in_dim(
        table_full, place * heads_here, heads_here, 1
    )
    near_ids = jnp.asarray(skew_buckets(), jnp.int32)
    near_hot = (near_ids[:, None] == jnp.arange(BUCKETS, dtype=jnp.int32)).astype(jnp.float32)
    base_bias = (
        jnp.dot(near_hot, table_own, precision=lax.Precision.HIGHEST).reshape(3, 2 * tile, heads_here)
        * log2e
    )
    base_bias = jnp.transpose(base_bias, (2, 0, 1)).reshape(heads_here * 3, 2 * tile)
    far_bias = jnp.stack([table_own[15], table_own[31]], axis=1) * log2e

    mixed_own, totals, grads_received = attend_forward(
        prefix, far_bias, base_bias, qkv_own, grad_slots, far_slots, side_slots, columns_of
    )
    attended = exchange_mixed(mixed_own.reshape(groups, row_count, width), columns_of, 8)

    tokens_in = inputs.reshape(row_count, D).astype(jnp.float32)
    middle = tokens_in + nn_dot(attended, out_full)
    normed_two, norm_two_back = jax.vjp(rms_norm, middle, gain_moe)
    low_two = normed_two.astype(jnp.bfloat16)
    logits = nn_dot(low_two, router_full)
    router_out, router_back = jax.vjp(
        lambda logit_in: router_head(logit_in, token_routes, loss_weights), logits
    )
    gate_values = router_out[0]
    slot_gates = jnp.sum(
        slot_map.astype(jnp.float32) * jnp.transpose(gate_values)[None], axis=1
    )
    fused = columns_of * groups <= part_sources and experts_here == 4
    if fused:
        outgoing = nn_dot(slot_any, low_two).astype(jnp.bfloat16).reshape(groups, height, D)
        gate_block = jnp.pad(
            jnp.sum(slot_gates, axis=1).reshape(groups, 1, height),
            ((0, 0), (0, 7), (0, spare - height)),
        )
    else:
        gate_high = lax.reduce_precision(gate_values, 8, 7)
        gate_parts = jnp.stack([gate_high, gate_values - gate_high], axis=-1).astype(jnp.bfloat16)
        wide_rows = jnp.concatenate(
            [
                jnp.broadcast_to(low_two[None], (TOP, row_count, D)),
                jnp.pad(jnp.transpose(gate_parts, (1, 0, 2)), ((0, 0), (0, 0), (0, spare - 2))),
            ],
            axis=2,
        ).reshape(TOP * row_count, D + spare)
        outgoing = nn_dot(slot_pairs, wide_rows).astype(jnp.bfloat16)
        outgoing = outgoing.reshape(groups, height, D + spare)
    gate_across, up_across, down_across = (
        jnp.transpose(weight, (0, 2, 1)) for weight in (gate_weight, up_weight, down_weight)
    )
    if fused:
        (
            hidden,
            grad_gate,
            grad_up,
            result_part,
            rows_received,
            grad_returned,
            side_returned,
        ) = experts(
            outgoing, gate_block, grads_received, gate_across, up_across, down_across, columns_of
        )
        slot_grads = side_returned[:, 0, :height].reshape(groups * height)
        grad_gates = jnp.sum(
            jnp.where(slot_map, slot_grads[:, None, None], 0.0), axis=0
        )
        grad_gates = jnp.transpose(grad_gates)
        grad_returned = grad_returned.reshape(groups * height, D)
    else:
        rows_received = dispatch(outgoing, columns_of, 2)
        hidden, grad_gate, grad_up, result_part, back_part = expert_act(
            rows_received, grads_received, gate_across, up_across, down_across
        )
        grad_returned = collect(back_part, 3).reshape(groups * height, D + spare)
        grad_gates = jnp.transpose(
            tn_dot(slot_pairs, grad_returned[:, D:])[:, 0].reshape(TOP, row_count)
        )
    grad_low_two = nn_dot(token_slots, grad_returned[:, :D])
    grad_top = grad_low.astype(jnp.float32)
    grad_logits = router_back((grad_gates, jnp.ones((), jnp.float32)))[0]
    low_logits = grad_logits.astype(jnp.bfloat16)
    router_grad = tn_dot(low_two, low_logits)
    grad_low_two = grad_low_two + nt_dot(low_logits, router_full)
    grad_middle_norm, gain_moe_grad = norm_two_back(grad_low_two)
    grad_middle = grad_top + grad_middle_norm
    low_middle = grad_middle.astype(jnp.bfloat16)
    out_grad = tn_dot(attended, low_middle)
    grad_attended = nt_dot(low_middle, out_full).astype(jnp.bfloat16)
    grad_attended = jnp.transpose(grad_attended.reshape(row_count, groups, width), (1, 0, 2))
    grad_mixed = lax.all_to_all(
        grad_attended, "expert", split_axis=0, concat_axis=0, tiled=True
    )
    gate_grad, up_grad, down_grad = expert_weight_grads(
        rows_received, grads_received, hidden, grad_gate, grad_up, 2 if fused else 1
    )
    out_sums = lax.psum_scatter(
        out_grad.astype(jnp.bfloat16), "shard", scatter_dimension=0, tiled=True
    ).reshape(groups, shard_rows // groups, D)
    grad_qkv, near_sums, side_sums, returned, out_piece = attend_backward(
        prefix,
        far_bias,
        base_bias,
        qkv_own,
        mixed_own,
        grad_mixed.reshape(length, width),
        totals,
        result_part,
        out_sums,
        columns_of,
    )
    slot_high = lax.reduce_precision(slot_gates, 8, 7)
    slot_parts = jnp.concatenate([slot_high, slot_gates - slot_high], axis=1).astype(jnp.bfloat16)
    mixture = tn_dot(slot_parts, returned.reshape(groups * height, D))
    mixture = mixture[:row_count] + mixture[row_count:]
    output = (middle + mixture).astype(jnp.bfloat16)

    table_grad = jnp.einsum(
        "hil,ilb->bh",
        near_sums.reshape(heads_here, 3, 2 * tile),
        near_hot.reshape(3, 2 * tile, BUCKETS),
        precision=lax.Precision.HIGHEST,
    )
    far_sums = jnp.sum(side_sums, axis=(2, 3))
    bucket_ids = jnp.arange(BUCKETS, dtype=jnp.int32)[:, None]
    table_grad = table_grad + jnp.where(bucket_ids == 15, far_sums[:, 0][None], 0.0)
    table_grad = table_grad + jnp.where(bucket_ids == 31, far_sums[:, 1][None], 0.0)
    table_column = jnp.pad(
        table_grad.reshape(columns_of, table_rows * heads_here),
        ((0, 0), (0, shard_rows - table_rows * heads_here)),
    ).reshape(D, 1)

    extra = jnp.concatenate(
        [
            jnp.zeros((D, 1), jnp.float32),
            table_column,
            gain_moe_grad[:, None],
            router_grad,
            jnp.zeros((D, spare - 3 - EXPERTS), jnp.float32),
        ],
        axis=1,
    ).astype(jnp.bfloat16)
    grad_projected, last_all, out_all, qkv_full = tail_exchange(
        grad_qkv.reshape(groups, row_count, 3 * width),
        normed_all,
        small_full,
        extra,
        out_piece,
        qkv_weight,
        columns_of,
        7,
    )
    last_all = last_all.reshape(groups, shard_rows, 3 * width + spare)
    out_all = out_all.reshape(shard_rows, D)
    if width % 128 == 0:
        input_grad, qkv_total, out_total, extra_total = finish(
            grad_projected,
            qkv_full,
            last_all,
            inputs.reshape(row_count, D),
            gain_attn[None],
            grad_middle,
            out_all,
            width,
        )
    else:
        grad_projected = jnp.transpose(
            grad_projected.reshape(groups, row_count, 3, width), (1, 2, 0, 3)
        ).reshape(row_count, 3 * D)
        grad_low_one = nt_dot(grad_projected, qkv_full.reshape(D, 3 * D))
        _, norm_one_back = jax.vjp(lambda features: rms_norm(features, gain_attn), tokens_in)
        input_grad = grad_middle + norm_one_back(grad_low_one)[0]
        qkv_total = jnp.transpose(
            last_all[:, :, : 3 * width].reshape(groups, shard_rows, 3, width), (1, 2, 0, 3)
        ).reshape(shard_rows, 3 * D).astype(jnp.float32)
        out_total = out_all.astype(jnp.float32)
        extra_total = jnp.sum(last_all[:, :, 3 * width :].astype(jnp.float32), axis=0).T
    table_part = last_all[:, : table_rows * heads_here, 3 * width + 1].astype(jnp.float32)
    table_total = jnp.transpose(
        table_part.reshape(groups, table_rows, heads_here), (1, 0, 2)
    ).reshape(table_rows, HEADS)
    return (
        output.reshape(row_count, 1, D),
        input_grad.reshape(row_count, 1, D),
        extra_total[0] / norm_attn.astype(jnp.float32),
        extra_total[2],
        qkv_total,
        out_total,
        table_total,
        extra_total[3 : 3 + EXPERTS].T,
        jnp.transpose(gate_grad, (0, 2, 1)),
        jnp.transpose(up_grad, (0, 2, 1)),
        jnp.transpose(down_grad, (0, 2, 1)),
    )


def solution(mesh):
    placed = (
        P("expert", "shard", None),
        P("expert", "shard", None),
        P("shard"),
        P("expert", "shard", None),
        P("expert", "shard", None),
        P(),
        P("shard"),
        P("shard"),
        P("shard", None),
        P("shard", None),
        P("shard", None),
        P("shard", None),
        P("expert", None, "shard"),
        P("expert", None, "shard"),
        P("expert", None, "shard"),
    )
    return jax.shard_map(
        shards,
        mesh=mesh,
        in_specs=placed,
        out_specs=(
            P("expert", "shard", None),
            P("expert", "shard", None),
            P("shard"),
            P("shard"),
            P("shard", None),
            P("shard", None),
            P("shard", None),
            P("shard", None),
            P("expert", None, "shard"),
            P("expert", None, "shard"),
            P("expert", None, "shard"),
        ),
        check_vma=False,
    )
```

```python
import functools
import math

import jax
import jax.numpy as jnp
import numpy as np
from jax import lax
from jax.experimental import pallas as pl
from jax.experimental.pallas import tpu as pltpu
from jax.sharding import PartitionSpec as P

D = 1024
HEADS = 16
HEAD = 64
FF = 2816
EXPERTS = 32
TOP = 2
BUCKETS = 32
CAP = 18

epsilon = 1e-06
masked_score = -1e30
far_bounds = (12, 16, 23, 32, 46, 64, 91)
tile = 256
main_slots = 16
tail_slots = CAP - main_slots
log2e = math.log2(math.e)
score_scale = HEAD ** (-0.5)
mega = 1024 * 1024
part_sources = 32
spare = 128


MESH = pl.DeviceIdType.MESH


def flip(index, key):
    out, bit = index, 1
    while bit <= key:
        if key & bit:
            out = out + bit * (1 - 2 * ((index // bit) % 2))
        bit *= 2
    return out


def near_keys(groups):
    return list(range(1, groups // 2))


def far_keys(groups):
    return list(range(groups // 2, groups))


def early_keys(groups):
    return [key for key in far_keys(groups) if key % line_shape(groups)[1] == 0]


class Spot:
    def __init__(self, groups, columns):
        self.groups, self.columns = groups, columns
        self.place = lax.axis_index("expert")
        self.lane = lax.axis_index("shard")
        self.half = columns // 2
        self.chip = self.lane // 2
        self.core = self.lane % 2
        self.partner = self.chip * 2 + 1 - self.core

    def across(self, step):
        return ((self.chip + step) % self.half) * 2 + self.core

    def behind(self, step):
        return ((self.chip + self.half - step) % self.half) * 2 + self.core

    def lane_at(self, step, other):
        chip = (self.chip + step) % self.half
        return chip * 2 + ((1 - self.core) if other else self.core)

    def meet(self):
        barrier = pltpu.get_barrier_semaphore()
        for key in range(1, self.groups):
            peer = (flip(self.place, key), self.lane)
            pl.semaphore_signal(barrier, inc=1, device_id=peer, device_id_type=MESH)
        for step in range(1, self.columns):
            peer = (self.place, (self.lane + step) % self.columns)
            pl.semaphore_signal(barrier, inc=1, device_id=peer, device_id_type=MESH)
        pl.semaphore_wait(barrier, self.groups + self.columns - 2)


def remote(source, target, send_sem, recv_sem, peer):
    return pltpu.make_async_remote_copy(
        src_ref=source,
        dst_ref=target,
        send_sem=send_sem,
        recv_sem=recv_sem,
        device_id=peer,
        device_id_type=MESH,
    )


def line_shape(groups):
    across = groups // 4
    return 4, across


class LineGather:
    def __init__(self, spot, own, full, local_sem, send_sems, recv_sems, rows=None):
        self.spot, self.own, self.full, self.rows = spot, own, full, rows
        self.local_sem, self.send_sems, self.recv_sems = local_sem, send_sems, recv_sems
        self.long, self.wide = line_shape(spot.groups)
        self.z = spot.place // self.wide
        self.y = spot.place % self.wide

    @staticmethod
    def sems(groups):
        long, wide = line_shape(groups)
        return [
            pltpu.SemaphoreType.DMA(()),
            pltpu.SemaphoreType.DMA((2 * long - 1, wide + 1)),
            pltpu.SemaphoreType.DMA((groups,)),
        ]

    def block(self, origin):
        return self.full.at[origin] if self.rows is None else self.full.at[origin, self.rows]

    def copy(self, job, way, origin, source, target):
        return remote(
            source,
            self.block(origin),
            self.send_sems.at[job, way],
            self.recv_sems.at[origin],
            (target, self.spot.lane),
        )

    def each(self, job, origin, source, up, down, act):
        place, wide = self.spot.place, self.wide
        if up:

            @pl.when(self.z + 1 < self.long)
            def _():
                act(self.copy(job, 0, origin, source, place + wide))

        if down:

            @pl.when(self.z >= 1)
            def _():
                act(self.copy(job, 1, origin, source, place - wide))

        for step in range(1, wide):
            target = self.z * wide + (self.y + step) % wide
            act(self.copy(job, 1 + step, origin, source, target))

    def begin(self):
        place = self.spot.place
        self.each(0, place, self.own, True, True, lambda copy: copy.start())
        pltpu.make_async_copy(self.own, self.block(place), self.local_sem).start()

    def arrive(self, origin):
        self.copy(0, 0, origin, self.own, self.spot.place).wait_recv()

    def hop(self, k):
        place, wide = self.spot.place, self.wide

        @pl.when(self.z >= k)
        def _():
            origin = place - k * wide
            self.arrive(origin)
            self.each(k, origin, self.block(origin), True, False, lambda copy: copy.start())

        @pl.when(self.z + k < self.long)
        def _():
            origin = place + k * wide
            self.arrive(origin)
            job = self.long - 1 + k
            self.each(job, origin, self.block(origin), False, True, lambda copy: copy.start())

    def finish(self):
        for row in range(self.long):
            for step in range(1, self.wide):
                self.arrive(row * self.wide + (self.y + step) % self.wide)
        self.settle()

    def settle(self):
        place, wide = self.spot.place, self.wide
        stop = lambda copy: copy.wait_send()
        self.each(0, place, self.own, True, True, stop)
        for k in range(1, self.long):

            @pl.when(self.z >= k)
            def _():
                origin = place - k * wide
                self.each(k, origin, self.block(origin), True, False, stop)

            @pl.when(self.z + k < self.long)
            def _():
                origin = place + k * wide
                job = self.long - 1 + k
                self.each(job, origin, self.block(origin), False, True, stop)

        pltpu.make_async_copy(self.own, self.block(place), self.local_sem).wait()


class ColumnGather:
    def __init__(self, spot, own, full, local_sem, across_send, across_recv, core_send, core_recv):
        self.spot, self.own, self.full = spot, own, full
        self.local_sem = local_sem
        self.across_send, self.across_recv = across_send, across_recv
        self.core_send, self.core_recv = core_send, core_recv

    @staticmethod
    def sems(columns):
        return [pltpu.SemaphoreType.DMA(())] + [pltpu.SemaphoreType.DMA((columns // 2,))] * 4

    def across_copy(self, step):
        spot = self.spot
        return remote(
            self.own,
            self.full.at[spot.lane],
            self.across_send.at[step],
            self.across_recv.at[step],
            (spot.place, spot.across(step)),
        )

    def core_copy(self, step):
        spot = self.spot
        source = self.own if step == 0 else self.full.at[spot.behind(step)]
        target = spot.lane if step == 0 else spot.behind(step)
        return remote(
            source,
            self.full.at[target],
            self.core_send.at[step],
            self.core_recv.at[step],
            (spot.place, spot.partner),
        )

    def begin(self):
        for step in range(1, self.spot.half):
            self.across_copy(step).start()
        self.core_copy(0).start()
        pltpu.make_async_copy(self.own, self.full.at[self.spot.lane], self.local_sem).start()

    def forward(self):
        for step in range(1, self.spot.half):
            self.across_copy(step).wait_recv()
            self.core_copy(step).start()

    def finish(self):
        for step in range(self.spot.half):
            self.core_copy(step).wait_recv()
        for step in range(self.spot.half):
            self.core_copy(step).wait_send()
        for step in range(1, self.spot.half):
            self.across_copy(step).wait_send()
        pltpu.make_async_copy(self.own, self.full.at[self.spot.lane], self.local_sem).wait()


def comm_params(which, limit=60):
    return pltpu.CompilerParams(
        collective_id=which, has_side_effects=True, vmem_limit_bytes=limit * mega
    )


anywhere = pl.BlockSpec(memory_space=pl.ANY)


def entry_kernel(
    groups,
    columns,
    tokens,
    gain,
    pack,
    out_weight,
    rows,
    tokens_all,
    normed_all,
    qkv_all,
    pack_all,
    out_all,
    far_rows,
    side_rows,
    gain_all,
    token_sc,
    normed_sc,
    qkv_sc,
    gain_sc,
    pack_sc,
    token_sem,
    normed_sems,
    qkv_sems,
    pack_sem,
    gain_sem,
    *sems,
):
    spot = Spot(groups, columns)
    half_rows = tokens.shape[0] // 2
    lines = [
        LineGather(spot, tokens.at[rows_at], tokens_all, *line_sems, rows=rows_at)
        for rows_at, line_sems in (
            (pl.ds(0, half_rows), sems[:3]),
            (pl.ds(half_rows, half_rows), sems[3:6]),
        )
    ]
    line, sems = lines[0], sems[3:]
    gains = ColumnGather(spot, gain, gain_sc, *sems[3:8])
    packs = ColumnGather(spot, pack, pack_sc, *sems[8:13])
    outs = ColumnGather(spot, out_weight, out_all, *sems[13:18])
    far_send, far_recv, side_send, side_recv = sems[18:]
    wide = qkv_sc.shape[2]

    def far_copy(key):
        peer = flip(spot.place, key)
        return remote(
            rows.at[peer],
            far_rows.at[spot.place],
            far_send.at[key],
            far_recv.at[key],
            (peer, spot.lane),
        )

    def side_copy(key, step):
        at = flip(spot.place, key)
        return remote(
            far_rows.at[at] if key else rows.at[at],
            side_rows.at[step - 1, at],
            side_send.at[key, step],
            side_recv.at[key, step],
            (spot.place, spot.across(step)),
        )

    def stores(origin):
        return (
            pltpu.make_async_copy(
                normed_sc.at[origin], normed_all.at[origin], normed_sems.at[origin]
            ),
            pltpu.make_async_copy(qkv_sc.at[origin], qkv_all.at[origin], qkv_sems.at[origin]),
        )

    def project(origin, source):
        load = pltpu.make_async_copy(source, token_sc, token_sem)
        load.start()
        load.wait()
        features = token_sc[...].astype(jnp.float32)
        factor = lax.rsqrt(jnp.mean(features * features, axis=-1, keepdims=True) + epsilon)
        gain_row = jnp.concatenate([gain_sc[at, 0:1, :] for at in range(columns)], axis=1)
        normed = (features * factor * gain_row).astype(jnp.bfloat16)
        normed_sc[origin] = normed
        weight = pack_sc[...].reshape(D, -1)[:, :wide]
        qkv_sc[origin] = nn_dot(normed, weight).astype(jnp.bfloat16)
        for store in stores(origin):
            store.start()

    spot.meet()
    for line in lines:
        line.begin()
    gains.begin()
    packs.begin()
    outs.begin()
    gains.forward()
    packs.forward()
    gains.finish()
    packs.finish()
    keep = pltpu.make_async_copy(pack_sc, pack_all, pack_sem)
    keep.start()
    keep_gain = pltpu.make_async_copy(gain_sc, gain_all, gain_sem)
    keep_gain.start()
    project(spot.place, tokens)
    for line in lines:
        line.hop(1)
    outs.forward()
    for step in range(1, spot.half):
        side_copy(0, step).start()
    for line in lines:
        line.hop(2)
    for key in early_keys(groups):
        far_copy(key).start()
    for line in lines:
        line.hop(3)

    def own_column(row, carry):
        @pl.when(row != line.z)
        def _():
            origin = row * line.wide + line.y
            project(origin, tokens_all.at[origin])

        return carry

    lax.fori_loop(0, line.long, own_column, 0)

    for key in early_keys(groups):
        far_copy(key).wait_recv()
        for step in range(1, spot.half):
            side_copy(key, step).start()

    def other_column(at, carry):
        row = line.z + ((at + 1) // 2) * (1 - 2 * (at % 2))

        @pl.when((row >= 0) & (row < line.long))
        def _():
            for step in range(1, line.wide):
                origin = row * line.wide + (line.y + step) % line.wide
                for part in lines:
                    part.arrive(origin)
                project(origin, tokens_all.at[origin])

        return carry

    lax.fori_loop(0, 2 * line.long - 1, other_column, 0)
    for line in lines:
        line.settle()
    for key in early_keys(groups):
        far_copy(key).wait_send()
    for key in [0] + early_keys(groups):
        for step in range(1, spot.half):
            side_copy(key, step).wait_recv()
            side_copy(key, step).wait_send()
    outs.finish()
    keep.wait()
    keep_gain.wait()
    for origin in range(groups):
        for store in stores(origin):
            store.wait()


def entry_gather(tokens, gain, pack, out_weight, rows, wide, which):
    groups = rows.shape[0]
    columns = D // out_weight.shape[0]
    count = tokens.shape[0]
    low = lambda *shape: jax.ShapeDtypeStruct(shape, jnp.bfloat16)
    dma = pltpu.SemaphoreType.DMA
    return pl.pallas_call(
        functools.partial(entry_kernel, groups, columns),
        out_shape=(
            low(groups, *tokens.shape),
            low(groups, *tokens.shape),
            low(groups, count, wide),
            low(columns, *pack.shape),
            low(columns, *out_weight.shape),
            low(*rows.shape),
            low(columns // 2 - 1, *rows.shape),
            jax.ShapeDtypeStruct((columns,) + gain.shape, jnp.float32),
        ),
        in_specs=[anywhere] * 5,
        out_specs=(anywhere,) * 8,
        scratch_shapes=[
            pltpu.VMEM(tokens.shape, jnp.bfloat16),
            pltpu.VMEM((groups,) + tokens.shape, jnp.bfloat16),
            pltpu.VMEM((groups, count, wide), jnp.bfloat16),
            pltpu.VMEM((columns,) + gain.shape, jnp.float32),
            pltpu.VMEM((columns,) + pack.shape, jnp.bfloat16),
            dma(()),
            dma((groups,)),
            dma((groups,)),
            dma(()),
            dma(()),
        ]
        + LineGather.sems(groups) * 2
        + ColumnGather.sems(columns) * 3
        + [dma((groups,))] * 2
        + [dma((groups, columns // 2))] * 2,
        compiler_params=comm_params(which),
        name="entry_gather",
    )(tokens, gain, pack, out_weight, rows)


class Dispatch:
    def __init__(self, spot, rows, full, sems):
        self.spot, self.rows, self.full = spot, rows, full
        self.local, self.send, self.recv = sems[:3]
        self.across_send, self.across_recv, self.core_send, self.core_recv = sems[3:]

    @staticmethod
    def sems(groups, columns):
        return (
            [pltpu.SemaphoreType.DMA(())]
            + [pltpu.SemaphoreType.DMA((groups,))] * 2
            + [pltpu.SemaphoreType.DMA((groups, columns // 2))] * 4
        )

    def own(self):
        spot = self.spot
        return pltpu.make_async_copy(
            self.rows.at[spot.place], self.full.at[spot.lane, spot.place], self.local
        )

    def swap(self, key):
        spot = self.spot
        peer = flip(spot.place, key)
        return remote(
            self.rows.at[peer],
            self.full.at[spot.lane, spot.place],
            self.send.at[key],
            self.recv.at[key],
            (peer, spot.lane),
        )

    def across(self, key, step):
        spot = self.spot
        block = self.full.at[spot.lane, flip(spot.place, key)]
        return remote(
            block,
            block,
            self.across_send.at[key, step],
            self.across_recv.at[key, step],
            (spot.place, spot.across(step)),
        )

    def core(self, key, step):
        spot = self.spot
        block = self.full.at[spot.behind(step), flip(spot.place, key)]
        return remote(
            block,
            block,
            self.core_send.at[key, step],
            self.core_recv.at[key, step],
            (spot.place, spot.partner),
        )

    def begin(self):
        groups = self.spot.groups
        self.own().start()
        for key in far_keys(groups) + near_keys(groups):
            self.swap(key).start()

    def advance(self, key):
        if key == 0:
            self.own().wait()
        else:
            self.swap(key).wait_recv()
        for step in range(1, self.spot.half):
            self.across(key, step).start()
        self.core(key, 0).start()

    def pass_on(self, key):
        for step in range(1, self.spot.half):
            self.across(key, step).wait_recv()
            self.core(key, step).start()

    def finish(self):
        groups, half = self.spot.groups, self.spot.half
        for key in range(groups):
            for step in range(half):
                self.core(key, step).wait_recv()
        for key in range(groups):
            if key > 0:
                self.swap(key).wait_send()
            for step in range(1, half):
                self.across(key, step).wait_send()
            for step in range(half):
                self.core(key, step).wait_send()


def dispatch_kernel(groups, columns, rows, full, *sems):
    spot = Spot(groups, columns)
    job = Dispatch(spot, rows, full, sems)
    spot.meet()
    job.begin()
    for key in range(groups):
        job.advance(key)
        if key:
            job.pass_on(key - 1)
    job.pass_on(groups - 1)
    job.finish()


def dispatch(rows, columns, which):
    groups = rows.shape[0]
    return pl.pallas_call(
        functools.partial(dispatch_kernel, groups, columns),
        out_shape=jax.ShapeDtypeStruct((columns,) + rows.shape, rows.dtype),
        in_specs=[anywhere],
        out_specs=anywhere,
        scratch_shapes=Dispatch.sems(groups, columns),
        compiler_params=comm_params(which),
        name="dispatch_rows",
    )(rows)


class Exchange:
    def __init__(self, spot, blocks, thirds, local, send, recv):
        self.spot, self.blocks, self.thirds = spot, blocks, range(thirds)
        self.local, self.send, self.recv = local, send, recv

    @staticmethod
    def sems(groups, thirds):
        return [pltpu.SemaphoreType.DMA((thirds,))] + [
            pltpu.SemaphoreType.DMA((groups, thirds))
        ] * 2

    def copy(self, key, third):
        spot = self.spot
        peer = flip(spot.place, key)
        source, target = self.blocks(peer, third)
        if key == 0:
            return pltpu.make_async_copy(source, target, self.local.at[third])
        return remote(
            source,
            target,
            self.send.at[key, third],
            self.recv.at[key, third],
            (peer, spot.lane),
        )

    def start(self, key):
        for third in self.thirds:
            self.copy(key, third).start()

    def begin(self):
        groups = self.spot.groups
        for key in far_keys(groups) + near_keys(groups) + [0]:
            self.start(key)

    def arrive(self):
        for key in range(self.spot.groups):
            for third in self.thirds:
                copy = self.copy(key, third)
                copy.wait() if key == 0 else copy.wait_recv()

    def finish(self):
        for key in range(1, self.spot.groups):
            for third in self.thirds:
                self.copy(key, third).wait_send()


class ColumnSum:
    def __init__(self, spot, chunks, order, part, bufs, sems):
        self.spot, self.chunks, self.order, self.part = spot, chunks, order, part
        self.pair_in, self.mine, self.across_out, self.across_in = bufs
        self.local, self.pair_send, self.pair_recv, self.across_send, self.across_recv = sems

    @staticmethod
    def scratch(columns, chunks, block):
        half = columns // 2
        return [pltpu.VMEM((half, chunks) + block, jnp.bfloat16)] * 4 + [
            pltpu.SemaphoreType.DMA((half, chunks))
        ] * 5

    def pair_copy(self, step, k):
        spot = self.spot
        return remote(
            self.part.at[spot.lane_at(step, True), self.order(k)],
            self.pair_in.at[step, k],
            self.pair_send.at[step, k],
            self.pair_recv.at[step, k],
            (spot.place, spot.partner),
        )

    def mine_copy(self, step, k):
        return pltpu.make_async_copy(
            self.part.at[self.spot.lane_at(step, False), self.order(k)],
            self.mine.at[step, k],
            self.local.at[step, k],
        )

    def across_copy(self, step, k):
        spot = self.spot
        return remote(
            self.across_out.at[step, k],
            self.across_in.at[step, k],
            self.across_send.at[step, k],
            self.across_recv.at[step, k],
            (spot.place, spot.across(step)),
        )

    def begin(self):
        half = self.spot.half
        for k in range(self.chunks):
            for step in list(range(1, half)) + [0]:
                self.pair_copy(step, k).start()
                self.mine_copy(step, k).start()

    def pair_sum(self, step, k):
        self.pair_copy(step, k).wait_recv()
        self.mine_copy(step, k).wait()
        return self.mine[step, k].astype(jnp.float32) + self.pair_in[step, k].astype(jnp.float32)

    def middle(self, k):
        for step in range(1, self.spot.half):
            self.across_out[step, k] = self.pair_sum(step, k).astype(jnp.bfloat16)
            self.across_copy(step, k).start()

    def last(self, k):
        total = self.pair_sum(0, k)
        for step in range(1, self.spot.half):
            self.across_copy(step, k).wait_recv()
            total = total + self.across_in[step, k].astype(jnp.float32)
        return total.astype(jnp.bfloat16)

    def finish(self):
        for k in range(self.chunks):
            for step in range(self.spot.half):
                self.pair_copy(step, k).wait_send()
                if step:
                    self.across_copy(step, k).wait_send()


class Collect:
    def __init__(self, spot, part, out, scratch):
        self.spot, self.total = spot, scratch[9]
        self.keys = far_keys(spot.groups) + near_keys(spot.groups) + [0]
        self.sums = ColumnSum(
            spot,
            spot.groups,
            lambda k: flip(spot.place, self.keys[k]),
            part,
            scratch[:4],
            scratch[4:9],
        )
        self.out = out
        self.local, self.send, self.recv = scratch[10:]

    @staticmethod
    def scratch(columns, groups, block):
        return (
            ColumnSum.scratch(columns, groups, block)
            + [pltpu.VMEM((groups,) + block, jnp.bfloat16)]
            + [pltpu.SemaphoreType.DMA(())]
            + [pltpu.SemaphoreType.DMA((groups,))] * 2
        )

    def copy(self, k):
        spot, key = self.spot, self.keys[k]
        target = self.out.at[spot.place]
        if key == 0:
            return pltpu.make_async_copy(self.total.at[k], target, self.local)
        peer = flip(spot.place, key)
        return remote(
            self.total.at[k], target, self.send.at[k], self.recv.at[k], (peer, spot.lane)
        )

    def begin(self):
        self.sums.begin()

    def middle(self, key):
        self.sums.middle(key)

    def last(self, key):
        self.total[key] = self.sums.last(key)
        self.copy(key).start()

    def finish(self):
        last = self.spot.groups - 1
        for k in range(last):
            self.copy(k).wait_recv()
        for k in range(last):
            self.copy(k).wait_send()
        self.copy(last).wait()
        self.sums.finish()


def collect_kernel(groups, columns, part, out, *scratch):
    spot = Spot(groups, columns)
    job = Collect(spot, part, out, scratch)
    spot.meet()
    job.begin()
    ahead = 2
    for key in range(ahead):
        job.middle(key)
    for key in range(groups):
        if key + ahead < groups:
            job.middle(key + ahead)
        job.last(key)
    job.finish()


def collect(part, which):
    columns, groups = part.shape[:2]
    block = part.shape[2:]
    return pl.pallas_call(
        functools.partial(collect_kernel, groups, columns),
        out_shape=jax.ShapeDtypeStruct((groups,) + block, part.dtype),
        in_specs=[anywhere],
        out_specs=anywhere,
        scratch_shapes=Collect.scratch(columns, groups, block),
        compiler_params=comm_params(which),
        name="collect_rows",
    )(part)


def lanes_at(place, width):
    return pl.ds(pl.multiple_of(place * width, 128), width)


def mixed_kernel(groups, columns, mixed, attended, *sems):
    spot = Spot(groups, columns)
    width = mixed.shape[2]

    def blocks(at, third):
        if width % 128:
            return mixed.at[at], attended.at[spot.place]
        return mixed.at[at], attended.at[:, lanes_at(spot.place, width)]

    job = Exchange(spot, blocks, 1, *sems)
    spot.meet()
    job.begin()
    job.arrive()
    job.finish()


def exchange_mixed(mixed, columns, which):
    groups, rows, width = mixed.shape
    shape = mixed.shape if width % 128 else (rows, groups * width)
    out = pl.pallas_call(
        functools.partial(mixed_kernel, groups, columns),
        out_shape=jax.ShapeDtypeStruct(shape, mixed.dtype),
        in_specs=[anywhere],
        out_specs=anywhere,
        scratch_shapes=Exchange.sems(groups, 1),
        compiler_params=comm_params(which),
        name="exchange_mixed",
    )(mixed)
    if width % 128:
        out = jnp.transpose(out, (1, 0, 2)).reshape(rows, groups * width)
    return out


class Tail:
    def __init__(self, spot, chunks, refs, scratch):
        grads, part, piece, weight, grads_out, sum_all, piece_all, weight_all = refs
        groups = spot.groups
        width = grads.shape[2] // 3
        thirds = 3 if width % 128 == 0 else 1

        def blocks(at, third):
            if thirds == 1:
                return grads.at[at], grads_out.at[spot.place]
            columns_to = pl.ds(pl.multiple_of(third * D + spot.place * width, 128), width)
            return grads.at[at, :, pl.ds(third * width, width)], grads_out.at[:, columns_to]

        self.chunks = chunks
        self.sums = ColumnSum(spot, chunks, lambda k: k, part, scratch[:4], scratch[4:9])
        self.own_sum = scratch[9]
        self.swap = Exchange(spot, blocks, thirds, *scratch[10:13])
        self.line = LineGather(spot, self.own_sum, sum_all, *scratch[13:16])
        self.side = LineGather(spot, piece, piece_all, *scratch[16:19])
        self.column = ColumnGather(spot, weight, weight_all, *scratch[19:24])

    @staticmethod
    def scratch(columns, groups, chunks, block, thirds):
        return (
            ColumnSum.scratch(columns, chunks, block)
            + [pltpu.VMEM((chunks,) + block, jnp.bfloat16)]
            + Exchange.sems(groups, thirds)
            + LineGather.sems(groups) * 2
            + ColumnGather.sems(columns)
        )


def tail_kernel(
    groups,
    columns,
    chunks,
    grads,
    normed,
    own_weight,
    extra,
    piece,
    weight,
    grads_out,
    sum_all,
    piece_all,
    weight_all,
    grads_sc,
    normed_sc,
    load_sems,
    part,
    *scratch,
):
    spot = Spot(groups, columns)
    refs = (grads, part, piece, weight, grads_out, sum_all, piece_all, weight_all)
    tail = Tail(spot, chunks, refs, scratch)
    wide = grads.shape[2]
    block_rows = D // (columns * chunks)
    loads = [
        pltpu.make_async_copy(grads, grads_sc, load_sems.at[0]),
        pltpu.make_async_copy(normed, normed_sc, load_sems.at[1]),
    ]
    for load in loads:
        load.start()
    far = far_keys(groups)
    early, late = far[: len(far) // 2], far[len(far) // 2 :]
    spot.meet()
    tail.side.begin()
    for key in early + near_keys(groups) + [0]:
        tail.swap.start(key)
    for load in loads:
        load.wait()
    all_grads = grads_sc[...].reshape(-1, wide)

    for at in range(columns * chunks):
        rows = pl.ds(at * block_rows, block_rows)
        grad = tn_dot(normed_sc[:, rows], all_grads)
        weights = own_weight[rows, :][:, :wide].astype(jnp.float32)
        gain = jnp.sum(grad * weights, axis=1, keepdims=True)
        lanes = lax.broadcasted_iota(jnp.int32, (block_rows, spare), 1)
        side = jnp.where(lanes == 0, gain, extra[rows, :].astype(jnp.float32))
        part[at // chunks, at % chunks] = jnp.concatenate([grad, side], axis=1).astype(jnp.bfloat16)
    tail.sums.begin()
    for k in range(chunks):
        tail.sums.middle(k)
    tail.column.begin()
    tail.side.hop(1)
    for k in range(chunks):
        tail.own_sum[k] = tail.sums.last(k)
    tail.line.begin()
    tail.side.hop(2)
    tail.line.hop(1)
    tail.side.hop(3)
    tail.line.hop(2)
    for key in late:
        tail.swap.start(key)
    tail.line.hop(3)
    tail.column.forward()
    tail.side.finish()
    tail.swap.arrive()
    tail.line.finish()
    tail.column.finish()
    tail.swap.finish()
    tail.sums.finish()


def tail_exchange(grads, normed, own_weight, extra, piece, weight, columns, which):
    groups, row_count, wide = grads.shape
    apart = wide // 3 % 128 != 0
    grads_shape = grads.shape if apart else (row_count, wide * groups)
    chunks = 2
    block = (D // columns // chunks, wide + spare)
    shape_of = lambda shape: jax.ShapeDtypeStruct(shape, jnp.bfloat16)
    inside = pl.BlockSpec(memory_space=pltpu.VMEM)
    return pl.pallas_call(
        functools.partial(tail_kernel, groups, columns, chunks),
        out_shape=(
            shape_of(grads_shape),
            shape_of((groups, chunks) + block),
            shape_of((groups,) + piece.shape),
            shape_of((columns,) + weight.shape),
        ),
        in_specs=[anywhere, anywhere, inside, inside, anywhere, anywhere],
        out_specs=(anywhere,) * 4,
        scratch_shapes=[
            pltpu.VMEM(grads.shape, jnp.bfloat16),
            pltpu.VMEM(normed.shape, jnp.bfloat16),
            pltpu.SemaphoreType.DMA((2,)),
            pltpu.VMEM((columns, chunks) + block, jnp.bfloat16),
        ]
        + Tail.scratch(columns, groups, chunks, block, 1 if apart else 3),
        compiler_params=comm_params(which),
        name="tail_exchange",
    )(grads, normed, own_weight, extra, piece, weight)


def finish_kernel(
    width,
    grads,
    weight,
    packed,
    packed_extra,
    tokens,
    gain,
    grad_middle,
    out_low,
    input_grad,
    qkv_grad,
    out_grad,
    extra,
    total_sc,
):
    third = pl.program_id(0)
    for group in range(packed.shape[0]):
        qkv_grad[:, group * width : (group + 1) * width] = packed[group].astype(jnp.float32)
    part = nt_dot(grads[...], weight[...].reshape(D, -1))

    @pl.when(third == 0)
    def _():
        total_sc[...] = part

    @pl.when(third > 0)
    def _():
        total_sc[...] += part

    @pl.when(third == 2)
    def _():
        features = tokens[...].astype(jnp.float32)
        factor = lax.rsqrt(jnp.mean(features * features, axis=-1, keepdims=True) + epsilon)
        unit = features * factor
        scaled = total_sc[...] * gain[...]
        inner = jnp.mean(scaled * unit, axis=-1, keepdims=True)
        input_grad[...] = grad_middle[...] + factor * (scaled - unit * inner)
        out_grad[...] = out_low[...].astype(jnp.float32)
        extra[...] = jnp.transpose(jnp.sum(packed_extra[...].astype(jnp.float32), axis=0))


def finish(grads, weight, packed, tokens, gain, grad_middle, out_low, width):
    groups, shard_rows = packed.shape[:2]
    columns = weight.shape[0]
    rows = grads.shape[0]
    whole = lambda t: (0, 0)
    full = jax.ShapeDtypeStruct((rows, D), jnp.float32)
    return pl.pallas_call(
        functools.partial(finish_kernel, width),
        grid=(3,),
        out_shape=(
            full,
            jax.ShapeDtypeStruct((shard_rows, 3 * D), jnp.float32),
            jax.ShapeDtypeStruct((shard_rows, D), jnp.float32),
            jax.ShapeDtypeStruct((spare, shard_rows), jnp.float32),
        ),
        in_specs=[
            pl.BlockSpec((rows, D), lambda t: (0, t)),
            pl.BlockSpec((columns, shard_rows, D), lambda t: (0, 0, t)),
            pl.BlockSpec((groups, shard_rows, width), lambda t: (0, 0, t)),
            pl.BlockSpec((groups, shard_rows, spare), lambda t: (0, 0, 3 * width // spare)),
            pl.BlockSpec((rows, D), whole),
            pl.BlockSpec((1, D), whole),
            pl.BlockSpec((rows, D), whole),
            pl.BlockSpec((shard_rows, D), whole),
        ],
        out_specs=(
            pl.BlockSpec((rows, D), whole),
            pl.BlockSpec((shard_rows, D), lambda t: (0, t)),
            pl.BlockSpec((shard_rows, D), whole),
            pl.BlockSpec((spare, shard_rows), whole),
        ),
        scratch_shapes=[pltpu.VMEM((rows, D), jnp.float32)],
        compiler_params=pltpu.CompilerParams(vmem_limit_bytes=60 * mega),
        name="finish",
    )(grads, weight, packed, packed, tokens, gain, grad_middle, out_low)


def rms_norm(features, scales):
    factor = lax.rsqrt(jnp.mean(features * features, axis=-1, keepdims=True) + epsilon)
    return features * factor * scales


def buckets_of(offsets):
    distance = np.abs(offsets)
    beyond = 8 + np.sum(distance[..., None] >= np.array(far_bounds), axis=-1)
    return np.where(distance < 8, distance, beyond) + 16 * (offsets > 0)


def skew_buckets():
    lanes = np.arange(2 * tile)
    from_query = np.where(lanes < tile, -lanes, 2 * tile - lanes)
    return np.concatenate([buckets_of(near * tile + from_query) for near in (-1, 0, 1)])


def lane_row_mask(head, width, rows):
    lanes = lax.broadcasted_iota(jnp.int32, (rows, width), 1)
    return (lanes >= head * HEAD) & (lanes < (head + 1) * HEAD)


def fold_rows(block, op):
    return op(block.reshape(block.shape[0] // 8, 8, block.shape[1]), axis=0)


def nt_dot(left, right):
    return lax.dot_general(left, right, (((1,), (1,)), ((), ())), preferred_element_type=jnp.float32)


def tn_dot(left, right):
    return lax.dot_general(left, right, (((0,), (0,)), ((), ())), preferred_element_type=jnp.float32)


def nn_dot(left, right):
    return jnp.dot(left, right, preferred_element_type=jnp.float32)


def build_bias(base_ref, far_ref, bias_sc, heads_here):
    for head in range(heads_here):
        for near in range(3):
            row = base_ref[pl.ds(head * 3 + near, 1), :]
            wide = jnp.broadcast_to(row, (tile, 2 * tile))
            skewed = pltpu.roll(wide, 0, 1, stride=1, stride_axis=0)
            bias_sc[head, near] = skewed[:, :tile]
        bias_sc[head, 3] = jnp.full((tile, tile), far_ref[head, 1], jnp.float32)


def unskew_sum(wide):
    lanes = wide.shape[1]
    half = wide.shape[0] // 2
    while half >= 8:
        wide = wide[:half] + pltpu.roll(wide[half:], lanes - half, 1)
        half //= 2
    total = wide[0:1]
    for row in range(1, 8):
        total = total + pltpu.roll(wide[row : row + 1], lanes - row, 1)
    return total


def rows_at(index):
    return pl.ds(pl.multiple_of(index * tile, tile), tile)


def visible_tile(key_tile, query_tile, prefix_length):
    key_pos = key_tile * tile + lax.broadcasted_iota(jnp.int32, (tile, tile), 0)
    query_pos = query_tile * tile + lax.broadcasted_iota(jnp.int32, (tile, tile), 1)
    return (key_pos <= query_pos) | (key_pos < prefix_length)


class Spread:
    def __init__(self, spot, rows, far_rows, side_rows, full, sems):
        self.spot, self.rows, self.full = spot, rows, full
        self.far_rows, self.side_rows = far_rows, side_rows
        self.send, self.recv, self.local = sems[:3]
        self.across_send, self.across_recv, self.core_send, self.core_recv = sems[3:]
        self.early = early_keys(spot.groups)
        self.rest = [key for key in far_keys(spot.groups) if key not in self.early]
        self.near = near_keys(spot.groups)

    @staticmethod
    def sems(groups, columns):
        half = columns // 2
        return [pltpu.SemaphoreType.DMA((groups,))] * 2 + [
            pltpu.SemaphoreType.DMA((groups, half))
        ] * 5

    def source(self, key, step):
        spot = self.spot
        at = flip(spot.place, key)
        if key and key not in self.early:
            return self.full.at[spot.behind(step), at]
        if step:
            return self.side_rows.at[step - 1, at]
        return self.far_rows.at[at] if key else self.rows.at[at]

    def local_copy(self, key, step):
        spot = self.spot
        target = self.full.at[spot.behind(step), flip(spot.place, key)]
        return pltpu.make_async_copy(self.source(key, step), target, self.local.at[key, step])

    def swap(self, key):
        spot = self.spot
        peer = flip(spot.place, key)
        return remote(
            self.rows.at[peer],
            self.full.at[spot.lane, spot.place],
            self.send.at[key],
            self.recv.at[key],
            (peer, spot.lane),
        )

    def across(self, key, step):
        spot = self.spot
        block = self.full.at[spot.lane, flip(spot.place, key)]
        return remote(
            block,
            block,
            self.across_send.at[key, step],
            self.across_recv.at[key, step],
            (spot.place, spot.across(step)),
        )

    def core(self, key, step):
        spot = self.spot
        return remote(
            self.source(key, step),
            self.full.at[spot.behind(step), flip(spot.place, key)],
            self.core_send.at[key, step],
            self.core_recv.at[key, step],
            (spot.place, spot.partner),
        )

    def begin(self):
        for key in self.rest + self.near:
            self.swap(key).start()
        for key in [0] + self.early:
            for step in range(self.spot.half):
                self.core(key, step).start()
                self.local_copy(key, step).start()

    def advance(self, key):
        self.swap(key).wait_recv()
        for step in range(1, self.spot.half):
            self.across(key, step).start()
        self.core(key, 0).start()

    def pass_on(self, key):
        for step in range(1, self.spot.half):
            self.across(key, step).wait_recv()
            self.core(key, step).start()

    def finish(self):
        half = self.spot.half
        keys = range(self.spot.groups)
        for key in keys:
            for step in range(half):
                self.core(key, step).wait_recv()
        for key in keys:
            moved = key in self.near + self.rest
            if moved:
                self.swap(key).wait_send()
            for step in range(half):
                self.core(key, step).wait_send()
                if not moved:
                    self.local_copy(key, step).wait()
                elif step:
                    self.across(key, step).wait_send()


def attend_forward_kernel(
    heads_here,
    groups,
    columns,
    prefix_ref,
    far_ref,
    base_ref,
    qkv_ref,
    rows_ref,
    far_rows_ref,
    side_rows_ref,
    mixed_ref,
    totals_ref,
    full_ref,
    bias_sc,
    score_sc,
    value_sc,
    *sems,
):
    width = heads_here * HEAD
    query_tile = pl.program_id(0)
    tiles = qkv_ref.shape[0] // tile
    spot = Spot(groups, columns)
    job = Spread(spot, rows_ref, far_rows_ref, side_rows_ref, full_ref, sems)

    @pl.when(query_tile == 0)
    def _():
        spot.meet()
        job.begin()

    prefix_length = prefix_ref[0]
    heads = range(heads_here)

    @pl.when(query_tile == 0)
    def _():
        build_bias(base_ref, far_ref, bias_sc, heads_here)
        for key_tile in range(value_sc.shape[1] // tile):
            rows = pl.ds(key_tile * tile, tile)
            values = qkv_ref[rows, 2 * width : 3 * width].astype(jnp.float32)
            value_sc[:, rows] = jnp.transpose(values).astype(jnp.bfloat16)

    queries = qkv_ref[rows_at(query_tile), :width]
    head_queries = [
        jnp.where(lane_row_mask(head, width, tile), queries, jnp.zeros_like(queries)) for head in heads
    ]

    def score_tiles(key_tile, tops, finish):
        keys = qkv_ref[rows_at(key_tile), width : 2 * width]
        out = []
        for head in heads:
            scores = finish(head, nt_dot(keys, head_queries[head]) * (score_scale * log2e))
            score_sc[head, rows_at(key_tile), :] = scores
            out.append(jnp.maximum(tops[head], fold_rows(scores, jnp.max)))
        return tuple(out)

    def far_body(key_tile, tops):
        return score_tiles(key_tile, tops, lambda head, raw: raw + far_ref[head, 0])

    def near_body(key_tile, tops):
        return score_tiles(key_tile, tops, lambda head, raw: raw + bias_sc[head, 0])

    def tail_body(key_tile, tops):
        shown = visible_tile(key_tile, query_tile, prefix_length)
        which = 1 + jnp.minimum(key_tile - query_tile, 2)
        return score_tiles(
            key_tile, tops, lambda head, raw: jnp.where(shown, raw + bias_sc[head, which], masked_score)
        )

    tile_count = jnp.maximum(query_tile + 1, tiles // 2)
    near_start = jnp.maximum(query_tile - 1, 0)
    tops = tuple(jnp.full((8, tile), masked_score, jnp.float32) for _ in heads)
    tops = lax.fori_loop(0, near_start, far_body, tops)
    tops = lax.fori_loop(near_start, query_tile, near_body, tops)
    tops = lax.fori_loop(query_tile, tile_count, tail_body, tops)
    tops = [jnp.max(top, axis=0, keepdims=True) for top in tops]

    def mix_body(key_tile, carry):
        sums, mixes = carry
        new_sums, new_mixes = [], []
        for head in heads:
            expos = jnp.exp2(score_sc[head, rows_at(key_tile), :] - tops[head])
            new_sums.append(sums[head] + fold_rows(expos, jnp.sum))
            values = value_sc[head * HEAD : (head + 1) * HEAD, rows_at(key_tile)]
            new_mixes.append(mixes[head] + nn_dot(values, expos.astype(jnp.bfloat16)))
        return (tuple(new_sums), tuple(new_mixes))

    sums, mixes = lax.fori_loop(
        0,
        tile_count,
        mix_body,
        (
            tuple(jnp.zeros((8, tile), jnp.float32) for _ in heads),
            tuple(jnp.zeros((HEAD, tile), jnp.float32) for _ in heads),
        ),
    )
    parts = []
    for head in heads:
        total = jnp.sum(sums[head], axis=0, keepdims=True)
        parts.append(mixes[head] / total)
        totals_ref[0, pl.ds(head, 1), :] = tops[head] + jnp.log2(total)
    mixed_ref[...] = jnp.transpose(jnp.concatenate(parts, axis=0)).astype(jnp.bfloat16)

    @pl.when(query_tile == tiles // 2)
    def _():
        for key in job.near:
            job.advance(key)

    @pl.when(query_tile == tiles - 2)
    def _():
        for key in job.near[:1]:
            job.pass_on(key)

    @pl.when(query_tile == tiles - 2)
    def _():
        for key in job.rest:
            job.advance(key)

    @pl.when(query_tile == tiles - 1)
    def _():
        for key in job.near[1:] + job.rest:
            job.pass_on(key)
        job.finish()


def attend_forward(prefix, far_bias, base_bias, qkv, rows, far_rows, side_rows, columns):
    length = qkv.shape[0]
    groups = rows.shape[0]
    width = qkv.shape[1] // 3
    heads_here = width // HEAD
    tiles = length // tile
    return pl.pallas_call(
        functools.partial(attend_forward_kernel, heads_here, groups, columns),
        grid=(tiles,),
        out_shape=(
            jax.ShapeDtypeStruct((length, width), jnp.bfloat16),
            jax.ShapeDtypeStruct((tiles, heads_here, tile), jnp.float32),
            jax.ShapeDtypeStruct((columns,) + rows.shape, rows.dtype),
        ),
        in_specs=[
            pl.BlockSpec(memory_space=pltpu.SMEM),
            pl.BlockSpec(memory_space=pltpu.SMEM),
            pl.BlockSpec(base_bias.shape, lambda i: (0, 0)),
            pl.BlockSpec(qkv.shape, lambda i: (0, 0)),
            anywhere,
            anywhere,
            anywhere,
        ],
        out_specs=(
            pl.BlockSpec((tile, width), lambda i: (i, 0)),
            pl.BlockSpec((1, heads_here, tile), lambda i: (i, 0, 0)),
            anywhere,
        ),
        scratch_shapes=[
            pltpu.VMEM((heads_here, 4, tile, tile), jnp.float32),
            pltpu.VMEM((heads_here, length, tile), jnp.float32),
            pltpu.VMEM((width, length), jnp.bfloat16),
        ]
        + Spread.sems(groups, columns),
        compiler_params=comm_params(5),
        cost_estimate=pl.CostEstimate(
            flops=40 * length * length * width, transcendentals=length * length * heads_here,
            bytes_accessed=8 * length * width,
        ),
        name="attend_forward",
    )(prefix, far_bias, base_bias, qkv, rows, far_rows, side_rows)


def attend_backward_kernel(
    heads_here,
    groups,
    columns,
    prefix_ref,
    far_ref,
    base_ref,
    qkv_ref,
    mixed_ref,
    grad_ref,
    totals_ref,
    part_ref,
    sums_ref,
    out_ref,
    near_ref,
    side_ref,
    result_ref,
    piece_ref,
    bias_sc,
    key_sc,
    grad_key_sc,
    grad_value_sc,
    near_sc,
    *scratch,
):
    width = heads_here * HEAD
    query_tile = pl.program_id(0)
    tiles = qkv_ref.shape[0] // tile
    spot = Spot(groups, columns)
    pieces = scratch[0]
    swap = Exchange(
        spot, lambda at, third: (sums_ref.at[at], pieces.at[spot.place]), 1, *scratch[1:4]
    )
    job = Collect(spot, part_ref, result_ref, scratch[4:])

    @pl.when(query_tile == 0)
    def _():
        spot.meet()
        job.begin()
        swap.begin()

    prefix_length = prefix_ref[0]
    heads = range(heads_here)

    @pl.when(query_tile == 0)
    def _():
        build_bias(base_ref, far_ref, bias_sc, heads_here)
        for key_tile in range(key_sc.shape[1] // tile):
            rows = pl.ds(key_tile * tile, tile)
            keys = qkv_ref[rows, width : 2 * width].astype(jnp.float32)
            key_sc[:, rows] = jnp.transpose(keys).astype(jnp.bfloat16)
        grad_key_sc[...] = jnp.zeros_like(grad_key_sc)
        grad_value_sc[...] = jnp.zeros_like(grad_value_sc)
        near_sc[...] = jnp.zeros_like(near_sc)
        side_ref[...] = jnp.zeros_like(side_ref)

    queries = qkv_ref[rows_at(query_tile), :width]
    grads = grad_ref[rows_at(query_tile), :]
    products = grads.astype(jnp.float32) * mixed_ref[rows_at(query_tile), :].astype(jnp.float32)
    head_queries, head_grads, inners, totals = [], [], [], []
    for head in heads:
        mask = lane_row_mask(head, width, tile)
        head_queries.append(jnp.where(mask, queries, jnp.zeros_like(queries)))
        head_grads.append(jnp.where(mask, grads, jnp.zeros_like(grads)))
        ones = jnp.where(lane_row_mask(head, width, 8), 1.0, 0.0)
        inner = lax.dot_general(
            ones,
            products,
            (((1,), (1,)), ((), ())),
            precision=lax.Precision.HIGHEST,
            preferred_element_type=jnp.float32,
        )
        inners.append(inner[0:1, :])
        totals.append(totals_ref[0, pl.ds(head, 1), :])

    def step(key_tile, carry, finish, keep):
        sides, grad_queries = carry
        keys = qkv_ref[rows_at(key_tile), width : 2 * width]
        values = qkv_ref[rows_at(key_tile), 2 * width : 3 * width]
        new_sides, new_queries = [], []
        key_part, value_part = None, None
        for head in heads:
            raw = nt_dot(keys, head_queries[head]) * (score_scale * log2e)
            attention = jnp.exp2(finish(head, raw))
            grad_weights = nt_dot(values, head_grads[head])
            grad_scores = attention * (grad_weights - inners[head])
            new_sides.append(keep(head, grad_scores, sides[head]))
            low_scores = grad_scores.astype(jnp.bfloat16)
            keys_across = key_sc[head * HEAD : (head + 1) * HEAD, rows_at(key_tile)]
            new_queries.append(grad_queries[head] + nn_dot(keys_across, low_scores))
            value_one = nn_dot(attention.astype(jnp.bfloat16), head_grads[head])
            key_one = nn_dot(low_scores, head_queries[head])
            value_part = value_one if value_part is None else value_part + value_one
            key_part = key_one if key_part is None else key_part + key_one
        grad_key_sc[rows_at(key_tile), :] += key_part
        grad_value_sc[rows_at(key_tile), :] += value_part
        return (tuple(new_sides), tuple(new_queries))

    def add_side(head, grad_scores, side):
        return side + fold_rows(grad_scores, jnp.sum)

    def far_body(key_tile, carry):
        return step(
            key_tile, carry, lambda head, raw: raw + (far_ref[head, 0] - totals[head]), add_side
        )

    def near_body(key_tile, carry):
        def keep(head, grad_scores, side):
            near_sc[head, 0] += grad_scores
            return side

        return step(
            key_tile, carry, lambda head, raw: raw + bias_sc[head, 0] - totals[head], keep
        )

    def tail_body(key_tile, carry):
        shown = visible_tile(key_tile, query_tile, prefix_length)
        which = 1 + jnp.minimum(key_tile - query_tile, 2)

        def keep(head, grad_scores, side):
            near_sc[head, which] += grad_scores
            return side

        return step(
            key_tile,
            carry,
            lambda head, raw: jnp.where(
                shown, raw + bias_sc[head, which] - totals[head], masked_score
            ),
            keep,
        )

    tile_count = jnp.maximum(query_tile + 1, tiles // 2)
    near_start = jnp.maximum(query_tile - 1, 0)
    carry = (
        tuple(jnp.zeros((8, tile), jnp.float32) for _ in heads),
        tuple(jnp.zeros((HEAD, tile), jnp.float32) for _ in heads),
    )
    carry = lax.fori_loop(0, near_start, far_body, carry)
    carry = lax.fori_loop(near_start, query_tile, near_body, carry)
    carry = lax.fori_loop(query_tile, tile_count, tail_body, carry)
    sides, grad_queries = carry
    for head in heads:
        side_ref[head, 0] += sides[head]
    across = jnp.concatenate(grad_queries, axis=0) * score_scale
    out_ref[rows_at(query_tile), :width] = jnp.transpose(across).astype(jnp.bfloat16)

    for step in range(tiles):
        middles = [key for key in range(groups) if key * 2 // groups == step]
        lasts = [key for key in range(groups) if min(tiles - 1, 2 + key * 3 // 4) == step]

        @pl.when(query_tile == step)
        def _():
            for key in middles:
                job.middle(key)
            for key in lasts:
                job.last(key)

    @pl.when(query_tile == tiles - 1)
    def _():
        out_ref[:, width : 2 * width] = (grad_key_sc[...] * score_scale).astype(jnp.bfloat16)
        out_ref[:, 2 * width : 3 * width] = grad_value_sc[...].astype(jnp.bfloat16)
        for head in heads:
            side_ref[head, 1] = fold_rows(near_sc[head, 3], jnp.sum)
            for near in range(3):
                wide = jnp.concatenate(
                    [near_sc[head, near], jnp.zeros((tile, tile), jnp.float32)], axis=1
                )
                near_ref[pl.ds(head * 3 + near, 1), :] = unskew_sum(wide)

    @pl.when(query_tile == tiles - 1)
    def _():
        swap.arrive()
        piece_ref[...] = jnp.sum(pieces[...].astype(jnp.float32), axis=0).astype(jnp.bfloat16)
        job.finish()
        swap.finish()


def attend_backward(
    prefix, far_bias, base_bias, qkv, mixed, grad_mixed, totals, part, sums, columns
):
    length = qkv.shape[0]
    groups, piece_rows, piece_width = sums.shape
    block = part.shape[2:]
    width = qkv.shape[1] // 3
    heads_here = width // HEAD
    tiles = length // tile
    whole = lambda i: (0, 0)
    return pl.pallas_call(
        functools.partial(attend_backward_kernel, heads_here, groups, columns),
        grid=(tiles,),
        out_shape=(
            jax.ShapeDtypeStruct((length, 3 * width), jnp.bfloat16),
            jax.ShapeDtypeStruct((heads_here * 3, 2 * tile), jnp.float32),
            jax.ShapeDtypeStruct((heads_here, 2, 8, tile), jnp.float32),
            jax.ShapeDtypeStruct((groups,) + block, jnp.bfloat16),
            jax.ShapeDtypeStruct((piece_rows, piece_width), jnp.bfloat16),
        ),
        in_specs=[
            pl.BlockSpec(memory_space=pltpu.SMEM),
            pl.BlockSpec(memory_space=pltpu.SMEM),
            pl.BlockSpec(base_bias.shape, whole),
            pl.BlockSpec(qkv.shape, whole),
            pl.BlockSpec(mixed.shape, whole),
            pl.BlockSpec(mixed.shape, whole),
            pl.BlockSpec((1, heads_here, tile), lambda i: (i, 0, 0)),
            anywhere,
            anywhere,
        ],
        out_specs=(
            pl.BlockSpec((length, 3 * width), whole),
            pl.BlockSpec((heads_here * 3, 2 * tile), whole),
            pl.BlockSpec((heads_here, 2, 8, tile), lambda i: (0, 0, 0, 0)),
            anywhere,
            pl.BlockSpec((piece_rows, piece_width), whole),
        ),
        scratch_shapes=[
            pltpu.VMEM((heads_here, 4, tile, tile), jnp.float32),
            pltpu.VMEM((width, length), jnp.bfloat16),
            pltpu.VMEM((length, width), jnp.float32),
            pltpu.VMEM((length, width), jnp.float32),
            pltpu.VMEM((heads_here, 4, tile, tile), jnp.float32),
            pltpu.VMEM(sums.shape, jnp.bfloat16),
        ]
        + Exchange.sems(groups, 1)
        + Collect.scratch(columns, groups, block),
        compiler_params=comm_params(6, 60),
        cost_estimate=pl.CostEstimate(
            flops=70 * length * length * width, transcendentals=length * length * heads_here,
            bytes_accessed=16 * length * width,
        ),
        name="attend_backward",
    )(prefix, far_bias, base_bias, qkv, mixed, grad_mixed, totals, part, sums)


def gelu_parts(act):
    inner = math.sqrt(2.0 / math.pi) * (act + 0.044715 * act * act * act)
    tanh = jnp.tanh(inner)
    half = 0.5 * (1.0 + tanh)
    slope = math.sqrt(2.0 / math.pi) * (1.0 + 3.0 * 0.044715 * act * act)
    return act * half, half + 0.5 * act * (1.0 - tanh * tanh) * slope


def slot_rows(experts_here):
    return experts_here * main_slots + -(-experts_here * tail_slots // 8) * 8


def tail_select(expert, sources, tail_height):
    rows = lax.broadcasted_iota(jnp.int32, (sources * tail_slots, sources * tail_height), 0)
    columns = lax.broadcasted_iota(jnp.int32, (sources * tail_slots, sources * tail_height), 1)
    wanted = (rows // tail_slots) * tail_height + expert * tail_slots + rows % tail_slots
    return jnp.where(columns == wanted, 1.0, 0.0).astype(jnp.bfloat16)


def expert_input(main_ref, tail_ref, select):
    width = main_ref.shape[-1]
    main = main_ref[...].reshape(-1, width)
    tail = nn_dot(select, tail_ref[...].reshape(-1, width)).astype(jnp.bfloat16)
    return jnp.concatenate([main, tail], axis=0)


def gates_of(wide_rows):
    return wide_rows[:, D : D + 1].astype(jnp.float32) + wide_rows[:, D + 1 : D + 2].astype(
        jnp.float32
    )


def expert_output(value, select, expert, main_sc, tail_sc):
    low = value.astype(jnp.bfloat16)
    main_count = main_sc.shape[0] * main_sc.shape[1] * main_slots
    main_sc[...] = low[:main_count].reshape(main_sc.shape)
    spread = tn_dot(select, low[main_count:]).astype(jnp.bfloat16).reshape(tail_sc.shape)

    @pl.when(expert == 0)
    def _():
        tail_sc[...] = spread

    @pl.when(expert > 0)
    def _():
        tail_sc[...] += spread


def expert_math(rows, gates, raw_hidden, gate_weight, up_weight, down_weight):
    gate_act = nt_dot(rows, gate_weight)
    up_act = nt_dot(rows, up_weight)
    gelu, slope = gelu_parts(gate_act)
    hidden = gelu * up_act
    low_hidden = hidden.astype(jnp.bfloat16)
    grad_gates = jnp.sum(raw_hidden * low_hidden.astype(jnp.float32), axis=1, keepdims=True)
    grad_hidden = raw_hidden * gates
    grad_gate = (grad_hidden * up_act * slope).astype(jnp.bfloat16)
    grad_up = (grad_hidden * gelu).astype(jnp.bfloat16)
    back = nn_dot(grad_gate, gate_weight) + nn_dot(grad_up, up_weight)
    gated = (hidden * gates).astype(jnp.bfloat16)
    return gated, grad_gate, grad_up, back, grad_gates, nn_dot(low_hidden, down_weight)


def slot_lanes(expert, experts_here, sources):
    main = sources * main_slots
    count = sources * CAP
    rows = lax.broadcasted_iota(jnp.int32, (count, sources), 0)
    source = jnp.where(rows < main, rows // main_slots, (rows - main) // tail_slots)
    hot = jnp.where(lax.broadcasted_iota(jnp.int32, (count, sources), 1) == source, 1.0, 0.0)
    rows = lax.broadcasted_iota(jnp.int32, (count, spare), 0)
    lane = jnp.where(
        rows < main,
        expert * main_slots + rows % main_slots,
        experts_here * main_slots + expert * tail_slots + (rows - main) % tail_slots,
    )
    return hot.astype(jnp.bfloat16), lax.broadcasted_iota(jnp.int32, (count, spare), 1) == lane


def split_low(values):
    high = values.astype(jnp.bfloat16)
    return high, (values - high.astype(jnp.float32)).astype(jnp.bfloat16)


def expert_act_kernel(
    experts_here,
    row_main,
    row_tail,
    grad_main,
    grad_tail,
    gate_weight,
    up_weight,
    down_weight,
    hidden_ref,
    grad_gate_ref,
    grad_up_ref,
    result_ref,
    back_ref,
    result_main,
    result_tail,
    back_main,
    back_tail,
    sems,
):
    part, expert = pl.program_id(0), pl.program_id(1)
    shards_part = row_main.shape[0]
    sources = shards_part * row_main.shape[1]
    tail_height = row_tail.shape[2]
    sources_at = pl.ds(part * shards_part, shards_part)
    select = tail_select(expert, sources, tail_height)
    wide_rows = expert_input(row_main, row_tail, select)
    grads = expert_input(grad_main, grad_tail, select)
    hidden, grad_gate, grad_up, back, grad_gates, result = expert_math(
        wide_rows[:, :D],
        gates_of(wide_rows),
        nt_dot(grads, down_weight[0]),
        gate_weight[0],
        up_weight[0],
        down_weight[0],
    )
    lanes = lax.broadcasted_iota(jnp.int32, (back.shape[0], spare), 1)
    back = jnp.concatenate([back, jnp.where(lanes == 0, grad_gates, 0.0)], axis=1)
    hidden_ref[0] = hidden
    grad_gate_ref[0] = grad_gate
    grad_up_ref[0] = grad_up

    def main_copies(at):
        place = pl.ds(pl.multiple_of(at * main_slots, main_slots), main_slots)
        return (
            pltpu.make_async_copy(result_main, result_ref.at[sources_at, :, place, :], sems.at[0]),
            pltpu.make_async_copy(back_main, back_ref.at[sources_at, :, place, :], sems.at[1]),
        )

    @pl.when(expert > 0)
    def _():
        for copy in main_copies(expert - 1):
            copy.wait()

    expert_output(result, select, expert, result_main, result_tail)
    expert_output(back, select, expert, back_main, back_tail)
    for copy in main_copies(expert):
        copy.start()

    @pl.when(expert == experts_here - 1)
    def _():
        place = pl.ds(experts_here * main_slots, tail_height)
        tails = (
            pltpu.make_async_copy(result_tail, result_ref.at[sources_at, :, place, :], sems.at[2]),
            pltpu.make_async_copy(back_tail, back_ref.at[sources_at, :, place, :], sems.at[3]),
        )
        for copy in tails:
            copy.start()
        for copy in main_copies(expert):
            copy.wait()
        for copy in tails:
            copy.wait()


def parts_of(rows):
    shards, groups = rows.shape[:2]
    return max(1, shards * groups // part_sources)


def row_specs(rows, experts_here, order):
    shards, groups, height, width = rows.shape
    shards_part = shards // parts_of(rows)
    tail_height = slot_rows(experts_here) - experts_here * main_slots
    tail_at = experts_here * main_slots // tail_height
    main_at = lambda e, c: (c, 0, e, 0)
    side_at = lambda e, c: (c, 0, tail_at, 0)
    return [
        pl.BlockSpec((shards_part, groups, main_slots, width), order(main_at)),
        pl.BlockSpec((shards_part, groups, tail_height, width), order(side_at)),
    ]


def expert_act(rows, grads, gate_weight, up_weight, down_weight):
    experts_here, units, width = gate_weight.shape
    shards, groups = rows.shape[:2]
    count = shards * groups * CAP
    parts = parts_of(rows)
    height = slot_rows(experts_here)
    tail_height = height - experts_here * main_slots
    order = lambda index: lambda c, e: index(e, c)
    weight_spec = pl.BlockSpec((1, units, width), lambda c, e: (e, 0, 0))
    act_spec = pl.BlockSpec((1, count // parts, units), lambda c, e: (e, c, 0))
    act_shape = jax.ShapeDtypeStruct((experts_here, count, units), jnp.bfloat16)
    slot_shape = lambda lanes: jax.ShapeDtypeStruct(
        (shards, groups, height, lanes), jnp.bfloat16
    )
    scratch = [
        pltpu.VMEM((shards // parts, groups, rows_of, lanes), jnp.bfloat16)
        for lanes in (width, width + spare)
        for rows_of in (main_slots, tail_height)
    ]
    return pl.pallas_call(
        functools.partial(expert_act_kernel, experts_here),
        grid=(parts, experts_here),
        out_shape=(act_shape, act_shape, act_shape, slot_shape(width), slot_shape(width + spare)),
        in_specs=row_specs(rows, experts_here, order)
        + row_specs(grads, experts_here, order)
        + [weight_spec] * 3,
        out_specs=(
            act_spec,
            act_spec,
            act_spec,
            pl.BlockSpec(memory_space=pl.ANY),
            pl.BlockSpec(memory_space=pl.ANY),
        ),
        scratch_shapes=scratch + [pltpu.SemaphoreType.DMA((4,))],
        compiler_params=pltpu.CompilerParams(vmem_limit_bytes=60 * mega),
        cost_estimate=pl.CostEstimate(
            flops=12 * experts_here * count * width * units,
            transcendentals=experts_here * count * units,
            bytes_accessed=6 * experts_here * width * units + 8 * experts_here * count * width,
        ),
        name="expert_act",
    )(rows, rows, grads, grads, gate_weight, up_weight, down_weight)


class RowChunk:
    def __init__(self, spot, number, place_rows, rows_in, rows_all, back_out, bufs, sems):
        self.spot, self.number, self.place_rows = spot, number, place_rows
        self.rows_in, self.rows_all, self.back_out = rows_in, rows_all, back_out
        self.rows, self.back, self.pair_in, self.across_out, self.across_in, self.total = bufs
        (
            self.local,
            self.send,
            self.recv,
            self.across_send,
            self.across_recv,
            self.core_send,
            self.core_recv,
            self.pair_send,
            self.pair_recv,
            self.sum_send,
            self.sum_recv,
            self.back_send,
            self.back_recv,
        ) = sems

    @staticmethod
    def sems(groups, columns, chunks):
        half = columns // 2
        dma = pltpu.SemaphoreType.DMA
        return (
            [dma((chunks, 4))]
            + [dma((chunks, groups))] * 2
            + [dma((chunks, half, 2))] * 8
            + [dma((chunks, groups))] * 2
        )

    def keys(self, near):
        groups = self.spot.groups
        return [0] + near_keys(groups) if near else far_keys(groups)

    def side(self, near):
        half = self.spot.groups // 2
        here = self.spot.place // half
        return pl.ds((here if near else 1 - here) * half, half)

    def swap(self, key):
        spot, at = self.spot, self.number
        peer = flip(spot.place, key)
        source = self.rows_in.at[peer, self.place_rows]
        target = self.rows.at[spot.lane, spot.place]
        if key == 0:
            return pltpu.make_async_copy(source, target, self.local.at[at, 0])
        return remote(
            source, target, self.send.at[at, key], self.recv.at[at, key], (peer, spot.lane)
        )

    def keep(self, near):
        side = self.side(near)
        return pltpu.make_async_copy(
            self.rows.at[:, side],
            self.rows_all.at[:, side, self.place_rows],
            self.local.at[self.number, 1 + near],
        )

    def across(self, near, step):
        spot, at = self.spot, self.number
        block = self.rows.at[spot.lane, self.side(near)]
        return remote(
            block,
            block,
            self.across_send.at[at, step, near],
            self.across_recv.at[at, step, near],
            (spot.place, spot.across(step)),
        )

    def core(self, near, step):
        spot, at = self.spot, self.number
        block = self.rows.at[spot.behind(step), self.side(near)]
        return remote(
            block,
            block,
            self.core_send.at[at, step, near],
            self.core_recv.at[at, step, near],
            (spot.place, spot.partner),
        )

    def begin(self, near):
        for key in self.keys(near):
            self.swap(key).start()

    def advance(self, near):
        for key in self.keys(near):
            self.swap(key).wait_recv() if key else self.swap(key).wait()
        for step in range(1, self.spot.half):
            self.across(near, step).start()
        self.core(near, 0).start()

    def complete(self, near):
        half = self.spot.half
        for step in range(1, half):
            self.across(near, step).wait_recv()
            self.core(near, step).start()
        for step in range(half):
            self.core(near, step).wait_recv()
        if self.rows_all is not None:
            self.keep(near).start()

    def pair_copy(self, step, near):
        spot, at = self.spot, self.number
        side = self.side(near)
        return remote(
            self.back.at[spot.lane_at(step, True), side],
            self.pair_in.at[step, side],
            self.pair_send.at[at, step, near],
            self.pair_recv.at[at, step, near],
            (spot.place, spot.partner),
        )

    def sum_copy(self, step, near):
        spot, at = self.spot, self.number
        side = self.side(near)
        return remote(
            self.across_out.at[step, side],
            self.across_in.at[step, side],
            self.sum_send.at[at, step, near],
            self.sum_recv.at[at, step, near],
            (spot.place, spot.across(step)),
        )

    def back_copy(self, key):
        spot, at = self.spot, self.number
        peer = flip(spot.place, key)
        target = self.back_out.at[spot.place, self.place_rows]
        if key == 0:
            return pltpu.make_async_copy(self.total.at[peer], target, self.local.at[at, 3])
        return remote(
            self.total.at[peer],
            target,
            self.back_send.at[at, key],
            self.back_recv.at[at, key],
            (peer, spot.lane),
        )

    def pair(self, near):
        for step in list(range(1, self.spot.half)) + [0]:
            self.pair_copy(step, near).start()

    def pair_sum(self, step, near):
        side = self.side(near)
        mine = self.back[self.spot.lane_at(step, False), side].astype(jnp.float32)
        return mine + self.pair_in[step, side].astype(jnp.float32)

    def middle(self, near):
        for step in range(1, self.spot.half):
            self.pair_copy(step, near).wait_recv()
            total = self.pair_sum(step, near)
            self.across_out[step, self.side(near)] = total.astype(self.total.dtype)
            self.sum_copy(step, near).start()
        self.pair_copy(0, near).wait_recv()

    def last(self, near):
        total = self.pair_sum(0, near)
        for step in range(1, self.spot.half):
            self.sum_copy(step, near).wait_recv()
            total = total + self.across_in[step, self.side(near)].astype(jnp.float32)
        self.total[self.side(near)] = total.astype(self.total.dtype)
        for key in self.keys(near):
            self.back_copy(key).start()

    def finish(self):
        groups, half = self.spot.groups, self.spot.half
        for key in range(1, groups):
            self.back_copy(key).wait_recv()
        self.back_copy(0).wait()
        for near in range(2):
            if self.rows_all is not None:
                self.keep(near).wait()
            for step in range(half):
                self.core(near, step).wait_send()
                self.pair_copy(step, near).wait_send()
                if step:
                    self.across(near, step).wait_send()
                    self.sum_copy(step, near).wait_send()
        for key in range(groups):
            if key:
                self.swap(key).wait_send()
                self.back_copy(key).wait_send()


half_chunks = ((1, 0), (1, 1), (0, 0), (0, 1), (0, 2), (0, 3), (1, 2), (1, 3))


def half_expert(step):
    return step - 2 * ((step // 2 + 1) // 2)


def half_far(step):
    return (step // 2 + 1) // 2 % 2


def experts_kernel(
    experts_here,
    groups,
    columns,
    rows_in,
    gates_in,
    grad_main,
    grad_tail,
    gate_weight,
    up_weight,
    down_weight,
    hidden_ref,
    grad_gate_ref,
    grad_up_ref,
    result_ref,
    rows_all,
    back_out,
    gates_out,
    act_sc,
    act_sems,
    result_main,
    result_tail,
    result_sems,
    *scratch,
):
    now = pl.program_id(0)
    expert = half_expert(now)
    tail_height = result_tail.shape[2]
    half_groups = groups // 2
    sources = half_groups * columns
    main_count, count = sources * main_slots, sources * CAP
    spot = Spot(groups, columns)
    here = spot.place // half_groups
    side_at = here + half_far(now) * (1 - 2 * here)
    side = pl.ds(side_at * half_groups, half_groups)
    mains, tails, sides, sems = scratch[:6], scratch[6:12], scratch[12:18], scratch[18:]
    chunks = [
        RowChunk(
            spot,
            at,
            pl.ds(at * main_slots, main_slots),
            rows_in,
            rows_all,
            back_out,
            [buf.at[at] for buf in mains],
            sems,
        )
        for at in range(experts_here)
    ]
    tail = RowChunk(
        spot,
        experts_here,
        pl.ds(experts_here * main_slots, tail_height),
        rows_in,
        rows_all,
        back_out,
        tails,
        sems,
    )
    scalars = RowChunk(
        spot, experts_here + 1, pl.ds(0, 8), gates_in, None, gates_out, sides, sems
    )

    @pl.when(now == 0)
    def _():
        spot.meet()
        scalars.begin(1)
        tail.begin(1)
        chunks[0].begin(1)
        chunks[1].begin(1)
        scalars.begin(0)
        tail.begin(0)
        chunks[0].begin(0)
        sides[1][...] = jnp.zeros_like(sides[1])

    select = tail_select(expert, sources, tail_height)

    def joined(main, low):
        width = main.shape[-1]
        low = nn_dot(select, low.reshape(-1, width)).astype(jnp.bfloat16)
        return jnp.concatenate([main.reshape(-1, width), low], axis=0)

    raw_hidden = nt_dot(joined(grad_main[:, side], grad_tail[:, side]), down_weight[0])

    def before(step):
        if step == 0:
            scalars.advance(1)
            tail.advance(1)
            chunks[0].advance(1)
            chunks[1].begin(0)
            chunks[1].advance(1)
            scalars.complete(1)
            tail.complete(1)
        elif step == 1:
            scalars.advance(0)
            tail.advance(0)
            chunks[0].advance(0)
            chunks[2].begin(0)
        elif step == 2:
            chunks[1].advance(0)
            chunks[3].begin(0)
            scalars.complete(0)
            tail.complete(0)
        elif step == 3:
            chunks[2].advance(0)
            chunks[2].begin(1)
            chunks[3].begin(1)
        elif step == 4:
            chunks[3].advance(0)
        elif step == 5:
            chunks[2].advance(1)
        elif step == 6:
            chunks[3].advance(1)
        near, at = half_chunks[step]
        chunks[at].complete(near)
        if step:
            near, at = half_chunks[step - 1]
            chunks[at].middle(near)
        if step == 6:
            tail.middle(0)
            scalars.middle(0)

    for step in range(len(half_chunks)):

        @pl.when(now == step)
        def _():
            before(step)

    rows = joined(mains[0][expert, :, side], tails[0][:, side])
    hot, of_slot = slot_lanes(expert, experts_here, sources)
    gate_high, gate_rest = split_low(sides[0][:, side, 0, :].reshape(sources, spare))
    gates = nn_dot(hot, gate_high) + nn_dot(hot, gate_rest)
    gates = jnp.sum(jnp.where(of_slot, gates, 0.0), axis=1, keepdims=True)
    hidden, grad_gate, grad_up, back, grad_gates, result = expert_math(
        rows, gates, raw_hidden, gate_weight[0], up_weight[0], down_weight[0]
    )

    def spread(value, main_target, tail_target):
        low = value.astype(jnp.bfloat16)
        main_target(low[:main_count].reshape(columns, half_groups, main_slots, -1))
        part = tn_dot(select, low[main_count:]).astype(jnp.bfloat16)
        part = part.reshape(columns, half_groups, tail_height, -1)

        @pl.when(expert == 0)
        def _():
            tail_target[:, side] = part

        @pl.when(expert > 0)
        def _():
            tail_target[:, side] += part

    def store_back(value):
        mains[1][expert, :, side] = value

    spread(back, store_back, tails[1])
    side_high, side_rest = split_low(jnp.where(of_slot, grad_gates, 0.0))
    lanes = (tn_dot(hot, side_high) + tn_dot(hot, side_rest)).reshape(columns, half_groups, spare)
    sides[1][:, side, 0, :] += lanes

    def after(step):
        near, at = half_chunks[step]
        chunks[at].pair(near)
        if step == 5:
            tail.pair(0)
            scalars.pair(0)
        if step == 7:
            tail.pair(1)
            scalars.pair(1)
            chunks[at].middle(1)
            tail.middle(1)
            scalars.middle(1)
        if step:
            near, at = half_chunks[step - 1]
            chunks[at].last(near)
        if step == 6:
            tail.last(0)
            scalars.last(0)

    for step in range(len(half_chunks)):

        @pl.when(now == step)
        def _():
            after(step)

    act_rows = pl.ds(pl.multiple_of(side_at * count, 32), count)

    def act_copies():
        outs = (hidden_ref, grad_gate_ref, grad_up_ref)
        return [
            pltpu.make_async_copy(act_sc.at[k], out.at[expert, act_rows], act_sems.at[k])
            for k, out in enumerate(outs)
        ]

    def result_copy():
        place = pl.ds(pl.multiple_of(expert * main_slots, main_slots), main_slots)
        return pltpu.make_async_copy(
            result_main, result_ref.at[:, side, place], result_sems.at[0]
        )

    @pl.when(now > 0)
    def _():
        result_copy().wait()
        for copy in act_copies():
            copy.wait()

    def store_result(value):
        result_main[...] = value

    spread(result, store_result, result_tail)
    act_sc[0] = hidden
    act_sc[1] = grad_gate
    act_sc[2] = grad_up
    result_copy().start()
    for copy in act_copies():
        copy.start()

    @pl.when(now == len(half_chunks) - 1)
    def _():
        place = pl.ds(experts_here * main_slots, tail_height)
        low = pltpu.make_async_copy(result_tail, result_ref.at[:, :, place], result_sems.at[1])
        low.start()
        chunks[-1].last(1)
        tail.last(1)
        scalars.last(1)
        for chunk in chunks + [tail, scalars]:
            chunk.finish()
        result_copy().wait()
        for copy in act_copies():
            copy.wait()
        low.wait()


def experts(rows, gates, grads, gate_weight, up_weight, down_weight, columns):
    experts_here, units, width = gate_weight.shape
    groups, height, wide = rows.shape
    half = columns // 2
    count = columns * groups * CAP
    tail_height = height - experts_here * main_slots
    weight_spec = pl.BlockSpec((1, units, width), lambda t: (half_expert(t), 0, 0))
    act_shape = jax.ShapeDtypeStruct((experts_here, count, units), jnp.bfloat16)
    low = lambda *shape: pltpu.VMEM(shape, jnp.bfloat16)
    bufs = lambda lead, *block, kind=jnp.bfloat16: [
        pltpu.VMEM((*lead, *first, groups, *block), kind)
        for first in ((columns,), (columns,), (half,), (half,), (half,), ())
    ]
    return pl.pallas_call(
        functools.partial(experts_kernel, experts_here, groups, columns),
        grid=(len(half_chunks),),
        out_shape=(
            act_shape,
            act_shape,
            act_shape,
            jax.ShapeDtypeStruct((columns, groups, height, width), jnp.bfloat16),
            jax.ShapeDtypeStruct((columns,) + rows.shape, jnp.bfloat16),
            jax.ShapeDtypeStruct(rows.shape, jnp.bfloat16),
            jax.ShapeDtypeStruct(gates.shape, jnp.float32),
        ),
        in_specs=[anywhere, anywhere]
        + row_specs(grads, experts_here, lambda index: lambda t: index(half_expert(t), 0))
        + [weight_spec] * 3,
        out_specs=(anywhere,) * 7,
        scratch_shapes=[
            low(3, count // 2, units),
            pltpu.SemaphoreType.DMA((3,)),
            low(columns, groups // 2, main_slots, width),
            low(columns, groups, tail_height, width),
            pltpu.SemaphoreType.DMA((2,)),
        ]
        + bufs((experts_here,), main_slots, wide)
        + bufs((), tail_height, wide)
        + bufs((), 8, spare, kind=jnp.float32)
        + RowChunk.sems(groups, columns, experts_here + 2),
        compiler_params=comm_params(10),
        cost_estimate=pl.CostEstimate(
            flops=12 * experts_here * count * width * units,
            transcendentals=experts_here * count * units,
            bytes_accessed=6 * experts_here * width * units + 8 * experts_here * count * width,
        ),
        name="experts",
    )(rows, gates, grads, grads, gate_weight, up_weight, down_weight)


def expert_weight_kernel(
    parts,
    halves,
    row_main,
    row_tail,
    grad_main,
    grad_tail,
    hidden_ref,
    grad_gate_ref,
    grad_up_ref,
    gate_out,
    up_out,
    down_out,
):
    expert, part = pl.program_id(0), pl.program_id(1)
    sources = row_main.shape[0] * row_main.shape[1]
    select = tail_select(expert, sources, row_tail.shape[2])
    if halves == 1:
        rows = expert_input(row_main, row_tail, select)[:, :D]
        grads = expert_input(grad_main, grad_tail, select)
    else:
        groups = row_main.shape[1] // halves
        select = tail_select(expert, sources // halves, row_tail.shape[2])
        sides = [slice(at * groups, (at + 1) * groups) for at in range(halves)]
        both = lambda main, low: jnp.concatenate(
            [expert_input(main[:, side], low[:, side], select) for side in sides], axis=0
        )
        rows, grads = both(row_main, row_tail), both(grad_main, grad_tail)

    @pl.when(part == 0)
    def _():
        gate_out[0] = tn_dot(grad_gate_ref[0], rows)
        up_out[0] = tn_dot(grad_up_ref[0], rows)
        down_out[0] = tn_dot(hidden_ref[0], grads)

    if parts > 1:

        @pl.when(part > 0)
        def _():
            gate_out[0] += tn_dot(grad_gate_ref[0], rows)
            up_out[0] += tn_dot(grad_up_ref[0], rows)
            down_out[0] += tn_dot(hidden_ref[0], grads)


def expert_weight_grads(rows, grads, hidden, grad_gate, grad_up, halves):
    experts_here, count, units = hidden.shape
    width = grads.shape[-1]
    parts = parts_of(rows)
    order = lambda index: index
    act_spec = pl.BlockSpec((1, count // parts, units), lambda e, c: (e, c, 0))
    out_spec = pl.BlockSpec((1, units, width), lambda e, c: (e, 0, 0))
    out_shape = jax.ShapeDtypeStruct((experts_here, units, width), jnp.float32)
    return pl.pallas_call(
        functools.partial(expert_weight_kernel, parts, halves),
        grid=(experts_here, parts),
        out_shape=(out_shape, out_shape, out_shape),
        in_specs=row_specs(rows, experts_here, order)
        + row_specs(grads, experts_here, order)
        + [act_spec] * 3,
        out_specs=(out_spec, out_spec, out_spec),
        compiler_params=pltpu.CompilerParams(vmem_limit_bytes=60 * mega),
        cost_estimate=pl.CostEstimate(
            flops=6 * experts_here * count * width * units,
            transcendentals=0,
            bytes_accessed=12 * experts_here * width * units + 10 * experts_here * count * width,
        ),
        name="expert_weight_grads",
    )(rows, rows, grads, grads, hidden, grad_gate, grad_up)


def pair_slots(token_routes, ranks, experts_here):
    row_count = token_routes.shape[0]
    expert_pair = jnp.concatenate([token_routes[:, 0], token_routes[:, 1]])
    rank_pair = jnp.concatenate([ranks, ranks + row_count])
    earlier = (expert_pair[None, :] == expert_pair[:, None]) & (
        rank_pair[None, :] < rank_pair[:, None]
    )
    slot_index = jnp.sum(earlier.astype(jnp.int32), axis=1)
    height = slot_rows(experts_here)
    local = expert_pair % experts_here
    main_at = local * main_slots + slot_index
    tail_at = experts_here * main_slots + local * tail_slots + slot_index - main_slots
    row = jnp.where(slot_index < main_slots, main_at, tail_at)
    slots = (expert_pair // experts_here) * height + row
    return jnp.where(slot_index < CAP, slots, -1)


def router_head(logits, token_routes, weights):
    token_count = logits.shape[0]
    probabilities = jax.nn.softmax(logits, axis=-1)
    log_totals = jax.nn.logsumexp(logits, axis=-1)
    picked = (token_routes[:, :, None] == jnp.arange(EXPERTS, dtype=jnp.int32)).astype(jnp.float32)
    chosen = jnp.sum(picked * probabilities[:, None, :], axis=-1)
    gate_values = chosen / jnp.sum(chosen, axis=1, keepdims=True)
    shares = jnp.sum(picked, axis=(0, 1)) / (token_count * TOP)
    balance = EXPERTS * jnp.sum(shares * jnp.sum(probabilities, axis=0))
    return (gate_values, weights[0] * jnp.sum(log_totals * log_totals) + weights[1] * balance)


def column(values, rows):
    return jnp.pad(values, (0, rows - values.shape[0]))[:, None]


def shards(
    inputs,
    grad_out,
    prefix,
    routes,
    priority,
    loss_weights,
    norm_attn,
    norm_moe,
    qkv_weight,
    out_weight,
    bias_table,
    router_weight,
    gate_weight,
    up_weight,
    down_weight,
):
    row_count = inputs.shape[0]
    groups = lax.axis_size("expert")
    columns_of = lax.axis_size("shard")
    place = lax.axis_index("expert")
    length = row_count * groups
    heads_here = HEADS // groups
    width = heads_here * HEAD
    experts_here = EXPERTS // groups
    shard_rows = D // columns_of
    height = slot_rows(experts_here)

    packed_small = jnp.concatenate(
        [
            lax.dynamic_slice(
                qkv_weight, (0, third * D + place * width), (shard_rows, width)
            )
            for third in range(3)
        ]
        + [jnp.pad(router_weight, ((0, 0), (0, spare - EXPERTS)))],
        axis=1,
    )
    table_rows = BUCKETS // columns_of
    table_low = bias_table.astype(jnp.float32).reshape(1, table_rows * HEADS)
    gain_rows = jnp.concatenate(
        [
            norm_attn.astype(jnp.float32)[None],
            norm_moe.astype(jnp.float32)[None],
            jnp.pad(table_low, ((0, 0), (0, shard_rows - table_rows * HEADS))),
            jnp.zeros((5, shard_rows), jnp.float32),
        ],
        axis=0,
    )
    token_routes = routes.reshape(row_count, TOP)
    slots = pair_slots(token_routes, priority.reshape(row_count), experts_here)
    slot_map = (
        jnp.arange(groups * height, dtype=jnp.int32)[:, None] == slots[None, :]
    ).reshape(groups * height, TOP, row_count)
    slot_any = jnp.any(slot_map, axis=1).astype(jnp.bfloat16)
    token_slots = jnp.any(
        slots.reshape(TOP, row_count)[:, :, None] == jnp.arange(groups * height, dtype=jnp.int32),
        axis=0,
    ).astype(jnp.bfloat16)
    slot_pairs = slot_map.astype(jnp.bfloat16).reshape(groups * height, TOP * row_count)
    grad_low = grad_out.reshape(row_count, D)
    grad_slots = nn_dot(slot_any, grad_low).astype(jnp.bfloat16).reshape(groups, height, D)
    _, normed_all, qkv_own, small_full, out_full, far_slots, side_slots, gains = entry_gather(
        inputs.reshape(row_count, D),
        gain_rows,
        packed_small,
        out_weight,
        grad_slots,
        3 * width,
        1,
    )
    normed_all = normed_all.reshape(length, D)
    qkv_own = qkv_own.reshape(length, 3 * width)
    small_full = small_full.reshape(D, 3 * width + spare)
    out_full = out_full.reshape(D, D)
    router_full = small_full[:, 3 * width : 3 * width + EXPERTS]
    gain_attn = gains[:, 0].reshape(D)
    gain_moe = gains[:, 1].reshape(D)
    table_full = gains[:, 2, : table_rows * HEADS].reshape(BUCKETS, HEADS)
    table_own = lax.dynamic_slice_in_dim(
        table_full, place * heads_here, heads_here, 1
    )
    near_ids = jnp.asarray(skew_buckets(), jnp.int32)
    near_hot = (near_ids[:, None] == jnp.arange(BUCKETS, dtype=jnp.int32)).astype(jnp.float32)
    base_bias = (
        jnp.dot(near_hot, table_own, precision=lax.Precision.HIGHEST).reshape(3, 2 * tile, heads_here)
        * log2e
    )
    base_bias = jnp.transpose(base_bias, (2, 0, 1)).reshape(heads_here * 3, 2 * tile)
    far_bias = jnp.stack([table_own[15], table_own[31]], axis=1) * log2e

    mixed_own, totals, grads_received = attend_forward(
        prefix, far_bias, base_bias, qkv_own, grad_slots, far_slots, side_slots, columns_of
    )
    attended = exchange_mixed(mixed_own.reshape(groups, row_count, width), columns_of, 8)

    tokens_in = inputs.reshape(row_count, D).astype(jnp.float32)
    middle = tokens_in + nn_dot(attended, out_full)
    normed_two, norm_two_back = jax.vjp(rms_norm, middle, gain_moe)
    low_two = normed_two.astype(jnp.bfloat16)
    logits = nn_dot(low_two, router_full)
    router_out, router_back = jax.vjp(
        lambda logit_in: router_head(logit_in, token_routes, loss_weights), logits
    )
    gate_values = router_out[0]
    slot_gates = jnp.sum(
        slot_map.astype(jnp.float32) * jnp.transpose(gate_values)[None], axis=1
    )
    fused = columns_of * groups <= part_sources and experts_here == 4
    if fused:
        outgoing = nn_dot(slot_any, low_two).astype(jnp.bfloat16).reshape(groups, height, D)
        gate_block = jnp.pad(
            jnp.sum(slot_gates, axis=1).reshape(groups, 1, height),
            ((0, 0), (0, 7), (0, spare - height)),
        )
    else:
        gate_high = lax.reduce_precision(gate_values, 8, 7)
        gate_parts = jnp.stack([gate_high, gate_values - gate_high], axis=-1).astype(jnp.bfloat16)
        wide_rows = jnp.concatenate(
            [
                jnp.broadcast_to(low_two[None], (TOP, row_count, D)),
                jnp.pad(jnp.transpose(gate_parts, (1, 0, 2)), ((0, 0), (0, 0), (0, spare - 2))),
            ],
            axis=2,
        ).reshape(TOP * row_count, D + spare)
        outgoing = nn_dot(slot_pairs, wide_rows).astype(jnp.bfloat16)
        outgoing = outgoing.reshape(groups, height, D + spare)
    gate_across, up_across, down_across = (
        jnp.transpose(weight, (0, 2, 1)) for weight in (gate_weight, up_weight, down_weight)
    )
    if fused:
        (
            hidden,
            grad_gate,
            grad_up,
            result_part,
            rows_received,
            grad_returned,
            side_returned,
        ) = experts(
            outgoing, gate_block, grads_received, gate_across, up_across, down_across, columns_of
        )
        slot_grads = side_returned[:, 0, :height].reshape(groups * height)
        grad_gates = jnp.sum(
            jnp.where(slot_map, slot_grads[:, None, None], 0.0), axis=0
        )
        grad_gates = jnp.transpose(grad_gates)
        grad_returned = grad_returned.reshape(groups * height, D)
    else:
        rows_received = dispatch(outgoing, columns_of, 2)
        hidden, grad_gate, grad_up, result_part, back_part = expert_act(
            rows_received, grads_received, gate_across, up_across, down_across
        )
        grad_returned = collect(back_part, 3).reshape(groups * height, D + spare)
        grad_gates = jnp.transpose(
            tn_dot(slot_pairs, grad_returned[:, D:])[:, 0].reshape(TOP, row_count)
        )
    grad_low_two = nn_dot(token_slots, grad_returned[:, :D])
    grad_top = grad_low.astype(jnp.float32)
    grad_logits = router_back((grad_gates, jnp.ones((), jnp.float32)))[0]
    low_logits = grad_logits.astype(jnp.bfloat16)
    router_grad = tn_dot(low_two, low_logits)
    grad_low_two = grad_low_two + nt_dot(low_logits, router_full)
    grad_middle_norm, gain_moe_grad = norm_two_back(grad_low_two)
    grad_middle = grad_top + grad_middle_norm
    low_middle = grad_middle.astype(jnp.bfloat16)
    out_grad = tn_dot(attended, low_middle)
    grad_attended = nt_dot(low_middle, out_full).astype(jnp.bfloat16)
    grad_attended = jnp.transpose(grad_attended.reshape(row_count, groups, width), (1, 0, 2))
    grad_mixed = lax.all_to_all(
        grad_attended, "expert", split_axis=0, concat_axis=0, tiled=True
    )
    gate_grad, up_grad, down_grad = expert_weight_grads(
        rows_received, grads_received, hidden, grad_gate, grad_up, 2 if fused else 1
    )
    out_sums = lax.psum_scatter(
        out_grad.astype(jnp.bfloat16), "shard", scatter_dimension=0, tiled=True
    ).reshape(groups, shard_rows // groups, D)
    grad_qkv, near_sums, side_sums, returned, out_piece = attend_backward(
        prefix,
        far_bias,
        base_bias,
        qkv_own,
        mixed_own,
        grad_mixed.reshape(length, width),
        totals,
        result_part,
        out_sums,
        columns_of,
    )
    slot_high = lax.reduce_precision(slot_gates, 8, 7)
    slot_parts = jnp.concatenate([slot_high, slot_gates - slot_high], axis=1).astype(jnp.bfloat16)
    mixture = tn_dot(slot_parts, returned.reshape(groups * height, D))
    mixture = mixture[:row_count] + mixture[row_count:]
    output = (middle + mixture).astype(jnp.bfloat16)

    table_grad = jnp.einsum(
        "hil,ilb->bh",
        near_sums.reshape(heads_here, 3, 2 * tile),
        near_hot.reshape(3, 2 * tile, BUCKETS),
        precision=lax.Precision.HIGHEST,
    )
    far_sums = jnp.sum(side_sums, axis=(2, 3))
    bucket_ids = jnp.arange(BUCKETS, dtype=jnp.int32)[:, None]
    table_grad = table_grad + jnp.where(bucket_ids == 15, far_sums[:, 0][None], 0.0)
    table_grad = table_grad + jnp.where(bucket_ids == 31, far_sums[:, 1][None], 0.0)
    table_column = jnp.pad(
        table_grad.reshape(columns_of, table_rows * heads_here),
        ((0, 0), (0, shard_rows - table_rows * heads_here)),
    ).reshape(D, 1)

    extra = jnp.concatenate(
        [
            jnp.zeros((D, 1), jnp.float32),
            table_column,
            gain_moe_grad[:, None],
            router_grad,
            jnp.zeros((D, spare - 3 - EXPERTS), jnp.float32),
        ],
        axis=1,
    ).astype(jnp.bfloat16)
    grad_projected, last_all, out_all, qkv_full = tail_exchange(
        grad_qkv.reshape(groups, row_count, 3 * width),
        normed_all,
        small_full,
        extra,
        out_piece,
        qkv_weight,
        columns_of,
        7,
    )
    last_all = last_all.reshape(groups, shard_rows, 3 * width + spare)
    out_all = out_all.reshape(shard_rows, D)
    if width % 128 == 0:
        input_grad, qkv_total, out_total, extra_total = finish(
            grad_projected,
            qkv_full,
            last_all,
            inputs.reshape(row_count, D),
            gain_attn[None],
            grad_middle,
            out_all,
            width,
        )
    else:
        grad_projected = jnp.transpose(
            grad_projected.reshape(groups, row_count, 3, width), (1, 2, 0, 3)
        ).reshape(row_count, 3 * D)
        grad_low_one = nt_dot(grad_projected, qkv_full.reshape(D, 3 * D))
        _, norm_one_back = jax.vjp(lambda features: rms_norm(features, gain_attn), tokens_in)
        input_grad = grad_middle + norm_one_back(grad_low_one)[0]
        qkv_total = jnp.transpose(
            last_all[:, :, : 3 * width].reshape(groups, shard_rows, 3, width), (1, 2, 0, 3)
        ).reshape(shard_rows, 3 * D).astype(jnp.float32)
        out_total = out_all.astype(jnp.float32)
        extra_total = jnp.sum(last_all[:, :, 3 * width :].astype(jnp.float32), axis=0).T
    table_part = last_all[:, : table_rows * heads_here, 3 * width + 1].astype(jnp.float32)
    table_total = jnp.transpose(
        table_part.reshape(groups, table_rows, heads_here), (1, 0, 2)
    ).reshape(table_rows, HEADS)
    return (
        output.reshape(row_count, 1, D),
        input_grad.reshape(row_count, 1, D),
        extra_total[0] / norm_attn.astype(jnp.float32),
        extra_total[2],
        qkv_total,
        out_total,
        table_total,
        extra_total[3 : 3 + EXPERTS].T,
        jnp.transpose(gate_grad, (0, 2, 1)),
        jnp.transpose(up_grad, (0, 2, 1)),
        jnp.transpose(down_grad, (0, 2, 1)),
    )


def solution(mesh):
    placed = (
        P("expert", "shard", None),
        P("expert", "shard", None),
        P("shard"),
        P("expert", "shard", None),
        P("expert", "shard", None),
        P(),
        P("shard"),
        P("shard"),
        P("shard", None),
        P("shard", None),
        P("shard", None),
        P("shard", None),
        P("expert", None, "shard"),
        P("expert", None, "shard"),
        P("expert", None, "shard"),
    )
    return jax.shard_map(
        shards,
        mesh=mesh,
        in_specs=placed,
        out_specs=(
            P("expert", "shard", None),
            P("expert", "shard", None),
            P("shard"),
            P("shard"),
            P("shard", None),
            P("shard", None),
            P("shard", None),
            P("shard", None),
            P("expert", None, "shard"),
            P("expert", None, "shard"),
            P("expert", None, "shard"),
        ),
        check_vma=False,
    )
```

```python
import functools
import math

import jax
import jax.numpy as jnp
import numpy as np
from jax import lax
from jax.experimental import pallas as pl
from jax.experimental.pallas import tpu as pltpu
from jax.sharding import PartitionSpec as P

D = 1024
HEADS = 16
HEAD = 64
FF = 2816
EXPERTS = 32
TOP = 2
BUCKETS = 32
CAP = 18

epsilon = 1e-06
masked_score = -1e30
far_bounds = (12, 16, 23, 32, 46, 64, 91)
tile = 256
main_slots = 16
tail_slots = CAP - main_slots
log2e = math.log2(math.e)
score_scale = HEAD ** (-0.5)
mega = 1024 * 1024
part_sources = 32
spare = 128


MESH = pl.DeviceIdType.MESH


def flip(index, key):
    out, bit = index, 1
    while bit <= key:
        if key & bit:
            out = out + bit * (1 - 2 * ((index // bit) % 2))
        bit *= 2
    return out


def near_keys(groups):
    return list(range(1, groups // 2))


def far_keys(groups):
    return list(range(groups // 2, groups))


def early_keys(groups):
    return [key for key in far_keys(groups) if key % line_shape(groups)[1] == 0]


class Spot:
    def __init__(self, groups, columns):
        self.groups, self.columns = groups, columns
        self.place = lax.axis_index("expert")
        self.lane = lax.axis_index("shard")
        self.half = columns // 2
        self.chip = self.lane // 2
        self.core = self.lane % 2
        self.partner = self.chip * 2 + 1 - self.core

    def across(self, step):
        return ((self.chip + step) % self.half) * 2 + self.core

    def behind(self, step):
        return ((self.chip + self.half - step) % self.half) * 2 + self.core

    def lane_at(self, step, other):
        chip = (self.chip + step) % self.half
        return chip * 2 + ((1 - self.core) if other else self.core)

    def meet(self):
        barrier = pltpu.get_barrier_semaphore()
        for key in range(1, self.groups):
            peer = (flip(self.place, key), self.lane)
            pl.semaphore_signal(barrier, inc=1, device_id=peer, device_id_type=MESH)
        for step in range(1, self.columns):
            peer = (self.place, (self.lane + step) % self.columns)
            pl.semaphore_signal(barrier, inc=1, device_id=peer, device_id_type=MESH)
        pl.semaphore_wait(barrier, self.groups + self.columns - 2)


def remote(source, target, send_sem, recv_sem, peer):
    return pltpu.make_async_remote_copy(
        src_ref=source,
        dst_ref=target,
        send_sem=send_sem,
        recv_sem=recv_sem,
        device_id=peer,
        device_id_type=MESH,
    )


def line_shape(groups):
    across = groups // 4
    return 4, across


class LineGather:
    def __init__(self, spot, own, full, local_sem, send_sems, recv_sems, rows=None):
        self.spot, self.own, self.full, self.rows = spot, own, full, rows
        self.local_sem, self.send_sems, self.recv_sems = local_sem, send_sems, recv_sems
        self.long, self.wide = line_shape(spot.groups)
        self.z = spot.place // self.wide
        self.y = spot.place % self.wide

    @staticmethod
    def sems(groups):
        long, wide = line_shape(groups)
        return [
            pltpu.SemaphoreType.DMA(()),
            pltpu.SemaphoreType.DMA((2 * long - 1, wide + 1)),
            pltpu.SemaphoreType.DMA((groups,)),
        ]

    def block(self, origin):
        return self.full.at[origin] if self.rows is None else self.full.at[origin, self.rows]

    def copy(self, job, way, origin, source, target):
        return remote(
            source,
            self.block(origin),
            self.send_sems.at[job, way],
            self.recv_sems.at[origin],
            (target, self.spot.lane),
        )

    def each(self, job, origin, source, up, down, act):
        place, wide = self.spot.place, self.wide
        if up:

            @pl.when(self.z + 1 < self.long)
            def _():
                act(self.copy(job, 0, origin, source, place + wide))

        if down:

            @pl.when(self.z >= 1)
            def _():
                act(self.copy(job, 1, origin, source, place - wide))

        for step in range(1, wide):
            target = self.z * wide + (self.y + step) % wide
            act(self.copy(job, 1 + step, origin, source, target))

    def begin(self):
        place = self.spot.place
        self.each(0, place, self.own, True, True, lambda copy: copy.start())
        pltpu.make_async_copy(self.own, self.block(place), self.local_sem).start()

    def arrive(self, origin):
        self.copy(0, 0, origin, self.own, self.spot.place).wait_recv()

    def hop(self, k):
        place, wide = self.spot.place, self.wide

        @pl.when(self.z >= k)
        def _():
            origin = place - k * wide
            self.arrive(origin)
            self.each(k, origin, self.block(origin), True, False, lambda copy: copy.start())

        @pl.when(self.z + k < self.long)
        def _():
            origin = place + k * wide
            self.arrive(origin)
            job = self.long - 1 + k
            self.each(job, origin, self.block(origin), False, True, lambda copy: copy.start())

    def finish(self):
        for row in range(self.long):
            for step in range(1, self.wide):
                self.arrive(row * self.wide + (self.y + step) % self.wide)
        self.settle()

    def settle(self):
        place, wide = self.spot.place, self.wide
        stop = lambda copy: copy.wait_send()
        self.each(0, place, self.own, True, True, stop)
        for k in range(1, self.long):

            @pl.when(self.z >= k)
            def _():
                origin = place - k * wide
                self.each(k, origin, self.block(origin), True, False, stop)

            @pl.when(self.z + k < self.long)
            def _():
                origin = place + k * wide
                job = self.long - 1 + k
                self.each(job, origin, self.block(origin), False, True, stop)

        pltpu.make_async_copy(self.own, self.block(place), self.local_sem).wait()


class ColumnGather:
    def __init__(self, spot, own, full, local_sem, across_send, across_recv, core_send, core_recv):
        self.spot, self.own, self.full = spot, own, full
        self.local_sem = local_sem
        self.across_send, self.across_recv = across_send, across_recv
        self.core_send, self.core_recv = core_send, core_recv

    @staticmethod
    def sems(columns):
        return [pltpu.SemaphoreType.DMA(())] + [pltpu.SemaphoreType.DMA((columns // 2,))] * 4

    def across_copy(self, step):
        spot = self.spot
        return remote(
            self.own,
            self.full.at[spot.lane],
            self.across_send.at[step],
            self.across_recv.at[step],
            (spot.place, spot.across(step)),
        )

    def core_copy(self, step):
        spot = self.spot
        source = self.own if step == 0 else self.full.at[spot.behind(step)]
        target = spot.lane if step == 0 else spot.behind(step)
        return remote(
            source,
            self.full.at[target],
            self.core_send.at[step],
            self.core_recv.at[step],
            (spot.place, spot.partner),
        )

    def begin(self):
        for step in range(1, self.spot.half):
            self.across_copy(step).start()
        self.core_copy(0).start()
        pltpu.make_async_copy(self.own, self.full.at[self.spot.lane], self.local_sem).start()

    def forward(self):
        for step in range(1, self.spot.half):
            self.across_copy(step).wait_recv()
            self.core_copy(step).start()

    def finish(self):
        for step in range(self.spot.half):
            self.core_copy(step).wait_recv()
        for step in range(self.spot.half):
            self.core_copy(step).wait_send()
        for step in range(1, self.spot.half):
            self.across_copy(step).wait_send()
        pltpu.make_async_copy(self.own, self.full.at[self.spot.lane], self.local_sem).wait()


def comm_params(which, limit=60):
    return pltpu.CompilerParams(
        collective_id=which, has_side_effects=True, vmem_limit_bytes=limit * mega
    )


anywhere = pl.BlockSpec(memory_space=pl.ANY)


def entry_kernel(
    groups,
    columns,
    tokens,
    gain,
    pack,
    out_weight,
    rows,
    tokens_all,
    normed_all,
    qkv_all,
    pack_all,
    out_all,
    far_rows,
    side_rows,
    gain_all,
    token_sc,
    normed_sc,
    qkv_sc,
    gain_sc,
    pack_sc,
    token_sem,
    normed_sems,
    qkv_sems,
    pack_sem,
    gain_sem,
    *sems,
):
    spot = Spot(groups, columns)
    half_rows = tokens.shape[0] // 2
    lines = [
        LineGather(spot, tokens.at[rows_at], tokens_all, *line_sems, rows=rows_at)
        for rows_at, line_sems in (
            (pl.ds(0, half_rows), sems[:3]),
            (pl.ds(half_rows, half_rows), sems[3:6]),
        )
    ]
    line, sems = lines[0], sems[3:]
    gains = ColumnGather(spot, gain, gain_sc, *sems[3:8])
    packs = ColumnGather(spot, pack, pack_sc, *sems[8:13])
    outs = ColumnGather(spot, out_weight, out_all, *sems[13:18])
    far_send, far_recv, side_send, side_recv = sems[18:]
    wide = qkv_sc.shape[2]

    def far_copy(key):
        peer = flip(spot.place, key)
        return remote(
            rows.at[peer],
            far_rows.at[spot.place],
            far_send.at[key],
            far_recv.at[key],
            (peer, spot.lane),
        )

    def side_copy(key, step):
        at = flip(spot.place, key)
        return remote(
            far_rows.at[at] if key else rows.at[at],
            side_rows.at[step - 1, at],
            side_send.at[key, step],
            side_recv.at[key, step],
            (spot.place, spot.across(step)),
        )

    def stores(origin):
        return (
            pltpu.make_async_copy(
                normed_sc.at[origin], normed_all.at[origin], normed_sems.at[origin]
            ),
            pltpu.make_async_copy(qkv_sc.at[origin], qkv_all.at[origin], qkv_sems.at[origin]),
        )

    def project(origin, source):
        load = pltpu.make_async_copy(source, token_sc, token_sem)
        load.start()
        load.wait()
        features = token_sc[...].astype(jnp.float32)
        factor = lax.rsqrt(jnp.mean(features * features, axis=-1, keepdims=True) + epsilon)
        gain_row = jnp.concatenate([gain_sc[at, 0:1, :] for at in range(columns)], axis=1)
        normed = (features * factor * gain_row).astype(jnp.bfloat16)
        normed_sc[origin] = normed
        weight = pack_sc[...].reshape(D, -1)[:, :wide]
        qkv_sc[origin] = nn_dot(normed, weight).astype(jnp.bfloat16)
        for store in stores(origin):
            store.start()

    spot.meet()
    for line in lines:
        line.begin()
    gains.begin()
    packs.begin()
    outs.begin()
    gains.forward()
    packs.forward()
    gains.finish()
    packs.finish()
    keep = pltpu.make_async_copy(pack_sc, pack_all, pack_sem)
    keep.start()
    keep_gain = pltpu.make_async_copy(gain_sc, gain_all, gain_sem)
    keep_gain.start()
    project(spot.place, tokens)
    for line in lines:
        line.hop(1)
    outs.forward()
    for step in range(1, spot.half):
        side_copy(0, step).start()
    for line in lines:
        line.hop(2)
    for key in early_keys(groups):
        far_copy(key).start()
    for line in lines:
        line.hop(3)

    def own_column(row, carry):
        @pl.when(row != line.z)
        def _():
            origin = row * line.wide + line.y
            project(origin, tokens_all.at[origin])

        return carry

    lax.fori_loop(0, line.long, own_column, 0)

    for key in early_keys(groups):
        far_copy(key).wait_recv()
        for step in range(1, spot.half):
            side_copy(key, step).start()

    def other_column(at, carry):
        row = line.z + ((at + 1) // 2) * (1 - 2 * (at % 2))

        @pl.when((row >= 0) & (row < line.long))
        def _():
            for step in range(1, line.wide):
                origin = row * line.wide + (line.y + step) % line.wide
                for part in lines:
                    part.arrive(origin)
                project(origin, tokens_all.at[origin])

        return carry

    lax.fori_loop(0, 2 * line.long - 1, other_column, 0)
    for line in lines:
        line.settle()
    for key in early_keys(groups):
        far_copy(key).wait_send()
    for key in [0] + early_keys(groups):
        for step in range(1, spot.half):
            side_copy(key, step).wait_recv()
            side_copy(key, step).wait_send()
    outs.finish()
    keep.wait()
    keep_gain.wait()
    for origin in range(groups):
        for store in stores(origin):
            store.wait()


def entry_gather(tokens, gain, pack, out_weight, rows, wide, which):
    groups = rows.shape[0]
    columns = D // out_weight.shape[0]
    count = tokens.shape[0]
    low = lambda *shape: jax.ShapeDtypeStruct(shape, jnp.bfloat16)
    dma = pltpu.SemaphoreType.DMA
    return pl.pallas_call(
        functools.partial(entry_kernel, groups, columns),
        out_shape=(
            low(groups, *tokens.shape),
            low(groups, *tokens.shape),
            low(groups, count, wide),
            low(columns, *pack.shape),
            low(columns, *out_weight.shape),
            low(*rows.shape),
            low(columns // 2 - 1, *rows.shape),
            jax.ShapeDtypeStruct((columns,) + gain.shape, jnp.float32),
        ),
        in_specs=[anywhere] * 5,
        out_specs=(anywhere,) * 8,
        scratch_shapes=[
            pltpu.VMEM(tokens.shape, jnp.bfloat16),
            pltpu.VMEM((groups,) + tokens.shape, jnp.bfloat16),
            pltpu.VMEM((groups, count, wide), jnp.bfloat16),
            pltpu.VMEM((columns,) + gain.shape, jnp.float32),
            pltpu.VMEM((columns,) + pack.shape, jnp.bfloat16),
            dma(()),
            dma((groups,)),
            dma((groups,)),
            dma(()),
            dma(()),
        ]
        + LineGather.sems(groups) * 2
        + ColumnGather.sems(columns) * 3
        + [dma((groups,))] * 2
        + [dma((groups, columns // 2))] * 2,
        compiler_params=comm_params(which),
        name="entry_gather",
    )(tokens, gain, pack, out_weight, rows)


class Dispatch:
    def __init__(self, spot, rows, full, sems):
        self.spot, self.rows, self.full = spot, rows, full
        self.local, self.send, self.recv = sems[:3]
        self.across_send, self.across_recv, self.core_send, self.core_recv = sems[3:]

    @staticmethod
    def sems(groups, columns):
        return (
            [pltpu.SemaphoreType.DMA(())]
            + [pltpu.SemaphoreType.DMA((groups,))] * 2
            + [pltpu.SemaphoreType.DMA((groups, columns // 2))] * 4
        )

    def own(self):
        spot = self.spot
        return pltpu.make_async_copy(
            self.rows.at[spot.place], self.full.at[spot.lane, spot.place], self.local
        )

    def swap(self, key):
        spot = self.spot
        peer = flip(spot.place, key)
        return remote(
            self.rows.at[peer],
            self.full.at[spot.lane, spot.place],
            self.send.at[key],
            self.recv.at[key],
            (peer, spot.lane),
        )

    def across(self, key, step):
        spot = self.spot
        block = self.full.at[spot.lane, flip(spot.place, key)]
        return remote(
            block,
            block,
            self.across_send.at[key, step],
            self.across_recv.at[key, step],
            (spot.place, spot.across(step)),
        )

    def core(self, key, step):
        spot = self.spot
        block = self.full.at[spot.behind(step), flip(spot.place, key)]
        return remote(
            block,
            block,
            self.core_send.at[key, step],
            self.core_recv.at[key, step],
            (spot.place, spot.partner),
        )

    def begin(self):
        groups = self.spot.groups
        self.own().start()
        for key in far_keys(groups) + near_keys(groups):
            self.swap(key).start()

    def advance(self, key):
        if key == 0:
            self.own().wait()
        else:
            self.swap(key).wait_recv()
        for step in range(1, self.spot.half):
            self.across(key, step).start()
        self.core(key, 0).start()

    def pass_on(self, key):
        for step in range(1, self.spot.half):
            self.across(key, step).wait_recv()
            self.core(key, step).start()

    def finish(self):
        groups, half = self.spot.groups, self.spot.half
        for key in range(groups):
            for step in range(half):
                self.core(key, step).wait_recv()
        for key in range(groups):
            if key > 0:
                self.swap(key).wait_send()
            for step in range(1, half):
                self.across(key, step).wait_send()
            for step in range(half):
                self.core(key, step).wait_send()


def dispatch_kernel(groups, columns, rows, full, *sems):
    spot = Spot(groups, columns)
    job = Dispatch(spot, rows, full, sems)
    spot.meet()
    job.begin()
    for key in range(groups):
        job.advance(key)
        if key:
            job.pass_on(key - 1)
    job.pass_on(groups - 1)
    job.finish()


def dispatch(rows, columns, which):
    groups = rows.shape[0]
    return pl.pallas_call(
        functools.partial(dispatch_kernel, groups, columns),
        out_shape=jax.ShapeDtypeStruct((columns,) + rows.shape, rows.dtype),
        in_specs=[anywhere],
        out_specs=anywhere,
        scratch_shapes=Dispatch.sems(groups, columns),
        compiler_params=comm_params(which),
        name="dispatch_rows",
    )(rows)


class Exchange:
    def __init__(self, spot, blocks, thirds, local, send, recv):
        self.spot, self.blocks, self.thirds = spot, blocks, range(thirds)
        self.local, self.send, self.recv = local, send, recv

    @staticmethod
    def sems(groups, thirds):
        return [pltpu.SemaphoreType.DMA((thirds,))] + [
            pltpu.SemaphoreType.DMA((groups, thirds))
        ] * 2

    def copy(self, key, third):
        spot = self.spot
        peer = flip(spot.place, key)
        source, target = self.blocks(peer, third)
        if key == 0:
            return pltpu.make_async_copy(source, target, self.local.at[third])
        return remote(
            source,
            target,
            self.send.at[key, third],
            self.recv.at[key, third],
            (peer, spot.lane),
        )

    def start(self, key):
        for third in self.thirds:
            self.copy(key, third).start()

    def begin(self):
        groups = self.spot.groups
        for key in far_keys(groups) + near_keys(groups) + [0]:
            self.start(key)

    def arrive(self):
        for key in range(self.spot.groups):
            for third in self.thirds:
                copy = self.copy(key, third)
                copy.wait() if key == 0 else copy.wait_recv()

    def finish(self):
        for key in range(1, self.spot.groups):
            for third in self.thirds:
                self.copy(key, third).wait_send()


class ColumnSum:
    def __init__(self, spot, chunks, order, part, bufs, sems):
        self.spot, self.chunks, self.order, self.part = spot, chunks, order, part
        self.pair_in, self.mine, self.across_out, self.across_in = bufs
        self.local, self.pair_send, self.pair_recv, self.across_send, self.across_recv = sems

    @staticmethod
    def scratch(columns, chunks, block):
        half = columns // 2
        return [pltpu.VMEM((half, chunks) + block, jnp.bfloat16)] * 4 + [
            pltpu.SemaphoreType.DMA((half, chunks))
        ] * 5

    def pair_copy(self, step, k):
        spot = self.spot
        return remote(
            self.part.at[spot.lane_at(step, True), self.order(k)],
            self.pair_in.at[step, k],
            self.pair_send.at[step, k],
            self.pair_recv.at[step, k],
            (spot.place, spot.partner),
        )

    def mine_copy(self, step, k):
        return pltpu.make_async_copy(
            self.part.at[self.spot.lane_at(step, False), self.order(k)],
            self.mine.at[step, k],
            self.local.at[step, k],
        )

    def across_copy(self, step, k):
        spot = self.spot
        return remote(
            self.across_out.at[step, k],
            self.across_in.at[step, k],
            self.across_send.at[step, k],
            self.across_recv.at[step, k],
            (spot.place, spot.across(step)),
        )

    def begin(self):
        half = self.spot.half
        for k in range(self.chunks):
            for step in list(range(1, half)) + [0]:
                self.pair_copy(step, k).start()
                self.mine_copy(step, k).start()

    def pair_sum(self, step, k):
        self.pair_copy(step, k).wait_recv()
        self.mine_copy(step, k).wait()
        return self.mine[step, k].astype(jnp.float32) + self.pair_in[step, k].astype(jnp.float32)

    def middle(self, k):
        for step in range(1, self.spot.half):
            self.across_out[step, k] = self.pair_sum(step, k).astype(jnp.bfloat16)
            self.across_copy(step, k).start()

    def last(self, k):
        total = self.pair_sum(0, k)
        for step in range(1, self.spot.half):
            self.across_copy(step, k).wait_recv()
            total = total + self.across_in[step, k].astype(jnp.float32)
        return total.astype(jnp.bfloat16)

    def finish(self):
        for k in range(self.chunks):
            for step in range(self.spot.half):
                self.pair_copy(step, k).wait_send()
                if step:
                    self.across_copy(step, k).wait_send()


class Collect:
    def __init__(self, spot, part, out, scratch):
        self.spot, self.total = spot, scratch[9]
        self.keys = far_keys(spot.groups) + near_keys(spot.groups) + [0]
        self.sums = ColumnSum(
            spot,
            spot.groups,
            lambda k: flip(spot.place, self.keys[k]),
            part,
            scratch[:4],
            scratch[4:9],
        )
        self.out = out
        self.local, self.send, self.recv = scratch[10:]

    @staticmethod
    def scratch(columns, groups, block):
        return (
            ColumnSum.scratch(columns, groups, block)
            + [pltpu.VMEM((groups,) + block, jnp.bfloat16)]
            + [pltpu.SemaphoreType.DMA(())]
            + [pltpu.SemaphoreType.DMA((groups,))] * 2
        )

    def copy(self, k):
        spot, key = self.spot, self.keys[k]
        target = self.out.at[spot.place]
        if key == 0:
            return pltpu.make_async_copy(self.total.at[k], target, self.local)
        peer = flip(spot.place, key)
        return remote(
            self.total.at[k], target, self.send.at[k], self.recv.at[k], (peer, spot.lane)
        )

    def begin(self):
        self.sums.begin()

    def middle(self, key):
        self.sums.middle(key)

    def last(self, key):
        self.total[key] = self.sums.last(key)
        self.copy(key).start()

    def finish(self):
        last = self.spot.groups - 1
        for k in range(last):
            self.copy(k).wait_recv()
        for k in range(last):
            self.copy(k).wait_send()
        self.copy(last).wait()
        self.sums.finish()


def collect_kernel(groups, columns, part, out, *scratch):
    spot = Spot(groups, columns)
    job = Collect(spot, part, out, scratch)
    spot.meet()
    job.begin()
    ahead = 2
    for key in range(ahead):
        job.middle(key)
    for key in range(groups):
        if key + ahead < groups:
            job.middle(key + ahead)
        job.last(key)
    job.finish()


def collect(part, which):
    columns, groups = part.shape[:2]
    block = part.shape[2:]
    return pl.pallas_call(
        functools.partial(collect_kernel, groups, columns),
        out_shape=jax.ShapeDtypeStruct((groups,) + block, part.dtype),
        in_specs=[anywhere],
        out_specs=anywhere,
        scratch_shapes=Collect.scratch(columns, groups, block),
        compiler_params=comm_params(which),
        name="collect_rows",
    )(part)


def lanes_at(place, width):
    return pl.ds(pl.multiple_of(place * width, 128), width)


def mixed_kernel(groups, columns, mixed, attended, *sems):
    spot = Spot(groups, columns)
    width = mixed.shape[2]

    def blocks(at, third):
        if width % 128:
            return mixed.at[at], attended.at[spot.place]
        return mixed.at[at], attended.at[:, lanes_at(spot.place, width)]

    job = Exchange(spot, blocks, 1, *sems)
    spot.meet()
    job.begin()
    job.arrive()
    job.finish()


def exchange_mixed(mixed, columns, which):
    groups, rows, width = mixed.shape
    shape = mixed.shape if width % 128 else (rows, groups * width)
    out = pl.pallas_call(
        functools.partial(mixed_kernel, groups, columns),
        out_shape=jax.ShapeDtypeStruct(shape, mixed.dtype),
        in_specs=[anywhere],
        out_specs=anywhere,
        scratch_shapes=Exchange.sems(groups, 1),
        compiler_params=comm_params(which),
        name="exchange_mixed",
    )(mixed)
    if width % 128:
        out = jnp.transpose(out, (1, 0, 2)).reshape(rows, groups * width)
    return out


class Tail:
    def __init__(self, spot, chunks, refs, scratch):
        grads, part, piece, weight, grads_out, sum_all, piece_all, weight_all = refs
        groups = spot.groups
        width = grads.shape[2] // 3
        thirds = 3 if width % 128 == 0 else 1

        def blocks(at, third):
            if thirds == 1:
                return grads.at[at], grads_out.at[spot.place]
            columns_to = pl.ds(pl.multiple_of(third * D + spot.place * width, 128), width)
            return grads.at[at, :, pl.ds(third * width, width)], grads_out.at[:, columns_to]

        self.chunks = chunks
        self.sums = ColumnSum(spot, chunks, lambda k: k, part, scratch[:4], scratch[4:9])
        self.own_sum = scratch[9]
        self.swap = Exchange(spot, blocks, thirds, *scratch[10:13])
        self.line = LineGather(spot, self.own_sum, sum_all, *scratch[13:16])
        self.side = LineGather(spot, piece, piece_all, *scratch[16:19])
        self.column = ColumnGather(spot, weight, weight_all, *scratch[19:24])

    @staticmethod
    def scratch(columns, groups, chunks, block, thirds):
        return (
            ColumnSum.scratch(columns, chunks, block)
            + [pltpu.VMEM((chunks,) + block, jnp.bfloat16)]
            + Exchange.sems(groups, thirds)
            + LineGather.sems(groups) * 2
            + ColumnGather.sems(columns)
        )


def tail_kernel(
    groups,
    columns,
    chunks,
    grads,
    normed,
    own_weight,
    extra,
    piece,
    weight,
    grads_out,
    sum_all,
    piece_all,
    weight_all,
    grads_sc,
    normed_sc,
    load_sems,
    part,
    *scratch,
):
    spot = Spot(groups, columns)
    refs = (grads, part, piece, weight, grads_out, sum_all, piece_all, weight_all)
    tail = Tail(spot, chunks, refs, scratch)
    wide = grads.shape[2]
    block_rows = D // (columns * chunks)
    loads = [
        pltpu.make_async_copy(grads, grads_sc, load_sems.at[0]),
        pltpu.make_async_copy(normed, normed_sc, load_sems.at[1]),
    ]
    for load in loads:
        load.start()
    far = far_keys(groups)
    early, late = far[: len(far) // 2], far[len(far) // 2 :]
    spot.meet()
    tail.side.begin()
    for key in early + near_keys(groups) + [0]:
        tail.swap.start(key)
    for load in loads:
        load.wait()
    all_grads = grads_sc[...].reshape(-1, wide)

    for at in range(columns * chunks):
        rows = pl.ds(at * block_rows, block_rows)
        grad = tn_dot(normed_sc[:, rows], all_grads)
        weights = own_weight[rows, :][:, :wide].astype(jnp.float32)
        gain = jnp.sum(grad * weights, axis=1, keepdims=True)
        lanes = lax.broadcasted_iota(jnp.int32, (block_rows, spare), 1)
        side = jnp.where(lanes == 0, gain, extra[rows, :].astype(jnp.float32))
        part[at // chunks, at % chunks] = jnp.concatenate([grad, side], axis=1).astype(jnp.bfloat16)
    tail.sums.begin()
    for k in range(chunks):
        tail.sums.middle(k)
    tail.column.begin()
    tail.side.hop(1)
    for k in range(chunks):
        tail.own_sum[k] = tail.sums.last(k)
    tail.line.begin()
    tail.side.hop(2)
    tail.line.hop(1)
    tail.side.hop(3)
    tail.line.hop(2)
    tail.line.hop(3)
    for key in late:
        tail.swap.start(key)
    tail.column.forward()
    tail.side.finish()
    tail.swap.arrive()
    tail.line.finish()
    tail.column.finish()
    tail.swap.finish()
    tail.sums.finish()


def tail_exchange(grads, normed, own_weight, extra, piece, weight, columns, which):
    groups, row_count, wide = grads.shape
    apart = wide // 3 % 128 != 0
    grads_shape = grads.shape if apart else (row_count, wide * groups)
    chunks = 2
    block = (D // columns // chunks, wide + spare)
    shape_of = lambda shape: jax.ShapeDtypeStruct(shape, jnp.bfloat16)
    inside = pl.BlockSpec(memory_space=pltpu.VMEM)
    return pl.pallas_call(
        functools.partial(tail_kernel, groups, columns, chunks),
        out_shape=(
            shape_of(grads_shape),
            shape_of((groups, chunks) + block),
            shape_of((groups,) + piece.shape),
            shape_of((columns,) + weight.shape),
        ),
        in_specs=[anywhere, anywhere, inside, inside, anywhere, anywhere],
        out_specs=(anywhere,) * 4,
        scratch_shapes=[
            pltpu.VMEM(grads.shape, jnp.bfloat16),
            pltpu.VMEM(normed.shape, jnp.bfloat16),
            pltpu.SemaphoreType.DMA((2,)),
            pltpu.VMEM((columns, chunks) + block, jnp.bfloat16),
        ]
        + Tail.scratch(columns, groups, chunks, block, 1 if apart else 3),
        compiler_params=comm_params(which),
        name="tail_exchange",
    )(grads, normed, own_weight, extra, piece, weight)


def finish_kernel(
    width,
    grads,
    weight,
    packed,
    packed_extra,
    tokens,
    gain,
    grad_middle,
    out_low,
    input_grad,
    qkv_grad,
    out_grad,
    extra,
    total_sc,
):
    third = pl.program_id(0)
    for group in range(packed.shape[0]):
        qkv_grad[:, group * width : (group + 1) * width] = packed[group].astype(jnp.float32)
    part = nt_dot(grads[...], weight[...].reshape(D, -1))

    @pl.when(third == 0)
    def _():
        total_sc[...] = part

    @pl.when(third > 0)
    def _():
        total_sc[...] += part

    @pl.when(third == 2)
    def _():
        features = tokens[...].astype(jnp.float32)
        factor = lax.rsqrt(jnp.mean(features * features, axis=-1, keepdims=True) + epsilon)
        unit = features * factor
        scaled = total_sc[...] * gain[...]
        inner = jnp.mean(scaled * unit, axis=-1, keepdims=True)
        input_grad[...] = grad_middle[...] + factor * (scaled - unit * inner)
        out_grad[...] = out_low[...].astype(jnp.float32)
        extra[...] = jnp.transpose(jnp.sum(packed_extra[...].astype(jnp.float32), axis=0))


def finish(grads, weight, packed, tokens, gain, grad_middle, out_low, width):
    groups, shard_rows = packed.shape[:2]
    columns = weight.shape[0]
    rows = grads.shape[0]
    whole = lambda t: (0, 0)
    full = jax.ShapeDtypeStruct((rows, D), jnp.float32)
    return pl.pallas_call(
        functools.partial(finish_kernel, width),
        grid=(3,),
        out_shape=(
            full,
            jax.ShapeDtypeStruct((shard_rows, 3 * D), jnp.float32),
            jax.ShapeDtypeStruct((shard_rows, D), jnp.float32),
            jax.ShapeDtypeStruct((spare, shard_rows), jnp.float32),
        ),
        in_specs=[
            pl.BlockSpec((rows, D), lambda t: (0, t)),
            pl.BlockSpec((columns, shard_rows, D), lambda t: (0, 0, t)),
            pl.BlockSpec((groups, shard_rows, width), lambda t: (0, 0, t)),
            pl.BlockSpec((groups, shard_rows, spare), lambda t: (0, 0, 3 * width // spare)),
            pl.BlockSpec((rows, D), whole),
            pl.BlockSpec((1, D), whole),
            pl.BlockSpec((rows, D), whole),
            pl.BlockSpec((shard_rows, D), whole),
        ],
        out_specs=(
            pl.BlockSpec((rows, D), whole),
            pl.BlockSpec((shard_rows, D), lambda t: (0, t)),
            pl.BlockSpec((shard_rows, D), whole),
            pl.BlockSpec((spare, shard_rows), whole),
        ),
        scratch_shapes=[pltpu.VMEM((rows, D), jnp.float32)],
        compiler_params=pltpu.CompilerParams(vmem_limit_bytes=60 * mega),
        name="finish",
    )(grads, weight, packed, packed, tokens, gain, grad_middle, out_low)


def rms_norm(features, scales):
    factor = lax.rsqrt(jnp.mean(features * features, axis=-1, keepdims=True) + epsilon)
    return features * factor * scales


def buckets_of(offsets):
    distance = np.abs(offsets)
    beyond = 8 + np.sum(distance[..., None] >= np.array(far_bounds), axis=-1)
    return np.where(distance < 8, distance, beyond) + 16 * (offsets > 0)


def skew_buckets():
    lanes = np.arange(2 * tile)
    from_query = np.where(lanes < tile, -lanes, 2 * tile - lanes)
    return np.concatenate([buckets_of(near * tile + from_query) for near in (-1, 0, 1)])


def lane_row_mask(head, width, rows):
    lanes = lax.broadcasted_iota(jnp.int32, (rows, width), 1)
    return (lanes >= head * HEAD) & (lanes < (head + 1) * HEAD)


def fold_rows(block, op):
    return op(block.reshape(block.shape[0] // 8, 8, block.shape[1]), axis=0)


def nt_dot(left, right):
    return lax.dot_general(left, right, (((1,), (1,)), ((), ())), preferred_element_type=jnp.float32)


def tn_dot(left, right):
    return lax.dot_general(left, right, (((0,), (0,)), ((), ())), preferred_element_type=jnp.float32)


def nn_dot(left, right):
    return jnp.dot(left, right, preferred_element_type=jnp.float32)


def build_bias(base_ref, far_ref, bias_sc, heads_here):
    for head in range(heads_here):
        for near in range(3):
            row = base_ref[pl.ds(head * 3 + near, 1), :]
            wide = jnp.broadcast_to(row, (tile, 2 * tile))
            skewed = pltpu.roll(wide, 0, 1, stride=1, stride_axis=0)
            bias_sc[head, near] = skewed[:, :tile]
        bias_sc[head, 3] = jnp.full((tile, tile), far_ref[head, 1], jnp.float32)


def unskew_sum(wide):
    lanes = wide.shape[1]
    half = wide.shape[0] // 2
    while half >= 8:
        wide = wide[:half] + pltpu.roll(wide[half:], lanes - half, 1)
        half //= 2
    total = wide[0:1]
    for row in range(1, 8):
        total = total + pltpu.roll(wide[row : row + 1], lanes - row, 1)
    return total


def rows_at(index):
    return pl.ds(pl.multiple_of(index * tile, tile), tile)


def visible_tile(key_tile, query_tile, prefix_length):
    key_pos = key_tile * tile + lax.broadcasted_iota(jnp.int32, (tile, tile), 0)
    query_pos = query_tile * tile + lax.broadcasted_iota(jnp.int32, (tile, tile), 1)
    return (key_pos <= query_pos) | (key_pos < prefix_length)


class Spread:
    def __init__(self, spot, rows, far_rows, side_rows, full, sems):
        self.spot, self.rows, self.full = spot, rows, full
        self.far_rows, self.side_rows = far_rows, side_rows
        self.send, self.recv, self.local = sems[:3]
        self.across_send, self.across_recv, self.core_send, self.core_recv = sems[3:]
        self.early = early_keys(spot.groups)
        self.rest = [key for key in far_keys(spot.groups) if key not in self.early]
        self.near = near_keys(spot.groups)

    @staticmethod
    def sems(groups, columns):
        half = columns // 2
        return [pltpu.SemaphoreType.DMA((groups,))] * 2 + [
            pltpu.SemaphoreType.DMA((groups, half))
        ] * 5

    def source(self, key, step):
        spot = self.spot
        at = flip(spot.place, key)
        if key and key not in self.early:
            return self.full.at[spot.behind(step), at]
        if step:
            return self.side_rows.at[step - 1, at]
        return self.far_rows.at[at] if key else self.rows.at[at]

    def local_copy(self, key, step):
        spot = self.spot
        target = self.full.at[spot.behind(step), flip(spot.place, key)]
        return pltpu.make_async_copy(self.source(key, step), target, self.local.at[key, step])

    def swap(self, key):
        spot = self.spot
        peer = flip(spot.place, key)
        return remote(
            self.rows.at[peer],
            self.full.at[spot.lane, spot.place],
            self.send.at[key],
            self.recv.at[key],
            (peer, spot.lane),
        )

    def across(self, key, step):
        spot = self.spot
        block = self.full.at[spot.lane, flip(spot.place, key)]
        return remote(
            block,
            block,
            self.across_send.at[key, step],
            self.across_recv.at[key, step],
            (spot.place, spot.across(step)),
        )

    def core(self, key, step):
        spot = self.spot
        return remote(
            self.source(key, step),
            self.full.at[spot.behind(step), flip(spot.place, key)],
            self.core_send.at[key, step],
            self.core_recv.at[key, step],
            (spot.place, spot.partner),
        )

    def begin(self):
        for key in self.rest + self.near:
            self.swap(key).start()
        for key in [0] + self.early:
            for step in range(self.spot.half):
                self.core(key, step).start()
                self.local_copy(key, step).start()

    def advance(self, key):
        self.swap(key).wait_recv()
        for step in range(1, self.spot.half):
            self.across(key, step).start()
        self.core(key, 0).start()

    def pass_on(self, key):
        for step in range(1, self.spot.half):
            self.across(key, step).wait_recv()
            self.core(key, step).start()

    def finish(self):
        half = self.spot.half
        keys = range(self.spot.groups)
        for key in keys:
            for step in range(half):
                self.core(key, step).wait_recv()
        for key in keys:
            moved = key in self.near + self.rest
            if moved:
                self.swap(key).wait_send()
            for step in range(half):
                self.core(key, step).wait_send()
                if not moved:
                    self.local_copy(key, step).wait()
                elif step:
                    self.across(key, step).wait_send()


def attend_forward_kernel(
    heads_here,
    groups,
    columns,
    prefix_ref,
    far_ref,
    base_ref,
    qkv_ref,
    rows_ref,
    far_rows_ref,
    side_rows_ref,
    mixed_ref,
    totals_ref,
    full_ref,
    bias_sc,
    score_sc,
    value_sc,
    *sems,
):
    width = heads_here * HEAD
    query_tile = pl.program_id(0)
    tiles = qkv_ref.shape[0] // tile
    spot = Spot(groups, columns)
    job = Spread(spot, rows_ref, far_rows_ref, side_rows_ref, full_ref, sems)

    @pl.when(query_tile == 0)
    def _():
        spot.meet()
        job.begin()

    prefix_length = prefix_ref[0]
    heads = range(heads_here)

    @pl.when(query_tile == 0)
    def _():
        build_bias(base_ref, far_ref, bias_sc, heads_here)
        for key_tile in range(value_sc.shape[1] // tile):
            rows = pl.ds(key_tile * tile, tile)
            values = qkv_ref[rows, 2 * width : 3 * width].astype(jnp.float32)
            value_sc[:, rows] = jnp.transpose(values).astype(jnp.bfloat16)

    queries = qkv_ref[rows_at(query_tile), :width]
    head_queries = [
        jnp.where(lane_row_mask(head, width, tile), queries, jnp.zeros_like(queries)) for head in heads
    ]

    def score_tiles(key_tile, tops, finish):
        keys = qkv_ref[rows_at(key_tile), width : 2 * width]
        out = []
        for head in heads:
            scores = finish(head, nt_dot(keys, head_queries[head]) * (score_scale * log2e))
            score_sc[head, rows_at(key_tile), :] = scores
            out.append(jnp.maximum(tops[head], fold_rows(scores, jnp.max)))
        return tuple(out)

    def far_body(key_tile, tops):
        return score_tiles(key_tile, tops, lambda head, raw: raw + far_ref[head, 0])

    def near_body(key_tile, tops):
        return score_tiles(key_tile, tops, lambda head, raw: raw + bias_sc[head, 0])

    def tail_body(key_tile, tops):
        shown = visible_tile(key_tile, query_tile, prefix_length)
        which = 1 + jnp.minimum(key_tile - query_tile, 2)
        return score_tiles(
            key_tile, tops, lambda head, raw: jnp.where(shown, raw + bias_sc[head, which], masked_score)
        )

    tile_count = jnp.maximum(query_tile + 1, tiles // 2)
    near_start = jnp.maximum(query_tile - 1, 0)
    tops = tuple(jnp.full((8, tile), masked_score, jnp.float32) for _ in heads)
    tops = lax.fori_loop(0, near_start, far_body, tops)
    tops = lax.fori_loop(near_start, query_tile, near_body, tops)
    tops = lax.fori_loop(query_tile, tile_count, tail_body, tops)
    tops = [jnp.max(top, axis=0, keepdims=True) for top in tops]

    def mix_body(key_tile, carry):
        sums, mixes = carry
        new_sums, new_mixes = [], []
        for head in heads:
            expos = jnp.exp2(score_sc[head, rows_at(key_tile), :] - tops[head])
            new_sums.append(sums[head] + fold_rows(expos, jnp.sum))
            values = value_sc[head * HEAD : (head + 1) * HEAD, rows_at(key_tile)]
            new_mixes.append(mixes[head] + nn_dot(values, expos.astype(jnp.bfloat16)))
        return (tuple(new_sums), tuple(new_mixes))

    sums, mixes = lax.fori_loop(
        0,
        tile_count,
        mix_body,
        (
            tuple(jnp.zeros((8, tile), jnp.float32) for _ in heads),
            tuple(jnp.zeros((HEAD, tile), jnp.float32) for _ in heads),
        ),
    )
    parts = []
    for head in heads:
        total = jnp.sum(sums[head], axis=0, keepdims=True)
        parts.append(mixes[head] / total)
        totals_ref[0, pl.ds(head, 1), :] = tops[head] + jnp.log2(total)
    mixed_ref[...] = jnp.transpose(jnp.concatenate(parts, axis=0)).astype(jnp.bfloat16)

    @pl.when(query_tile == tiles // 2)
    def _():
        for key in job.near:
            job.advance(key)

    @pl.when(query_tile == tiles - 2)
    def _():
        for key in job.near[:1]:
            job.pass_on(key)

    @pl.when(query_tile == tiles - 2)
    def _():
        for key in job.rest:
            job.advance(key)

    @pl.when(query_tile == tiles - 1)
    def _():
        for key in job.near[1:] + job.rest:
            job.pass_on(key)
        job.finish()


def attend_forward(prefix, far_bias, base_bias, qkv, rows, far_rows, side_rows, columns):
    length = qkv.shape[0]
    groups = rows.shape[0]
    width = qkv.shape[1] // 3
    heads_here = width // HEAD
    tiles = length // tile
    return pl.pallas_call(
        functools.partial(attend_forward_kernel, heads_here, groups, columns),
        grid=(tiles,),
        out_shape=(
            jax.ShapeDtypeStruct((length, width), jnp.bfloat16),
            jax.ShapeDtypeStruct((tiles, heads_here, tile), jnp.float32),
            jax.ShapeDtypeStruct((columns,) + rows.shape, rows.dtype),
        ),
        in_specs=[
            pl.BlockSpec(memory_space=pltpu.SMEM),
            pl.BlockSpec(memory_space=pltpu.SMEM),
            pl.BlockSpec(base_bias.shape, lambda i: (0, 0)),
            pl.BlockSpec(qkv.shape, lambda i: (0, 0)),
            anywhere,
            anywhere,
            anywhere,
        ],
        out_specs=(
            pl.BlockSpec((tile, width), lambda i: (i, 0)),
            pl.BlockSpec((1, heads_here, tile), lambda i: (i, 0, 0)),
            anywhere,
        ),
        scratch_shapes=[
            pltpu.VMEM((heads_here, 4, tile, tile), jnp.float32),
            pltpu.VMEM((heads_here, length, tile), jnp.float32),
            pltpu.VMEM((width, length), jnp.bfloat16),
        ]
        + Spread.sems(groups, columns),
        compiler_params=comm_params(5),
        cost_estimate=pl.CostEstimate(
            flops=40 * length * length * width, transcendentals=length * length * heads_here,
            bytes_accessed=8 * length * width,
        ),
        name="attend_forward",
    )(prefix, far_bias, base_bias, qkv, rows, far_rows, side_rows)


def attend_backward_kernel(
    heads_here,
    groups,
    columns,
    prefix_ref,
    far_ref,
    base_ref,
    qkv_ref,
    mixed_ref,
    grad_ref,
    totals_ref,
    part_ref,
    sums_ref,
    out_ref,
    near_ref,
    side_ref,
    result_ref,
    piece_ref,
    bias_sc,
    key_sc,
    grad_key_sc,
    grad_value_sc,
    near_sc,
    *scratch,
):
    width = heads_here * HEAD
    query_tile = pl.program_id(0)
    tiles = qkv_ref.shape[0] // tile
    spot = Spot(groups, columns)
    pieces = scratch[0]
    swap = Exchange(
        spot, lambda at, third: (sums_ref.at[at], pieces.at[spot.place]), 1, *scratch[1:4]
    )
    job = Collect(spot, part_ref, result_ref, scratch[4:])

    @pl.when(query_tile == 0)
    def _():
        spot.meet()
        job.begin()
        swap.begin()

    prefix_length = prefix_ref[0]
    heads = range(heads_here)

    @pl.when(query_tile == 0)
    def _():
        build_bias(base_ref, far_ref, bias_sc, heads_here)
        for key_tile in range(key_sc.shape[1] // tile):
            rows = pl.ds(key_tile * tile, tile)
            keys = qkv_ref[rows, width : 2 * width].astype(jnp.float32)
            key_sc[:, rows] = jnp.transpose(keys).astype(jnp.bfloat16)
        grad_key_sc[...] = jnp.zeros_like(grad_key_sc)
        grad_value_sc[...] = jnp.zeros_like(grad_value_sc)
        near_sc[...] = jnp.zeros_like(near_sc)
        side_ref[...] = jnp.zeros_like(side_ref)

    queries = qkv_ref[rows_at(query_tile), :width]
    grads = grad_ref[rows_at(query_tile), :]
    products = grads.astype(jnp.float32) * mixed_ref[rows_at(query_tile), :].astype(jnp.float32)
    head_queries, head_grads, inners, totals = [], [], [], []
    for head in heads:
        mask = lane_row_mask(head, width, tile)
        head_queries.append(jnp.where(mask, queries, jnp.zeros_like(queries)))
        head_grads.append(jnp.where(mask, grads, jnp.zeros_like(grads)))
        ones = jnp.where(lane_row_mask(head, width, 8), 1.0, 0.0)
        inner = lax.dot_general(
            ones,
            products,
            (((1,), (1,)), ((), ())),
            precision=lax.Precision.HIGHEST,
            preferred_element_type=jnp.float32,
        )
        inners.append(inner[0:1, :])
        totals.append(totals_ref[0, pl.ds(head, 1), :])

    def step(key_tile, carry, finish, keep):
        sides, grad_queries = carry
        keys = qkv_ref[rows_at(key_tile), width : 2 * width]
        values = qkv_ref[rows_at(key_tile), 2 * width : 3 * width]
        new_sides, new_queries = [], []
        key_part, value_part = None, None
        for head in heads:
            raw = nt_dot(keys, head_queries[head]) * (score_scale * log2e)
            attention = jnp.exp2(finish(head, raw))
            grad_weights = nt_dot(values, head_grads[head])
            grad_scores = attention * (grad_weights - inners[head])
            new_sides.append(keep(head, grad_scores, sides[head]))
            low_scores = grad_scores.astype(jnp.bfloat16)
            keys_across = key_sc[head * HEAD : (head + 1) * HEAD, rows_at(key_tile)]
            new_queries.append(grad_queries[head] + nn_dot(keys_across, low_scores))
            value_one = nn_dot(attention.astype(jnp.bfloat16), head_grads[head])
            key_one = nn_dot(low_scores, head_queries[head])
            value_part = value_one if value_part is None else value_part + value_one
            key_part = key_one if key_part is None else key_part + key_one
        grad_key_sc[rows_at(key_tile), :] += key_part
        grad_value_sc[rows_at(key_tile), :] += value_part
        return (tuple(new_sides), tuple(new_queries))

    def add_side(head, grad_scores, side):
        return side + fold_rows(grad_scores, jnp.sum)

    def far_body(key_tile, carry):
        return step(
            key_tile, carry, lambda head, raw: raw + (far_ref[head, 0] - totals[head]), add_side
        )

    def near_body(key_tile, carry):
        def keep(head, grad_scores, side):
            near_sc[head, 0] += grad_scores
            return side

        return step(
            key_tile, carry, lambda head, raw: raw + bias_sc[head, 0] - totals[head], keep
        )

    def tail_body(key_tile, carry):
        shown = visible_tile(key_tile, query_tile, prefix_length)
        which = 1 + jnp.minimum(key_tile - query_tile, 2)

        def keep(head, grad_scores, side):
            near_sc[head, which] += grad_scores
            return side

        return step(
            key_tile,
            carry,
            lambda head, raw: jnp.where(
                shown, raw + bias_sc[head, which] - totals[head], masked_score
            ),
            keep,
        )

    tile_count = jnp.maximum(query_tile + 1, tiles // 2)
    near_start = jnp.maximum(query_tile - 1, 0)
    carry = (
        tuple(jnp.zeros((8, tile), jnp.float32) for _ in heads),
        tuple(jnp.zeros((HEAD, tile), jnp.float32) for _ in heads),
    )
    carry = lax.fori_loop(0, near_start, far_body, carry)
    carry = lax.fori_loop(near_start, query_tile, near_body, carry)
    carry = lax.fori_loop(query_tile, tile_count, tail_body, carry)
    sides, grad_queries = carry
    for head in heads:
        side_ref[head, 0] += sides[head]
    across = jnp.concatenate(grad_queries, axis=0) * score_scale
    out_ref[rows_at(query_tile), :width] = jnp.transpose(across).astype(jnp.bfloat16)

    for step in range(tiles):
        middles = [key for key in range(groups) if key * 2 // groups == step]
        lasts = [key for key in range(groups) if min(tiles - 1, 2 + key * 3 // 4) == step]

        @pl.when(query_tile == step)
        def _():
            for key in middles:
                job.middle(key)
            for key in lasts:
                job.last(key)

    @pl.when(query_tile == tiles - 1)
    def _():
        out_ref[:, width : 2 * width] = (grad_key_sc[...] * score_scale).astype(jnp.bfloat16)
        out_ref[:, 2 * width : 3 * width] = grad_value_sc[...].astype(jnp.bfloat16)
        for head in heads:
            side_ref[head, 1] = fold_rows(near_sc[head, 3], jnp.sum)
            for near in range(3):
                wide = jnp.concatenate(
                    [near_sc[head, near], jnp.zeros((tile, tile), jnp.float32)], axis=1
                )
                near_ref[pl.ds(head * 3 + near, 1), :] = unskew_sum(wide)

    @pl.when(query_tile == tiles - 1)
    def _():
        swap.arrive()
        piece_ref[...] = jnp.sum(pieces[...].astype(jnp.float32), axis=0).astype(jnp.bfloat16)
        job.finish()
        swap.finish()


def attend_backward(
    prefix, far_bias, base_bias, qkv, mixed, grad_mixed, totals, part, sums, columns
):
    length = qkv.shape[0]
    groups, piece_rows, piece_width = sums.shape
    block = part.shape[2:]
    width = qkv.shape[1] // 3
    heads_here = width // HEAD
    tiles = length // tile
    whole = lambda i: (0, 0)
    return pl.pallas_call(
        functools.partial(attend_backward_kernel, heads_here, groups, columns),
        grid=(tiles,),
        out_shape=(
            jax.ShapeDtypeStruct((length, 3 * width), jnp.bfloat16),
            jax.ShapeDtypeStruct((heads_here * 3, 2 * tile), jnp.float32),
            jax.ShapeDtypeStruct((heads_here, 2, 8, tile), jnp.float32),
            jax.ShapeDtypeStruct((groups,) + block, jnp.bfloat16),
            jax.ShapeDtypeStruct((piece_rows, piece_width), jnp.bfloat16),
        ),
        in_specs=[
            pl.BlockSpec(memory_space=pltpu.SMEM),
            pl.BlockSpec(memory_space=pltpu.SMEM),
            pl.BlockSpec(base_bias.shape, whole),
            pl.BlockSpec(qkv.shape, whole),
            pl.BlockSpec(mixed.shape, whole),
            pl.BlockSpec(mixed.shape, whole),
            pl.BlockSpec((1, heads_here, tile), lambda i: (i, 0, 0)),
            anywhere,
            anywhere,
        ],
        out_specs=(
            pl.BlockSpec((length, 3 * width), whole),
            pl.BlockSpec((heads_here * 3, 2 * tile), whole),
            pl.BlockSpec((heads_here, 2, 8, tile), lambda i: (0, 0, 0, 0)),
            anywhere,
            pl.BlockSpec((piece_rows, piece_width), whole),
        ),
        scratch_shapes=[
            pltpu.VMEM((heads_here, 4, tile, tile), jnp.float32),
            pltpu.VMEM((width, length), jnp.bfloat16),
            pltpu.VMEM((length, width), jnp.float32),
            pltpu.VMEM((length, width), jnp.float32),
            pltpu.VMEM((heads_here, 4, tile, tile), jnp.float32),
            pltpu.VMEM(sums.shape, jnp.bfloat16),
        ]
        + Exchange.sems(groups, 1)
        + Collect.scratch(columns, groups, block),
        compiler_params=comm_params(6, 60),
        cost_estimate=pl.CostEstimate(
            flops=70 * length * length * width, transcendentals=length * length * heads_here,
            bytes_accessed=16 * length * width,
        ),
        name="attend_backward",
    )(prefix, far_bias, base_bias, qkv, mixed, grad_mixed, totals, part, sums)


def gelu_parts(act):
    inner = math.sqrt(2.0 / math.pi) * (act + 0.044715 * act * act * act)
    tanh = jnp.tanh(inner)
    half = 0.5 * (1.0 + tanh)
    slope = math.sqrt(2.0 / math.pi) * (1.0 + 3.0 * 0.044715 * act * act)
    return act * half, half + 0.5 * act * (1.0 - tanh * tanh) * slope


def slot_rows(experts_here):
    return experts_here * main_slots + -(-experts_here * tail_slots // 8) * 8


def tail_select(expert, sources, tail_height):
    rows = lax.broadcasted_iota(jnp.int32, (sources * tail_slots, sources * tail_height), 0)
    columns = lax.broadcasted_iota(jnp.int32, (sources * tail_slots, sources * tail_height), 1)
    wanted = (rows // tail_slots) * tail_height + expert * tail_slots + rows % tail_slots
    return jnp.where(columns == wanted, 1.0, 0.0).astype(jnp.bfloat16)


def expert_input(main_ref, tail_ref, select):
    width = main_ref.shape[-1]
    main = main_ref[...].reshape(-1, width)
    tail = nn_dot(select, tail_ref[...].reshape(-1, width)).astype(jnp.bfloat16)
    return jnp.concatenate([main, tail], axis=0)


def gates_of(wide_rows):
    return wide_rows[:, D : D + 1].astype(jnp.float32) + wide_rows[:, D + 1 : D + 2].astype(
        jnp.float32
    )


def expert_output(value, select, expert, main_sc, tail_sc):
    low = value.astype(jnp.bfloat16)
    main_count = main_sc.shape[0] * main_sc.shape[1] * main_slots
    main_sc[...] = low[:main_count].reshape(main_sc.shape)
    spread = tn_dot(select, low[main_count:]).astype(jnp.bfloat16).reshape(tail_sc.shape)

    @pl.when(expert == 0)
    def _():
        tail_sc[...] = spread

    @pl.when(expert > 0)
    def _():
        tail_sc[...] += spread


def expert_math(rows, gates, raw_hidden, gate_weight, up_weight, down_weight):
    gate_act = nt_dot(rows, gate_weight)
    up_act = nt_dot(rows, up_weight)
    gelu, slope = gelu_parts(gate_act)
    hidden = gelu * up_act
    low_hidden = hidden.astype(jnp.bfloat16)
    grad_gates = jnp.sum(raw_hidden * low_hidden.astype(jnp.float32), axis=1, keepdims=True)
    grad_hidden = raw_hidden * gates
    grad_gate = (grad_hidden * up_act * slope).astype(jnp.bfloat16)
    grad_up = (grad_hidden * gelu).astype(jnp.bfloat16)
    back = nn_dot(grad_gate, gate_weight) + nn_dot(grad_up, up_weight)
    gated = (hidden * gates).astype(jnp.bfloat16)
    return gated, grad_gate, grad_up, back, grad_gates, nn_dot(low_hidden, down_weight)


def slot_lanes(expert, experts_here, sources):
    main = sources * main_slots
    count = sources * CAP
    rows = lax.broadcasted_iota(jnp.int32, (count, sources), 0)
    source = jnp.where(rows < main, rows // main_slots, (rows - main) // tail_slots)
    hot = jnp.where(lax.broadcasted_iota(jnp.int32, (count, sources), 1) == source, 1.0, 0.0)
    rows = lax.broadcasted_iota(jnp.int32, (count, spare), 0)
    lane = jnp.where(
        rows < main,
        expert * main_slots + rows % main_slots,
        experts_here * main_slots + expert * tail_slots + (rows - main) % tail_slots,
    )
    return hot.astype(jnp.bfloat16), lax.broadcasted_iota(jnp.int32, (count, spare), 1) == lane


def split_low(values):
    high = values.astype(jnp.bfloat16)
    return high, (values - high.astype(jnp.float32)).astype(jnp.bfloat16)


def expert_act_kernel(
    experts_here,
    row_main,
    row_tail,
    grad_main,
    grad_tail,
    gate_weight,
    up_weight,
    down_weight,
    hidden_ref,
    grad_gate_ref,
    grad_up_ref,
    result_ref,
    back_ref,
    result_main,
    result_tail,
    back_main,
    back_tail,
    sems,
):
    part, expert = pl.program_id(0), pl.program_id(1)
    shards_part = row_main.shape[0]
    sources = shards_part * row_main.shape[1]
    tail_height = row_tail.shape[2]
    sources_at = pl.ds(part * shards_part, shards_part)
    select = tail_select(expert, sources, tail_height)
    wide_rows = expert_input(row_main, row_tail, select)
    grads = expert_input(grad_main, grad_tail, select)
    hidden, grad_gate, grad_up, back, grad_gates, result = expert_math(
        wide_rows[:, :D],
        gates_of(wide_rows),
        nt_dot(grads, down_weight[0]),
        gate_weight[0],
        up_weight[0],
        down_weight[0],
    )
    lanes = lax.broadcasted_iota(jnp.int32, (back.shape[0], spare), 1)
    back = jnp.concatenate([back, jnp.where(lanes == 0, grad_gates, 0.0)], axis=1)
    hidden_ref[0] = hidden
    grad_gate_ref[0] = grad_gate
    grad_up_ref[0] = grad_up

    def main_copies(at):
        place = pl.ds(pl.multiple_of(at * main_slots, main_slots), main_slots)
        return (
            pltpu.make_async_copy(result_main, result_ref.at[sources_at, :, place, :], sems.at[0]),
            pltpu.make_async_copy(back_main, back_ref.at[sources_at, :, place, :], sems.at[1]),
        )

    @pl.when(expert > 0)
    def _():
        for copy in main_copies(expert - 1):
            copy.wait()

    expert_output(result, select, expert, result_main, result_tail)
    expert_output(back, select, expert, back_main, back_tail)
    for copy in main_copies(expert):
        copy.start()

    @pl.when(expert == experts_here - 1)
    def _():
        place = pl.ds(experts_here * main_slots, tail_height)
        tails = (
            pltpu.make_async_copy(result_tail, result_ref.at[sources_at, :, place, :], sems.at[2]),
            pltpu.make_async_copy(back_tail, back_ref.at[sources_at, :, place, :], sems.at[3]),
        )
        for copy in tails:
            copy.start()
        for copy in main_copies(expert):
            copy.wait()
        for copy in tails:
            copy.wait()


def parts_of(rows):
    shards, groups = rows.shape[:2]
    return max(1, shards * groups // part_sources)


def row_specs(rows, experts_here, order):
    shards, groups, height, width = rows.shape
    shards_part = shards // parts_of(rows)
    tail_height = slot_rows(experts_here) - experts_here * main_slots
    tail_at = experts_here * main_slots // tail_height
    main_at = lambda e, c: (c, 0, e, 0)
    side_at = lambda e, c: (c, 0, tail_at, 0)
    return [
        pl.BlockSpec((shards_part, groups, main_slots, width), order(main_at)),
        pl.BlockSpec((shards_part, groups, tail_height, width), order(side_at)),
    ]


def expert_act(rows, grads, gate_weight, up_weight, down_weight):
    experts_here, units, width = gate_weight.shape
    shards, groups = rows.shape[:2]
    count = shards * groups * CAP
    parts = parts_of(rows)
    height = slot_rows(experts_here)
    tail_height = height - experts_here * main_slots
    order = lambda index: lambda c, e: index(e, c)
    weight_spec = pl.BlockSpec((1, units, width), lambda c, e: (e, 0, 0))
    act_spec = pl.BlockSpec((1, count // parts, units), lambda c, e: (e, c, 0))
    act_shape = jax.ShapeDtypeStruct((experts_here, count, units), jnp.bfloat16)
    slot_shape = lambda lanes: jax.ShapeDtypeStruct(
        (shards, groups, height, lanes), jnp.bfloat16
    )
    scratch = [
        pltpu.VMEM((shards // parts, groups, rows_of, lanes), jnp.bfloat16)
        for lanes in (width, width + spare)
        for rows_of in (main_slots, tail_height)
    ]
    return pl.pallas_call(
        functools.partial(expert_act_kernel, experts_here),
        grid=(parts, experts_here),
        out_shape=(act_shape, act_shape, act_shape, slot_shape(width), slot_shape(width + spare)),
        in_specs=row_specs(rows, experts_here, order)
        + row_specs(grads, experts_here, order)
        + [weight_spec] * 3,
        out_specs=(
            act_spec,
            act_spec,
            act_spec,
            pl.BlockSpec(memory_space=pl.ANY),
            pl.BlockSpec(memory_space=pl.ANY),
        ),
        scratch_shapes=scratch + [pltpu.SemaphoreType.DMA((4,))],
        compiler_params=pltpu.CompilerParams(vmem_limit_bytes=60 * mega),
        cost_estimate=pl.CostEstimate(
            flops=12 * experts_here * count * width * units,
            transcendentals=experts_here * count * units,
            bytes_accessed=6 * experts_here * width * units + 8 * experts_here * count * width,
        ),
        name="expert_act",
    )(rows, rows, grads, grads, gate_weight, up_weight, down_weight)


class RowChunk:
    def __init__(self, spot, number, place_rows, rows_in, rows_all, back_out, bufs, sems):
        self.spot, self.number, self.place_rows = spot, number, place_rows
        self.rows_in, self.rows_all, self.back_out = rows_in, rows_all, back_out
        self.rows, self.back, self.pair_in, self.across_out, self.across_in, self.total = bufs
        (
            self.local,
            self.send,
            self.recv,
            self.across_send,
            self.across_recv,
            self.core_send,
            self.core_recv,
            self.pair_send,
            self.pair_recv,
            self.sum_send,
            self.sum_recv,
            self.back_send,
            self.back_recv,
        ) = sems

    @staticmethod
    def sems(groups, columns, chunks):
        half = columns // 2
        dma = pltpu.SemaphoreType.DMA
        return (
            [dma((chunks, 4))]
            + [dma((chunks, groups))] * 2
            + [dma((chunks, half, 2))] * 8
            + [dma((chunks, groups))] * 2
        )

    def keys(self, near):
        groups = self.spot.groups
        return [0] + near_keys(groups) if near else far_keys(groups)

    def side(self, near):
        half = self.spot.groups // 2
        here = self.spot.place // half
        return pl.ds((here if near else 1 - here) * half, half)

    def swap(self, key):
        spot, at = self.spot, self.number
        peer = flip(spot.place, key)
        source = self.rows_in.at[peer, self.place_rows]
        target = self.rows.at[spot.lane, spot.place]
        if key == 0:
            return pltpu.make_async_copy(source, target, self.local.at[at, 0])
        return remote(
            source, target, self.send.at[at, key], self.recv.at[at, key], (peer, spot.lane)
        )

    def keep(self, near):
        side = self.side(near)
        return pltpu.make_async_copy(
            self.rows.at[:, side],
            self.rows_all.at[:, side, self.place_rows],
            self.local.at[self.number, 1 + near],
        )

    def across(self, near, step):
        spot, at = self.spot, self.number
        block = self.rows.at[spot.lane, self.side(near)]
        return remote(
            block,
            block,
            self.across_send.at[at, step, near],
            self.across_recv.at[at, step, near],
            (spot.place, spot.across(step)),
        )

    def core(self, near, step):
        spot, at = self.spot, self.number
        block = self.rows.at[spot.behind(step), self.side(near)]
        return remote(
            block,
            block,
            self.core_send.at[at, step, near],
            self.core_recv.at[at, step, near],
            (spot.place, spot.partner),
        )

    def begin(self, near):
        for key in self.keys(near):
            self.swap(key).start()

    def advance(self, near):
        for key in self.keys(near):
            self.swap(key).wait_recv() if key else self.swap(key).wait()
        for step in range(1, self.spot.half):
            self.across(near, step).start()
        self.core(near, 0).start()

    def complete(self, near):
        half = self.spot.half
        for step in range(1, half):
            self.across(near, step).wait_recv()
            self.core(near, step).start()
        for step in range(half):
            self.core(near, step).wait_recv()
        if self.rows_all is not None:
            self.keep(near).start()

    def pair_copy(self, step, near):
        spot, at = self.spot, self.number
        side = self.side(near)
        return remote(
            self.back.at[spot.lane_at(step, True), side],
            self.pair_in.at[step, side],
            self.pair_send.at[at, step, near],
            self.pair_recv.at[at, step, near],
            (spot.place, spot.partner),
        )

    def sum_copy(self, step, near):
        spot, at = self.spot, self.number
        side = self.side(near)
        return remote(
            self.across_out.at[step, side],
            self.across_in.at[step, side],
            self.sum_send.at[at, step, near],
            self.sum_recv.at[at, step, near],
            (spot.place, spot.across(step)),
        )

    def back_copy(self, key):
        spot, at = self.spot, self.number
        peer = flip(spot.place, key)
        target = self.back_out.at[spot.place, self.place_rows]
        if key == 0:
            return pltpu.make_async_copy(self.total.at[peer], target, self.local.at[at, 3])
        return remote(
            self.total.at[peer],
            target,
            self.back_send.at[at, key],
            self.back_recv.at[at, key],
            (peer, spot.lane),
        )

    def pair(self, near):
        for step in list(range(1, self.spot.half)) + [0]:
            self.pair_copy(step, near).start()

    def pair_sum(self, step, near):
        side = self.side(near)
        mine = self.back[self.spot.lane_at(step, False), side].astype(jnp.float32)
        return mine + self.pair_in[step, side].astype(jnp.float32)

    def middle(self, near):
        for step in range(1, self.spot.half):
            self.pair_copy(step, near).wait_recv()
            total = self.pair_sum(step, near)
            self.across_out[step, self.side(near)] = total.astype(self.total.dtype)
            self.sum_copy(step, near).start()
        self.pair_copy(0, near).wait_recv()

    def last(self, near):
        total = self.pair_sum(0, near)
        for step in range(1, self.spot.half):
            self.sum_copy(step, near).wait_recv()
            total = total + self.across_in[step, self.side(near)].astype(jnp.float32)
        self.total[self.side(near)] = total.astype(self.total.dtype)
        for key in self.keys(near):
            self.back_copy(key).start()

    def finish(self):
        groups, half = self.spot.groups, self.spot.half
        for key in range(1, groups):
            self.back_copy(key).wait_recv()
        self.back_copy(0).wait()
        for near in range(2):
            if self.rows_all is not None:
                self.keep(near).wait()
            for step in range(half):
                self.core(near, step).wait_send()
                self.pair_copy(step, near).wait_send()
                if step:
                    self.across(near, step).wait_send()
                    self.sum_copy(step, near).wait_send()
        for key in range(groups):
            if key:
                self.swap(key).wait_send()
                self.back_copy(key).wait_send()


half_chunks = ((1, 0), (1, 1), (0, 0), (0, 1), (0, 2), (0, 3), (1, 2), (1, 3))


def half_expert(step):
    return step - 2 * ((step // 2 + 1) // 2)


def half_far(step):
    return (step // 2 + 1) // 2 % 2


def experts_kernel(
    experts_here,
    groups,
    columns,
    rows_in,
    gates_in,
    grad_main,
    grad_tail,
    gate_weight,
    up_weight,
    down_weight,
    hidden_ref,
    grad_gate_ref,
    grad_up_ref,
    result_ref,
    rows_all,
    back_out,
    gates_out,
    act_sc,
    act_sems,
    result_main,
    result_tail,
    result_sems,
    *scratch,
):
    now = pl.program_id(0)
    expert = half_expert(now)
    tail_height = result_tail.shape[2]
    half_groups = groups // 2
    sources = half_groups * columns
    main_count, count = sources * main_slots, sources * CAP
    spot = Spot(groups, columns)
    here = spot.place // half_groups
    side_at = here + half_far(now) * (1 - 2 * here)
    side = pl.ds(side_at * half_groups, half_groups)
    mains, tails, sides, sems = scratch[:6], scratch[6:12], scratch[12:18], scratch[18:]
    chunks = [
        RowChunk(
            spot,
            at,
            pl.ds(at * main_slots, main_slots),
            rows_in,
            rows_all,
            back_out,
            [buf.at[at] for buf in mains],
            sems,
        )
        for at in range(experts_here)
    ]
    tail = RowChunk(
        spot,
        experts_here,
        pl.ds(experts_here * main_slots, tail_height),
        rows_in,
        rows_all,
        back_out,
        tails,
        sems,
    )
    scalars = RowChunk(
        spot, experts_here + 1, pl.ds(0, 8), gates_in, None, gates_out, sides, sems
    )

    @pl.when(now == 0)
    def _():
        spot.meet()
        scalars.begin(1)
        tail.begin(1)
        chunks[0].begin(1)
        chunks[1].begin(1)
        scalars.begin(0)
        tail.begin(0)
        chunks[0].begin(0)
        sides[1][...] = jnp.zeros_like(sides[1])

    select = tail_select(expert, sources, tail_height)

    def joined(main, low):
        width = main.shape[-1]
        low = nn_dot(select, low.reshape(-1, width)).astype(jnp.bfloat16)
        return jnp.concatenate([main.reshape(-1, width), low], axis=0)

    raw_hidden = nt_dot(joined(grad_main[:, side], grad_tail[:, side]), down_weight[0])

    def before(step):
        if step == 0:
            scalars.advance(1)
            tail.advance(1)
            chunks[0].advance(1)
            chunks[1].begin(0)
            chunks[1].advance(1)
            scalars.complete(1)
            tail.complete(1)
        elif step == 1:
            scalars.advance(0)
            tail.advance(0)
            chunks[0].advance(0)
            chunks[2].begin(0)
        elif step == 2:
            chunks[1].advance(0)
            chunks[3].begin(0)
            scalars.complete(0)
            tail.complete(0)
        elif step == 3:
            chunks[2].advance(0)
            chunks[2].begin(1)
            chunks[3].begin(1)
        elif step == 4:
            chunks[3].advance(0)
        elif step == 5:
            chunks[2].advance(1)
        elif step == 6:
            chunks[3].advance(1)
        near, at = half_chunks[step]
        chunks[at].complete(near)
        if step:
            near, at = half_chunks[step - 1]
            chunks[at].middle(near)
        if step == 6:
            tail.middle(0)
            scalars.middle(0)

    for step in range(len(half_chunks)):

        @pl.when(now == step)
        def _():
            before(step)

    rows = joined(mains[0][expert, :, side], tails[0][:, side])
    hot, of_slot = slot_lanes(expert, experts_here, sources)
    gate_high, gate_rest = split_low(sides[0][:, side, 0, :].reshape(sources, spare))
    gates = nn_dot(hot, gate_high) + nn_dot(hot, gate_rest)
    gates = jnp.sum(jnp.where(of_slot, gates, 0.0), axis=1, keepdims=True)
    hidden, grad_gate, grad_up, back, grad_gates, result = expert_math(
        rows, gates, raw_hidden, gate_weight[0], up_weight[0], down_weight[0]
    )

    def spread(value, main_target, tail_target):
        low = value.astype(jnp.bfloat16)
        main_target(low[:main_count].reshape(columns, half_groups, main_slots, -1))
        part = tn_dot(select, low[main_count:]).astype(jnp.bfloat16)
        part = part.reshape(columns, half_groups, tail_height, -1)

        @pl.when(expert == 0)
        def _():
            tail_target[:, side] = part

        @pl.when(expert > 0)
        def _():
            tail_target[:, side] += part

    def store_back(value):
        mains[1][expert, :, side] = value

    spread(back, store_back, tails[1])
    side_high, side_rest = split_low(jnp.where(of_slot, grad_gates, 0.0))
    lanes = (tn_dot(hot, side_high) + tn_dot(hot, side_rest)).reshape(columns, half_groups, spare)
    sides[1][:, side, 0, :] += lanes

    def after(step):
        near, at = half_chunks[step]
        chunks[at].pair(near)
        if step == 5:
            tail.pair(0)
            scalars.pair(0)
        if step == 7:
            tail.pair(1)
            scalars.pair(1)
            chunks[at].middle(1)
            tail.middle(1)
            scalars.middle(1)
        if step:
            near, at = half_chunks[step - 1]
            chunks[at].last(near)
        if step == 6:
            tail.last(0)
            scalars.last(0)

    for step in range(len(half_chunks)):

        @pl.when(now == step)
        def _():
            after(step)

    act_rows = pl.ds(pl.multiple_of(side_at * count, 32), count)

    def act_copies():
        outs = (hidden_ref, grad_gate_ref, grad_up_ref)
        return [
            pltpu.make_async_copy(act_sc.at[k], out.at[expert, act_rows], act_sems.at[k])
            for k, out in enumerate(outs)
        ]

    def result_copy():
        place = pl.ds(pl.multiple_of(expert * main_slots, main_slots), main_slots)
        return pltpu.make_async_copy(
            result_main, result_ref.at[:, side, place], result_sems.at[0]
        )

    @pl.when(now > 0)
    def _():
        result_copy().wait()
        for copy in act_copies():
            copy.wait()

    def store_result(value):
        result_main[...] = value

    spread(result, store_result, result_tail)
    act_sc[0] = hidden
    act_sc[1] = grad_gate
    act_sc[2] = grad_up
    result_copy().start()
    for copy in act_copies():
        copy.start()

    @pl.when(now == len(half_chunks) - 1)
    def _():
        place = pl.ds(experts_here * main_slots, tail_height)
        low = pltpu.make_async_copy(result_tail, result_ref.at[:, :, place], result_sems.at[1])
        low.start()
        chunks[-1].last(1)
        tail.last(1)
        scalars.last(1)
        for chunk in chunks + [tail, scalars]:
            chunk.finish()
        result_copy().wait()
        for copy in act_copies():
            copy.wait()
        low.wait()


def experts(rows, gates, grads, gate_weight, up_weight, down_weight, columns):
    experts_here, units, width = gate_weight.shape
    groups, height, wide = rows.shape
    half = columns // 2
    count = columns * groups * CAP
    tail_height = height - experts_here * main_slots
    weight_spec = pl.BlockSpec((1, units, width), lambda t: (half_expert(t), 0, 0))
    act_shape = jax.ShapeDtypeStruct((experts_here, count, units), jnp.bfloat16)
    low = lambda *shape: pltpu.VMEM(shape, jnp.bfloat16)
    bufs = lambda lead, *block, kind=jnp.bfloat16: [
        pltpu.VMEM((*lead, *first, groups, *block), kind)
        for first in ((columns,), (columns,), (half,), (half,), (half,), ())
    ]
    return pl.pallas_call(
        functools.partial(experts_kernel, experts_here, groups, columns),
        grid=(len(half_chunks),),
        out_shape=(
            act_shape,
            act_shape,
            act_shape,
            jax.ShapeDtypeStruct((columns, groups, height, width), jnp.bfloat16),
            jax.ShapeDtypeStruct((columns,) + rows.shape, jnp.bfloat16),
            jax.ShapeDtypeStruct(rows.shape, jnp.bfloat16),
            jax.ShapeDtypeStruct(gates.shape, jnp.float32),
        ),
        in_specs=[anywhere, anywhere]
        + row_specs(grads, experts_here, lambda index: lambda t: index(half_expert(t), 0))
        + [weight_spec] * 3,
        out_specs=(anywhere,) * 7,
        scratch_shapes=[
            low(3, count // 2, units),
            pltpu.SemaphoreType.DMA((3,)),
            low(columns, groups // 2, main_slots, width),
            low(columns, groups, tail_height, width),
            pltpu.SemaphoreType.DMA((2,)),
        ]
        + bufs((experts_here,), main_slots, wide)
        + bufs((), tail_height, wide)
        + bufs((), 8, spare, kind=jnp.float32)
        + RowChunk.sems(groups, columns, experts_here + 2),
        compiler_params=comm_params(10),
        cost_estimate=pl.CostEstimate(
            flops=12 * experts_here * count * width * units,
            transcendentals=experts_here * count * units,
            bytes_accessed=6 * experts_here * width * units + 8 * experts_here * count * width,
        ),
        name="experts",
    )(rows, gates, grads, grads, gate_weight, up_weight, down_weight)


def expert_weight_kernel(
    parts,
    halves,
    row_main,
    row_tail,
    grad_main,
    grad_tail,
    hidden_ref,
    grad_gate_ref,
    grad_up_ref,
    gate_out,
    up_out,
    down_out,
):
    expert, part = pl.program_id(0), pl.program_id(1)
    sources = row_main.shape[0] * row_main.shape[1]
    select = tail_select(expert, sources, row_tail.shape[2])
    if halves == 1:
        rows = expert_input(row_main, row_tail, select)[:, :D]
        grads = expert_input(grad_main, grad_tail, select)
    else:
        groups = row_main.shape[1] // halves
        select = tail_select(expert, sources // halves, row_tail.shape[2])
        sides = [slice(at * groups, (at + 1) * groups) for at in range(halves)]
        both = lambda main, low: jnp.concatenate(
            [expert_input(main[:, side], low[:, side], select) for side in sides], axis=0
        )
        rows, grads = both(row_main, row_tail), both(grad_main, grad_tail)

    @pl.when(part == 0)
    def _():
        gate_out[0] = tn_dot(grad_gate_ref[0], rows)
        up_out[0] = tn_dot(grad_up_ref[0], rows)
        down_out[0] = tn_dot(hidden_ref[0], grads)

    if parts > 1:

        @pl.when(part > 0)
        def _():
            gate_out[0] += tn_dot(grad_gate_ref[0], rows)
            up_out[0] += tn_dot(grad_up_ref[0], rows)
            down_out[0] += tn_dot(hidden_ref[0], grads)


def expert_weight_grads(rows, grads, hidden, grad_gate, grad_up, halves):
    experts_here, count, units = hidden.shape
    width = grads.shape[-1]
    parts = parts_of(rows)
    order = lambda index: index
    act_spec = pl.BlockSpec((1, count // parts, units), lambda e, c: (e, c, 0))
    out_spec = pl.BlockSpec((1, units, width), lambda e, c: (e, 0, 0))
    out_shape = jax.ShapeDtypeStruct((experts_here, units, width), jnp.float32)
    return pl.pallas_call(
        functools.partial(expert_weight_kernel, parts, halves),
        grid=(experts_here, parts),
        out_shape=(out_shape, out_shape, out_shape),
        in_specs=row_specs(rows, experts_here, order)
        + row_specs(grads, experts_here, order)
        + [act_spec] * 3,
        out_specs=(out_spec, out_spec, out_spec),
        compiler_params=pltpu.CompilerParams(vmem_limit_bytes=60 * mega),
        cost_estimate=pl.CostEstimate(
            flops=6 * experts_here * count * width * units,
            transcendentals=0,
            bytes_accessed=12 * experts_here * width * units + 10 * experts_here * count * width,
        ),
        name="expert_weight_grads",
    )(rows, rows, grads, grads, hidden, grad_gate, grad_up)


def pair_slots(token_routes, ranks, experts_here):
    row_count = token_routes.shape[0]
    expert_pair = jnp.concatenate([token_routes[:, 0], token_routes[:, 1]])
    rank_pair = jnp.concatenate([ranks, ranks + row_count])
    earlier = (expert_pair[None, :] == expert_pair[:, None]) & (
        rank_pair[None, :] < rank_pair[:, None]
    )
    slot_index = jnp.sum(earlier.astype(jnp.int32), axis=1)
    height = slot_rows(experts_here)
    local = expert_pair % experts_here
    main_at = local * main_slots + slot_index
    tail_at = experts_here * main_slots + local * tail_slots + slot_index - main_slots
    row = jnp.where(slot_index < main_slots, main_at, tail_at)
    slots = (expert_pair // experts_here) * height + row
    return jnp.where(slot_index < CAP, slots, -1)


def router_head(logits, token_routes, weights):
    token_count = logits.shape[0]
    probabilities = jax.nn.softmax(logits, axis=-1)
    log_totals = jax.nn.logsumexp(logits, axis=-1)
    picked = (token_routes[:, :, None] == jnp.arange(EXPERTS, dtype=jnp.int32)).astype(jnp.float32)
    chosen = jnp.sum(picked * probabilities[:, None, :], axis=-1)
    gate_values = chosen / jnp.sum(chosen, axis=1, keepdims=True)
    shares = jnp.sum(picked, axis=(0, 1)) / (token_count * TOP)
    balance = EXPERTS * jnp.sum(shares * jnp.sum(probabilities, axis=0))
    return (gate_values, weights[0] * jnp.sum(log_totals * log_totals) + weights[1] * balance)


def column(values, rows):
    return jnp.pad(values, (0, rows - values.shape[0]))[:, None]


def shards(
    inputs,
    grad_out,
    prefix,
    routes,
    priority,
    loss_weights,
    norm_attn,
    norm_moe,
    qkv_weight,
    out_weight,
    bias_table,
    router_weight,
    gate_weight,
    up_weight,
    down_weight,
):
    row_count = inputs.shape[0]
    groups = lax.axis_size("expert")
    columns_of = lax.axis_size("shard")
    place = lax.axis_index("expert")
    length = row_count * groups
    heads_here = HEADS // groups
    width = heads_here * HEAD
    experts_here = EXPERTS // groups
    shard_rows = D // columns_of
    height = slot_rows(experts_here)

    packed_small = jnp.concatenate(
        [
            lax.dynamic_slice(
                qkv_weight, (0, third * D + place * width), (shard_rows, width)
            )
            for third in range(3)
        ]
        + [jnp.pad(router_weight, ((0, 0), (0, spare - EXPERTS)))],
        axis=1,
    )
    table_rows = BUCKETS // columns_of
    table_low = bias_table.astype(jnp.float32).reshape(1, table_rows * HEADS)
    gain_rows = jnp.concatenate(
        [
            norm_attn.astype(jnp.float32)[None],
            norm_moe.astype(jnp.float32)[None],
            jnp.pad(table_low, ((0, 0), (0, shard_rows - table_rows * HEADS))),
            jnp.zeros((5, shard_rows), jnp.float32),
        ],
        axis=0,
    )
    token_routes = routes.reshape(row_count, TOP)
    slots = pair_slots(token_routes, priority.reshape(row_count), experts_here)
    slot_map = (
        jnp.arange(groups * height, dtype=jnp.int32)[:, None] == slots[None, :]
    ).reshape(groups * height, TOP, row_count)
    slot_any = jnp.any(slot_map, axis=1).astype(jnp.bfloat16)
    token_slots = jnp.any(
        slots.reshape(TOP, row_count)[:, :, None] == jnp.arange(groups * height, dtype=jnp.int32),
        axis=0,
    ).astype(jnp.bfloat16)
    slot_pairs = slot_map.astype(jnp.bfloat16).reshape(groups * height, TOP * row_count)
    grad_low = grad_out.reshape(row_count, D)
    grad_slots = nn_dot(slot_any, grad_low).astype(jnp.bfloat16).reshape(groups, height, D)
    _, normed_all, qkv_own, small_full, out_full, far_slots, side_slots, gains = entry_gather(
        inputs.reshape(row_count, D),
        gain_rows,
        packed_small,
        out_weight,
        grad_slots,
        3 * width,
        1,
    )
    normed_all = normed_all.reshape(length, D)
    qkv_own = qkv_own.reshape(length, 3 * width)
    small_full = small_full.reshape(D, 3 * width + spare)
    out_full = out_full.reshape(D, D)
    router_full = small_full[:, 3 * width : 3 * width + EXPERTS]
    gain_attn = gains[:, 0].reshape(D)
    gain_moe = gains[:, 1].reshape(D)
    table_full = gains[:, 2, : table_rows * HEADS].reshape(BUCKETS, HEADS)
    table_own = lax.dynamic_slice_in_dim(
        table_full, place * heads_here, heads_here, 1
    )
    near_ids = jnp.asarray(skew_buckets(), jnp.int32)
    near_hot = (near_ids[:, None] == jnp.arange(BUCKETS, dtype=jnp.int32)).astype(jnp.float32)
    base_bias = (
        jnp.dot(near_hot, table_own, precision=lax.Precision.HIGHEST).reshape(3, 2 * tile, heads_here)
        * log2e
    )
    base_bias = jnp.transpose(base_bias, (2, 0, 1)).reshape(heads_here * 3, 2 * tile)
    far_bias = jnp.stack([table_own[15], table_own[31]], axis=1) * log2e

    mixed_own, totals, grads_received = attend_forward(
        prefix, far_bias, base_bias, qkv_own, grad_slots, far_slots, side_slots, columns_of
    )
    attended = exchange_mixed(mixed_own.reshape(groups, row_count, width), columns_of, 8)

    tokens_in = inputs.reshape(row_count, D).astype(jnp.float32)
    middle = tokens_in + nn_dot(attended, out_full)
    normed_two, norm_two_back = jax.vjp(rms_norm, middle, gain_moe)
    low_two = normed_two.astype(jnp.bfloat16)
    logits = nn_dot(low_two, router_full)
    router_out, router_back = jax.vjp(
        lambda logit_in: router_head(logit_in, token_routes, loss_weights), logits
    )
    gate_values = router_out[0]
    slot_gates = jnp.sum(
        slot_map.astype(jnp.float32) * jnp.transpose(gate_values)[None], axis=1
    )
    fused = columns_of * groups <= part_sources and experts_here == 4
    if fused:
        outgoing = nn_dot(slot_any, low_two).astype(jnp.bfloat16).reshape(groups, height, D)
        gate_block = jnp.pad(
            jnp.sum(slot_gates, axis=1).reshape(groups, 1, height),
            ((0, 0), (0, 7), (0, spare - height)),
        )
    else:
        gate_high = lax.reduce_precision(gate_values, 8, 7)
        gate_parts = jnp.stack([gate_high, gate_values - gate_high], axis=-1).astype(jnp.bfloat16)
        wide_rows = jnp.concatenate(
            [
                jnp.broadcast_to(low_two[None], (TOP, row_count, D)),
                jnp.pad(jnp.transpose(gate_parts, (1, 0, 2)), ((0, 0), (0, 0), (0, spare - 2))),
            ],
            axis=2,
        ).reshape(TOP * row_count, D + spare)
        outgoing = nn_dot(slot_pairs, wide_rows).astype(jnp.bfloat16)
        outgoing = outgoing.reshape(groups, height, D + spare)
    gate_across, up_across, down_across = (
        jnp.transpose(weight, (0, 2, 1)) for weight in (gate_weight, up_weight, down_weight)
    )
    if fused:
        (
            hidden,
            grad_gate,
            grad_up,
            result_part,
            rows_received,
            grad_returned,
            side_returned,
        ) = experts(
            outgoing, gate_block, grads_received, gate_across, up_across, down_across, columns_of
        )
        slot_grads = side_returned[:, 0, :height].reshape(groups * height)
        grad_gates = jnp.sum(
            jnp.where(slot_map, slot_grads[:, None, None], 0.0), axis=0
        )
        grad_gates = jnp.transpose(grad_gates)
        grad_returned = grad_returned.reshape(groups * height, D)
    else:
        rows_received = dispatch(outgoing, columns_of, 2)
        hidden, grad_gate, grad_up, result_part, back_part = expert_act(
            rows_received, grads_received, gate_across, up_across, down_across
        )
        grad_returned = collect(back_part, 3).reshape(groups * height, D + spare)
        grad_gates = jnp.transpose(
            tn_dot(slot_pairs, grad_returned[:, D:])[:, 0].reshape(TOP, row_count)
        )
    grad_low_two = nn_dot(token_slots, grad_returned[:, :D])
    grad_top = grad_low.astype(jnp.float32)
    grad_logits = router_back((grad_gates, jnp.ones((), jnp.float32)))[0]
    low_logits = grad_logits.astype(jnp.bfloat16)
    router_grad = tn_dot(low_two, low_logits)
    grad_low_two = grad_low_two + nt_dot(low_logits, router_full)
    grad_middle_norm, gain_moe_grad = norm_two_back(grad_low_two)
    grad_middle = grad_top + grad_middle_norm
    low_middle = grad_middle.astype(jnp.bfloat16)
    out_grad = tn_dot(attended, low_middle)
    grad_attended = nt_dot(low_middle, out_full).astype(jnp.bfloat16)
    grad_attended = jnp.transpose(grad_attended.reshape(row_count, groups, width), (1, 0, 2))
    grad_mixed = lax.all_to_all(
        grad_attended, "expert", split_axis=0, concat_axis=0, tiled=True
    )
    gate_grad, up_grad, down_grad = expert_weight_grads(
        rows_received, grads_received, hidden, grad_gate, grad_up, 2 if fused else 1
    )
    out_sums = lax.psum_scatter(
        out_grad.astype(jnp.bfloat16), "shard", scatter_dimension=0, tiled=True
    ).reshape(groups, shard_rows // groups, D)
    grad_qkv, near_sums, side_sums, returned, out_piece = attend_backward(
        prefix,
        far_bias,
        base_bias,
        qkv_own,
        mixed_own,
        grad_mixed.reshape(length, width),
        totals,
        result_part,
        out_sums,
        columns_of,
    )
    slot_high = lax.reduce_precision(slot_gates, 8, 7)
    slot_parts = jnp.concatenate([slot_high, slot_gates - slot_high], axis=1).astype(jnp.bfloat16)
    mixture = tn_dot(slot_parts, returned.reshape(groups * height, D))
    mixture = mixture[:row_count] + mixture[row_count:]
    output = (middle + mixture).astype(jnp.bfloat16)

    table_grad = jnp.einsum(
        "hil,ilb->bh",
        near_sums.reshape(heads_here, 3, 2 * tile),
        near_hot.reshape(3, 2 * tile, BUCKETS),
        precision=lax.Precision.HIGHEST,
    )
    far_sums = jnp.sum(side_sums, axis=(2, 3))
    bucket_ids = jnp.arange(BUCKETS, dtype=jnp.int32)[:, None]
    table_grad = table_grad + jnp.where(bucket_ids == 15, far_sums[:, 0][None], 0.0)
    table_grad = table_grad + jnp.where(bucket_ids == 31, far_sums[:, 1][None], 0.0)
    table_column = jnp.pad(
        table_grad.reshape(columns_of, table_rows * heads_here),
        ((0, 0), (0, shard_rows - table_rows * heads_here)),
    ).reshape(D, 1)

    extra = jnp.concatenate(
        [
            jnp.zeros((D, 1), jnp.float32),
            table_column,
            gain_moe_grad[:, None],
            router_grad,
            jnp.zeros((D, spare - 3 - EXPERTS), jnp.float32),
        ],
        axis=1,
    ).astype(jnp.bfloat16)
    grad_projected, last_all, out_all, qkv_full = tail_exchange(
        grad_qkv.reshape(groups, row_count, 3 * width),
        normed_all,
        small_full,
        extra,
        out_piece,
        qkv_weight,
        columns_of,
        7,
    )
    last_all = last_all.reshape(groups, shard_rows, 3 * width + spare)
    out_all = out_all.reshape(shard_rows, D)
    if width % 128 == 0:
        input_grad, qkv_total, out_total, extra_total = finish(
            grad_projected,
            qkv_full,
            last_all,
            inputs.reshape(row_count, D),
            gain_attn[None],
            grad_middle,
            out_all,
            width,
        )
    else:
        grad_projected = jnp.transpose(
            grad_projected.reshape(groups, row_count, 3, width), (1, 2, 0, 3)
        ).reshape(row_count, 3 * D)
        grad_low_one = nt_dot(grad_projected, qkv_full.reshape(D, 3 * D))
        _, norm_one_back = jax.vjp(lambda features: rms_norm(features, gain_attn), tokens_in)
        input_grad = grad_middle + norm_one_back(grad_low_one)[0]
        qkv_total = jnp.transpose(
            last_all[:, :, : 3 * width].reshape(groups, shard_rows, 3, width), (1, 2, 0, 3)
        ).reshape(shard_rows, 3 * D).astype(jnp.float32)
        out_total = out_all.astype(jnp.float32)
        extra_total = jnp.sum(last_all[:, :, 3 * width :].astype(jnp.float32), axis=0).T
    table_part = last_all[:, : table_rows * heads_here, 3 * width + 1].astype(jnp.float32)
    table_total = jnp.transpose(
        table_part.reshape(groups, table_rows, heads_here), (1, 0, 2)
    ).reshape(table_rows, HEADS)
    return (
        output.reshape(row_count, 1, D),
        input_grad.reshape(row_count, 1, D),
        extra_total[0] / norm_attn.astype(jnp.float32),
        extra_total[2],
        qkv_total,
        out_total,
        table_total,
        extra_total[3 : 3 + EXPERTS].T,
        jnp.transpose(gate_grad, (0, 2, 1)),
        jnp.transpose(up_grad, (0, 2, 1)),
        jnp.transpose(down_grad, (0, 2, 1)),
    )


def solution(mesh):
    placed = (
        P("expert", "shard", None),
        P("expert", "shard", None),
        P("shard"),
        P("expert", "shard", None),
        P("expert", "shard", None),
        P(),
        P("shard"),
        P("shard"),
        P("shard", None),
        P("shard", None),
        P("shard", None),
        P("shard", None),
        P("expert", None, "shard"),
        P("expert", None, "shard"),
        P("expert", None, "shard"),
    )
    return jax.shard_map(
        shards,
        mesh=mesh,
        in_specs=placed,
        out_specs=(
            P("expert", "shard", None),
            P("expert", "shard", None),
            P("shard"),
            P("shard"),
            P("shard", None),
            P("shard", None),
            P("shard", None),
            P("shard", None),
            P("expert", None, "shard"),
            P("expert", None, "shard"),
            P("expert", None, "shard"),
        ),
        check_vma=False,
    )
```
